32 devices in a mesh: dp: 4 (over y, x), seq: 8 (over z, core).
Axes of the slice: x: 2, y: 2, z: 4, core: 2. Of those that a mesh axis runs over, the one named last changes fastest.
Arguments:
- patches: bfloat16 [8, 2304, 1280], P('dp', 'seq'), may hold values from -6 to 6
- ln1_gain: bfloat16 [1280], P('dp'), may hold values from 0.099609375 to 1.8984375
- ln1_bias: bfloat16 [1280], P('dp'), may hold values from -3 to 3
- qkv_weight: bfloat16 [1280, 3840], P('dp'), may hold values from -0.15625 to 0.15625
- q_bias: bfloat16 [1280], P('dp'), may hold values from -3 to 3
- v_bias: bfloat16 [1280], P('dp'), may hold values from -3 to 3
- proj_weight: bfloat16 [1280, 1280], P('dp'), may hold values from -6 to 6
- proj_bias: bfloat16 [1280], P('dp'), may hold values from -3 to 3
- ln2_gain: bfloat16 [1280], P('dp'), may hold values from 0.099609375 to 1.8984375
- ln2_bias: bfloat16 [1280], P('dp'), may hold values from -3 to 3
- fc1_weight: bfloat16 [1280, 5120], P('dp'), may hold values from -0.15625 to 0.15625
- fc1_bias: bfloat16 [5120], P('dp'), may hold values from -3 to 3
- fc2_weight: bfloat16 [5120, 1280], P('dp'), may hold values from -0.078125 to 0.078125
- fc2_bias: bfloat16 [1280], P('dp'), may hold values from -3 to 3
- rel_pos_h: bfloat16 [95, 80], replicated, may hold values from -0.5 to 0.5
- rel_pos_w: bfloat16 [95, 80], replicated, may hold values from -0.5 to 0.5
- cotangent: bfloat16 [8, 2304, 1280], P('dp', 'seq'), may hold values from -6 to 6
Outputs:
- output: bfloat16 [8, 2304, 1280], P('dp', 'seq')
- grad_patches: bfloat16 [8, 2304, 1280], P('dp', 'seq')
- grad_ln1_gain: float32 [1280], P('dp')
- grad_ln1_bias: float32 [1280], P('dp')
- grad_qkv_weight: float32 [1280, 3840], P('dp', 'seq')
- grad_q_bias: float32 [1280], P('dp')
- grad_v_bias: float32 [1280], P('dp')
- grad_proj_weight: float32 [1280, 1280], P('dp', 'seq')
- grad_proj_bias: float32 [1280], P('dp')
- grad_ln2_gain: float32 [1280], P('dp')
- grad_ln2_bias: float32 [1280], P('dp')
- grad_fc1_weight: float32 [1280, 5120], P('dp', 'seq')
- grad_fc1_bias: float32 [5120], P('dp')
- grad_fc2_weight: float32 [5120, 1280], P('dp', 'seq')
- grad_fc2_bias: float32 [1280], P('dp')
- grad_rel_pos_h: float32 [95, 80], replicated
- grad_rel_pos_w: float32 [95, 80], replicated
The draws below stay inside these ranges and needn't reach their ends.
All inputs are finite; a program needn't handle non-finite values.
Results may differ from the reference program's by a relative error of at most 0.017.
Values may be sent and summed in bfloat16 or wider, within the bound.
A program may use at most 256 MiB of HBM per device.

```python
from functools import partial
import jax
import jax.numpy as jnp
from jax import lax

D = 1280
H = 16
HD = 80
FF = 5120
SIDE = 48
IMAGES = 8
SEQLEN = 2304


def block_levels(key, dims, shards, least, largest):
    factor_of = 1.0
    for dim, shards_of in shards:
        heights = jax.random.uniform(jax.random.fold_in(jax.random.fold_in(key, 6), dim), (shards_of,), jnp.float32, least / len(shards), largest / len(shards))
        factor_of = factor_of * jnp.repeat(jnp.exp(heights), dims[dim] // shards_of).reshape((-1,) + (1,) * (len(dims) - 1 - dim))
    return factor_of


def scatter_about(own_key, shape, scale, bound, pieces=(), held_as=jnp.bfloat16):
    values = scale * jax.random.normal(own_key, shape, jnp.float32)
    if pieces:
        values = values * block_levels(own_key, shape, pieces, -0.22, 0.18)
    return jnp.clip(values, -bound, bound).astype(held_as)


def setup_inputs(seed: int = 0) -> dict:
    arg_keys = jax.random.split(jax.random.key(seed), 18)
    return {
        "patches": scatter_about(arg_keys[0], (IMAGES, SEQLEN, D), 1.0, 6.0, ((0, 4), (1, 8))),
        "ln1_gain": jnp.clip(1.0 + 0.18 * jax.random.normal(arg_keys[1], (D,), jnp.float32), 0.099609375, 1.8984375).astype(jnp.bfloat16),
        "ln1_bias": scatter_about(arg_keys[2], (D,), 0.5, 3.0, ((0, 4),)),
        "qkv_weight": scatter_about(arg_keys[3], (D, 3 * D), D ** -0.5, 0.15625, ((0, 4),)),
        "q_bias": scatter_about(arg_keys[4], (D,), 0.5, 3.0, ((0, 4),)),
        "v_bias": scatter_about(arg_keys[5], (D,), 0.5, 3.0, ((0, 4),)),
        "proj_weight": scatter_about(arg_keys[6], (D, D), (max(1, D // 1024)) ** -0.5, 6.0, ((0, 4),)),
        "proj_bias": scatter_about(arg_keys[7], (D,), 0.5, 3.0, ((0, 4),)),
        "ln2_gain": jnp.clip(1.0 + 0.18 * jax.random.normal(arg_keys[8], (D,), jnp.float32), 0.099609375, 1.8984375).astype(jnp.bfloat16),
        "ln2_bias": scatter_about(arg_keys[9], (D,), 0.5, 3.0, ((0, 4),)),
        "fc1_weight": scatter_about(arg_keys[10], (D, FF), D ** -0.5, 0.15625, ((0, 4),)),
        "fc1_bias": scatter_about(arg_keys[11], (FF,), 0.5, 3.0, ((0, 4),)),
        "fc2_weight": scatter_about(arg_keys[12], (FF, D), FF ** -0.5, 0.078125, ((0, 4),)),
        "fc2_bias": scatter_about(arg_keys[13], (D,), 0.5, 3.0, ((0, 4),)),
        "rel_pos_h": scatter_about(arg_keys[14], (2 * SIDE - 1, HD), 0.08, 0.5),
        "rel_pos_w": scatter_about(arg_keys[15], (2 * SIDE - 1, HD), 0.08, 0.5),
        "cotangent": scatter_about(arg_keys[16], (IMAGES, SEQLEN, D), 1.0, 6.0, ((0, 4), (1, 8))),
    }


EPSILON = 1e-06
HIGHEST = lax.Precision.HIGHEST

@jax.custom_vjp
def low(v):
    return lax.optimization_barrier(v.astype(jnp.bfloat16)).astype(jnp.float32)

@jax.custom_vjp
def low_back(v):
    return v

def low_keep(v):
    return (low(v), None)

def low_pass(kept, grad):
    return (grad,)

def back_keep(v):
    return (v, None)

def back_low(kept, grad):
    return (low(grad),)
low.defvjp(low_keep, low_pass)
low_back.defvjp(back_keep, back_low)

def layer_norm(values, gain_vec, shift_vec):
    center = values - lax.optimization_barrier(jnp.mean(values, -1, keepdims=True))
    spread = lax.optimization_barrier(jnp.mean(center * center, -1, keepdims=True))
    return center * lax.rsqrt(spread + EPSILON) * gain_vec + shift_vec

def rel_tables(rel_h, rel_w):
    places = jnp.arange(SIDE)
    lookup = places[:, None] - places[None, :] + (SIDE - 1)
    return (rel_h[lookup], rel_w[lookup])

def split_heads(flat):
    return flat.reshape(SIDE * SIDE, H, HD).transpose(1, 0, 2)

def head_attend(triple, table_h, table_w):
    query_rows, key_rows, value_rows = triple
    block_rows = SIDE * SIDE // max(1, SIDE * SIDE // 512)
    per_block = block_rows // SIDE
    blocks = SIDE * SIDE // block_rows

    def block_out(bundle):
        query_block, table_rows = bundle
        scores = jnp.dot(query_block, key_rows.T, precision=HIGHEST) * HD ** (-0.5)
        query_grid = query_block.reshape(per_block, SIDE, HD)
        rel_rows = jnp.einsum('hwc,hkc->hwk', query_grid, table_rows, precision=HIGHEST)
        rel_cols = jnp.einsum('hwc,wkc->hwk', query_grid, table_w, precision=HIGHEST)
        scores = scores.reshape(per_block, SIDE, SIDE, SIDE) + rel_rows[:, :, :, None] + rel_cols[:, :, None, :]
        scores = low_back(scores.reshape(block_rows, SIDE * SIDE))
        row_max = lax.optimization_barrier(jnp.max(scores, -1, keepdims=True))
        exp_scores = jnp.exp(scores - row_max)
        attn_probs = exp_scores / lax.optimization_barrier(jnp.sum(exp_scores, -1, keepdims=True))
        return jnp.dot(low(attn_probs), value_rows, precision=HIGHEST)
    outputs = lax.map(jax.checkpoint(block_out), (query_rows.reshape(blocks, block_rows, HD), table_h.reshape(blocks, per_block, SIDE, HD)))
    return outputs.reshape(SIDE * SIDE, HD)

def forward(params, one_image):
    gain_one, shift_one, qkv_full, q_shift, v_shift, proj_full, proj_shift, gain_two, shift_two, fc1_full, fc1_shift, fc2_full, fc2_shift, rel_h, rel_w = params
    normed = low(layer_norm(one_image, gain_one, shift_one))
    joined = jnp.dot(normed, qkv_full, precision=HIGHEST)
    queries = low(low_back(joined[:, :D] + q_shift))
    key_part = low(low_back(joined[:, D:2 * D]))
    value_part = low(low_back(joined[:, 2 * D:] + v_shift))
    table_h, table_w = rel_tables(rel_h, rel_w)
    outputs = lax.map(partial(head_attend, table_h=table_h, table_w=table_w), (split_heads(queries), split_heads(key_part), split_heads(value_part)))
    mixed_rows = low(low_back(outputs.transpose(1, 0, 2).reshape(SIDE * SIDE, D)))
    middle = one_image + low_back(jnp.dot(mixed_rows, proj_full, precision=HIGHEST) + proj_shift)
    normed_two = low(layer_norm(middle, gain_two, shift_two))
    before_act = low_back(jnp.dot(normed_two, fc1_full, precision=HIGHEST) + fc1_shift)
    activated = low(jax.nn.gelu(before_act, approximate=False))
    return middle + low_back(jnp.dot(activated, fc2_full, precision=HIGHEST) + fc2_shift)

def reference(patches, ln1_gain, ln1_bias, qkv_weight, q_bias, v_bias, proj_weight, proj_bias, ln2_gain, ln2_bias, fc1_weight, fc1_bias, fc2_weight, fc2_bias, rel_pos_h, rel_pos_w, cotangent):
    params = tuple((member.astype(jnp.float32) for member in (ln1_gain, ln1_bias, qkv_weight, q_bias, v_bias, proj_weight, proj_bias, ln2_gain, ln2_bias, fc1_weight, fc1_bias, fc2_weight, fc2_bias, rel_pos_h, rel_pos_w)))

    def per_image(totals, inputs_pair):
        one_image, grad_image_out = inputs_pair
        result, pullback = jax.vjp(forward, params, one_image.astype(jnp.float32))
        grad_params, grad_image = pullback(grad_image_out.astype(jnp.float32))
        totals = jax.tree.map(jnp.add, totals, grad_params)
        return (totals, (result.astype(jnp.bfloat16), grad_image.astype(jnp.bfloat16)))
    starting = tuple((jnp.zeros(member.shape, jnp.float32) for member in params))
    totals, (output, grad_patches) = lax.scan(per_image, starting, (patches, cotangent))
    return (output, grad_patches, totals[0], totals[1], totals[2], totals[3], totals[4], totals[5], totals[6], totals[7], totals[8], totals[9], totals[10], totals[11], totals[12], totals[13], totals[14])
```

```python
import math
from functools import partial

import jax
import jax.numpy as jnp
from jax import lax
from jax.experimental import pallas as pl
from jax.experimental.pallas import tpu as pltpu
from jax.sharding import PartitionSpec as P

H = 16
HD = 80


EPSILON = 1e-06
ROWS_DIMS = (((0,), (0,)), ((), ()))
COLS_DIMS = (((1,), (1,)), ((), ()))


NT = (((1,), (1,)), ((), ()))
TN = (((0,), (0,)), ((), ()))
BF = jnp.bfloat16
F32 = jnp.float32
LOG2E = 1.4426950408889634


def dot(a, b, dims=(((1,), (0,)), ((), ()))):
    return lax.dot_general(a, b, dims, preferred_element_type=F32)


def hot_table(seq_len, side):
    token = lax.broadcasted_iota(jnp.int32, (seq_len, 256), 0)
    lane = lax.broadcasted_iota(jnp.int32, (seq_len, 256), 1)
    row_hit = (lane >= HD) & (token // side == lane - HD)
    col_hit = (lane >= HD + side) & (token % side == lane - HD - side)
    ones = (lane >= HD + 2 * side) & (lane < HD + 2 * side + 3)
    return (row_hit | col_hit | ones).astype(BF)


def flip_tables(rel_h, rel_w):
    entries = rel_h.shape[0]
    pad = ((0, 128 - entries), (0, 0))
    return jnp.concatenate([jnp.pad(rel_h[::-1], pad), jnp.pad(rel_w[::-1], pad)], 0)


def fwd_kernel(heads, side, tq, x_ref, hot_ref, f_ref, o_ref, qa_ref, kp, vp, osc):
    seq_len = x_ref.shape[0]
    lanes = heads * HD
    step = pl.program_id(0)
    factor = LOG2E / math.sqrt(HD)

    @pl.when(step == 0)
    def _():
        rows = seq_len // 9

        def prep(i, c):
            part = pl.ds(pl.multiple_of(i * rows, rows), rows)
            hot = hot_ref[part, :]
            for h in range(heads):
                kp[h, part, :] = hot
                kp[h, part, 0:HD] = x_ref[part, lanes + h * HD : lanes + (h + 1) * HD]
                vp[h, part, :] = jnp.ones((rows, 128), BF)
                vp[h, part, 0:HD] = x_ref[part, 2 * lanes + h * HD : 2 * lanes + (h + 1) * HD]
            return c

        lax.fori_loop(0, 9, prep, 0)

    base = pl.ds(pl.multiple_of(step * tq, tq), tq)
    groups = tq // side
    lane = lax.broadcasted_iota(jnp.int32, (tq, 128), 1)
    for h in range(heads):
        q = x_ref[base, h * HD : (h + 1) * HD]
        g = dot(q, f_ref[...], NT) * math.sqrt(HD)
        gh = [
            pltpu.roll(g[i * side : (i + 1) * side, :128], 33 + step * groups + i, axis=1)
            for i in range(groups)
        ]
        gw = [
            pltpu.roll(g[i * side : (i + 1) * side, 128:], 81, axis=1, stride=1, stride_axis=0)
            for i in range(groups)
        ]
        qa_ref[h, :, 0:128] = jnp.concatenate(gh, 0).astype(BF)
        qa_ref[h, :, 0:HD] = q
        qa_ref[h, :, 128:256] = jnp.where(lane < side, jnp.concatenate(gw, 0), 0.0).astype(BF)

    def one(h, c):
        s = dot(qa_ref[h], kp[h], NT)
        m = jnp.max(s, -1, keepdims=True)
        p = jnp.exp2((s - m) * factor).astype(BF)
        o = dot(p, vp[h])
        total = o[:, HD : HD + 1]
        osc[h] = o / total
        norm = m + jnp.log2(total) / factor
        hi = norm.astype(BF).astype(F32)
        mid = (norm - hi).astype(BF).astype(F32)
        low = norm - hi - mid
        old = qa_ref[h, :, 128:256].astype(F32)
        old = jnp.where(lane == side, -hi, old)
        old = jnp.where(lane == side + 1, -mid, old)
        old = jnp.where(lane == side + 2, -low, old)
        qa_ref[h, :, 128:256] = old.astype(BF)
        return c

    lax.fori_loop(0, heads, one, 0)
    for h in range(heads):
        o_ref[:, h * HD : (h + 1) * HD] = osc[h][:, 0:HD].astype(BF)


def attention_forward(x, hot, tables, side, tq=192):
    seq_len, width = x.shape
    heads = width // (3 * HD)
    return pl.pallas_call(
        partial(fwd_kernel, heads, side, tq),
        grid=(seq_len // tq,),
        in_specs=[
            pl.BlockSpec((seq_len, width), lambda i: (0, 0), pipeline_mode=pl.Buffered(1)),
            pl.BlockSpec((seq_len, 256), lambda i: (0, 0), pipeline_mode=pl.Buffered(1)),
            pl.BlockSpec((256, HD), lambda i: (0, 0), pipeline_mode=pl.Buffered(1)),
        ],
        out_specs=[
            pl.BlockSpec((tq, heads * HD), lambda i: (i, 0)),
            pl.BlockSpec((heads, tq, 256), lambda i: (0, i, 0)),
        ],
        out_shape=[
            jax.ShapeDtypeStruct((seq_len, heads * HD), BF),
            jax.ShapeDtypeStruct((heads, seq_len, 256), BF),
        ],
        scratch_shapes=[
            pltpu.VMEM((heads, seq_len, 256), BF),
            pltpu.VMEM((heads, seq_len, 128), BF),
            pltpu.VMEM((heads, tq, 128), F32),
        ],
        compiler_params=pltpu.CompilerParams(
            dimension_semantics=("arbitrary",), vmem_limit_bytes=60 << 20
        ),
        name="attention_forward",
    )(x, hot, tables)


def bwd_kernel(heads, side, tb, uc, x_ref, hot_ref, f_ref, qa_ref, o_ref, go_ref, dx_ref, gt_ref, kp, kt, vp, dop, dk, dv, dq):
    seq_len = x_ref.shape[0]
    lanes = heads * HD
    h = pl.program_id(0)
    step = pl.program_id(1)
    factor = LOG2E / math.sqrt(HD)
    scale = HD ** (-0.5)

    @pl.when((h == 0) & (step == 0))
    def _():
        gt_ref[...] = jnp.zeros_like(gt_ref)
        rows = seq_len // 9

        def prep(i, c):
            part = pl.ds(pl.multiple_of(i * rows, rows), rows)
            hot = hot_ref[part, :]
            lane = lax.broadcasted_iota(jnp.int32, (rows, 128), 1)
            for n in range(heads):
                kp[n, part, :] = hot
                kp[n, part, 0:HD] = x_ref[part, lanes + n * HD : lanes + (n + 1) * HD]
                vp[n, part, :] = jnp.ones((rows, 128), BF)
                vp[n, part, 0:HD] = x_ref[part, 2 * lanes + n * HD : 2 * lanes + (n + 1) * HD]
                go = go_ref[part, n * HD : (n + 1) * HD]
                inner = jnp.sum(
                    go.astype(F32) * o_ref[part, n * HD : (n + 1) * HD].astype(F32), -1, keepdims=True
                )
                hi = inner.astype(BF).astype(F32)
                low = inner - hi
                tail = jnp.where(lane == HD, -hi, jnp.where(lane == HD + 1, -low, 0.0))
                dop[n, part, :] = tail.astype(BF)
                dop[n, part, 0:HD] = go
                kt[n, :, part] = kp[n, part, :].T
            return c

        lax.fori_loop(0, 9, prep, 0)

    @pl.when(step == 0)
    def _():
        dk[h] = jnp.zeros_like(dk[h])
        dv[h] = jnp.zeros_like(dv[h])

    base = pl.ds(pl.multiple_of(step * tb, tb), tb)
    qa = qa_ref[0]
    do = dop[h, base, :]

    def one(j, acc):
        part = pl.ds(pl.multiple_of(j * uc, uc), uc)
        s = dot(kp[h, part, :], qa, NT)
        dp = dot(vp[h, part, :], do, NT)
        p = jnp.exp2(s * factor)
        ds = (p * dp).astype(BF)
        dv[h, part, :] += dot(p.astype(BF), do)
        dk[h, part, :] += dot(ds, qa[:, 0:128])
        return acc + dot(kt[h, :, part], ds)

    acc = lax.fori_loop(0, seq_len // uc, one, jnp.zeros((256, tb), F32), unroll=True)
    acc = acc.T
    lane = lax.broadcasted_iota(jnp.int32, (tb, 128), 1)
    groups = tb // side
    first = jnp.where(lane < HD, 0.0, acc[:, :128])
    second = jnp.where(lane < side, acc[:, 128:], 0.0)
    back_h = [
        pltpu.roll(first[i * side : (i + 1) * side], 256 - 33 - step * groups - i, axis=1)
        for i in range(groups)
    ]
    back_w = [
        unroll_w(second[i * side : (i + 1) * side], side) for i in range(groups)
    ]
    both = jnp.concatenate([jnp.concatenate(back_h, 0), jnp.concatenate(back_w, 0)], 1).astype(BF)
    rel = dot(both, f_ref[...])
    dq[h, base, :] = acc[:, :HD] * scale + rel
    gt_ref[...] += dot(both, qa[:, 0:128], TN)

    @pl.when((h == heads - 1) & (step == pl.num_programs(1) - 1))
    def _():
        rows = seq_len // 9

        def post(i, c):
            part = pl.ds(pl.multiple_of(i * rows, rows), rows)
            for n in range(heads):
                dx_ref[part, n * HD : (n + 1) * HD] = dq[n, part, :].astype(BF)
                dx_ref[part, lanes + n * HD : lanes + (n + 1) * HD] = (dk[n, part, 0:HD] * scale).astype(BF)
                dx_ref[part, 2 * lanes + n * HD : 2 * lanes + (n + 1) * HD] = dv[n, part, 0:HD].astype(BF)
            return c

        lax.fori_loop(0, 9, post, 0)


def unroll_w(val, side):
    out = val
    row = lax.broadcasted_iota(jnp.int32, val.shape, 0)
    shift = side - 1 - row
    bit = 1
    while bit < side:
        out = jnp.where((shift & bit) != 0, pltpu.roll(out, bit, axis=1), out)
        bit *= 2
    return out


def attention_backward(x, hot, tables, qa, o, go, side, tb=768, uc=256):
    seq_len, width = x.shape
    heads = width // (3 * HD)
    whole = lambda *shape: pl.BlockSpec(shape, lambda h, i: (0,) * len(shape), pipeline_mode=pl.Buffered(1))
    return pl.pallas_call(
        partial(bwd_kernel, heads, side, tb, uc),
        grid=(heads, seq_len // tb),
        in_specs=[
            whole(seq_len, width),
            whole(seq_len, 256),
            whole(256, HD),
            pl.BlockSpec((1, tb, 256), lambda h, i: (h, i, 0)),
            whole(seq_len, heads * HD),
            whole(seq_len, heads * HD),
        ],
        out_specs=[
            whole(seq_len, width),
            whole(256, 128),
        ],
        out_shape=[
            jax.ShapeDtypeStruct((seq_len, width), BF),
            jax.ShapeDtypeStruct((256, 128), F32),
        ],
        scratch_shapes=[
            pltpu.VMEM((heads, seq_len, 256), BF),
            pltpu.VMEM((heads, 256, seq_len), BF),
            pltpu.VMEM((heads, seq_len, 128), BF),
            pltpu.VMEM((heads, seq_len, 128), BF),
            pltpu.VMEM((heads, seq_len, 128), F32),
            pltpu.VMEM((heads, seq_len, 128), F32),
            pltpu.VMEM((heads, seq_len, HD), F32),
        ],
        compiler_params=pltpu.CompilerParams(
            dimension_semantics=("arbitrary", "arbitrary"), vmem_limit_bytes=63 << 20
        ),
        name="attention_backward",
    )(x, hot, tables, qa, o, go)


def layer_norm(values, gain_vec, shift_vec):
    center = values - jnp.mean(values, -1, keepdims=True)
    spread = jnp.mean(center * center, -1, keepdims=True)
    return center * lax.rsqrt(spread + EPSILON) * gain_vec + shift_vec


def norm_back(values, gain_vec, upstream):

    def normalize(inputs_in, gains_in):
        return layer_norm(inputs_in, gains_in, 0.0)

    unused, pullback = jax.vjp(normalize, values, gain_vec)
    grad_values, grad_gain = pullback(upstream)
    return (grad_values, grad_gain, jnp.sum(upstream, 0))


def to_heads(parts, images, ranks):
    group = ranks // images
    stacked = jnp.stack([p.reshape(images, -1, group, H * HD // group) for p in parts], 3)
    rows = stacked.shape[1]
    return stacked.transpose(0, 2, 1, 3, 4).reshape(ranks, rows, len(parts) * H * HD // group)


def from_heads(stacked, images, parts):
    ranks, rows, width = stacked.shape
    group = ranks // images
    split = stacked.reshape(images, group, rows, parts, width // parts)
    return split.transpose(0, 2, 3, 1, 4).reshape(images * rows, parts * H * HD)


def exchange(stacked):
    return lax.all_to_all(stacked, "seq", split_axis=0, concat_axis=0, tiled=True)


def on_device(
    patches,
    ln1_gain,
    ln1_bias,
    qkv_weight,
    q_bias,
    v_bias,
    proj_weight,
    proj_bias,
    ln2_gain,
    ln2_bias,
    fc1_weight,
    fc1_bias,
    fc2_weight,
    fc2_bias,
    rel_pos_h,
    rel_pos_w,
    cotangent,
):
    images, row_count, model_width = patches.shape
    gathered = (
        lax.all_gather(ln1_gain, "dp", axis=0, tiled=True),
        lax.all_gather(ln1_bias, "dp", axis=0, tiled=True),
        lax.all_gather(qkv_weight, "dp", axis=0, tiled=True),
        lax.all_gather(q_bias, "dp", axis=0, tiled=True),
        lax.all_gather(v_bias, "dp", axis=0, tiled=True),
        lax.all_gather(proj_weight, "dp", axis=0, tiled=True),
        lax.all_gather(proj_bias, "dp", axis=0, tiled=True),
        lax.all_gather(ln2_gain, "dp", axis=0, tiled=True),
        lax.all_gather(ln2_bias, "dp", axis=0, tiled=True),
        lax.all_gather(fc1_weight, "dp", axis=0, tiled=True),
        lax.all_gather(fc1_bias, "dp", axis=0, tiled=True),
        lax.all_gather(fc2_weight, "dp", axis=0, tiled=True),
        lax.all_gather(fc2_bias, "dp", axis=0, tiled=True),
    )
    (
        gain_one,
        shift_one,
        qkv_full,
        q_shift,
        v_shift,
        proj_full,
        proj_shift,
        gain_two,
        shift_two,
        fc1_full,
        fc1_shift,
        fc2_full,
        fc2_shift,
    ) = gathered
    inputs_f = patches.reshape(images * row_count, model_width).astype(jnp.float32)
    normed = layer_norm(
        inputs_f, gain_one.astype(jnp.float32), shift_one.astype(jnp.float32)
    ).astype(jnp.bfloat16)
    joined = jnp.dot(normed, qkv_full, preferred_element_type=jnp.float32)
    queries = (joined[:, :model_width] + q_shift.astype(jnp.float32)).astype(jnp.bfloat16)
    key_part = joined[:, model_width : 2 * model_width].astype(jnp.bfloat16)
    value_part = (joined[:, 2 * model_width :] + v_shift.astype(jnp.float32)).astype(jnp.bfloat16)
    ranks = lax.axis_size("seq")
    head_rows = exchange(to_heads((queries, key_part, value_part), images, ranks))
    seq_len = ranks * row_count
    head_rows = head_rows.reshape(seq_len, -1)
    side = (rel_pos_h.shape[0] + 1) // 2
    hot = hot_table(seq_len, side)
    tables = flip_tables(rel_pos_h, rel_pos_w)
    attended, query_aug = attention_forward(head_rows, hot, tables, side)
    mixed_rows = from_heads(exchange(attended.reshape(ranks, row_count, -1)), images, 1)
    middle = (
        inputs_f
        + jnp.dot(mixed_rows, proj_full, preferred_element_type=jnp.float32)
        + proj_shift.astype(jnp.float32)
    )
    normed_two = layer_norm(
        middle, gain_two.astype(jnp.float32), shift_two.astype(jnp.float32)
    ).astype(jnp.bfloat16)
    before_act = jnp.dot(
        normed_two, fc1_full, preferred_element_type=jnp.float32
    ) + fc1_shift.astype(jnp.float32)
    activated = jax.nn.gelu(before_act, approximate=False).astype(jnp.bfloat16)
    result = (
        middle
        + jnp.dot(activated, fc2_full, preferred_element_type=jnp.float32)
        + fc2_shift.astype(jnp.float32)
    )
    output = result.astype(jnp.bfloat16).reshape(images, row_count, model_width)
    qkv_back, proj_back, fc1_back, fc2_back = (qkv_full, proj_full, fc1_full, fc2_full)
    gain_one_back, gain_two_back = (gain_one, gain_two)
    grad_out = cotangent.reshape(images * row_count, model_width).astype(jnp.float32)
    grad_branch = grad_out.astype(jnp.bfloat16)
    grad_fc2 = lax.dot_general(
        activated, grad_branch, ROWS_DIMS, preferred_element_type=jnp.float32
    )
    grad_fc2_shift = jnp.sum(grad_branch.astype(jnp.float32), 0)
    grad_activated = lax.dot_general(
        grad_branch, fc2_back, COLS_DIMS, preferred_element_type=jnp.float32
    )
    unused, gelu_pull = jax.vjp(partial(jax.nn.gelu, approximate=False), before_act)
    grad_before = gelu_pull(grad_activated)[0].astype(jnp.bfloat16)
    grad_fc1 = lax.dot_general(
        normed_two, grad_before, ROWS_DIMS, preferred_element_type=jnp.float32
    )
    grad_fc1_shift = jnp.sum(grad_before.astype(jnp.float32), 0)
    grad_normed_two = lax.dot_general(
        grad_before, fc1_back, COLS_DIMS, preferred_element_type=jnp.float32
    )
    grad_middle_norm, grad_gain_two, grad_shift_two = norm_back(
        middle, gain_two_back.astype(jnp.float32), grad_normed_two
    )
    grad_middle = grad_out + grad_middle_norm
    grad_proj_in = grad_middle.astype(jnp.bfloat16)
    grad_proj = lax.dot_general(
        mixed_rows, grad_proj_in, ROWS_DIMS, preferred_element_type=jnp.float32
    )
    grad_proj_shift = jnp.sum(grad_proj_in.astype(jnp.float32), 0)
    grad_mixed = lax.dot_general(
        grad_proj_in, proj_back, COLS_DIMS, preferred_element_type=jnp.float32
    ).astype(jnp.bfloat16)
    grad_heads = exchange(to_heads((grad_mixed,), images, ranks)).reshape(seq_len, -1)
    grad_rows, grad_tables = attention_backward(
        head_rows, hot, tables, query_aug, attended, grad_heads, side
    )
    grad_joined = from_heads(exchange(grad_rows.reshape(ranks, row_count, -1)), images, 3)
    grad_queries = grad_joined[:, :model_width]
    grad_value_part = grad_joined[:, 2 * model_width :]
    grad_qkv = lax.dot_general(normed, grad_joined, ROWS_DIMS, preferred_element_type=jnp.float32)
    grad_q_shift = jnp.sum(grad_queries.astype(jnp.float32), 0)
    grad_v_shift = jnp.sum(grad_value_part.astype(jnp.float32), 0)
    grad_normed = lax.dot_general(
        grad_joined, qkv_back, COLS_DIMS, preferred_element_type=jnp.float32
    )
    grad_inputs_norm, grad_gain_one, grad_shift_one = norm_back(
        inputs_f, gain_one_back.astype(jnp.float32), grad_normed
    )
    grad_patches = (
        (grad_middle + grad_inputs_norm)
        .astype(jnp.bfloat16)
        .reshape(images, row_count, model_width)
    )
    entries = rel_pos_h.shape[0]
    grad_rel_h = grad_tables[:entries, :HD][::-1]
    grad_rel_w = grad_tables[128 : 128 + entries, :HD][::-1]
    matrix_sums = (
        lax.psum_scatter(
            grad_qkv.astype(jnp.bfloat16), "seq", scatter_dimension=1, tiled=True
        ).astype(jnp.float32),
        lax.psum_scatter(
            grad_proj.astype(jnp.bfloat16), "seq", scatter_dimension=1, tiled=True
        ).astype(jnp.float32),
        lax.psum_scatter(
            grad_fc1.astype(jnp.bfloat16), "seq", scatter_dimension=1, tiled=True
        ).astype(jnp.float32),
        lax.psum_scatter(
            grad_fc2.astype(jnp.bfloat16), "seq", scatter_dimension=1, tiled=True
        ).astype(jnp.float32),
    )
    vector_sums = (
        lax.psum(grad_gain_one.astype(jnp.bfloat16), "seq").astype(jnp.float32),
        lax.psum(grad_shift_one.astype(jnp.bfloat16), "seq").astype(jnp.float32),
        lax.psum(grad_q_shift.astype(jnp.bfloat16), "seq").astype(jnp.float32),
        lax.psum(grad_v_shift.astype(jnp.bfloat16), "seq").astype(jnp.float32),
        lax.psum(grad_proj_shift.astype(jnp.bfloat16), "seq").astype(jnp.float32),
        lax.psum(grad_gain_two.astype(jnp.bfloat16), "seq").astype(jnp.float32),
        lax.psum(grad_shift_two.astype(jnp.bfloat16), "seq").astype(jnp.float32),
        lax.psum(grad_fc1_shift.astype(jnp.bfloat16), "seq").astype(jnp.float32),
        lax.psum(grad_fc2_shift.astype(jnp.bfloat16), "seq").astype(jnp.float32),
    )
    owned = (
        lax.psum_scatter(
            matrix_sums[0].astype(jnp.bfloat16), "dp", scatter_dimension=0, tiled=True
        ).astype(jnp.float32),
        lax.psum_scatter(
            matrix_sums[1].astype(jnp.bfloat16), "dp", scatter_dimension=0, tiled=True
        ).astype(jnp.float32),
        lax.psum_scatter(
            matrix_sums[2].astype(jnp.bfloat16), "dp", scatter_dimension=0, tiled=True
        ).astype(jnp.float32),
        lax.psum_scatter(
            matrix_sums[3].astype(jnp.bfloat16), "dp", scatter_dimension=0, tiled=True
        ).astype(jnp.float32),
        lax.psum_scatter(
            vector_sums[0].astype(jnp.bfloat16), "dp", scatter_dimension=0, tiled=True
        ).astype(jnp.float32),
        lax.psum_scatter(
            vector_sums[1].astype(jnp.bfloat16), "dp", scatter_dimension=0, tiled=True
        ).astype(jnp.float32),
        lax.psum_scatter(
            vector_sums[2].astype(jnp.bfloat16), "dp", scatter_dimension=0, tiled=True
        ).astype(jnp.float32),
        lax.psum_scatter(
            vector_sums[3].astype(jnp.bfloat16), "dp", scatter_dimension=0, tiled=True
        ).astype(jnp.float32),
        lax.psum_scatter(
            vector_sums[4].astype(jnp.bfloat16), "dp", scatter_dimension=0, tiled=True
        ).astype(jnp.float32),
        lax.psum_scatter(
            vector_sums[5].astype(jnp.bfloat16), "dp", scatter_dimension=0, tiled=True
        ).astype(jnp.float32),
        lax.psum_scatter(
            vector_sums[6].astype(jnp.bfloat16), "dp", scatter_dimension=0, tiled=True
        ).astype(jnp.float32),
        lax.psum_scatter(
            vector_sums[7].astype(jnp.bfloat16), "dp", scatter_dimension=0, tiled=True
        ).astype(jnp.float32),
        lax.psum_scatter(
            vector_sums[8].astype(jnp.bfloat16), "dp", scatter_dimension=0, tiled=True
        ).astype(jnp.float32),
    )
    table_sums = lax.psum((grad_rel_h, grad_rel_w), ("dp", "seq"))
    return (
        output,
        grad_patches,
        owned[4],
        owned[5],
        owned[0],
        owned[6],
        owned[7],
        owned[1],
        owned[8],
        owned[9],
        owned[10],
        owned[2],
        owned[11],
        owned[3],
        owned[12],
        table_sums[0],
        table_sums[1],
    )


def solution(mesh):
    placed = (
        P("dp", "seq", None),
        P("dp"),
        P("dp"),
        P("dp", None),
        P("dp"),
        P("dp"),
        P("dp", None),
        P("dp"),
        P("dp"),
        P("dp"),
        P("dp", None),
        P("dp"),
        P("dp", None),
        P("dp"),
        P(),
        P(),
        P("dp", "seq", None),
    )
    return jax.shard_map(
        on_device,
        mesh=mesh,
        in_specs=placed,
        out_specs=(
            P("dp", "seq", None),
            P("dp", "seq", None),
            P("dp"),
            P("dp"),
            P("dp", "seq"),
            P("dp"),
            P("dp"),
            P("dp", "seq"),
            P("dp"),
            P("dp"),
            P("dp"),
            P("dp", "seq"),
            P("dp"),
            P("dp", "seq"),
            P("dp"),
            P(),
            P(),
        ),
        check_vma=False,
    )
```

```python
import math
from functools import partial

import jax
import jax.numpy as jnp
from jax import lax
from jax.experimental import pallas as pl
from jax.experimental.pallas import tpu as pltpu
from jax.sharding import PartitionSpec as P

H = 16
HD = 80
EPSILON = 1e-06
ROWS_DIMS = (((0,), (0,)), ((), ()))
COLS_DIMS = (((1,), (1,)), ((), ()))
NT = (((1,), (1,)), ((), ()))
TN = (((0,), (0,)), ((), ()))
BF = jnp.bfloat16
F32 = jnp.float32
LOG2E = 1.4426950408889634


def dot(a, b, dims=(((1,), (0,)), ((), ()))):
    return lax.dot_general(a, b, dims, preferred_element_type=F32)


def hot_table(seq_len, side):
    token = lax.broadcasted_iota(jnp.int32, (seq_len, 256), 0)
    lane = lax.broadcasted_iota(jnp.int32, (seq_len, 256), 1)
    row_hit = (lane >= HD) & (token // side == lane - HD)
    col_hit = (lane >= HD + side) & (token % side == lane - HD - side)
    ones = (lane >= HD + 2 * side) & (lane < HD + 2 * side + 3)
    return (row_hit | col_hit | ones).astype(BF)


def flip_tables(rel_h, rel_w):
    entries = rel_h.shape[0]
    pad = ((0, 128 - entries), (0, 0))
    return jnp.concatenate([jnp.pad(rel_h[::-1], pad), jnp.pad(rel_w[::-1], pad)], 0)


def fwd_kernel(heads, side, tq, x_ref, hot_ref, f_ref, o_ref, of_ref, qa_ref, kp, vp, osc):
    seq_len = x_ref.shape[0]
    lanes = heads * HD
    step = pl.program_id(0)
    factor = LOG2E / math.sqrt(HD)

    @pl.when(step == 0)
    def _():
        rows = seq_len // 9

        def prep(i, c):
            part = pl.ds(pl.multiple_of(i * rows, rows), rows)
            hot = hot_ref[part, :]
            for h in range(heads):
                kp[h, part, :] = hot
                kp[h, part, 0:HD] = x_ref[part, lanes + h * HD : lanes + (h + 1) * HD]
                vp[h, part, :] = jnp.ones((rows, 128), BF)
                vp[h, part, 0:HD] = x_ref[part, 2 * lanes + h * HD : 2 * lanes + (h + 1) * HD]
            return c

        lax.fori_loop(0, 9, prep, 0)

    base = pl.ds(pl.multiple_of(step * tq, tq), tq)
    groups = tq // side
    lane = lax.broadcasted_iota(jnp.int32, (tq, 128), 1)
    for h in range(heads):
        q = x_ref[base, h * HD : (h + 1) * HD]
        g = dot(q, f_ref[...], NT) * math.sqrt(HD)
        gh = [
            pltpu.roll(g[i * side : (i + 1) * side, :128], 33 + step * groups + i, axis=1)
            for i in range(groups)
        ]
        gw = [
            pltpu.roll(g[i * side : (i + 1) * side, 128:], 81, axis=1, stride=1, stride_axis=0)
            for i in range(groups)
        ]
        qa_ref[h, :, 0:128] = jnp.concatenate(gh, 0).astype(BF)
        qa_ref[h, :, 0:HD] = q
        qa_ref[h, :, 128:256] = jnp.where(lane < side, jnp.concatenate(gw, 0), 0.0).astype(BF)

    def one(h, c):
        s = dot(qa_ref[h], kp[h], NT)
        m = jnp.max(s, -1, keepdims=True)
        p = jnp.exp2((s - m) * factor).astype(BF)
        o = dot(p, vp[h])
        total = o[:, HD : HD + 1]
        osc[h] = o / total
        norm = m + jnp.log2(total) / factor
        hi = norm.astype(BF).astype(F32)
        mid = (norm - hi).astype(BF).astype(F32)
        low = norm - hi - mid
        old = qa_ref[h, :, 128:256].astype(F32)
        old = jnp.where(lane == side, -hi, old)
        old = jnp.where(lane == side + 1, -mid, old)
        old = jnp.where(lane == side + 2, -low, old)
        qa_ref[h, :, 128:256] = old.astype(BF)
        return c

    lax.fori_loop(0, heads, one, 0)
    for h in range(heads):
        o_ref[:, h * HD : (h + 1) * HD] = osc[h][:, 0:HD].astype(BF)
        of_ref[:, h * HD : (h + 1) * HD] = osc[h][:, 0:HD]


def attention_forward(x, hot, tables, side, tq=192):
    seq_len, width = x.shape
    heads = width // (3 * HD)
    return pl.pallas_call(
        partial(fwd_kernel, heads, side, tq),
        grid=(seq_len // tq,),
        in_specs=[
            pl.BlockSpec((seq_len, width), lambda i: (0, 0), pipeline_mode=pl.Buffered(1)),
            pl.BlockSpec((seq_len, 256), lambda i: (0, 0), pipeline_mode=pl.Buffered(1)),
            pl.BlockSpec((256, HD), lambda i: (0, 0), pipeline_mode=pl.Buffered(1)),
        ],
        out_specs=[
            pl.BlockSpec((tq, heads * HD), lambda i: (i, 0)),
            pl.BlockSpec((tq, heads * HD), lambda i: (i, 0)),
            pl.BlockSpec((heads, tq, 256), lambda i: (0, i, 0)),
        ],
        out_shape=[
            jax.ShapeDtypeStruct((seq_len, heads * HD), BF),
            jax.ShapeDtypeStruct((seq_len, heads * HD), F32),
            jax.ShapeDtypeStruct((heads, seq_len, 256), BF),
        ],
        scratch_shapes=[
            pltpu.VMEM((heads, seq_len, 256), BF),
            pltpu.VMEM((heads, seq_len, 128), BF),
            pltpu.VMEM((heads, tq, 128), F32),
        ],
        compiler_params=pltpu.CompilerParams(
            dimension_semantics=("arbitrary",), vmem_limit_bytes=60 << 20
        ),
        name="attention_forward",
    )(x, hot, tables)


def bwd_kernel(heads, side, tb, uc, x_ref, hot_ref, f_ref, qa_ref, o_ref, go_ref, dx_ref, gt_ref, kp, kt, vp, dop, dk, dv, dq):
    seq_len = x_ref.shape[0]
    lanes = heads * HD
    h = pl.program_id(0)
    step = pl.program_id(1)
    factor = LOG2E / math.sqrt(HD)
    scale = HD ** (-0.5)

    @pl.when((h == 0) & (step == 0))
    def _():
        gt_ref[...] = jnp.zeros_like(gt_ref)
        rows = seq_len // 9

        def prep(i, c):
            part = pl.ds(pl.multiple_of(i * rows, rows), rows)
            hot = hot_ref[part, :]
            lane = lax.broadcasted_iota(jnp.int32, (rows, 128), 1)
            for n in range(heads):
                kp[n, part, :] = hot
                kp[n, part, 0:HD] = x_ref[part, lanes + n * HD : lanes + (n + 1) * HD]
                vp[n, part, :] = jnp.ones((rows, 128), BF)
                vp[n, part, 0:HD] = x_ref[part, 2 * lanes + n * HD : 2 * lanes + (n + 1) * HD]
                go = go_ref[part, n * HD : (n + 1) * HD]
                inner = jnp.sum(
                    go.astype(F32) * o_ref[part, n * HD : (n + 1) * HD], -1, keepdims=True
                )
                hi = inner.astype(BF).astype(F32)
                low = inner - hi
                tail = jnp.where(lane == HD, -hi, jnp.where(lane == HD + 1, -low, 0.0))
                dop[n, part, :] = tail.astype(BF)
                dop[n, part, 0:HD] = go
                kt[n, :, part] = kp[n, part, :].T
            return c

        lax.fori_loop(0, 9, prep, 0)

    @pl.when(step == 0)
    def _():
        dk[h] = jnp.zeros_like(dk[h])
        dv[h] = jnp.zeros_like(dv[h])

    base = pl.ds(pl.multiple_of(step * tb, tb), tb)
    qa = qa_ref[0]
    do = dop[h, base, :]

    def one(j, acc):
        part = pl.ds(pl.multiple_of(j * uc, uc), uc)
        s = dot(kp[h, part, :], qa, NT)
        dp = dot(vp[h, part, :], do, NT)
        p = jnp.exp2(s * factor)
        ds = (p * dp).astype(BF)
        dv[h, part, :] += dot(p.astype(BF), do)
        dk[h, part, :] += dot(ds, qa[:, 0:128])
        return acc + dot(kt[h, :, part], ds)

    acc = lax.fori_loop(0, seq_len // uc, one, jnp.zeros((256, tb), F32), unroll=True)
    acc = acc.T
    lane = lax.broadcasted_iota(jnp.int32, (tb, 128), 1)
    groups = tb // side
    first = jnp.where(lane < HD, 0.0, acc[:, :128])
    second = jnp.where(lane < side, acc[:, 128:], 0.0)
    back_h = [
        pltpu.roll(first[i * side : (i + 1) * side], 256 - 33 - step * groups - i, axis=1)
        for i in range(groups)
    ]
    back_w = [
        unroll_w(second[i * side : (i + 1) * side], side) for i in range(groups)
    ]
    both = jnp.concatenate([jnp.concatenate(back_h, 0), jnp.concatenate(back_w, 0)], 1).astype(BF)
    rel = dot(both, f_ref[...])
    dq[h, base, :] = acc[:, :HD] * scale + rel
    gt_ref[...] += dot(both, qa[:, 0:128], TN)

    @pl.when((h == heads - 1) & (step == pl.num_programs(1) - 1))
    def _():
        rows = seq_len // 9

        def post(i, c):
            part = pl.ds(pl.multiple_of(i * rows, rows), rows)
            for n in range(heads):
                dx_ref[part, n * HD : (n + 1) * HD] = dq[n, part, :].astype(BF)
                dx_ref[part, lanes + n * HD : lanes + (n + 1) * HD] = (dk[n, part, 0:HD] * scale).astype(BF)
                dx_ref[part, 2 * lanes + n * HD : 2 * lanes + (n + 1) * HD] = dv[n, part, 0:HD].astype(BF)
            return c

        lax.fori_loop(0, 9, post, 0)


def unroll_w(val, side):
    out = val
    row = lax.broadcasted_iota(jnp.int32, val.shape, 0)
    shift = side - 1 - row
    bit = 1
    while bit < side:
        out = jnp.where((shift & bit) != 0, pltpu.roll(out, bit, axis=1), out)
        bit *= 2
    return out


def attention_backward(x, hot, tables, qa, o, go, side, tb=768, uc=256):
    seq_len, width = x.shape
    heads = width // (3 * HD)
    whole = lambda *shape: pl.BlockSpec(shape, lambda h, i: (0,) * len(shape), pipeline_mode=pl.Buffered(1))
    return pl.pallas_call(
        partial(bwd_kernel, heads, side, tb, uc),
        grid=(heads, seq_len // tb),
        in_specs=[
            whole(seq_len, width),
            whole(seq_len, 256),
            whole(256, HD),
            pl.BlockSpec((1, tb, 256), lambda h, i: (h, i, 0)),
            whole(seq_len, heads * HD),
            whole(seq_len, heads * HD),
        ],
        out_specs=[
            whole(seq_len, width),
            whole(256, 128),
        ],
        out_shape=[
            jax.ShapeDtypeStruct((seq_len, width), BF),
            jax.ShapeDtypeStruct((256, 128), F32),
        ],
        scratch_shapes=[
            pltpu.VMEM((heads, seq_len, 256), BF),
            pltpu.VMEM((heads, 256, seq_len), BF),
            pltpu.VMEM((heads, seq_len, 128), BF),
            pltpu.VMEM((heads, seq_len, 128), BF),
            pltpu.VMEM((heads, seq_len, 128), F32),
            pltpu.VMEM((heads, seq_len, 128), F32),
            pltpu.VMEM((heads, seq_len, HD), F32),
        ],
        compiler_params=pltpu.CompilerParams(
            dimension_semantics=("arbitrary", "arbitrary"), vmem_limit_bytes=63 << 20
        ),
        name="attention_backward",
    )(x, hot, tables, qa, o, go)


def mlp_kernel(chunk, n_own, n_other, g_own, g_other, w1, b1, w2, out, gn, gw1, gw2, gb1, n2, gb, n2t, act, gbef):
    half = n_own.shape[0]
    tokens = 2 * half

    @pl.when(pl.program_id(0) == 0)
    def _():
        n2[0:half, :] = n_own[...]
        n2[half:tokens, :] = n_other[...]
        gb[0:half, :] = g_own[...]
        gb[half:tokens, :] = g_other[...]
        n2t[:, 0:half] = n_own[...].T
        n2t[:, half:tokens] = n_other[...].T
        out[...] = jnp.zeros_like(out)
        gn[...] = jnp.zeros_like(gn)

    gb1[...] = jnp.zeros_like(gb1)

    def rows(i, c):
        part = pl.ds(pl.multiple_of(i * chunk, chunk), chunk)
        before = dot(n2[part, :], w1[...]) + b1[...]
        cdf = 0.5 + 0.5 * lax.erf(before * math.sqrt(0.5))
        activated = (before * cdf).astype(BF)
        slope = cdf + before * (jnp.exp(-0.5 * before * before) * (1.0 / math.sqrt(2.0 * math.pi)))
        act[part, :] = activated
        out[part, :] += dot(activated, w2[...])
        grad_act = dot(gb[part, :], w2[...], NT)
        grad_before = (slope * grad_act).astype(BF)
        gbef[part, :] = grad_before
        gn[part, :] += dot(grad_before, w1[...], NT)
        gb1[...] += jnp.sum(grad_before.astype(F32), 0, keepdims=True)
        return c

    lax.fori_loop(0, tokens // chunk, rows, 0)
    gw2[...] = dot(act[...], gb[...], TN).astype(BF)
    gw1[...] = dot(n2t[...], gbef[...]).astype(BF)


def mlp(n_own, n_other, g_own, g_other, w1, b1, w2, tile=512, chunk=None):
    half, width = n_own.shape
    hidden = w1.shape[1]
    tokens = 2 * half
    chunk = chunk or min(tokens, 288)
    fixed = lambda rows, cols: pl.BlockSpec((rows, cols), lambda i: (0, 0), pipeline_mode=pl.Buffered(1))
    return pl.pallas_call(
        partial(mlp_kernel, chunk),
        grid=(hidden // tile,),
        in_specs=[
            fixed(half, width),
            fixed(half, width),
            fixed(half, width),
            fixed(half, width),
            pl.BlockSpec((width, tile), lambda i: (0, i)),
            pl.BlockSpec((1, tile), lambda i: (0, i)),
            pl.BlockSpec((tile, width), lambda i: (i, 0)),
        ],
        out_specs=[
            fixed(tokens, width),
            fixed(tokens, width),
            pl.BlockSpec((width, tile), lambda i: (0, i)),
            pl.BlockSpec((tile, width), lambda i: (i, 0)),
            pl.BlockSpec((1, tile), lambda i: (0, i)),
        ],
        out_shape=[
            jax.ShapeDtypeStruct((tokens, width), F32),
            jax.ShapeDtypeStruct((tokens, width), F32),
            jax.ShapeDtypeStruct((width, hidden), BF),
            jax.ShapeDtypeStruct((hidden, width), BF),
            jax.ShapeDtypeStruct((1, hidden), F32),
        ],
        scratch_shapes=[
            pltpu.VMEM((tokens, width), BF),
            pltpu.VMEM((tokens, width), BF),
            pltpu.VMEM((width, tokens), BF),
            pltpu.VMEM((tokens, tile), BF),
            pltpu.VMEM((tokens, tile), BF),
        ],
        compiler_params=pltpu.CompilerParams(
            dimension_semantics=("arbitrary",), vmem_limit_bytes=60 << 20
        ),
        name="mlp_both_ways",
    )(n_own, n_other, g_own, g_other, w1, b1, w2)


def split_sizes(patches, ranks):
    images = patches.shape[0]
    return images, ranks // images // 2


def norm_parts(values):
    center = values - jnp.mean(values, -1, keepdims=True)
    spread = jnp.mean(center * center, -1, keepdims=True)
    return center, lax.rsqrt(spread + EPSILON)


def norm_back(values, gain_vec, upstream):
    center, inverse = norm_parts(values)
    normal = center * inverse
    scaled = upstream * gain_vec
    inner = jnp.mean(scaled * normal, -1, keepdims=True)
    grad_values = inverse * (scaled - jnp.mean(scaled, -1, keepdims=True) - normal * inner)
    return grad_values, jnp.sum(upstream * normal, 0), jnp.sum(upstream, 0)


def flip(value, axis, size, bit):
    return lax.ppermute(value, axis, [(i, i ^ bit) for i in range(size)])


def butterfly(value, axis, size):
    bit = 1
    while bit < size:
        value = value + flip(value, axis, size, bit)
        bit *= 2
    return value


def gather_pieces(value, axis, size, me):
    full = jnp.zeros((size,) + value.shape, value.dtype)
    full = lax.dynamic_update_index_in_dim(full, value, me, 0)
    for bit in range(1, size):
        full = lax.dynamic_update_index_in_dim(full, flip(value, axis, size, bit), me ^ bit, 0)
    return full


def scatter_sum(value, axis, size, me):
    total = lax.dynamic_index_in_dim(value, me, 0, keepdims=False).astype(jnp.float32)
    for bit in range(1, size):
        away = lax.dynamic_index_in_dim(value, me ^ bit, 0, keepdims=False)
        total = total + flip(away, axis, size, bit).astype(jnp.float32)
    return total


def pick(value, index, axis=0):
    return lax.dynamic_index_in_dim(value, index, axis, keepdims=False)


def on_device(
    patches,
    ln1_gain,
    ln1_bias,
    qkv_weight,
    q_bias,
    v_bias,
    proj_weight,
    proj_bias,
    ln2_gain,
    ln2_bias,
    fc1_weight,
    fc1_bias,
    fc2_weight,
    fc2_bias,
    rel_pos_h,
    rel_pos_w,
    cotangent,
):
    images, row_count, width = patches.shape
    dp, ng, np_, nc = (lax.axis_size(name) for name in ("dp", "g", "p", "c"))
    i_dp, i_g, i_p, i_c = (lax.axis_index(name) for name in ("dp", "g", "p", "c"))
    chips = ng * np_
    ranks = chips * nc
    seq_len = ranks * row_count
    own_rows = images * row_count
    heads = H * images // ranks
    shard_heads = H // dp
    core_heads = shard_heads // nc
    piece = core_heads * HD
    pieces = heads // core_heads
    lanes = heads * HD
    core_lanes = np_ * lanes
    hidden = fc1_weight.shape[1]
    unit = hidden // ranks
    side = (rel_pos_h.shape[0] + 1) // 2

    shard = width // dp
    hidden_shard = hidden // dp
    core_bias = pick(fc1_bias.reshape(hidden_shard // (nc * unit), nc, unit), i_c, 1).reshape(-1, shard)
    packed = jnp.concatenate(
        [
            jnp.stack([ln1_gain, ln1_bias, q_bias, v_bias, proj_bias, ln2_gain, ln2_bias, fc2_bias]),
            core_bias,
        ]
    )
    vectors = gather_pieces(packed, "dp", dp, i_dp).astype(jnp.float32)
    whole_vec = vectors[:, :8].transpose(1, 0, 2).reshape(8, width)
    gain_one, shift_one, q_shift, v_shift, proj_shift, gain_two, shift_two, fc2_shift = whole_vec
    fc1_shift = vectors[:, 8:].reshape(1, hidden // nc)

    starts = [
        part * width + (i_p * pieces + q) * shard_heads * HD + i_c * piece
        for part in range(3)
        for q in range(pieces)
    ]
    qkv_own = jnp.concatenate(
        [lax.dynamic_slice_in_dim(qkv_weight, start, piece, 1) for start in starts], 1
    )
    qkv_full = gather_pieces(qkv_own, "dp", dp, i_dp).reshape(width, 3 * lanes)

    def own_vec(vec):
        return jnp.concatenate(
            [lax.dynamic_slice_in_dim(vec, starts[q], piece, 0) for q in range(pieces)]
        )

    qkv_shift = jnp.concatenate([own_vec(q_shift), jnp.zeros((lanes,), jnp.float32), own_vec(v_shift)])

    proj_own = lax.dynamic_slice_in_dim(proj_weight, i_c * piece, piece, 0)
    fc1_own = pick(fc1_weight.reshape(shard, hidden // (nc * unit), nc, unit), i_c, 2).reshape(shard, -1)
    fc2_own = pick(fc2_weight.reshape(hidden_shard // (nc * unit), nc, unit, width), i_c, 1).reshape(-1, width)
    proj_half = lax.all_gather(proj_own, "dp", axis=0, tiled=True)
    fc1_half = lax.all_gather(fc1_own, "dp", axis=0, tiled=True)
    fc2_half = lax.all_gather(fc2_own, "dp", axis=0, tiled=True)

    inputs_f = patches.astype(jnp.float32)
    center, inverse = norm_parts(inputs_f)
    normed_own = (center * inverse * gain_one + shift_one).astype(jnp.bfloat16)
    place = lambda g, p, c: ((g * np_ + p) * nc + c) * row_count
    chunks = []
    for bit in range(ng):
        chunk = pick(normed_own, i_g ^ bit)
        chunk = chunk if bit == 0 else flip(chunk, "g", ng, bit)
        for bit_p in range(np_):
            moved = chunk if bit_p == 0 else flip(chunk, "p", np_, bit_p)
            chunks.append((bit, bit_p, 0, moved))
            chunks.append((bit, bit_p, 1, flip(moved, "c", nc, 1)))
    normed = jnp.zeros((seq_len, width), jnp.bfloat16)
    for bit, bit_p, bit_c, chunk in chunks:
        start = place(i_g ^ bit, i_p ^ bit_p, i_c ^ bit_c)
        normed = lax.dynamic_update_slice_in_dim(normed, chunk, start, 0)
    joined = jnp.dot(normed, qkv_full, preferred_element_type=jnp.float32)
    head_rows = (joined + qkv_shift).astype(jnp.bfloat16)

    hot = hot_table(seq_len, side)
    tables = flip_tables(rel_pos_h, rel_pos_w)
    attended, attended_f, query_aug = attention_forward(head_rows, hot, tables, side)

    def exchange(stacked):
        return lax.all_to_all(stacked, ("g", "p"), split_axis=0, concat_axis=0, tiled=True)

    def to_own_other(value):
        return pick(value, i_c, 0), pick(value, 1 - i_c, 0)

    def from_own_other(own, other):
        return jnp.where(i_c == 0, jnp.stack([own, other]), jnp.stack([other, own]))

    returned = exchange(attended.reshape(chips, nc * row_count, lanes))
    returned = returned.reshape(ng, np_, nc, row_count, lanes).transpose(2, 0, 3, 1, 4)
    mixed_own, mixed_other = to_own_other(returned.reshape(nc, own_rows, core_lanes))
    mixed = jnp.concatenate([mixed_own, mixed_other])
    partial_own = jnp.dot(mixed_own, proj_half, preferred_element_type=jnp.float32)
    partial_other = jnp.dot(mixed_other, proj_half, preferred_element_type=jnp.float32)
    inputs_rows = inputs_f.reshape(own_rows, width)
    middle = inputs_rows + partial_own + flip(partial_other, "c", nc, 1) + proj_shift
    center, inverse = norm_parts(middle)
    two_own = (center * inverse * gain_two + shift_two).astype(jnp.bfloat16)
    two_other = flip(two_own, "c", nc, 1)
    branch_own = cotangent.reshape(own_rows, width)
    branch_other = flip(branch_own, "c", nc, 1)
    grad_out = branch_own.astype(jnp.float32)

    out_part, back_part, grad_fc1, grad_fc2, grad_fc1_shift = mlp(
        two_own, two_other, branch_own, branch_other, fc1_half, fc1_shift, fc2_half
    )
    grad_two = back_part[:own_rows] + flip(back_part[own_rows:], "c", nc, 1)
    result = middle + out_part[:own_rows] + flip(out_part[own_rows:], "c", nc, 1) + fc2_shift
    output = result.astype(jnp.bfloat16).reshape(patches.shape)

    grad_norm, grad_gain_two, grad_shift_two = norm_back(middle, gain_two, grad_two)
    grad_middle = grad_out + grad_norm
    back_own = grad_middle.astype(jnp.bfloat16)
    back_other = flip(back_own, "c", nc, 1)
    grad_mixed_own = lax.dot_general(
        back_own, proj_half, COLS_DIMS, preferred_element_type=jnp.float32
    ).astype(jnp.bfloat16)
    grad_mixed_other = lax.dot_general(
        back_other, proj_half, COLS_DIMS, preferred_element_type=jnp.float32
    ).astype(jnp.bfloat16)
    grad_proj = lax.dot_general(
        mixed, jnp.concatenate([back_own, back_other]), ROWS_DIMS, preferred_element_type=jnp.float32
    ).astype(jnp.bfloat16)
    grad_mixed = from_own_other(grad_mixed_own, grad_mixed_other)
    grad_mixed = grad_mixed.reshape(nc, ng, row_count, np_, lanes).transpose(1, 3, 0, 2, 4)
    grad_heads = exchange(grad_mixed.reshape(chips, nc * row_count, lanes)).reshape(seq_len, lanes)

    sum_fc2 = lax.psum_scatter(grad_fc2, "dp", scatter_dimension=0, tiled=True)
    sum_fc1 = lax.psum_scatter(grad_fc1, "dp", scatter_dimension=0, tiled=True)
    sum_proj = lax.psum_scatter(grad_proj, "dp", scatter_dimension=0, tiled=True)
    sum_fc2 = lax.psum_scatter(sum_fc2, ("g", "p"), scatter_dimension=1, tiled=True)
    sum_fc1 = lax.psum_scatter(sum_fc1, ("g", "p"), scatter_dimension=1, tiled=True)
    sum_proj = lax.psum_scatter(sum_proj, ("g", "p"), scatter_dimension=1, tiled=True)
    out_fc1 = sum_fc1.astype(jnp.float32)

    def swap_columns(value):
        columns = value.shape[1] // nc
        split = value.reshape(value.shape[0], nc, columns)
        mine = pick(split, i_c, 1)
        theirs = flip(pick(split, 1 - i_c, 1), "c", nc, 1)
        return jnp.where(i_c == 0, jnp.stack([mine, theirs]), jnp.stack([theirs, mine]))

    out_fc2 = swap_columns(sum_fc2).reshape(nc, hidden_shard // (nc * unit), unit, -1)
    out_fc2 = out_fc2.transpose(1, 0, 2, 3).reshape(hidden_shard, -1).astype(jnp.float32)
    out_proj = swap_columns(sum_proj).reshape(shard, -1).astype(jnp.float32)

    grad_rows, grad_tables = attention_backward(
        head_rows, hot, tables, query_aug, attended_f, grad_heads, side
    )
    grad_qkv = lax.dot_general(normed, grad_rows, ROWS_DIMS, preferred_element_type=jnp.float32)
    grad_qkv = grad_qkv.astype(jnp.bfloat16).reshape(dp, shard, 3 * lanes)
    grad_full = lax.dot_general(
        grad_rows, qkv_full, COLS_DIMS, preferred_element_type=jnp.float32
    ).astype(jnp.bfloat16)

    split = grad_full.reshape(chips, nc, row_count, width)
    keep = pick(split, i_c, 1).astype(jnp.float32)
    summed = keep + flip(pick(split, 1 - i_c, 1), "c", nc, 1).astype(jnp.float32)
    by_chip = summed.astype(jnp.bfloat16).reshape(ng, np_, row_count, width)
    homes = []
    for bit in range(ng):
        rows = scatter_sum(pick(by_chip, i_g ^ bit), "p", np_, i_p)
        if bit:
            rows = flip(rows.astype(jnp.bfloat16), "g", ng, bit).astype(jnp.float32)
        homes.append(rows)
    grad_normed = jnp.where(i_g == 0, jnp.stack(homes), jnp.stack(homes[::-1])) if ng == 2 else homes[0][None]
    grad_normed = grad_normed.reshape(own_rows, width)
    grad_norm, grad_gain_one, grad_shift_one = norm_back(inputs_rows, gain_one, grad_normed)
    grad_patches = (grad_middle + grad_norm).astype(jnp.bfloat16).reshape(patches.shape)

    qkv_rows = scatter_sum(grad_qkv, "dp", dp, i_dp).astype(jnp.bfloat16)
    qkv_rows = qkv_rows.reshape(ng, shard // ng, 3 * lanes)
    qkv_rows = scatter_sum(qkv_rows, "g", ng, i_g).astype(jnp.bfloat16)
    cell = width // ranks
    send = jnp.zeros((ranks * 3, shard // ng, cell), jnp.bfloat16)
    for q, start in enumerate(starts):
        for u in range(piece // cell):
            column = q * piece + u * cell
            block = qkv_rows[None, :, column : column + cell]
            send = lax.dynamic_update_slice_in_dim(send, block, start // cell + u, 0)
    taken = lax.all_to_all(
        send.reshape(ranks, 3, shard // ng, cell), ("g", "p", "c"), split_axis=0, concat_axis=0, tiled=True
    )
    taken = taken.reshape(ng, np_ * nc, 3, shard // ng, cell).astype(jnp.float32).sum(1)
    out_qkv = taken.transpose(0, 2, 1, 3).reshape(shard, 3 * cell)

    def spread(vec):
        full = jnp.zeros((width,), jnp.float32)
        for q in range(pieces):
            full = lax.dynamic_update_slice_in_dim(full, vec[q * piece : (q + 1) * piece], starts[q], 0)
        return full

    def everywhere(value):
        for name, size in (("c", nc), ("p", np_), ("g", ng)):
            value = butterfly(value, name, size)
        return value

    bias_half = grad_fc1_shift.reshape(dp, hidden_shard // (nc * unit), 1, unit)
    bias_full = jnp.concatenate([bias_half, bias_half], 2)
    core = lax.broadcasted_iota(jnp.int32, bias_full.shape, 2)
    bias_full = jnp.where(core == i_c, bias_full, 0.0).reshape(dp, -1, shard)
    rows_f = lambda value: jnp.sum(value.astype(jnp.float32), 0)
    early = jnp.stack([grad_gain_two, grad_shift_two, rows_f(back_own), rows_f(branch_own)])
    early = jnp.concatenate([early.reshape(4, dp, shard).transpose(1, 0, 2), bias_full], 1)
    early = everywhere(scatter_sum(early, "dp", dp, i_dp))
    late = jnp.stack(
        [
            grad_gain_one,
            grad_shift_one,
            spread(rows_f(grad_rows[:, :lanes])),
            spread(rows_f(grad_rows[:, 2 * lanes :])),
        ]
    )
    late = everywhere(scatter_sum(late.reshape(4, dp, shard).transpose(1, 0, 2), "dp", dp, i_dp))
    entries = rel_pos_h.shape[0]
    rel = jnp.stack([grad_tables[:entries, :HD], grad_tables[128 : 128 + entries, :HD]])
    rel = butterfly(everywhere(rel), "dp", dp)[:, ::-1]
    return (
        output,
        grad_patches,
        late[0],
        late[1],
        out_qkv,
        late[2],
        late[3],
        out_proj,
        early[2],
        early[0],
        early[1],
        out_fc1,
        early[4:].reshape(-1),
        out_fc2,
        early[3],
        rel[0],
        rel[1],
    )


def solution(mesh):
    dp, ranks = mesh.shape["dp"], mesh.shape["seq"]

    def call(*args):
        images = args[0].shape[0] // dp
        shape = (dp, images, ranks // images // 2, 2)
        fine = jax.sharding.Mesh(mesh.devices.reshape(shape), ("dp", "g", "p", "c"))
        seq = ("g", "p", "c")
        tokens, rows, both = P("dp", seq, None), P("dp", None), P("dp", seq)
        vec = P("dp")
        return jax.shard_map(
            on_device,
            mesh=fine,
            in_specs=(
                tokens, vec, vec, rows, vec, vec, rows, vec, vec, vec, rows, vec, rows, vec, P(), P(), tokens
            ),
            out_specs=(
                tokens, tokens, vec, vec, both, vec, vec, both, vec, vec, vec, both, vec, both, vec, P(), P()
            ),
            check_vma=False,
        )(*args)

    return call
```

```python
import math
from functools import partial

import jax
import jax.numpy as jnp
from jax import lax
from jax.experimental import pallas as pl
from jax.experimental.pallas import tpu as pltpu
from jax.sharding import PartitionSpec as P

H = 16
HD = 80
EPSILON = 1e-06
NT = (((1,), (1,)), ((), ()))
TN = (((0,), (0,)), ((), ()))
BF = jnp.bfloat16
F32 = jnp.float32
LOG2E = 1.4426950408889634
FACTOR = LOG2E / math.sqrt(HD)
FREE = pl.CostEstimate(flops=1, bytes_accessed=1, transcendentals=0)


def dot(a, b, dims=(((1,), (0,)), ((), ()))):
    return lax.dot_general(a, b, dims, preferred_element_type=F32)


def params(axes, mib=60):
    return pltpu.CompilerParams(
        dimension_semantics=("arbitrary",) * axes, vmem_limit_bytes=mib << 20
    )


def whole(*shape):
    return pl.BlockSpec(shape, lambda *at: (0,) * len(shape), pipeline_mode=pl.Buffered(1))


def hot_table(seq_len, side):
    token = lax.broadcasted_iota(jnp.int32, (seq_len, 256), 0)
    lane = lax.broadcasted_iota(jnp.int32, (seq_len, 256), 1)
    row_hit = (lane >= HD) & (token // side == lane - HD)
    col_hit = (lane >= HD + side) & (token % side == lane - HD - side)
    ones = (lane >= HD + 2 * side) & (lane < HD + 2 * side + 3)
    return (row_hit | col_hit | ones).astype(BF)


def flip_tables(rel_h, rel_w):
    entries = rel_h.shape[0]
    pad = ((0, 128 - entries), (0, 0))
    return jnp.concatenate([jnp.pad(rel_h[::-1], pad), jnp.pad(rel_w[::-1], pad)], 0)


def normal_rows(values):
    center = values - jnp.mean(values, -1, keepdims=True)
    spread = jnp.mean(center * center, -1, keepdims=True)
    return center * lax.rsqrt(spread + EPSILON)


def qkv_kernel(pieces, group_heads, side, raw, gain, shift, w, bias, hot, tables, normed, qa, kp, vp):
    rows = raw.shape[0]
    rows_n = (normal_rows(raw[...].astype(F32)) * gain[...] + shift[...]).astype(BF)
    normed[...] = rows_n
    joined = (dot(rows_n, w[...]) + bias[...]).astype(BF)
    first_row = pl.program_id(0) * (rows // side)
    lane = lax.broadcasted_iota(jnp.int32, (rows, 128), 1)
    width = group_heads * HD
    for n in range(pieces * group_heads):
        q_at = (n // group_heads) * 3 * width + (n % group_heads) * HD
        q = joined[:, q_at : q_at + HD]
        g = dot(q, tables[...], NT) * math.sqrt(HD)
        gh = []
        gw = []
        for i in range(rows // side):
            part = g[i * side : (i + 1) * side]
            gh.append(pltpu.roll(part[:, :128], first_row + (33 + i), axis=1))
            gw.append(pltpu.roll(part[:, 128:], 81, axis=1, stride=1, stride_axis=0))
        qa[n, :, 0:128] = jnp.concatenate(gh, 0).astype(BF)
        qa[n, :, 0:HD] = q
        qa[n, :, 128:256] = jnp.where(lane < side, jnp.concatenate(gw, 0), 0.0).astype(BF)
        kp[n] = hot[...]
        kp[n, :, 0:HD] = joined[:, q_at + width : q_at + width + HD]
        vp[n] = jnp.ones((rows, 128), BF)
        vp[n, :, 0:HD] = joined[:, q_at + 2 * width : q_at + 2 * width + HD]


def qkv_rows(raw, gain, shift, w, bias, hot, tables, pieces, group_heads, side, rows=384):
    seq_len, width = raw.shape
    lanes = w.shape[1]
    heads = pieces * group_heads
    return pl.pallas_call(
        partial(qkv_kernel, pieces, group_heads, side),
        grid=(seq_len // rows,),
        in_specs=[
            pl.BlockSpec((rows, width), lambda i: (i, 0)),
            whole(1, width),
            whole(1, width),
            whole(width, lanes),
            whole(1, lanes),
            pl.BlockSpec((rows, 256), lambda i: (i, 0)),
            whole(256, HD),
        ],
        out_specs=[
            pl.BlockSpec((rows, width), lambda i: (i, 0)),
            pl.BlockSpec((heads, rows, 256), lambda i: (0, i, 0)),
            pl.BlockSpec((heads, rows, 256), lambda i: (0, i, 0)),
            pl.BlockSpec((heads, rows, 128), lambda i: (0, i, 0)),
        ],
        out_shape=[
            jax.ShapeDtypeStruct((seq_len, width), BF),
            jax.ShapeDtypeStruct((heads, seq_len, 256), BF),
            jax.ShapeDtypeStruct((heads, seq_len, 256), BF),
            jax.ShapeDtypeStruct((heads, seq_len, 128), BF),
        ],
        compiler_params=params(1),
        cost_estimate=FREE,
        name="qkv_rows",
    )(raw, gain, shift, w, bias, hot, tables)


def attend_kernel(heads, side, aliased, at, qa, kp, vp, *refs):
    o, of, qo = refs[2:] if aliased else refs
    rows = qa.shape[1]
    h = pl.program_id(0)
    part = pl.ds(pl.multiple_of(pl.program_id(1) * rows, rows), rows)
    s = dot(qa[0], kp[0], NT)
    m = jnp.max(s, -1, keepdims=True)
    p = jnp.exp2((s - m) * FACTOR).astype(BF)
    out = dot(p, vp[0])
    total = out[:, HD : HD + 1]
    out = out / total
    norm = m + jnp.log2(total) / FACTOR
    hi = norm.astype(BF).astype(F32)
    mid = (norm - hi).astype(BF).astype(F32)
    low = norm - hi - mid
    lane = lax.broadcasted_iota(jnp.int32, (rows, 128), 1)
    old = qa[0, :, 128:256].astype(F32)
    old = jnp.where(lane == side, -hi, old)
    old = jnp.where(lane == side + 1, -mid, old)
    old = jnp.where(lane == side + 2, -low, old)
    qo[0, :, 0:128] = qa[0, :, 0:128]
    qo[0, :, 128:256] = old.astype(BF)
    for n in range(heads):

        @pl.when(h == n)
        def _(n=n):
            o[part, n * HD : (n + 1) * HD] = out[:, 0:HD].astype(BF)
            of[part, n * HD : (n + 1) * HD] = out[:, 0:HD]


def attend(group, qa, kp, vp, side, groups, old=(), tq=192):
    heads, seq_len, _ = qa.shape
    rows = seq_len // groups
    steps = rows // tq
    lanes = heads * HD
    query = pl.BlockSpec((1, tq, 256), lambda h, i, at: (h, at[0] * steps + i, 0))
    return pl.pallas_call(
        partial(attend_kernel, heads, side, bool(old)),
        grid_spec=pltpu.PrefetchScalarGridSpec(
            num_scalar_prefetch=1,
            grid=(heads, steps),
            in_specs=[
                query,
                pl.BlockSpec((1, seq_len, 256), lambda h, i, at: (h, 0, 0)),
                pl.BlockSpec((1, seq_len, 128), lambda h, i, at: (h, 0, 0)),
            ]
            + [pl.BlockSpec(memory_space=pl.ANY)] * len(old),
            out_specs=[
                pl.BlockSpec((rows, lanes), lambda h, i, at: (0, 0)),
                pl.BlockSpec((rows, lanes), lambda h, i, at: (at[0], 0)),
                query,
            ],
        ),
        out_shape=[
            jax.ShapeDtypeStruct((rows, lanes), BF),
            jax.ShapeDtypeStruct((seq_len, lanes), F32),
            jax.ShapeDtypeStruct((heads, seq_len, 256), BF),
        ],
        input_output_aliases={4: 1, 5: 2} if old else {},
        compiler_params=params(2),
        cost_estimate=FREE,
        name="attend",
    )(jnp.stack([group]), qa, kp, vp, *old)


def attend_back_kernel(heads, first, side, uc, qa_ref, kp, vp, of, go, tables, dx, gt, kt, dop, dk, dv, dq):
    seq_len = kp.shape[1]
    tb = qa_ref.shape[1]
    h = pl.program_id(0)
    step = pl.program_id(1)
    last = pl.num_programs(1) - 1
    scale = HD ** (-0.5)
    rows = seq_len // 9

    @pl.when((h == 0) & (step == 0))
    def _():
        gt[...] = jnp.zeros_like(gt)

        def prep(i, c):
            part = pl.ds(pl.multiple_of(i * rows, rows), rows)
            lane = lax.broadcasted_iota(jnp.int32, (rows, 128), 1)
            for n in range(heads):
                at = (first + n) * HD
                rows_go = go[part, at : at + HD]
                inner = jnp.sum(rows_go.astype(F32) * of[part, at : at + HD], -1, keepdims=True)
                hi = inner.astype(BF).astype(F32)
                tail = jnp.where(lane == HD, -hi, jnp.where(lane == HD + 1, hi - inner, 0.0))
                dop[n, part, :] = tail.astype(BF)
                dop[n, part, 0:HD] = rows_go
            return c

        lax.fori_loop(0, 9, prep, 0)

    @pl.when(step == 0)
    def _():
        def prep(i, c):
            part = pl.ds(pl.multiple_of(i * rows, rows), rows)
            kt[:, part] = kp[0, part, :].T
            dk[part, :] = jnp.zeros((rows, 128), F32)
            dv[part, :] = jnp.zeros((rows, 128), F32)
            return c

        lax.fori_loop(0, 9, prep, 0)

    base = pl.ds(pl.multiple_of(step * tb, tb), tb)
    qa = qa_ref[0]
    do = dop[h, base, :]

    def one(j, acc):
        part = pl.ds(pl.multiple_of(j * uc, uc), uc)
        s = dot(kp[0, part, :], qa, NT)
        dp = dot(vp[0, part, :], do, NT)
        p = jnp.exp2(s * FACTOR)
        ds = (p * dp).astype(BF)
        dv[part, :] += dot(p.astype(BF), do)
        dk[part, :] += dot(ds, qa[:, 0:128])
        return acc + dot(kt[:, part], ds)

    acc = lax.fori_loop(0, seq_len // uc, one, jnp.zeros((256, tb), F32), unroll=True)
    acc = acc.T
    lane = lax.broadcasted_iota(jnp.int32, (tb, 128), 1)
    groups = tb // side
    rel_h = jnp.where(lane < HD, 0.0, acc[:, :128])
    rel_w = jnp.where(lane < side, acc[:, 128:], 0.0)
    back_h = []
    back_w = []
    for i in range(groups):
        part = slice(i * side, (i + 1) * side)
        back_h.append(pltpu.roll(rel_h[part], 256 - 33 - step * groups - i, axis=1))
        back_w.append(stagger(rel_w[part], side))
    both = jnp.concatenate([jnp.concatenate(back_h, 0), jnp.concatenate(back_w, 0)], 1).astype(BF)
    dq[base, :] = acc[:, :HD] * scale + dot(both, tables[...])
    gt[...] += dot(both, qa[:, 0:128], TN)

    width = heads * HD
    for n in range(heads):

        @pl.when((h == n) & (step == last))
        def _(n=n):
            def post(i, c):
                part = pl.ds(pl.multiple_of(i * rows, rows), rows)
                at = n * HD
                dx[part, at : at + HD] = dq[part, :].astype(BF)
                dx[part, width + at : width + at + HD] = (dk[part, 0:HD] * scale).astype(BF)
                dx[part, 2 * width + at : 2 * width + at + HD] = dv[part, 0:HD].astype(BF)
                return c

            lax.fori_loop(0, 9, post, 0)


def stagger(val, side):
    row = lax.broadcasted_iota(jnp.int32, val.shape, 0)
    shift = side - 1 - row
    bit = 1
    while bit < side:
        val = jnp.where((shift & bit) != 0, pltpu.roll(val, bit, axis=1), val)
        bit *= 2
    return val


def attend_back(first, count, qa, kp, vp, of, go, tables, side, tb=768, uc=256):
    heads, seq_len, _ = qa.shape
    lanes = heads * HD
    return pl.pallas_call(
        partial(attend_back_kernel, count, first, side, uc),
        grid=(count, seq_len // tb),
        in_specs=[
            pl.BlockSpec((1, tb, 256), lambda h, i: (first + h, i, 0)),
            pl.BlockSpec((1, seq_len, 256), lambda h, i: (first + h, 0, 0)),
            pl.BlockSpec((1, seq_len, 128), lambda h, i: (first + h, 0, 0)),
            whole(seq_len, lanes),
            whole(seq_len, lanes),
            whole(256, HD),
        ],
        out_specs=[whole(seq_len, 3 * count * HD), whole(256, 128)],
        out_shape=[
            jax.ShapeDtypeStruct((seq_len, 3 * count * HD), BF),
            jax.ShapeDtypeStruct((256, 128), F32),
        ],
        scratch_shapes=[
            pltpu.VMEM((256, seq_len), BF),
            pltpu.VMEM((count, seq_len, 128), BF),
            pltpu.VMEM((seq_len, 128), F32),
            pltpu.VMEM((seq_len, 128), F32),
            pltpu.VMEM((seq_len, HD), F32),
        ],
        compiler_params=params(2),
        cost_estimate=FREE,
        name="attend_back",
    )(qa, kp, vp, of, go, tables)


def project_kernel(chips, np_, at, *refs):
    pieces = refs[:chips]
    w, mixed, own, other = refs[chips:]
    i_g, i_p, i_c = at[0], at[1], at[2]
    rows = pieces[0].shape[0] // 2
    lanes = pieces[0].shape[1]
    images = chips // np_
    for k in range(chips):
        for swap in range(2):

            @pl.when(i_c == swap)
            def _(k=k, swap=swap):
                for b in range(2):
                    src = (swap ^ b) * rows
                    mixed[i_p ^ (k % np_), b, i_g ^ (k // np_)] = pieces[k][src : src + rows, :]

    for b, out in ((0, own), (1, other)):
        for n in range(images):
            total = None
            for p in range(np_):
                term = dot(mixed[p, b, n], w[p])
                total = term if total is None else total + term
            out[n] = total


def project(pieces, w, at, np_):
    chips = len(pieces)
    rows2, lanes = pieces[0].shape
    rows = rows2 // 2
    images = chips // np_
    width = w.shape[2]
    one = jax.ShapeDtypeStruct((images, rows, width), F32)
    return pl.pallas_call(
        partial(project_kernel, chips, np_),
        in_specs=[pl.BlockSpec(memory_space=pltpu.SMEM)]
        + [pl.BlockSpec(memory_space=pltpu.VMEM)] * (chips + 1),
        out_specs=[pl.BlockSpec(memory_space=pltpu.VMEM)] * 3,
        out_shape=[jax.ShapeDtypeStruct((np_, 2, images, rows, lanes), BF), one, one],
        compiler_params=pltpu.CompilerParams(vmem_limit_bytes=40 << 20),
        cost_estimate=FREE,
        name="project",
    )(at, *pieces, w)


def mlp_kernel(aliased, n_own, n_other, g_own, g_other, w1, b1, w2, *refs):
    if aliased:
        out_in, gn_in, out, gn, grads, gb1, n2t, gb, act, gbef = refs
    else:
        out, gn, grads, gb1, n2t, gb, act, gbef = refs
    half, width = n_own.shape
    step = pl.program_id(0)
    chunk = out.shape[0]
    per = half // chunk
    shards, shard, hidden = w1.shape
    first = w1[...].reshape(width, hidden)
    second = w2[...].reshape(hidden, width)

    @pl.when(step == 0)
    def _():
        gb1[...] = jnp.zeros_like(gb1)

    def rows(n_ref, g_ref, at):
        src = pl.ds(pl.multiple_of((step - at) * chunk, chunk), chunk)
        dst = pl.ds(pl.multiple_of(step * chunk, chunk), chunk)
        n2 = n_ref[src, :]
        g2 = g_ref[src, :]
        gb[dst, :] = g2
        before = dot(n2, first) + b1[...]
        cdf = 0.5 + 0.5 * lax.erf(before * math.sqrt(0.5))
        activated = (before * cdf).astype(BF)
        slope = cdf + before * (jnp.exp(-0.5 * before * before) * (1.0 / math.sqrt(2.0 * math.pi)))
        act[dst, :] = activated
        value = dot(activated, second)
        grad_before = (slope * dot(g2, second, NT)).astype(BF)
        gbef[dst, :] = grad_before
        back = dot(grad_before, first, NT)
        if aliased:
            value = value + out_in[...]
            back = back + gn_in[...]
        out[...] = value
        gn[...] = back
        gb1[...] += jnp.sum(grad_before.astype(F32), 0, keepdims=True)

    @pl.when(step < per)
    def _():
        rows(n_own, g_own, 0)

    @pl.when((step >= per) & (step < 2 * per))
    def _():
        rows(n_other, g_other, per)

    @pl.when(step == 2 * per)
    def _():
        n2t[:, 0:half] = n_own[...].T
        n2t[:, half : 2 * half] = n_other[...].T
        grads[:, 0:shard, :] = dot(n2t[...], gbef[...]).astype(BF).reshape(shards, shard, hidden)
        grads[:, shard : 2 * shard, :] = dot(act[...], gb[...], TN).astype(BF).reshape(shards, shard, width)


def mlp_half(which, n_own, n_other, g_own, g_other, weights, b1, old=(), chunk=288):
    half, width = n_own.shape
    dp = weights.shape[0]
    shard = width // dp
    hidden = width
    chunk = min(chunk, half)
    steps = 2 * half // chunk
    tile = pl.BlockSpec((chunk, width), lambda i: (jnp.minimum(i, steps - 1), 0))
    rows = jax.ShapeDtypeStruct((2 * half, width), F32)
    flops = 12 * 2 * half * width * hidden
    return pl.pallas_call(
        partial(mlp_kernel, bool(old)),
        grid=(steps + 1,),
        in_specs=[whole(half, width)] * 4
        + [
            pl.BlockSpec((dp, shard, width), lambda i: (0, which, 0), pipeline_mode=pl.Buffered(1)),
            whole(1, hidden),
            pl.BlockSpec((dp, shard, width), lambda i: (0, 2 + which, 0), pipeline_mode=pl.Buffered(1)),
        ]
        + [tile] * len(old),
        out_specs=[tile, tile, whole(dp, 2 * shard, width), whole(1, hidden)],
        out_shape=[
            rows,
            rows,
            jax.ShapeDtypeStruct((dp, 2 * shard, width), BF),
            jax.ShapeDtypeStruct((1, hidden), F32),
        ],
        input_output_aliases={7: 0, 8: 1} if old else {},
        scratch_shapes=[
            pltpu.VMEM((width, 2 * half), BF),
            pltpu.VMEM((2 * half, width), BF),
            pltpu.VMEM((2 * half, hidden), BF),
            pltpu.VMEM((2 * half, hidden), BF),
        ],
        compiler_params=params(1),
        cost_estimate=FREE,
        name="mlp_half",
    )(n_own, n_other, g_own, g_other, weights, b1, weights, *old)


def rows_back_kernel(pieces, np_, at, *refs):
    dx = refs[:pieces]
    raw, w, send, keep, sums = refs[pieces:]
    step = pl.program_id(0)
    total = None
    width = dx[0].shape[1]
    for q in range(pieces):
        term = dot(dx[q][...], w[:, q * width : (q + 1) * width], NT)
        total = term if total is None else total + term
    normal = normal_rows(raw[...].astype(F32))

    @pl.when(step == 0)
    def _():
        sums[...] = jnp.zeros_like(sums)

    sums[0:1, :] += jnp.sum(total * normal, 0, keepdims=True)
    sums[1:2, :] += jnp.sum(total, 0, keepdims=True)
    for q in range(pieces):
        sums[2 + q : 3 + q, 0:width] += jnp.sum(dx[q][...].astype(F32), 0, keepdims=True)

    @pl.when(step < np_)
    def _():
        send[0] = total.astype(BF)

    @pl.when(step >= np_)
    def _():
        keep[0] = total


def rows_back(group, core, dx, raw, w, np_, row_count):
    pieces = len(dx)
    seq_len, width = raw.shape
    lanes = dx[0].shape[1]

    def block(i, at):
        bit = jnp.where(i < np_, 1, 0)
        return (at[0] * np_ + i % np_) * 2 + (at[1] ^ bit), 0

    return pl.pallas_call(
        partial(rows_back_kernel, pieces, np_),
        grid_spec=pltpu.PrefetchScalarGridSpec(
            num_scalar_prefetch=1,
            grid=(2 * np_,),
            in_specs=[pl.BlockSpec((row_count, lanes), block)] * pieces
            + [pl.BlockSpec((row_count, width), block), whole(width, pieces * lanes)],
            out_specs=[
                pl.BlockSpec((1, row_count, width), lambda i, at: (jnp.minimum(i, np_ - 1), 0, 0)),
                pl.BlockSpec((1, row_count, width), lambda i, at: (jnp.maximum(i - np_, 0), 0, 0)),
                whole(8, width),
            ],
        ),
        out_shape=[
            jax.ShapeDtypeStruct((np_, row_count, width), BF),
            jax.ShapeDtypeStruct((np_, row_count, width), F32),
            jax.ShapeDtypeStruct((8, width), F32),
        ],
        compiler_params=params(1),
        cost_estimate=FREE,
        name="rows_back",
    )(jnp.stack([group, core]), *dx, raw, w)


def select_kernel(ng, np_, nc, at, qkv, fc1, fc2, proj, own, slab):
    i_p, i_c = at[1], at[2]
    shard = fc1.shape[0]
    width = proj.shape[1]
    hidden = fc1.shape[1]
    chips = ng * np_
    unit = hidden // (chips * nc)
    part = unit // 2
    piece = proj.shape[0] // nc
    shard_lanes = proj.shape[0]
    lanes = own.shape[1] // 3
    pieces = lanes // piece
    per = fc2.shape[0] // (nc * unit)
    for c in range(nc):

        @pl.when(i_c == c)
        def _(c=c):
            for u in range(2):
                for z in range(chips):
                    src = (z * nc + c) * unit + u * part
                    slab[u * shard : (u + 1) * shard, z * part : (z + 1) * part] = fc1[:, src : src + part]
                for b in range(per):
                    src = (b * nc + c) * unit + u * part
                    dst = (2 + u) * shard + b * part
                    slab[dst : dst + part, :] = fc2[src : src + part, :]
            slab[4 * shard : 4 * shard + piece, :] = proj[c * piece : (c + 1) * piece, :]

        for p in range(np_):

            @pl.when((i_c == c) & (i_p == p))
            def _(c=c, p=p):
                for q in range(pieces):
                    for t in range(3):
                        src = t * width + (p * pieces + q) * shard_lanes + c * piece
                        dst = (3 * q + t) * piece
                        own[:, dst : dst + piece] = qkv[:, src : src + piece]


def select(at, qkv, fc1, fc2, proj, ng, np_, nc, lanes):
    shard, width = proj.shape[0], proj.shape[1]
    return pl.pallas_call(
        partial(select_kernel, ng, np_, nc),
        in_specs=[pl.BlockSpec(memory_space=pltpu.SMEM)] + [pl.BlockSpec(memory_space=pltpu.VMEM)] * 4,
        out_specs=[pl.BlockSpec(memory_space=pltpu.VMEM)] * 2,
        out_shape=[
            jax.ShapeDtypeStruct((shard, 3 * lanes), BF),
            jax.ShapeDtypeStruct((4 * shard + shard // nc, width), BF),
        ],
        compiler_params=pltpu.CompilerParams(vmem_limit_bytes=40 << 20),
        cost_estimate=FREE,
        name="select",
    )(at, qkv, fc1, fc2, proj)


def start_kernel(sizes, split, patches, own, vec, rows, full, vecs, local, send, recv):
    dp, ng, np_ = sizes
    i_dp, i_g, i_p, i_c = (lax.axis_index(name) for name in ("dp", "g", "p", "c"))
    count = patches.shape[1]
    step = count // split

    barrier = pltpu.get_barrier_semaphore()
    peers = [{"dp": i_dp ^ k} for k in range(1, dp)]
    peers += [{"g": i_g ^ k} for k in range(1, ng)]
    peers += [{"p": i_p ^ k} for k in range(1, np_)]
    peers += [{"c": 1 - i_c}]
    for peer in peers:
        pl.semaphore_signal(barrier, inc=1, device_id=peer, device_id_type=pl.DeviceIdType.MESH)
    pl.semaphore_wait(barrier, len(peers))

    used = []

    def remote(src, dst, peer):
        n = len(used)
        copy = pltpu.make_async_remote_copy(
            src_ref=src,
            dst_ref=dst,
            send_sem=send.at[n],
            recv_sem=recv.at[n],
            device_id=peer,
            device_id_type=pl.DeviceIdType.MESH,
        )
        used.append(copy)
        return copy

    def place(g, p, c, part):
        start = ((g * np_ + p) * 2 + c) * count + part * step
        return rows.at[pl.ds(pl.multiple_of(start, 8), step)]

    mine = [patches.at[i_g, pl.ds(part * step, step)] for part in range(split)]
    home = [pltpu.make_async_copy(mine[part], place(i_g, i_p, i_c, part), local.at[part]) for part in range(split)]
    home.append(pltpu.make_async_copy(own, full.at[i_dp], local.at[split]))
    home.append(pltpu.make_async_copy(vec, vecs.at[i_dp], local.at[split + 1]))

    far = {}
    for part in range(split):
        for bit in range(1, ng):
            src = patches.at[i_g ^ bit, pl.ds(part * step, step)]
            far[bit, part] = remote(src, place(i_g, i_p, i_c, part), {"g": i_g ^ bit})
            far[bit, part].start()
    over_dp = []
    for bit in range(1, dp):
        over_dp.append(remote(vec, vecs.at[i_dp], {"dp": i_dp ^ bit}))
        over_dp.append(remote(own, full.at[i_dp], {"dp": i_dp ^ bit}))
    for copy in over_dp:
        copy.start()
    near = {}
    for bit in range(1, np_):
        for part in range(split):
            near[bit, part] = remote(mine[part], place(i_g, i_p, i_c, part), {"p": i_p ^ bit})
            near[bit, part].start()
    cores = []
    for part in range(split):
        cores.append(remote(mine[part], place(i_g, i_p, i_c, part), {"c": 1 - i_c}))
        cores[-1].start()
    for copy in home:
        copy.start()

    onward = {}
    for part in range(split):
        for bit in range(1, ng):
            far[bit, part].wait_recv()
            came = place(i_g ^ bit, i_p, i_c, part)
            for bit_p in range(1, np_):
                onward[bit, bit_p, part] = remote(came, came, {"p": i_p ^ bit_p})
                onward[bit, bit_p, part].start()
            cores.append(remote(came, came, {"c": 1 - i_c}))
            cores[-1].start()
        for bit in range(1, np_):
            near[bit, part].wait_recv()
            came = place(i_g, i_p ^ bit, i_c, part)
            cores.append(remote(came, came, {"c": 1 - i_c}))
            cores[-1].start()
    for (bit, bit_p, part), copy in onward.items():
        copy.wait_recv()
        came = place(i_g ^ bit, i_p ^ bit_p, i_c, part)
        cores.append(remote(came, came, {"c": 1 - i_c}))
        cores[-1].start()
    for copy in over_dp + cores:
        copy.wait_recv()
    for copy in used:
        copy.wait_send()
    for copy in home:
        copy.wait()


def start_exchange(patches, own, vec, sizes, split=3):
    dp, ng, np_ = sizes
    images, count, width = patches.shape
    chunk_copies = ng * np_ + (ng - 1) + (np_ - 1) + (ng - 1) * (np_ - 1)
    copies = 2 * (dp - 1) + split * chunk_copies
    hbm = pl.BlockSpec(memory_space=pl.ANY)
    return pl.pallas_call(
        partial(start_kernel, sizes, split),
        in_specs=[hbm] * 3,
        out_specs=[hbm] * 3,
        out_shape=[
            jax.ShapeDtypeStruct((ng * np_ * 2 * count, width), BF),
            jax.ShapeDtypeStruct((dp,) + own.shape, BF),
            jax.ShapeDtypeStruct((dp,) + vec.shape, BF),
        ],
        scratch_shapes=[
            pltpu.SemaphoreType.DMA((split + 2,)),
            pltpu.SemaphoreType.DMA((copies,)),
            pltpu.SemaphoreType.DMA((copies,)),
        ],
        compiler_params=pltpu.CompilerParams(collective_id=0, has_side_effects=True),
        cost_estimate=FREE,
        name="start_exchange",
    )(patches, own, vec)


def flip(value, axis, size, bit):
    return lax.ppermute(value, axis, [(i, i ^ bit) for i in range(size)])


def pick(value, index, axis=0):
    return lax.dynamic_index_in_dim(value, index, axis, keepdims=False)


def gather_pieces(value, axis, size, me):
    full = jnp.zeros((size,) + value.shape, value.dtype)
    full = lax.dynamic_update_index_in_dim(full, value, me, 0)
    for bit in range(1, size):
        full = lax.dynamic_update_index_in_dim(full, flip(value, axis, size, bit), me ^ bit, 0)
    return full


def scatter_sum(value, axis, size, me):
    total = pick(value, me).astype(F32)
    for bit in range(1, size):
        total = total + flip(pick(value, me ^ bit), axis, size, bit).astype(F32)
    return total


def tie(*values):
    return lax.optimization_barrier(values)


def after(value, *others):
    return tie(value, *others)[0]


def norm_back(values, gain_vec, upstream):
    center = values - jnp.mean(values, -1, keepdims=True)
    spread = jnp.mean(center * center, -1, keepdims=True)
    inverse = lax.rsqrt(spread + EPSILON)
    normal = center * inverse
    scaled = upstream * gain_vec
    inner = jnp.mean(scaled * normal, -1, keepdims=True)
    return inverse * (scaled - jnp.mean(scaled, -1, keepdims=True) - normal * inner), normal


def on_device(
    patches,
    ln1_gain,
    ln1_bias,
    qkv_weight,
    q_bias,
    v_bias,
    proj_weight,
    proj_bias,
    ln2_gain,
    ln2_bias,
    fc1_weight,
    fc1_bias,
    fc2_weight,
    fc2_bias,
    rel_pos_h,
    rel_pos_w,
    cotangent,
):
    images, row_count, width = patches.shape
    dp, ng, np_, nc = (lax.axis_size(name) for name in ("dp", "g", "p", "c"))
    i_dp, i_g, i_p, i_c = (lax.axis_index(name) for name in ("dp", "g", "p", "c"))
    chips = ng * np_
    i_z = i_g * np_ + i_p
    ranks = chips * nc
    seq_len = ranks * row_count
    own_rows = images * row_count
    heads = H * images // ranks
    shard_heads = H // dp
    core_heads = shard_heads // nc
    piece = core_heads * HD
    pieces = heads // core_heads
    lanes = heads * HD
    hidden = fc1_weight.shape[1]
    unit = hidden // ranks
    shard = width // dp
    per = hidden // dp // (nc * unit)
    side = (rel_pos_h.shape[0] + 1) // 2

    core_bias = pick(fc1_bias.reshape(per, nc, 2, unit // 2), i_c, 1).transpose(1, 0, 2)
    packed = jnp.concatenate(
        [
            jnp.stack([ln1_gain, ln1_bias, q_bias, v_bias, proj_bias, ln2_gain, ln2_bias, fc2_bias]),
            core_bias.reshape(-1, shard),
        ]
    )
    spot = jnp.stack([i_g, i_p, i_c])
    qkv_own, slab = select(spot, qkv_weight, fc1_weight, fc2_weight, proj_weight, ng, np_, nc, lanes)
    weights = lax.all_gather(slab, "dp", axis=0)
    proj_half = weights[:, 4 * shard :]
    raw, qkv_full, vectors = start_exchange(patches, qkv_own, packed, (dp, ng, np_))
    qkv_full = qkv_full.reshape(width, 3 * lanes)
    vectors = vectors.astype(F32)
    whole_vec = vectors.transpose(1, 0, 2).reshape(-1, width)
    gain_one, shift_one, q_shift, v_shift, proj_shift, gain_two, shift_two, fc2_shift = whole_vec[:8]
    fc1_shift = vectors[:, 8:].reshape(dp, 2, -1).transpose(1, 0, 2).reshape(2, 1, -1)

    starts = [
        part * width + (i_p * pieces + q) * shard_heads * HD + i_c * piece
        for q in range(pieces)
        for part in range(3)
    ]
    zero = jnp.zeros((piece,), F32)
    biases = []
    for q in range(pieces):
        at = starts[3 * q]
        biases += [lax.dynamic_slice_in_dim(q_shift, at, piece, 0), zero]
        biases += [lax.dynamic_slice_in_dim(v_shift, at, piece, 0)]
    qkv_shift = jnp.concatenate(biases)[None]

    branch_own = cotangent.reshape(own_rows, width)
    branch_other = flip(branch_own, "c", nc, 1)

    hot = hot_table(seq_len, side)
    tables = flip_tables(rel_pos_h, rel_pos_w)
    normed, query, key_rows, value_rows = qkv_rows(
        raw, gain_one[None], shift_one[None], qkv_full, qkv_shift, hot, tables, pieces, core_heads, side
    )
    far_att, att_f, query_a = attend(i_g ^ 1, query, key_rows, value_rows, side, ng)
    far_att = far_att.reshape(np_, nc * row_count, lanes)
    arrived = {}
    for bit_p in range(np_):
        arrived[1, bit_p] = flip(pick(far_att, i_p ^ bit_p), ("g", "p"), chips, np_ + bit_p)
    near_att, att_f, query_a = attend(i_g, query, key_rows, value_rows, side, ng, (att_f, query_a))
    near_att, *pinned = tie(near_att, *[arrived[1, k] for k in range(np_)])
    for k in range(np_):
        arrived[1, k] = pinned[k]
    near_att = near_att.reshape(np_, nc * row_count, lanes)
    arrived[0, 0] = pick(near_att, i_p)
    for bit_p in range(1, np_):
        arrived[0, bit_p] = flip(pick(near_att, i_p ^ bit_p), ("g", "p"), chips, bit_p)

    mixed, partial_own, partial_other = project(
        [arrived[k // np_, k % np_] for k in range(chips)], proj_half.reshape(np_, lanes, width), spot, np_
    )
    inputs_rows = patches.reshape(own_rows, width).astype(F32)
    partial_own = partial_own.reshape(own_rows, width)
    middle = inputs_rows + partial_own + flip(partial_other, "c", nc, 1).reshape(own_rows, width) + proj_shift
    center = middle - jnp.mean(middle, -1, keepdims=True)
    spread = jnp.mean(center * center, -1, keepdims=True)
    two_own = (center * lax.rsqrt(spread + EPSILON) * gain_two + shift_two).astype(BF)
    two_other = flip(two_own, "c", nc, 1)

    def over_dp(value):
        return lax.psum_scatter(value.reshape(-1, value.shape[-1]), "dp", scatter_dimension=0, tiled=True)

    out_a, back_a, grads_a, bias_a = mlp_half(
        0, two_own, two_other, branch_own, branch_other, weights, fc1_shift[0]
    )
    sum_a = over_dp(grads_a)
    out_b, back_b, grads_b, bias_b = mlp_half(
        1, two_own, two_other, branch_own, branch_other, weights, fc1_shift[1], (out_a, back_a)
    )
    grad_two = back_b[:own_rows] + flip(back_b[own_rows:], "c", nc, 1)
    result = middle + out_b[:own_rows] + flip(out_b[own_rows:], "c", nc, 1) + fc2_shift
    output = result.astype(BF).reshape(patches.shape)

    grad_norm, normal_two = norm_back(middle, gain_two, grad_two)
    grad_middle = branch_own.astype(F32) + grad_norm
    back_own = grad_middle.astype(BF)
    back_other = flip(back_own, "c", nc, 1)
    both = jnp.stack([back_own, back_other])
    proj_rows = proj_half.reshape(np_, lanes, width)
    grad_mixed = jnp.einsum("btd,pld->pbtl", both, proj_rows, preferred_element_type=F32).astype(BF)
    grad_mixed = grad_mixed.reshape(np_, nc, ng, row_count, lanes)
    grad_heads = jnp.zeros((chips, nc, row_count, lanes), BF)
    for k in list(range(1, chips)) + [0]:
        block = pick(pick(grad_mixed, i_p ^ (k % np_)), i_g ^ (k // np_), 1)
        block = jnp.where(i_c == 0, block, block[::-1])
        block = block if k == 0 else flip(block, ("g", "p"), chips, k)
        grad_heads = lax.dynamic_update_index_in_dim(grad_heads, block, i_z ^ k, 0)
    grad_heads = grad_heads.reshape(seq_len, lanes)
    sum_b = over_dp(grads_b)
    grad_proj = jnp.einsum(
        "pbtl,btd->pld", mixed.reshape(np_, nc, own_rows, lanes), both, preferred_element_type=F32
    ).astype(BF)
    sum_p = over_dp(grad_proj.reshape(dp, piece, width))

    def pieces_over_chips(value):
        split = value.reshape(value.shape[0], chips, width // chips).transpose(1, 0, 2)
        sent = [flip(pick(split, i_z ^ bit), ("g", "p"), chips, bit) for bit in range(1, chips)]
        return [pick(split, i_z)] + sent

    def add_up(values):
        return sum(value.astype(F32) for value in values)

    sum_a = pieces_over_chips(after(sum_a, grad_heads))
    dx = []
    grad_tables = 0.0
    for q in range(pieces):
        rows, table = attend_back(
            q * core_heads, core_heads, query_a, key_rows, value_rows, att_f, grad_heads, tables, side
        )
        if q == 0:
            rows, *sum_a = tie(rows, *sum_a)
            sum_b = pieces_over_chips(after(sum_b, rows))
            sum_p = pieces_over_chips(after(sum_p, rows))
            key_rows = after(key_rows, rows)
        elif q == 1:
            rows, *both_sums = tie(rows, *sum_b, *sum_p)
            sum_b, sum_p = both_sums[:chips], both_sums[chips:]
        dx.append(rows)
        grad_tables = grad_tables + table
    sum_a, sum_b, sum_p = add_up(sum_a), add_up(sum_b), add_up(sum_p)
    out_fc1 = jnp.stack([sum_a[:shard], sum_b[:shard]], 1).reshape(shard, unit)

    def swap_columns(value):
        split = value.reshape(value.shape[0], nc, -1)
        theirs = flip(pick(split, 1 - i_c, 1).astype(BF), "c", nc, 1).astype(F32)
        mine = pick(split, i_c, 1)
        return jnp.where(i_c == 0, jnp.stack([mine, theirs]), jnp.stack([theirs, mine]))

    out_fc2 = jnp.stack([sum_a[shard:].reshape(per, unit // 2, -1), sum_b[shard:].reshape(per, unit // 2, -1)], 1)
    out_fc2 = swap_columns(out_fc2.reshape(per * unit, -1)).reshape(nc, per, unit, -1)
    out_fc2 = out_fc2.transpose(1, 0, 2, 3).reshape(hidden // dp, -1)
    out_proj = swap_columns(sum_p).reshape(shard, -1)

    far_send, far_keep, sums = rows_back(i_g ^ 1, i_c, dx, raw, qkv_full, np_, row_count)
    far_came = flip(far_send, "c", nc, 1)
    near_send, near_keep, part = rows_back(i_g, i_c, after(tuple(dx), far_send), raw, qkv_full, np_, row_count)
    near_send, far_came = tie(near_send, far_came)
    sums = sums + part
    near_came = flip(near_send, "c", nc, 1)
    far_sum = (far_keep + far_came.astype(F32)).astype(BF)
    far_pieces = [pick(far_sum, i_p)] + [flip(pick(far_sum, i_p ^ k), "p", np_, k) for k in range(1, np_)]
    homes_start = [far_sum, near_send]
    homes_later = (far_pieces, near_keep, near_came)
    dx = tie(*dx, *homes_start)[: pieces]
    grad_qkv = [lax.dot_general(normed, rows, TN, preferred_element_type=F32).astype(BF) for rows in dx]
    grad_qkv, (far_pieces, near_keep, near_came) = tie(grad_qkv, homes_later)
    far_rows = flip(add_up(far_pieces).astype(BF), "g", ng, 1).astype(F32)
    near_rows = scatter_sum((near_keep + near_came.astype(F32)).astype(BF), "p", np_, i_p)
    grad_normed = jnp.where(i_g == 0, jnp.stack([near_rows, far_rows]), jnp.stack([far_rows, near_rows]))
    grad_norm, _ = norm_back(inputs_rows, gain_one, grad_normed.reshape(own_rows, width))
    grad_patches = (grad_middle + grad_norm).astype(BF).reshape(patches.shape)

    qkv_rows_sum = scatter_sum(jnp.concatenate(grad_qkv, 1).reshape(dp, shard, 3 * lanes), "dp", dp, i_dp).astype(BF)
    qkv_rows_sum = scatter_sum(qkv_rows_sum.reshape(ng, shard // ng, 3 * lanes), "g", ng, i_g).astype(BF)
    cell = width // ranks
    send = jnp.zeros((ranks * 3, shard // ng, cell), BF)
    for n, start in enumerate(starts):
        for u in range(piece // cell):
            column = n * piece + u * cell
            block = qkv_rows_sum[None, :, column : column + cell]
            send = lax.dynamic_update_slice_in_dim(send, block, start // cell + u, 0)
    taken = lax.all_to_all(
        send.reshape(ranks, 3, shard // ng, cell), ("g", "p", "c"), split_axis=0, concat_axis=0, tiled=True
    )
    taken = taken.reshape(ng, np_ * nc, 3, shard // ng, cell).astype(F32).sum(1)
    out_qkv = taken.transpose(0, 2, 1, 3).reshape(shard, 3 * cell)

    def everywhere(value):
        for name, size in (("c", nc), ("p", np_), ("g", ng), ("dp", dp)):
            bit = 1
            while bit < size:
                value = value + flip(value, name, size, bit)
                bit *= 2
        return value

    bias_half = jnp.stack([bias_a.reshape(dp, per, unit // 2), bias_b.reshape(dp, per, unit // 2)], 2)
    bias_half = bias_half.reshape(dp * per, 1, unit)
    bias_full = jnp.concatenate([bias_half] * nc, 1)
    core = lax.broadcasted_iota(jnp.int32, bias_full.shape, 1)
    bias_full = jnp.where(core == i_c, bias_full, 0.0).reshape(-1, width)
    rows_f = lambda value: jnp.sum(value.astype(F32), 0)
    early = jnp.stack([jnp.sum(grad_two * normal_two, 0), jnp.sum(grad_two, 0), rows_f(back_own), rows_f(branch_own)])
    early = everywhere(jnp.concatenate([early, bias_full]))

    def spread(part):
        full = jnp.zeros((width,), F32)
        for q in range(pieces):
            block = sums[2 + q, part * piece : (part + 1) * piece]
            full = lax.dynamic_update_slice_in_dim(full, block, starts[3 * q], 0)
        return full

    entries = rel_pos_h.shape[0]
    rel = jnp.stack([grad_tables[:entries, :HD], grad_tables[128 : 128 + entries, :HD]])[:, ::-1]
    late = jnp.concatenate([sums[0], sums[1], spread(0), spread(2), rel.reshape(-1)])
    late = everywhere(late)
    rel = late[4 * width :].reshape(2, entries, HD)

    def owned(vec):
        return lax.dynamic_slice_in_dim(vec, i_dp * (vec.shape[0] // dp), vec.shape[0] // dp, 0)

    late_vec = [owned(late[n * width : (n + 1) * width]) for n in range(4)]
    early_vec = [owned(early[n]) for n in range(4)]
    return (
        output,
        grad_patches,
        late_vec[0],
        late_vec[1],
        out_qkv,
        late_vec[2],
        late_vec[3],
        out_proj,
        early_vec[2],
        early_vec[0],
        early_vec[1],
        out_fc1,
        owned(early[4:].reshape(-1)),
        out_fc2,
        early_vec[3],
        rel[0],
        rel[1],
    )


def solution(mesh):
    dp, ranks = mesh.shape["dp"], mesh.shape["seq"]

    def call(*args):
        images = args[0].shape[0] // dp
        shape = (dp, images, ranks // images // 2, 2)
        fine = jax.sharding.Mesh(mesh.devices.reshape(shape), ("dp", "g", "p", "c"))
        seq = ("g", "p", "c")
        tokens, rows, both = P("dp", seq, None), P("dp", None), P("dp", seq)
        vec = P("dp")
        return jax.shard_map(
            on_device,
            mesh=fine,
            in_specs=(
                tokens, vec, vec, rows, vec, vec, rows, vec, vec, vec, rows, vec, rows, vec, P(), P(), tokens
            ),
            out_specs=(
                tokens, tokens, vec, vec, both, vec, vec, both, vec, vec, vec, both, vec, both, vec, P(), P()
            ),
            check_vma=False,
        )(*args)

    return call
```

```python
import math
from functools import partial

import jax
import jax.numpy as jnp
from jax import lax
from jax.experimental import pallas as pl
from jax.experimental.pallas import tpu as pltpu
from jax.sharding import PartitionSpec as P

H = 16
HD = 80
EPSILON = 1e-06
NT = (((1,), (1,)), ((), ()))
TN = (((0,), (0,)), ((), ()))
BF = jnp.bfloat16
F32 = jnp.float32
LOG2E = 1.4426950408889634
FACTOR = LOG2E / math.sqrt(HD)
FREE = pl.CostEstimate(flops=1, bytes_accessed=1, transcendentals=0)


def busy(gflops):
    return pl.CostEstimate(flops=gflops * 10**9, bytes_accessed=1, transcendentals=0)


def dot(a, b, dims=(((1,), (0,)), ((), ()))):
    return lax.dot_general(a, b, dims, preferred_element_type=F32)


def params(axes, mib=60):
    return pltpu.CompilerParams(
        dimension_semantics=("arbitrary",) * axes, vmem_limit_bytes=mib << 20
    )


def whole(*shape):
    return pl.BlockSpec(shape, lambda *at: (0,) * len(shape), pipeline_mode=pl.Buffered(1))


def flip_tables(rel_h, rel_w):
    entries = rel_h.shape[0]
    pad = ((0, 128 - entries), (0, 0))
    return jnp.concatenate([jnp.pad(rel_h[::-1], pad), jnp.pad(rel_w[::-1], pad)], 0)


def normal_rows(values):
    center = values - jnp.mean(values, -1, keepdims=True)
    spread = jnp.mean(center * center, -1, keepdims=True)
    return center * lax.rsqrt(spread + EPSILON)


def qkv_kernel(pieces, group_heads, side, raw, gain, shift, w, bias, tables, normed, qa, kp, vp):
    rows = raw.shape[0]
    rows_n = (normal_rows(raw[...].astype(F32)) * gain[...] + shift[...]).astype(BF)
    normed[...] = rows_n
    joined = (dot(rows_n, w[...]) + bias[...]).astype(BF)
    first_row = pl.program_id(0) * (rows // side)
    lane = lax.broadcasted_iota(jnp.int32, (rows, 128), 1)
    group_lane = lax.broadcasted_iota(jnp.int32, (side, 128), 1)
    group_row = lax.broadcasted_iota(jnp.int32, (side, 128), 0)
    col_hot = (group_lane == group_row) | ((group_lane >= side) & (group_lane < side + 3))
    col_hot = jnp.where(col_hot, 1.0, 0.0).astype(BF)
    hot = []
    for i in range(rows // side):
        hot.append(jnp.where(group_lane == first_row + (HD + i), 1.0, 0.0).astype(BF))
    row_hot = jnp.concatenate(hot, 0)
    col_hot = jnp.concatenate([col_hot] * (rows // side), 0)
    width = group_heads * HD
    for n in range(pieces * group_heads):
        q_at = (n // group_heads) * 3 * width + (n % group_heads) * HD
        q = joined[:, q_at : q_at + HD]
        g = dot(q, tables[...], NT) * math.sqrt(HD)
        gh = []
        gw = []
        for i in range(rows // side):
            part = g[i * side : (i + 1) * side]
            gh.append(pltpu.roll(part[:, :128], first_row + (33 + i), axis=1))
            gw.append(pltpu.roll(part[:, 128:], 81, axis=1, stride=1, stride_axis=0))
        qa[n, :, 0:128] = jnp.concatenate(gh, 0).astype(BF)
        qa[n, :, 0:HD] = q
        qa[n, :, 128:256] = jnp.where(lane < side, jnp.concatenate(gw, 0), 0.0).astype(BF)
        kp[n, :, 0:128] = row_hot
        kp[n, :, 128:256] = col_hot
        kp[n, :, 0:HD] = joined[:, q_at + width : q_at + width + HD]
        vp[n] = jnp.ones((rows, 128), BF)
        vp[n, :, 0:HD] = joined[:, q_at + 2 * width : q_at + 2 * width + HD]


def qkv_rows(raw, gain, shift, w, bias, tables, pieces, group_heads, side, rows=384):
    seq_len, width = raw.shape
    lanes = w.shape[1]
    heads = pieces * group_heads
    return pl.pallas_call(
        partial(qkv_kernel, pieces, group_heads, side),
        grid=(seq_len // rows,),
        in_specs=[
            pl.BlockSpec((rows, width), lambda i: (i, 0)),
            whole(1, width),
            whole(1, width),
            whole(width, lanes),
            whole(1, lanes),
            whole(256, HD),
        ],
        out_specs=[
            pl.BlockSpec((rows, width), lambda i: (i, 0)),
            pl.BlockSpec((heads, rows, 256), lambda i: (0, i, 0)),
            pl.BlockSpec((heads, rows, 256), lambda i: (0, i, 0)),
            pl.BlockSpec((heads, rows, 128), lambda i: (0, i, 0)),
        ],
        out_shape=[
            jax.ShapeDtypeStruct((seq_len, width), BF),
            jax.ShapeDtypeStruct((heads, seq_len, 256), BF),
            jax.ShapeDtypeStruct((heads, seq_len, 256), BF),
            jax.ShapeDtypeStruct((heads, seq_len, 128), BF),
        ],
        compiler_params=params(1),
        cost_estimate=FREE,
        name="qkv_rows",
    )(raw, gain, shift, w, bias, tables)


def attend_kernel(heads, side, aliased, sub, at, qa, kp, vp, *refs):
    o, of, qo = refs[2:] if aliased else refs
    rows = qa.shape[1]
    h = pl.program_id(0)
    base = pl.multiple_of(pl.program_id(1) * rows, rows)
    lane = lax.broadcasted_iota(jnp.int32, (sub, 128), 1)
    count = rows // sub
    scores = [dot(qa[0, 0:sub, :], kp[0], NT)]
    outs = []
    for n in range(count):
        part = slice(n * sub, (n + 1) * sub)
        if n + 1 < count:
            scores.append(dot(qa[0, (n + 1) * sub : (n + 2) * sub, :], kp[0], NT))
        s = scores[n]
        m = jnp.max(s, -1, keepdims=True)
        p = jnp.exp2(s * FACTOR - m * FACTOR).astype(BF)
        out = dot(p, vp[0])
        total = out[:, HD : HD + 1]
        out = out / total
        norm = m + jnp.log2(total) / FACTOR
        hi = norm.astype(BF).astype(F32)
        mid = (norm - hi).astype(BF).astype(F32)
        low = norm - hi - mid
        old = qa[0, part, 128:256].astype(F32)
        old = jnp.where(lane == side, -hi, old)
        old = jnp.where(lane == side + 1, -mid, old)
        old = jnp.where(lane == side + 2, -low, old)
        qo[0, part, 0:128] = qa[0, part, 0:128]
        qo[0, part, 128:256] = old.astype(BF)
        outs.append(out)
    out = jnp.concatenate(outs, 0)
    part = pl.ds(base, rows)
    for n in range(heads):

        @pl.when(h == n)
        def _(n=n):
            o[part, n * HD : (n + 1) * HD] = out[:, 0:HD].astype(BF)
            of[part, n * HD : (n + 1) * HD] = out[:, 0:HD]


def attend(group, qa, kp, vp, side, groups, old=(), tq=1152, sub=576):
    heads, seq_len, _ = qa.shape
    rows = seq_len // groups
    steps = rows // tq
    lanes = heads * HD
    query = pl.BlockSpec((1, tq, 256), lambda h, i, at: (h, at[0] * steps + i, 0))
    return pl.pallas_call(
        partial(attend_kernel, heads, side, bool(old), sub),
        grid_spec=pltpu.PrefetchScalarGridSpec(
            num_scalar_prefetch=1,
            grid=(heads, steps),
            in_specs=[
                query,
                pl.BlockSpec((1, seq_len, 256), lambda h, i, at: (h, 0, 0)),
                pl.BlockSpec((1, seq_len, 128), lambda h, i, at: (h, 0, 0)),
            ]
            + [pl.BlockSpec(memory_space=pl.ANY)] * len(old),
            out_specs=[
                pl.BlockSpec((rows, lanes), lambda h, i, at: (0, 0)),
                pl.BlockSpec((rows, lanes), lambda h, i, at: (at[0], 0)),
                query,
            ],
        ),
        out_shape=[
            jax.ShapeDtypeStruct((rows, lanes), BF),
            jax.ShapeDtypeStruct((seq_len, lanes), F32),
            jax.ShapeDtypeStruct((heads, seq_len, 256), BF),
        ],
        input_output_aliases={4: 1, 5: 2} if old else {},
        compiler_params=params(2),
        cost_estimate=busy(20),
        name="attend",
    )(jnp.stack([group]), qa, kp, vp, *old)


def attend_back_kernel(heads, first, side, uc, qa_ref, kp, vp, of, go, tables, dx, gt, kt, dop, dk, dv, dq):
    seq_len = kp.shape[1]
    tb = qa_ref.shape[1]
    h = pl.program_id(0)
    step = pl.program_id(1)
    last = pl.num_programs(1) - 1
    scale = HD ** (-0.5)
    rows = seq_len // 9

    @pl.when((h == 0) & (step == 0))
    def _():
        gt[...] = jnp.zeros_like(gt)

        def prep(i, c):
            part = pl.ds(pl.multiple_of(i * rows, rows), rows)
            lane = lax.broadcasted_iota(jnp.int32, (rows, 128), 1)
            for n in range(heads):
                at = (first + n) * HD
                rows_go = go[part, at : at + HD]
                inner = jnp.sum(rows_go.astype(F32) * of[part, at : at + HD], -1, keepdims=True)
                hi = inner.astype(BF).astype(F32)
                tail = jnp.where(lane == HD, -hi, jnp.where(lane == HD + 1, hi - inner, 0.0))
                dop[n, part, :] = tail.astype(BF)
                dop[n, part, 0:HD] = rows_go
            return c

        lax.fori_loop(0, 9, prep, 0)

    @pl.when(step == 0)
    def _():
        def prep(i, c):
            part = pl.ds(pl.multiple_of(i * rows, rows), rows)
            kt[:, part] = kp[0, part, :].T[0 : HD + 2 * side]
            dk[part, :] = jnp.zeros((rows, 128), F32)
            dv[part, :] = jnp.zeros((rows, 128), F32)
            return c

        lax.fori_loop(0, 9, prep, 0)

    base = pl.ds(pl.multiple_of(step * tb, tb), tb)
    qa = qa_ref[0]
    do = dop[h, base, :]

    def scores(j):
        part = slice(j * uc, (j + 1) * uc)
        return dot(kp[0, part, :], qa, NT), dot(vp[0, part, :], do, NT)

    acc = None
    count = seq_len // uc
    ahead = scores(0)
    for j in range(count):
        s, dp = ahead
        if j + 1 < count:
            ahead = scores(j + 1)
        part = slice(j * uc, (j + 1) * uc)
        p = jnp.exp2(s * FACTOR)
        ds = (p * dp).astype(BF)
        dv[part, :] += dot(p.astype(BF), do)
        dk[part, :] += dot(ds, qa[:, 0:128])
        term = dot(kt[:, part], ds)
        acc = term if acc is None else acc + term
    acc = jnp.concatenate([acc, jnp.zeros((256 - HD - 2 * side, tb), F32)], 0).T
    lane = lax.broadcasted_iota(jnp.int32, (tb, 128), 1)
    groups = tb // side
    rel_h = jnp.where(lane < HD, 0.0, acc[:, :128])
    rel_w = jnp.where(lane < side, acc[:, 128:], 0.0)
    back_h = []
    back_w = []
    for i in range(groups):
        part = slice(i * side, (i + 1) * side)
        back_h.append(pltpu.roll(rel_h[part], 256 - 33 - step * groups - i, axis=1))
        back_w.append(stagger(rel_w[part], side))
    both = jnp.concatenate([jnp.concatenate(back_h, 0), jnp.concatenate(back_w, 0)], 1).astype(BF)
    dq[base, :] = acc[:, :HD] * scale + dot(both, tables[...])
    gt[...] += dot(both, qa[:, 0:128], TN)

    width = heads * HD
    for n in range(heads):

        @pl.when((h == n) & (step == last))
        def _(n=n):
            def post(i, c):
                part = pl.ds(pl.multiple_of(i * rows, rows), rows)
                at = n * HD
                dx[part, at : at + HD] = dq[part, :].astype(BF)
                dx[part, width + at : width + at + HD] = (dk[part, 0:HD] * scale).astype(BF)
                dx[part, 2 * width + at : 2 * width + at + HD] = dv[part, 0:HD].astype(BF)
                return c

            lax.fori_loop(0, 9, post, 0)


def stagger(val, side):
    row = lax.broadcasted_iota(jnp.int32, val.shape, 0)
    shift = side - 1 - row
    bit = 1
    while bit < side:
        val = jnp.where((shift & bit) != 0, pltpu.roll(val, bit, axis=1), val)
        bit *= 2
    return val


def attend_back(first, count, qa, kp, vp, of, go, tables, side, tb=768, uc=256):
    heads, seq_len, _ = qa.shape
    lanes = heads * HD
    return pl.pallas_call(
        partial(attend_back_kernel, count, first, side, uc),
        grid=(count, seq_len // tb),
        in_specs=[
            pl.BlockSpec((1, tb, 256), lambda h, i: (first + h, i, 0)),
            pl.BlockSpec((1, seq_len, 256), lambda h, i: (first + h, 0, 0)),
            pl.BlockSpec((1, seq_len, 128), lambda h, i: (first + h, 0, 0)),
            whole(seq_len, lanes),
            whole(seq_len, lanes),
            whole(256, HD),
        ],
        out_specs=[whole(seq_len, 3 * count * HD), whole(256, 128)],
        out_shape=[
            jax.ShapeDtypeStruct((seq_len, 3 * count * HD), BF),
            jax.ShapeDtypeStruct((256, 128), F32),
        ],
        scratch_shapes=[
            pltpu.VMEM((HD + 2 * side, seq_len), BF),
            pltpu.VMEM((count, seq_len, 128), BF),
            pltpu.VMEM((seq_len, 128), F32),
            pltpu.VMEM((seq_len, 128), F32),
            pltpu.VMEM((seq_len, HD), F32),
        ],
        compiler_params=params(2),
        cost_estimate=busy(50),
        name="attend_back",
    )(qa, kp, vp, of, go, tables)


def mlp_kernel(aliased, per, n_own, n_other, g_own, g_other, w1, b1, w2, *refs):
    if aliased:
        out_in, gn_in, out, gn, grads, gb1, n2, gb, act, gbef = refs
    else:
        out, gn, grads, gb1, n2, gb, act, gbef = refs
    step = pl.program_id(0)
    chunk = out.shape[0]
    shards, shard, hidden = w1.shape
    width = n_own.shape[1]
    steps = 2 * per

    @pl.when(step == 0)
    def _():
        gb1[...] = jnp.zeros_like(gb1)

    @pl.when(step < steps)
    def _():
        first = w1[...].reshape(width, hidden)
        second = w2[...].reshape(hidden, width)
        dst = pl.ds(pl.multiple_of(step * chunk, chunk), chunk)
        mine = step < per
        n2[dst, :] = jnp.where(mine, n_own[...], n_other[...])
        gb[dst, :] = jnp.where(mine, g_own[...], g_other[...])
        before = dot(n2[dst, :], first) + b1[...]
        grad_act = dot(gb[dst, :], second, NT)
        cdf = 0.5 + 0.5 * lax.erf(before * math.sqrt(0.5))
        act[dst, :] = (before * cdf).astype(BF)
        slope = cdf + before * (jnp.exp(-0.5 * before * before) * (1.0 / math.sqrt(2.0 * math.pi)))
        grad_before = slope * grad_act
        gbef[dst, :] = grad_before.astype(BF)
        gb1[...] += jnp.sum(gbef[dst, :].astype(F32), 0, keepdims=True)
        value = dot(act[dst, :], second)
        back = dot(gbef[dst, :], first, NT)
        if aliased:
            value = value + out_in[...]
            back = back + gn_in[...]
        out[...] = value
        gn[...] = back

    for j in range(shards):

        @pl.when(step == steps + j)
        def _(j=j):
            rows = slice(j * shard, (j + 1) * shard)
            grads[0, 0:shard, :] = dot(n2[:, rows], gbef[...], TN).astype(BF)
            grads[0, shard : 2 * shard, :] = dot(act[:, rows], gb[...], TN).astype(BF)


def mlp_half(n_own, n_other, g_own, g_other, weights, b1, old=(), chunk=288):
    half, width = n_own.shape
    dp = weights.shape[0]
    shard = width // dp
    hidden = width
    chunk = min(chunk, half)
    per = half // chunk
    steps = 2 * per
    tile = pl.BlockSpec((chunk, width), lambda i: (jnp.minimum(i, steps - 1), 0))
    own = pl.BlockSpec((chunk, width), lambda i: (jnp.minimum(i, per - 1), 0))
    other = pl.BlockSpec((chunk, width), lambda i: (jnp.clip(i - per, 0, per - 1), 0))
    rows = jax.ShapeDtypeStruct((2 * half, width), F32)
    return pl.pallas_call(
        partial(mlp_kernel, bool(old), per),
        grid=(steps + dp,),
        in_specs=[own, other, own, other]
        + [
            pl.BlockSpec((dp, shard, width), lambda i: (0, 0, 0), pipeline_mode=pl.Buffered(1)),
            whole(1, hidden),
            pl.BlockSpec((dp, shard, width), lambda i: (0, 1, 0), pipeline_mode=pl.Buffered(1)),
        ]
        + [tile] * len(old),
        out_specs=[
            tile,
            tile,
            pl.BlockSpec((1, 2 * shard, width), lambda i: (jnp.maximum(i - steps, 0), 0, 0)),
            whole(1, hidden),
        ],
        out_shape=[
            rows,
            rows,
            jax.ShapeDtypeStruct((dp, 2 * shard, width), BF),
            jax.ShapeDtypeStruct((1, hidden), F32),
        ],
        input_output_aliases={7: 0, 8: 1} if old else {},
        scratch_shapes=[pltpu.VMEM((2 * half, width), BF)] * 4,
        compiler_params=params(1, 63),
        cost_estimate=busy(35),
        name="mlp_half",
    )(n_own, n_other, g_own, g_other, weights, b1, weights, *old)


def select_kernel(ng, np_, nc, at, qkv, fc1, fc2, proj, own, *slabs):
    i_p, i_c = at[1], at[2]
    shard = fc1.shape[0]
    width = proj.shape[1]
    hidden = fc1.shape[1]
    chips = ng * np_
    unit = hidden // (chips * nc)
    part = unit // 2
    piece = proj.shape[0] // nc
    shard_lanes = proj.shape[0]
    lanes = own.shape[1] // 3
    pieces = lanes // piece
    per = fc2.shape[0] // (nc * unit)
    for c in range(nc):

        @pl.when(i_c == c)
        def _(c=c):
            for u in range(2):
                for z in range(chips):
                    src = (z * nc + c) * unit + u * part
                    slabs[u][0:shard, z * part : (z + 1) * part] = fc1[:, src : src + part]
                for b in range(per):
                    src = (b * nc + c) * unit + u * part
                    dst = shard + b * part
                    slabs[u][dst : dst + part, :] = fc2[src : src + part, :]
            slabs[0][2 * shard : 2 * shard + piece, :] = proj[c * piece : (c + 1) * piece, :]

        for p in range(np_):

            @pl.when((i_c == c) & (i_p == p))
            def _(c=c, p=p):
                for q in range(pieces):
                    for t in range(3):
                        src = t * width + (p * pieces + q) * shard_lanes + c * piece
                        dst = (3 * q + t) * piece
                        own[:, dst : dst + piece] = qkv[:, src : src + piece]


def select(at, qkv, fc1, fc2, proj, ng, np_, nc, lanes):
    shard, width = proj.shape[0], proj.shape[1]
    return pl.pallas_call(
        partial(select_kernel, ng, np_, nc),
        in_specs=[pl.BlockSpec(memory_space=pltpu.SMEM)] + [pl.BlockSpec(memory_space=pltpu.VMEM)] * 4,
        out_specs=[pl.BlockSpec(memory_space=pltpu.VMEM)] * 3,
        out_shape=[
            jax.ShapeDtypeStruct((shard, 3 * lanes), BF),
            jax.ShapeDtypeStruct((2 * shard + shard // nc, width), BF),
            jax.ShapeDtypeStruct((2 * shard, width), BF),
        ],
        compiler_params=pltpu.CompilerParams(vmem_limit_bytes=40 << 20),
        cost_estimate=FREE,
        name="select",
    )(at, qkv, fc1, fc2, proj)


def start_kernel(sizes, split, patches, own, vec, rows, full, vecs, local, send, recv):
    dp, ng, np_ = sizes
    i_dp, i_g, i_p, i_c = (lax.axis_index(name) for name in ("dp", "g", "p", "c"))
    count = patches.shape[1]
    step = count // split

    barrier = pltpu.get_barrier_semaphore()
    peers = [{"dp": i_dp ^ k} for k in range(1, dp)]
    peers += [{"g": i_g ^ k} for k in range(1, ng)]
    peers += [{"p": i_p ^ k} for k in range(1, np_)]
    peers += [{"c": 1 - i_c}]
    for peer in peers:
        pl.semaphore_signal(barrier, inc=1, device_id=peer, device_id_type=pl.DeviceIdType.MESH)
    pl.semaphore_wait(barrier, len(peers))

    used = []

    def remote(src, dst, peer):
        n = len(used)
        copy = pltpu.make_async_remote_copy(
            src_ref=src,
            dst_ref=dst,
            send_sem=send.at[n],
            recv_sem=recv.at[n],
            device_id=peer,
            device_id_type=pl.DeviceIdType.MESH,
        )
        used.append(copy)
        return copy

    def place(g, p, c, part):
        start = ((g * np_ + p) * 2 + c) * count + part * step
        return rows.at[pl.ds(pl.multiple_of(start, 8), step)]

    mine = [patches.at[i_g, pl.ds(part * step, step)] for part in range(split)]
    home = [pltpu.make_async_copy(mine[part], place(i_g, i_p, i_c, part), local.at[part]) for part in range(split)]
    home.append(pltpu.make_async_copy(own, full.at[i_dp], local.at[split]))
    home.append(pltpu.make_async_copy(vec, vecs.at[i_dp], local.at[split + 1]))

    far = {}
    for part in range(split):
        for bit in range(1, ng):
            src = patches.at[i_g ^ bit, pl.ds(part * step, step)]
            far[bit, part] = remote(src, place(i_g, i_p, i_c, part), {"g": i_g ^ bit})
            far[bit, part].start()
    over_dp = []
    for bit in range(1, dp):
        over_dp.append(remote(vec, vecs.at[i_dp], {"dp": i_dp ^ bit}))
        over_dp.append(remote(own, full.at[i_dp], {"dp": i_dp ^ bit}))
    for copy in over_dp:
        copy.start()
    near = {}
    for bit in range(1, np_):
        for part in range(split):
            near[bit, part] = remote(mine[part], place(i_g, i_p, i_c, part), {"p": i_p ^ bit})
            near[bit, part].start()
    cores = []
    for part in range(split):
        cores.append(remote(mine[part], place(i_g, i_p, i_c, part), {"c": 1 - i_c}))
        cores[-1].start()
    for copy in home:
        copy.start()

    onward = {}
    for part in range(split):
        for bit in range(1, ng):
            far[bit, part].wait_recv()
            came = place(i_g ^ bit, i_p, i_c, part)
            for bit_p in range(1, np_):
                onward[bit, bit_p, part] = remote(came, came, {"p": i_p ^ bit_p})
                onward[bit, bit_p, part].start()
            cores.append(remote(came, came, {"c": 1 - i_c}))
            cores[-1].start()
        for bit in range(1, np_):
            near[bit, part].wait_recv()
            came = place(i_g, i_p ^ bit, i_c, part)
            cores.append(remote(came, came, {"c": 1 - i_c}))
            cores[-1].start()
    for (bit, bit_p, part), copy in onward.items():
        copy.wait_recv()
        came = place(i_g ^ bit, i_p ^ bit_p, i_c, part)
        cores.append(remote(came, came, {"c": 1 - i_c}))
        cores[-1].start()
    for copy in over_dp + cores:
        copy.wait_recv()
    for copy in used:
        copy.wait_send()
    for copy in home:
        copy.wait()


def start_exchange(patches, own, vec, sizes, split=3):
    dp, ng, np_ = sizes
    images, count, width = patches.shape
    chunk_copies = ng * np_ + (ng - 1) + (np_ - 1) + (ng - 1) * (np_ - 1)
    copies = 2 * (dp - 1) + split * chunk_copies
    hbm = pl.BlockSpec(memory_space=pl.ANY)
    return pl.pallas_call(
        partial(start_kernel, sizes, split),
        in_specs=[hbm] * 3,
        out_specs=[hbm] * 3,
        out_shape=[
            jax.ShapeDtypeStruct((ng * np_ * 2 * count, width), BF),
            jax.ShapeDtypeStruct((dp,) + own.shape, BF),
            jax.ShapeDtypeStruct((dp,) + vec.shape, BF),
        ],
        scratch_shapes=[
            pltpu.SemaphoreType.DMA((split + 2,)),
            pltpu.SemaphoreType.DMA((copies,)),
            pltpu.SemaphoreType.DMA((copies,)),
        ],
        compiler_params=pltpu.CompilerParams(collective_id=0, has_side_effects=True),
        cost_estimate=FREE,
        name="start_exchange",
    )(patches, own, vec)


def rows_back_kernel(pieces, *refs):
    dx = refs[:pieces]
    raw, w, out, sums = refs[pieces:]
    total = None
    width = dx[0].shape[1]
    for q in range(pieces):
        term = dot(dx[q][...], w[:, q * width : (q + 1) * width], NT)
        total = term if total is None else total + term
    normal = normal_rows(raw[...].astype(F32))

    @pl.when(pl.program_id(0) == 0)
    def _():
        sums[...] = jnp.zeros_like(sums)

    sums[0:1, :] += jnp.sum(total * normal, 0, keepdims=True)
    sums[1:2, :] += jnp.sum(total, 0, keepdims=True)
    for q in range(pieces):
        sums[2 + q : 3 + q, 0:width] += jnp.sum(dx[q][...].astype(F32), 0, keepdims=True)
    out[...] = total.astype(BF)


def rows_back(dx, raw, w, rows=384):
    pieces = len(dx)
    seq_len, width = raw.shape
    lanes = dx[0].shape[1]
    block = lambda cols: pl.BlockSpec((rows, cols), lambda i: (i, 0))
    return pl.pallas_call(
        partial(rows_back_kernel, pieces),
        grid=(seq_len // rows,),
        in_specs=[block(lanes)] * pieces + [block(width), whole(width, pieces * lanes)],
        out_specs=[block(width), whole(8, width)],
        out_shape=[jax.ShapeDtypeStruct((seq_len, width), BF), jax.ShapeDtypeStruct((8, width), F32)],
        compiler_params=params(1),
        cost_estimate=busy(15),
        name="rows_back",
    )(*dx, raw, w)


class Links:
    def __init__(self, send, recv):
        self.send, self.recv, self.copies = send, recv, []

    def __call__(self, src, dst, peer):
        n = len(self.copies)
        copy = pltpu.make_async_remote_copy(
            src_ref=src,
            dst_ref=dst,
            send_sem=self.send.at[n],
            recv_sem=self.recv.at[n],
            device_id=peer,
            device_id_type=pl.DeviceIdType.MESH,
        )
        copy.start()
        self.copies.append(copy)
        return copy

    def drain(self):
        for copy in self.copies:
            copy.wait_send()


def meet(peers):
    barrier = pltpu.get_barrier_semaphore()
    for peer in peers:
        pl.semaphore_signal(barrier, inc=1, device_id=peer, device_id_type=pl.DeviceIdType.MESH)
    pl.semaphore_wait(barrier, len(peers))


def finish_kernel(sizes, split, pieces, part_w, vec_block, *refs):
    dp, ng, np_ = sizes
    chips = ng * np_
    rows_in, vec, inputs, grad_mid, gain = refs[:5]
    grads = refs[5 : 5 + pieces]
    parts_a, parts_b, parts_p = (refs[5 + pieces + n * chips : 5 + pieces + (n + 1) * chips] for n in range(3))
    (home, owned, total, out_fc1, out_fc2, out_proj, keep, came, pair, far, slabs, cells, taken, by_dp, by_chip, by_core,
     give, got, give_p, got_p, sem, send, recv, cell_send, cell_recv) = refs[5 + pieces + 3 * chips :]
    i_dp, i_g, i_p, i_c = (lax.axis_index(name) for name in ("dp", "g", "p", "c"))
    count = keep.shape[1]
    step = count // split
    ranks = chips * 2
    shard = owned.shape[0]
    cell = owned.shape[1] // 3
    i_s = (i_g * np_ + i_p) * 2 + i_c

    peers = [{"dp": i_dp ^ k} for k in range(1, dp)]
    for k in range(1, ranks):
        bit_g, bit_p, bit_c = k // (np_ * 2), (k // 2) % np_, k % 2
        peers.append({"g": i_g ^ bit_g, "p": i_p ^ bit_p, "c": i_c ^ bit_c})
    meet(peers)
    link = Links(send, recv)

    order = list(range(np_, chips)) + list(range(np_))
    z_of = lambda k: (i_g ^ (k // np_)) * np_ + (i_p ^ (k % np_))
    part_rows = lambda part: pl.ds(part * step, step)

    def rows_at(k, c, part):
        start = (z_of(k) * 2 + c) * count + part * step
        return rows_in.at[pl.ds(pl.multiple_of(start, 8), step)]

    block = vec_block
    rest = vec.shape[0] - dp * block

    def vec_rows(j):
        return vec.at[pl.ds(pl.multiple_of(j * block, 8), block)]

    by_dp[i_dp, 0:block] = vec[pl.ds(pl.multiple_of(i_dp * block, 8), block), :]
    by_dp[i_dp, block : block + rest] = vec[dp * block : dp * block + rest, :]
    vec_dp = []
    for bit in range(1, dp):
        peer = {"dp": i_dp ^ bit}
        vec_dp.append(link(vec_rows(i_dp ^ bit), by_dp.at[i_dp, pl.ds(0, block)], peer))
        vec_dp.append(link(vec.at[pl.ds(dp * block, rest)], by_dp.at[i_dp, pl.ds(block, rest)], peer))

    loads = {}
    from_core = {}
    n = 0
    for k in order:
        for part in range(split):
            loads[k, part] = pltpu.make_async_copy(rows_at(k, i_c, part), keep.at[k, part_rows(part)], sem.at[n])
            loads[k, part].start()
            n += 1
            from_core[k, part] = link(rows_at(k, 1 - i_c, part), came.at[k, part_rows(part)], {"c": 1 - i_c})
    from_dp = []
    own_slab = []
    for q in range(pieces):
        src = grads[q].at[pl.ds(pl.multiple_of(i_dp * shard, 8), shard)]
        own_slab.append(pltpu.make_async_copy(src, slabs.at[0, q], sem.at[n]))
        own_slab[-1].start()
        n += 1
    for bit in range(1, dp):
        for q in range(pieces):
            src = grads[q].at[pl.ds(pl.multiple_of((i_dp ^ bit) * shard, 8), shard)]
            from_dp.append(link(src, slabs.at[bit, q], {"dp": i_dp ^ bit}))

    def sum_of(ref, count):
        value = ref[0]
        for n in range(1, count):
            value = value + ref[n]
        return value

    i_z = i_g * np_ + i_p
    vec_late = []

    def vec_over_chips():
        for copy in vec_dp:
            copy.wait_recv()
        by_chip[i_z] = sum_of(by_dp, dp)
        for k in range(1, chips):
            peer = {"g": i_g ^ (k // np_), "p": i_p ^ (k % np_)}
            vec_late.append(link(by_chip.at[i_z], by_chip.at[i_z], peer))

    def vec_over_cores():
        for copy in vec_late:
            copy.wait_recv()
        by_core[i_c] = sum_of(by_chip, chips)
        vec_late.append(link(by_core.at[i_c], by_core.at[i_c], {"c": 1 - i_c}))

    def collected(parts):
        value = parts[0][...].astype(F32)
        for ref in parts[1:]:
            value = value + ref[...].astype(F32)
        return value

    def halves(value, there, swaps):
        cols = value.shape[1] // 2
        mine = jnp.where(i_c == 0, value[:, :cols], value[:, cols:])
        there[...] = jnp.where(i_c == 0, value[:, cols:], value[:, :cols]).astype(BF)
        return mine

    fc_rows = shard
    hidden_rows = give.shape[1]
    swaps = []
    part_lanes = parts_a[0].shape[1]
    per_rows = out_fc1.shape[1] // 2
    blocks = hidden_rows // per_rows

    def place_fc2(u, core, value):
        for b in range(blocks):
            start = ((b * 2 + core) * 2 + u) * per_rows
            at = pl.ds(pl.multiple_of(start, 8), per_rows)
            out_fc2[at, :] = value[b * per_rows : (b + 1) * per_rows, :]

    def place_proj(core, value):
        rows_p = value.shape[0]
        out_proj[pl.ds(pl.multiple_of(core * rows_p, 8), rows_p), :] = value

    def collect():
        for u, parts in ((0, parts_a), (1, parts_b)):
            value = collected(parts)
            out_fc1[:, u * per_rows : (u + 1) * per_rows] = value[0:fc_rows]
            place_fc2(u, i_c, halves(value[fc_rows:], give.at[u], swaps))
            swaps.append(link(give.at[u], got.at[u], {"c": 1 - i_c}))
        place_proj(i_c, halves(collected(parts_p), give_p, swaps))
        swaps.append(link(give_p, got_p, {"c": 1 - i_c}))

    def swapped():
        for copy in swaps:
            copy.wait_recv()
        for u in range(2):
            place_fc2(u, 1 - i_c, got[u].astype(F32))
        place_proj(1 - i_c, got_p[...].astype(F32))

    def add(k, part):
        loads[k, part].wait()
        from_core[k, part].wait_recv()
        at = part_rows(part)
        keep[k, at, :] = (keep[k, at, :].astype(F32) + came[k, at, :].astype(F32)).astype(BF)

    collect()
    from_pair = {}
    for n, k in enumerate(order):
        if n == len(order) // 2:
            vec_over_chips()
        for part in range(split):
            add(k, part)
            bit_p = k % np_
            if bit_p:
                at = part_rows(part)
                dst = pair.at[k // np_, bit_p, at]
                from_pair[k // np_, bit_p, part] = link(keep.at[k, at], dst, {"p": i_p ^ bit_p})

    def over_pair(bit_g, part):
        at = part_rows(part)
        value = keep[bit_g * np_, at, :].astype(F32)
        for bit_p in range(1, np_):
            from_pair[bit_g, bit_p, part].wait_recv()
            value = value + pair[bit_g, bit_p, at, :].astype(F32)
        return value

    from_far = {}
    for part in range(split):
        at = part_rows(part)
        for bit_g in range(1, ng):
            pair[bit_g, 0, at, :] = over_pair(bit_g, part).astype(BF)
            from_far[bit_g, part] = link(pair.at[bit_g, 0, at], far.at[bit_g, at], {"g": i_g ^ bit_g})

    def arrived(image, at, value):
        grad, _ = norm_back(inputs[image, at, :].astype(F32), gain[...], value)
        home[image, at, :] = (grad_mid[image, at, :] + grad).astype(BF)

    for copy in own_slab:
        copy.wait()
    for copy in from_dp:
        copy.wait_recv()
    width = part_w * 3
    shard_lanes = grads[0].shape[0] // dp
    group_lanes = part_w
    cell_n = 0
    waits = []
    for q in range(pieces):
        value = slabs[0, q].astype(F32)
        for bit in range(1, dp):
            value = value + slabs[bit, q].astype(F32)
        value = value.astype(BF)
        for t in range(3):
            for u in range(part_w // cell):
                lane = t * part_w + u * cell
                cells[cell_n] = value[:, lane : lane + cell]
                start = (i_p * pieces + q) * (shard_lanes // cell) + i_c * (part_w // cell) + u
                unit = t * (dp * (shard_lanes // cell)) + start
                owner = unit // 3
                slot = unit % 3
                dst = taken.at[i_g, slot]
                o_c = owner % 2
                o_p = (owner // 2) % np_
                o_g = owner // (2 * np_)

                @pl.when(owner == i_s)
                def _(cell_n=cell_n, dst=dst, slot=slot):
                    pltpu.make_async_copy(cells.at[cell_n], dst, cell_recv.at[i_g * 3 + slot]).start()

                @pl.when(owner != i_s)
                def _(cell_n=cell_n, dst=dst, slot=slot, o_g=o_g, o_p=o_p, o_c=o_c):
                    pltpu.make_async_remote_copy(
                        src_ref=cells.at[cell_n],
                        dst_ref=dst,
                        send_sem=cell_send.at[cell_n],
                        recv_sem=cell_recv.at[i_g * 3 + slot],
                        device_id={"g": o_g, "p": o_p, "c": o_c},
                        device_id_type=pl.DeviceIdType.MESH,
                    ).start()

                waits.append((cell_n, owner))
                cell_n += 1
    for part in range(split):
        arrived(i_g, part_rows(part), over_pair(0, part))

    vec_over_cores()
    swapped()
    vec_late[-1].wait_recv()
    total[...] = sum_of(by_core, 2)

    for part in range(split):
        at = part_rows(part)
        for bit_g in range(1, ng):
            from_far[bit_g, part].wait_recv()
            arrived(i_g ^ bit_g, at, far[bit_g, at, :].astype(F32))
    for slot in range(3):
        value = None
        for g in range(ng):
            pltpu.make_async_copy(cells.at[0], taken.at[g, slot], cell_recv.at[g * 3 + slot]).wait()
            term = taken[g, slot].astype(F32)
            value = term if value is None else value + term
        owned[:, slot * cell : (slot + 1) * cell] = value
    for cell_n, owner in waits:

        @pl.when(owner != i_s)
        def _(cell_n=cell_n):
            pltpu.make_async_copy(cells.at[cell_n], cells.at[cell_n], cell_send.at[cell_n]).wait()

    link.drain()


def finish(rows_in, vec, vec_block, inputs, grad_mid, gain, grads, parts, sizes, part_w, split=3):
    count = inputs.shape[1]
    dp, ng, np_ = sizes
    chips = ng * np_
    pieces = len(grads)
    width = rows_in.shape[1]
    shard = grads[0].shape[0] // dp
    cell = width // (chips * 2)
    total_cells = pieces * 3 * (part_w // cell)
    parts_a, parts_b, parts_p = parts
    lanes = parts_a[0].shape[1]
    hidden_rows = parts_a[0].shape[0] - shard
    piece_rows = parts_p[0].shape[0]
    own_vec = vec.shape[0] - (dp - 1) * vec_block
    copies = split * (chips + ng * (np_ - 1) + ng - 1) + (dp - 1) * pieces + 2 * (dp - 1) + chips + 3
    hbm = pl.BlockSpec(memory_space=pl.ANY)
    vmem = pl.BlockSpec(memory_space=pltpu.VMEM)
    return pl.pallas_call(
        partial(finish_kernel, sizes, split, pieces, part_w, vec_block),
        in_specs=[hbm] + [vmem] * 4 + [hbm] * pieces + [vmem] * (3 * chips),
        out_specs=[vmem] * 6,
        out_shape=[
            jax.ShapeDtypeStruct((ng, count, width), BF),
            jax.ShapeDtypeStruct((shard, 3 * cell), F32),
            jax.ShapeDtypeStruct((own_vec, 128), F32),
            jax.ShapeDtypeStruct((shard, 2 * lanes), F32),
            jax.ShapeDtypeStruct((4 * hidden_rows, lanes // 2), F32),
            jax.ShapeDtypeStruct((2 * piece_rows, lanes // 2), F32),
        ],
        scratch_shapes=[
            pltpu.VMEM((chips, count, width), BF),
            pltpu.VMEM((chips, count, width), BF),
            pltpu.VMEM((ng, np_, count, width), BF),
            pltpu.VMEM((ng, count, width), BF),
            pltpu.VMEM((dp, pieces, shard, 3 * part_w), BF),
            pltpu.VMEM((total_cells, shard, cell), BF),
            pltpu.VMEM((ng, 3, shard, cell), BF),
            pltpu.VMEM((dp, own_vec, 128), F32),
            pltpu.VMEM((chips, own_vec, 128), F32),
            pltpu.VMEM((2, own_vec, 128), F32),
            pltpu.VMEM((2, hidden_rows, lanes // 2), BF),
            pltpu.VMEM((2, hidden_rows, lanes // 2), BF),
            pltpu.VMEM((piece_rows, lanes // 2), BF),
            pltpu.VMEM((piece_rows, lanes // 2), BF),
            pltpu.SemaphoreType.DMA((split * chips + pieces,)),
            pltpu.SemaphoreType.DMA((copies,)),
            pltpu.SemaphoreType.DMA((copies,)),
            pltpu.SemaphoreType.DMA((total_cells,)),
            pltpu.SemaphoreType.DMA((3 * ng,)),
        ],
        compiler_params=pltpu.CompilerParams(collective_id=1, has_side_effects=True, vmem_limit_bytes=56 << 20),
        cost_estimate=FREE,
        name="finish",
    )(rows_in, vec, inputs, grad_mid, gain, *grads, *parts_a, *parts_b, *parts_p)


def places():
    return tuple(lax.axis_index(name) for name in ("dp", "g", "p", "c"))


def middle_kernel(sizes, near, *refs):
    dp, ng, np_ = sizes
    far = refs[:np_]
    (w, patches, bias, gain, shift, mid, two_own, two_other, mixed,
     pieces, mine, away, came, sem, send, recv) = refs[np_:]
    i_dp, i_g, i_p, i_c = places()
    rows = patches.shape[1]
    core = {"c": 1 - i_c}
    meet([core] + [{"p": i_p ^ k} for k in range(1, np_)])
    link = Links(send, recv)
    here = pltpu.make_async_copy(near.at[i_p], pieces.at[0], sem.at[0])
    here.start()
    arrive = [link(near.at[i_p ^ k], pieces.at[k], {"p": i_p ^ k}) for k in range(1, np_)]

    def split(piece, p, image):
        for swap in range(2):

            @pl.when(i_c == swap)
            def _(swap=swap):
                for b in range(2):
                    mixed[p, b, image] = piece[(swap ^ b) * rows : ((swap ^ b) + 1) * rows, :]

    def product(b, image):
        total = None
        for p in range(np_):
            term = dot(mixed[p, b, image], w[p])
            total = term if total is None else total + term
        return total

    other = []
    for bit in (1, 0):
        image = i_g ^ bit
        if bit:
            for k in range(np_):
                split(far[k], i_p ^ k, image)
        else:
            here.wait()
            for copy in arrive:
                copy.wait_recv()
            for k in range(np_):
                split(pieces.at[k], i_p ^ k, image)
        away[image] = product(1, image)
        other.append(link(away.at[image], came.at[image], core))
        mine[image] = product(0, image)
    back = []
    for bit in (1, 0):
        image = i_g ^ bit
        other[1 - bit].wait_recv()
        value = patches[image].astype(F32) + mine[image] + came[image] + bias[...]
        mid[image] = value
        two_own[image] = (normal_rows(value) * gain[...] + shift[...]).astype(BF)
        back.append(link(two_own.at[image], two_other.at[image], core))
    for copy in back:
        copy.wait_recv()
    link.drain()


def middle_rows(near, far, w, patches, bias, gain, shift, sizes):
    dp, ng, np_ = sizes
    images, rows, width = patches.shape
    lanes = near.shape[2]
    vmem = pl.BlockSpec(memory_space=pltpu.VMEM)
    copies = np_ - 1 + 2 * images
    own = jax.ShapeDtypeStruct((images, rows, width), BF)
    return pl.pallas_call(
        partial(middle_kernel, sizes),
        in_specs=[pl.BlockSpec(memory_space=pl.ANY)] + [vmem] * (len(far) + 5),
        out_specs=[vmem] * 4,
        out_shape=[
            jax.ShapeDtypeStruct((images, rows, width), F32),
            own,
            own,
            jax.ShapeDtypeStruct((np_, 2, images, rows, lanes), BF),
        ],
        scratch_shapes=[
            pltpu.VMEM((np_, 2 * rows, lanes), BF),
            pltpu.VMEM((images, rows, width), F32),
            pltpu.VMEM((images, rows, width), F32),
            pltpu.VMEM((images, rows, width), F32),
            pltpu.SemaphoreType.DMA((1,)),
            pltpu.SemaphoreType.DMA((copies,)),
            pltpu.SemaphoreType.DMA((copies,)),
        ],
        compiler_params=pltpu.CompilerParams(collective_id=2, has_side_effects=True, vmem_limit_bytes=48 << 20),
        cost_estimate=FREE,
        name="middle_rows",
    )(near, *far, w, patches, bias, gain, shift)


def norm_back(values, gain, upstream):
    center = values - jnp.mean(values, -1, keepdims=True)
    spread = jnp.mean(center * center, -1, keepdims=True)
    inverse = lax.rsqrt(spread + EPSILON)
    normal = center * inverse
    scaled = upstream * gain
    inner = jnp.mean(scaled * normal, -1, keepdims=True)
    return inverse * (scaled - jnp.mean(scaled, -1, keepdims=True) - normal * inner), normal


def turn_kernel(sizes, mid, gn, out, branch, gain, shift, w, mixed, output, grad_mid, heads, grad_proj, sums,
                back_own, back_other, gn_own, gn_came, out_own, out_came, stage, sem, send, recv):
    dp, ng, np_ = sizes
    i_dp, i_g, i_p, i_c = places()
    images, rows, width = mid.shape
    i_z = i_g * np_ + i_p
    core = {"c": 1 - i_c}
    peers = [core]
    for k in range(1, ng * np_):
        peers.append({"g": i_g ^ (k // np_), "p": i_p ^ (k % np_)})
    meet(peers)
    link = Links(send, recv)
    turns = [i_g ^ 1, i_g]

    def half(ref, b, image):
        start = (b * images + image) * rows
        return ref.at[pl.ds(pl.multiple_of(start, 8), rows)]

    loads = []
    crossed = []
    for n, image in enumerate(turns):
        crossed.append(link(half(gn, 1, image), gn_came.at[image], core))
        loads.append(pltpu.make_async_copy(half(gn, 0, image), gn_own.at[image], sem.at[n]))
        loads[-1].start()
    locals_ = []
    sums[...] = jnp.zeros_like(sums)

    def give(n, b):
        image = turns[n]
        source = (back_own if b == 0 else back_other)[image]
        for k in range(np_):
            slot = (n * np_ + k) * 2 + b
            stage[slot] = dot(source, w[i_p ^ k], NT).astype(BF)
            start = (i_z * 2 + (i_c ^ b)) * rows
            dst = heads.at[pl.ds(pl.multiple_of(start, 8), rows)]
            if n == 1 and k == 0:
                locals_.append(pltpu.make_async_copy(stage.at[slot], dst, sem.at[2 * images + b]))
                locals_[-1].start()
            else:
                arrivals.append(link(stage.at[slot], dst, {"g": image, "p": i_p ^ k}))

    arrivals = []
    others = []
    for n, image in enumerate(turns):
        loads[n].wait()
        crossed[n].wait_recv()
        grad_two = gn_own[image] + gn_came[image]
        grad_out = branch[image].astype(F32)
        grad_norm, normal = norm_back(mid[image], gain[...], grad_two)
        grad = grad_out + grad_norm
        grad_mid[image] = grad
        back_own[image] = grad.astype(BF)
        others.append(link(back_own.at[image], back_other.at[image], core))
        sums[0:1, :] += jnp.sum(grad_two * normal, 0, keepdims=True)
        sums[1:2, :] += jnp.sum(grad_two, 0, keepdims=True)
        sums[2:3, :] += jnp.sum(back_own[image].astype(F32), 0, keepdims=True)
        sums[3:4, :] += jnp.sum(grad_out, 0, keepdims=True)
        give(n, 0)
    outs = []
    for n, image in enumerate(turns):
        others[n].wait_recv()
        give(n, 1)
        outs.append(link(half(out, 1, image), out_came.at[image], core))
        loads.append(pltpu.make_async_copy(half(out, 0, image), out_own.at[image], sem.at[images + n]))
        loads[-1].start()
    for p in range(np_):
        total = None
        for b, source in ((0, back_own), (1, back_other)):
            for image in range(images):
                term = dot(mixed[p, b, image], source[image], TN)
                total = term if total is None else total + term
        grad_proj[p] = total.astype(BF)
    for n, image in enumerate(turns):
        loads[images + n].wait()
        outs[n].wait_recv()
        value = mid[image] + out_own[image] + out_came[image] + shift[...]
        output[image] = value.astype(BF)
    for copy in locals_:
        copy.wait()
    for copy in arrivals:
        copy.wait_recv()
    link.drain()


def turn(mid, gn, out, branch, gain, shift, w, mixed, sizes):
    dp, ng, np_ = sizes
    images, rows, width = mid.shape
    lanes = w.shape[1]
    chips = ng * np_
    vmem = pl.BlockSpec(memory_space=pltpu.VMEM)
    hbm = pl.BlockSpec(memory_space=pl.ANY)
    copies = 3 * images + 2 * (chips - 1)
    own = (images, rows, width)
    return pl.pallas_call(
        partial(turn_kernel, sizes),
        in_specs=[vmem, hbm, hbm] + [vmem] * 5,
        out_specs=[vmem, vmem, hbm, vmem, vmem],
        out_shape=[
            jax.ShapeDtypeStruct(own, BF),
            jax.ShapeDtypeStruct(own, F32),
            jax.ShapeDtypeStruct((chips * 2 * rows, lanes), BF),
            jax.ShapeDtypeStruct((np_, lanes, width), BF),
            jax.ShapeDtypeStruct((8, width), F32),
        ],
        scratch_shapes=[
            pltpu.VMEM(own, BF),
            pltpu.VMEM(own, BF),
            pltpu.VMEM(own, F32),
            pltpu.VMEM(own, F32),
            pltpu.VMEM(own, F32),
            pltpu.VMEM(own, F32),
            pltpu.VMEM((chips * 2, rows, lanes), BF),
            pltpu.SemaphoreType.DMA((2 * images + 2,)),
            pltpu.SemaphoreType.DMA((copies,)),
            pltpu.SemaphoreType.DMA((copies,)),
        ],
        compiler_params=pltpu.CompilerParams(collective_id=3, has_side_effects=True, vmem_limit_bytes=56 << 20),
        cost_estimate=FREE,
        name="turn",
    )(mid, gn, out, branch, gain, shift, w, mixed)


def flip(value, axis, size, bit):
    return lax.ppermute(value, axis, [(i, i ^ bit) for i in range(size)])


def pick(value, index, axis=0):
    return lax.dynamic_index_in_dim(value, index, axis, keepdims=False)


def gather_pieces(value, axis, size, me):
    full = jnp.zeros((size,) + value.shape, value.dtype)
    full = lax.dynamic_update_index_in_dim(full, value, me, 0)
    for bit in range(1, size):
        full = lax.dynamic_update_index_in_dim(full, flip(value, axis, size, bit), me ^ bit, 0)
    return full


def scatter_sum(value, axis, size, me):
    total = pick(value, me).astype(F32)
    for bit in range(1, size):
        total = total + flip(pick(value, me ^ bit), axis, size, bit).astype(F32)
    return total


def tie(*values):
    return lax.optimization_barrier(values)


def after(value, *others):
    return tie(value, *others)[0]


def on_device(
    patches,
    ln1_gain,
    ln1_bias,
    qkv_weight,
    q_bias,
    v_bias,
    proj_weight,
    proj_bias,
    ln2_gain,
    ln2_bias,
    fc1_weight,
    fc1_bias,
    fc2_weight,
    fc2_bias,
    rel_pos_h,
    rel_pos_w,
    cotangent,
):
    images, row_count, width = patches.shape
    dp, ng, np_, nc = (lax.axis_size(name) for name in ("dp", "g", "p", "c"))
    i_dp, i_g, i_p, i_c = (lax.axis_index(name) for name in ("dp", "g", "p", "c"))
    chips = ng * np_
    i_z = i_g * np_ + i_p
    ranks = chips * nc
    seq_len = ranks * row_count
    own_rows = images * row_count
    heads = H * images // ranks
    shard_heads = H // dp
    core_heads = shard_heads // nc
    piece = core_heads * HD
    pieces = heads // core_heads
    lanes = heads * HD
    hidden = fc1_weight.shape[1]
    unit = hidden // ranks
    shard = width // dp
    per = hidden // dp // (nc * unit)
    side = (rel_pos_h.shape[0] + 1) // 2

    core_bias = pick(fc1_bias.reshape(per, nc, 2, unit // 2), i_c, 1).transpose(1, 0, 2)
    packed = jnp.concatenate(
        [
            jnp.stack([ln1_gain, ln1_bias, q_bias, v_bias, proj_bias, ln2_gain, ln2_bias, fc2_bias]),
            core_bias.reshape(-1, shard),
        ]
    )
    spot = jnp.stack([i_g, i_p, i_c])
    qkv_own, slab_a, slab_b = select(spot, qkv_weight, fc1_weight, fc2_weight, proj_weight, ng, np_, nc, lanes)
    weights_a = lax.all_gather(slab_a, "dp", axis=0)
    weights_b = lax.all_gather(slab_b, "dp", axis=0)
    proj_half = weights_a[:, 2 * shard :]
    raw, qkv_full, vectors = start_exchange(patches, qkv_own, packed, (dp, ng, np_))
    qkv_full = qkv_full.reshape(width, 3 * lanes)
    vectors = vectors.astype(F32)
    whole_vec = vectors.transpose(1, 0, 2).reshape(-1, width)
    gain_one, shift_one, q_shift, v_shift, proj_shift, gain_two, shift_two, fc2_shift = whole_vec[:8]
    fc1_shift = vectors[:, 8:].reshape(dp, 2, -1).transpose(1, 0, 2).reshape(2, 1, -1)

    starts = [
        part * width + (i_p * pieces + q) * shard_heads * HD + i_c * piece
        for q in range(pieces)
        for part in range(3)
    ]
    zero = jnp.zeros((piece,), F32)
    biases = []
    for q in range(pieces):
        at = starts[3 * q]
        biases += [lax.dynamic_slice_in_dim(q_shift, at, piece, 0), zero]
        biases += [lax.dynamic_slice_in_dim(v_shift, at, piece, 0)]
    qkv_shift = jnp.concatenate(biases)[None]

    branch_own = cotangent.reshape(own_rows, width)
    branch_other = flip(branch_own, "c", nc, 1)

    tables = flip_tables(rel_pos_h, rel_pos_w)
    normed, query, key_rows, value_rows = qkv_rows(
        raw, gain_one[None], shift_one[None], qkv_full, qkv_shift, tables, pieces, core_heads, side
    )
    far_att, att_f, query_a = attend(i_g ^ 1, query, key_rows, value_rows, side, ng)
    far_att = far_att.reshape(np_, nc * row_count, lanes)
    arrived = {}
    for bit_p in range(np_):
        arrived[1, bit_p] = flip(pick(far_att, i_p ^ bit_p), ("g", "p"), chips, np_ + bit_p)
    near_att, att_f, query_a = attend(i_g, query, key_rows, value_rows, side, ng, (att_f, query_a))
    near_att, *pinned = tie(near_att, *[arrived[1, k] for k in range(np_)])
    for k in range(np_):
        arrived[1, k] = pinned[k]
    near_att = near_att.reshape(np_, nc * row_count, lanes)
    proj_rows = proj_half.reshape(np_, lanes, width)
    sizes = (dp, ng, np_)
    middle, two_own, two_other, mixed = middle_rows(
        near_att,
        [arrived[1, k] for k in range(np_)],
        proj_rows,
        patches,
        proj_shift[None],
        gain_two[None],
        shift_two[None],
        sizes,
    )
    two_own, two_other = two_own.reshape(own_rows, width), two_other.reshape(own_rows, width)

    def over_dp(value):
        return lax.psum_scatter(value.reshape(-1, value.shape[-1]), "dp", scatter_dimension=0, tiled=True)

    out_a, back_a, grads_a, bias_a = mlp_half(
        two_own, two_other, branch_own, branch_other, weights_a, fc1_shift[0]
    )
    sum_a = over_dp(grads_a)
    out_b, back_b, grads_b, bias_b = mlp_half(
        two_own, two_other, branch_own, branch_other, weights_b, fc1_shift[1], (out_a, back_a)
    )
    output, grad_middle, grad_heads, grad_proj, early = turn(
        middle, back_b, out_b, cotangent, gain_two[None], fc2_shift[None], proj_rows, mixed, sizes
    )
    sum_b = over_dp(grads_b)
    sum_p = over_dp(grad_proj.reshape(dp, piece, width))

    def pieces_over_chips(value):
        split = value.reshape(value.shape[0], chips, width // chips).transpose(1, 0, 2)
        sent = [flip(pick(split, i_z ^ bit), ("g", "p"), chips, bit) for bit in range(1, chips)]
        return [pick(split, i_z)] + sent

    grad_heads, sum_a = tie(grad_heads, sum_a)
    sum_a = pieces_over_chips(sum_a)
    dx = []
    grad_tables = 0.0
    for q in range(pieces):
        rows, table = attend_back(
            q * core_heads, core_heads, query_a, key_rows, value_rows, att_f, grad_heads, tables, side
        )
        if q == 0:
            rows, *sum_a = tie(rows, *sum_a)
            sum_b = pieces_over_chips(after(sum_b, rows))
            key_rows = after(key_rows, rows)
        elif q == 1:
            rows, *sum_b = tie(rows, *sum_b)
        dx.append(rows)
        grad_tables = grad_tables + table
    dx[-1], sum_p = tie(dx[-1], sum_p)
    sum_p = pieces_over_chips(sum_p)

    grad_rows, sums = rows_back(dx, raw, qkv_full)
    grad_qkv = [lax.dot_general(normed, rows, TN, preferred_element_type=F32).astype(BF) for rows in dx]

    def spread(part):
        full = jnp.zeros((width,), F32)
        for q in range(pieces):
            block = sums[2 + q, part * piece : (part + 1) * piece]
            full = lax.dynamic_update_slice_in_dim(full, block, starts[3 * q], 0)
        return full

    entries = rel_pos_h.shape[0]
    rel = jnp.stack([grad_tables[:entries, :HD], grad_tables[128 : 128 + entries, :HD]])[:, ::-1]
    bias_half = jnp.stack([bias_a.reshape(dp, per, unit // 2), bias_b.reshape(dp, per, unit // 2)], 2)
    bias_half = bias_half.reshape(dp * per, 1, unit)
    bias_full = jnp.concatenate([bias_half] * nc, 1)
    core = lax.broadcasted_iota(jnp.int32, bias_full.shape, 1)
    bias_full = jnp.where(core == i_c, bias_full, 0.0).reshape(dp, -1)
    eight = jnp.concatenate([jnp.stack([sums[0], sums[1], spread(0), spread(2)]), early[:4]])
    vectors = jnp.concatenate([eight.reshape(8, dp, shard).transpose(1, 0, 2).reshape(dp, -1), bias_full], 1)
    block = -(-vectors.shape[1] // 1024) * 8
    vectors = jnp.pad(vectors, ((0, 0), (0, block * 128 - vectors.shape[1])))
    rel = rel.reshape(-1)
    vectors = jnp.concatenate([vectors.reshape(-1), jnp.pad(rel, (0, -rel.shape[0] % 1024))]).reshape(-1, 128)
    grad_patches, out_qkv, vectors, out_fc1, out_fc2, out_proj = finish(
        grad_rows,
        vectors,
        block,
        patches,
        grad_middle,
        gain_one[None],
        grad_qkv,
        (sum_a, sum_b, sum_p),
        sizes,
        piece,
    )
    rel = vectors[block:].reshape(-1)[: 2 * entries * HD].reshape(2, entries, HD)
    flat = vectors[:block].reshape(-1)
    vec = [flat[n * shard : (n + 1) * shard] for n in range(8)]
    fc1_vec = flat[8 * shard : 8 * shard + hidden // dp]
    return (
        output,
        grad_patches,
        vec[0],
        vec[1],
        out_qkv,
        vec[2],
        vec[3],
        out_proj,
        vec[6],
        vec[4],
        vec[5],
        out_fc1,
        fc1_vec,
        out_fc2,
        vec[7],
        rel[0],
        rel[1],
    )


def solution(mesh):
    dp, ranks = mesh.shape["dp"], mesh.shape["seq"]

    def call(*args):
        images = args[0].shape[0] // dp
        shape = (dp, images, ranks // images // 2, 2)
        fine = jax.sharding.Mesh(mesh.devices.reshape(shape), ("dp", "g", "p", "c"))
        seq = ("g", "p", "c")
        tokens, rows, both = P("dp", seq, None), P("dp", None), P("dp", seq)
        vec = P("dp")
        return jax.shard_map(
            on_device,
            mesh=fine,
            in_specs=(
                tokens, vec, vec, rows, vec, vec, rows, vec, vec, vec, rows, vec, rows, vec, P(), P(), tokens
            ),
            out_specs=(
                tokens, tokens, vec, vec, both, vec, vec, both, vec, vec, vec, both, vec, both, vec, P(), P()
            ),
            check_vma=False,
        )(*args)

    return call
```

```python
import math
from functools import partial

import jax
import jax.numpy as jnp
from jax import lax
from jax.experimental import pallas as pl
from jax.experimental.pallas import tpu as pltpu
from jax.sharding import PartitionSpec as P

H = 16
HD = 80
EPSILON = 1e-06
NT = (((1,), (1,)), ((), ()))
TN = (((0,), (0,)), ((), ()))
BF = jnp.bfloat16
F32 = jnp.float32
LOG2E = 1.4426950408889634
FACTOR = LOG2E / math.sqrt(HD)
FREE = pl.CostEstimate(flops=1, bytes_accessed=1, transcendentals=0)


def busy(gflops):
    return pl.CostEstimate(flops=gflops * 10**9, bytes_accessed=1, transcendentals=0)


def dot(a, b, dims=(((1,), (0,)), ((), ()))):
    return lax.dot_general(a, b, dims, preferred_element_type=F32)


def params(axes, mib=60):
    return pltpu.CompilerParams(
        dimension_semantics=("arbitrary",) * axes, vmem_limit_bytes=mib << 20
    )


def whole(*shape):
    return pl.BlockSpec(shape, lambda *at: (0,) * len(shape), pipeline_mode=pl.Buffered(1))


def flip_tables(rel_h, rel_w):
    entries = rel_h.shape[0]
    pad = ((0, 128 - entries), (0, 0))
    return jnp.concatenate([jnp.pad(rel_h[::-1], pad), jnp.pad(rel_w[::-1], pad)], 0)


def normal_rows(values):
    center = values - jnp.mean(values, -1, keepdims=True)
    spread = jnp.mean(center * center, -1, keepdims=True)
    return center * lax.rsqrt(spread + EPSILON)


def qkv_kernel(pieces, group_heads, side, raw, gain, shift, w, bias, tables, normed, qa, kp, vp):
    rows = raw.shape[0]
    rows_n = (normal_rows(raw[...].astype(F32)) * gain[...] + shift[...]).astype(BF)
    normed[...] = rows_n
    joined = (dot(rows_n, w[...]) + bias[...]).astype(BF)
    first_row = pl.program_id(0) * (rows // side)
    lane = lax.broadcasted_iota(jnp.int32, (rows, 128), 1)
    group_lane = lax.broadcasted_iota(jnp.int32, (side, 128), 1)
    group_row = lax.broadcasted_iota(jnp.int32, (side, 128), 0)
    col_hot = (group_lane == group_row) | ((group_lane >= side) & (group_lane < side + 3))
    col_hot = jnp.where(col_hot, 1.0, 0.0).astype(BF)
    hot = []
    for i in range(rows // side):
        hot.append(jnp.where(group_lane == first_row + (HD + i), 1.0, 0.0).astype(BF))
    row_hot = jnp.concatenate(hot, 0)
    col_hot = jnp.concatenate([col_hot] * (rows // side), 0)
    width = group_heads * HD
    for n in range(pieces * group_heads):
        q_at = (n // group_heads) * 3 * width + (n % group_heads) * HD
        q = joined[:, q_at : q_at + HD]
        g = dot(q, tables[...], NT) * math.sqrt(HD)
        gh = []
        gw = []
        for i in range(rows // side):
            part = g[i * side : (i + 1) * side]
            gh.append(pltpu.roll(part[:, :128], first_row + (33 + i), axis=1))
            gw.append(pltpu.roll(part[:, 128:], 81, axis=1, stride=1, stride_axis=0))
        qa[n, :, 0:128] = jnp.concatenate(gh, 0).astype(BF)
        qa[n, :, 0:HD] = q
        qa[n, :, 128:256] = jnp.where(lane < side, jnp.concatenate(gw, 0), 0.0).astype(BF)
        kp[n, :, 0:128] = row_hot
        kp[n, :, 128:256] = col_hot
        kp[n, :, 0:HD] = joined[:, q_at + width : q_at + width + HD]
        vp[n] = jnp.ones((rows, 128), BF)
        vp[n, :, 0:HD] = joined[:, q_at + 2 * width : q_at + 2 * width + HD]


def qkv_rows(raw, gain, shift, w, bias, tables, pieces, group_heads, side, rows=384):
    seq_len, width = raw.shape
    lanes = w.shape[1]
    heads = pieces * group_heads
    return pl.pallas_call(
        partial(qkv_kernel, pieces, group_heads, side),
        grid=(seq_len // rows,),
        in_specs=[
            pl.BlockSpec((rows, width), lambda i: (i, 0)),
            whole(1, width),
            whole(1, width),
            whole(width, lanes),
            whole(1, lanes),
            whole(256, HD),
        ],
        out_specs=[
            pl.BlockSpec((rows, width), lambda i: (i, 0)),
            pl.BlockSpec((heads, rows, 256), lambda i: (0, i, 0)),
            pl.BlockSpec((heads, rows, 256), lambda i: (0, i, 0)),
            pl.BlockSpec((heads, rows, 128), lambda i: (0, i, 0)),
        ],
        out_shape=[
            jax.ShapeDtypeStruct((seq_len, width), BF),
            jax.ShapeDtypeStruct((heads, seq_len, 256), BF),
            jax.ShapeDtypeStruct((heads, seq_len, 256), BF),
            jax.ShapeDtypeStruct((heads, seq_len, 128), BF),
        ],
        compiler_params=params(1),
        cost_estimate=FREE,
        name="qkv_rows",
    )(raw, gain, shift, w, bias, tables)


def attend_kernel(heads, side, aliased, sub, at, qa, kp, vp, *refs):
    o, of, qo = refs[2:] if aliased else refs
    rows = qa.shape[1]
    h = pl.program_id(0)
    base = pl.multiple_of(pl.program_id(1) * rows, rows)
    lane = lax.broadcasted_iota(jnp.int32, (sub, 128), 1)
    count = rows // sub
    scores = [dot(qa[0, 0:sub, :], kp[0], NT)]
    outs = []
    for n in range(count):
        part = slice(n * sub, (n + 1) * sub)
        if n + 1 < count:
            scores.append(dot(qa[0, (n + 1) * sub : (n + 2) * sub, :], kp[0], NT))
        s = scores[n]
        m = jnp.max(s, -1, keepdims=True)
        p = jnp.exp2(s * FACTOR - m * FACTOR).astype(BF)
        out = dot(p, vp[0])
        total = out[:, HD : HD + 1]
        out = out / total
        norm = m + jnp.log2(total) / FACTOR
        hi = norm.astype(BF).astype(F32)
        mid = (norm - hi).astype(BF).astype(F32)
        low = norm - hi - mid
        old = qa[0, part, 128:256].astype(F32)
        old = jnp.where(lane == side, -hi, old)
        old = jnp.where(lane == side + 1, -mid, old)
        old = jnp.where(lane == side + 2, -low, old)
        qo[0, part, 0:128] = qa[0, part, 0:128]
        qo[0, part, 128:256] = old.astype(BF)
        outs.append(out)
    out = jnp.concatenate(outs, 0)
    part = pl.ds(base, rows)
    for n in range(heads):

        @pl.when(h == n)
        def _(n=n):
            o[part, n * HD : (n + 1) * HD] = out[:, 0:HD].astype(BF)
            of[part, n * HD : (n + 1) * HD] = out[:, 0:HD]


def attend(group, qa, kp, vp, side, groups, old=(), tq=1152, sub=576):
    heads, seq_len, _ = qa.shape
    rows = seq_len // groups
    steps = rows // tq
    lanes = heads * HD
    query = pl.BlockSpec((1, tq, 256), lambda h, i, at: (h, at[0] * steps + i, 0))
    return pl.pallas_call(
        partial(attend_kernel, heads, side, bool(old), sub),
        grid_spec=pltpu.PrefetchScalarGridSpec(
            num_scalar_prefetch=1,
            grid=(heads, steps),
            in_specs=[
                query,
                pl.BlockSpec((1, seq_len, 256), lambda h, i, at: (h, 0, 0)),
                pl.BlockSpec((1, seq_len, 128), lambda h, i, at: (h, 0, 0)),
            ]
            + [pl.BlockSpec(memory_space=pl.ANY)] * len(old),
            out_specs=[
                pl.BlockSpec((rows, lanes), lambda h, i, at: (0, 0)),
                pl.BlockSpec((rows, lanes), lambda h, i, at: (at[0], 0)),
                query,
            ],
        ),
        out_shape=[
            jax.ShapeDtypeStruct((rows, lanes), BF),
            jax.ShapeDtypeStruct((seq_len, lanes), F32),
            jax.ShapeDtypeStruct((heads, seq_len, 256), BF),
        ],
        input_output_aliases={4: 1, 5: 2} if old else {},
        compiler_params=params(2),
        cost_estimate=busy(20),
        name="attend",
    )(jnp.stack([group]), qa, kp, vp, *old)


def attend_back_kernel(heads, first, side, uc, qa_ref, kp, vp, of, go, tables, dx, gt, kt, dop, dk, dv, dq):
    seq_len = kp.shape[1]
    tb = qa_ref.shape[1]
    h = pl.program_id(0)
    step = pl.program_id(1)
    last = pl.num_programs(1) - 1
    scale = HD ** (-0.5)
    rows = seq_len // 9

    @pl.when((h == 0) & (step == 0))
    def _():
        gt[...] = jnp.zeros_like(gt)

        def prep(i, c):
            part = pl.ds(pl.multiple_of(i * rows, rows), rows)
            lane = lax.broadcasted_iota(jnp.int32, (rows, 128), 1)
            for n in range(heads):
                at = (first + n) * HD
                rows_go = go[part, at : at + HD]
                inner = jnp.sum(rows_go.astype(F32) * of[part, at : at + HD], -1, keepdims=True)
                hi = inner.astype(BF).astype(F32)
                tail = jnp.where(lane == HD, -hi, jnp.where(lane == HD + 1, hi - inner, 0.0))
                dop[n, part, :] = tail.astype(BF)
                dop[n, part, 0:HD] = rows_go
            return c

        lax.fori_loop(0, 9, prep, 0)

    @pl.when(step == 0)
    def _():
        def prep(i, c):
            part = pl.ds(pl.multiple_of(i * rows, rows), rows)
            kt[:, part] = kp[0, part, :].T[0 : HD + 2 * side]
            dk[part, :] = jnp.zeros((rows, 128), F32)
            dv[part, :] = jnp.zeros((rows, 128), F32)
            return c

        lax.fori_loop(0, 9, prep, 0)

    base = pl.ds(pl.multiple_of(step * tb, tb), tb)
    qa = qa_ref[0]
    do = dop[h, base, :]

    def scores(j):
        part = slice(j * uc, (j + 1) * uc)
        return dot(kp[0, part, :], qa, NT), dot(vp[0, part, :], do, NT)

    acc = None
    count = seq_len // uc
    ahead = scores(0)
    for j in range(count):
        s, dp = ahead
        if j + 1 < count:
            ahead = scores(j + 1)
        part = slice(j * uc, (j + 1) * uc)
        p = jnp.exp2(s * FACTOR)
        ds = (p * dp).astype(BF)
        dv[part, :] += dot(p.astype(BF), do)
        dk[part, :] += dot(ds, qa[:, 0:128])
        term = dot(kt[:, part], ds)
        acc = term if acc is None else acc + term
    acc = jnp.concatenate([acc, jnp.zeros((256 - HD - 2 * side, tb), F32)], 0).T
    lane = lax.broadcasted_iota(jnp.int32, (tb, 128), 1)
    groups = tb // side
    rel_h = jnp.where(lane < HD, 0.0, acc[:, :128])
    rel_w = jnp.where(lane < side, acc[:, 128:], 0.0)
    back_h = []
    back_w = []
    for i in range(groups):
        part = slice(i * side, (i + 1) * side)
        back_h.append(pltpu.roll(rel_h[part], 256 - 33 - step * groups - i, axis=1))
        back_w.append(stagger(rel_w[part], side))
    both = jnp.concatenate([jnp.concatenate(back_h, 0), jnp.concatenate(back_w, 0)], 1).astype(BF)
    dq[base, :] = acc[:, :HD] * scale + dot(both, tables[...])
    gt[...] += dot(both, qa[:, 0:128], TN)

    width = heads * HD
    for n in range(heads):

        @pl.when((h == n) & (step == last))
        def _(n=n):
            def post(i, c):
                part = pl.ds(pl.multiple_of(i * rows, rows), rows)
                at = n * HD
                dx[part, at : at + HD] = dq[part, :].astype(BF)
                dx[part, width + at : width + at + HD] = (dk[part, 0:HD] * scale).astype(BF)
                dx[part, 2 * width + at : 2 * width + at + HD] = dv[part, 0:HD].astype(BF)
                return c

            lax.fori_loop(0, 9, post, 0)


def stagger(val, side):
    row = lax.broadcasted_iota(jnp.int32, val.shape, 0)
    shift = side - 1 - row
    bit = 1
    while bit < side:
        val = jnp.where((shift & bit) != 0, pltpu.roll(val, bit, axis=1), val)
        bit *= 2
    return val


def attend_back(first, count, qa, kp, vp, of, go, tables, side, tb=768, uc=256):
    heads, seq_len, _ = qa.shape
    lanes = heads * HD
    return pl.pallas_call(
        partial(attend_back_kernel, count, first, side, uc),
        grid=(count, seq_len // tb),
        in_specs=[
            pl.BlockSpec((1, tb, 256), lambda h, i: (first + h, i, 0)),
            pl.BlockSpec((1, seq_len, 256), lambda h, i: (first + h, 0, 0)),
            pl.BlockSpec((1, seq_len, 128), lambda h, i: (first + h, 0, 0)),
            whole(seq_len, lanes),
            whole(seq_len, lanes),
            whole(256, HD),
        ],
        out_specs=[whole(seq_len, 3 * count * HD), whole(256, 128)],
        out_shape=[
            jax.ShapeDtypeStruct((seq_len, 3 * count * HD), BF),
            jax.ShapeDtypeStruct((256, 128), F32),
        ],
        scratch_shapes=[
            pltpu.VMEM((HD + 2 * side, seq_len), BF),
            pltpu.VMEM((count, seq_len, 128), BF),
            pltpu.VMEM((seq_len, 128), F32),
            pltpu.VMEM((seq_len, 128), F32),
            pltpu.VMEM((seq_len, HD), F32),
        ],
        compiler_params=params(2),
        cost_estimate=busy(50),
        name="attend_back",
    )(qa, kp, vp, of, go, tables)


def mlp_kernel(aliased, per, n_own, n_other, g_own, g_other, w1, b1, w2, *refs):
    if aliased:
        out_in, gn_in, out, gn, grads, gb1, n2, gb, act, gbef = refs
    else:
        out, gn, grads, gb1, n2, gb, act, gbef = refs
    step = pl.program_id(0)
    chunk = out.shape[0]
    shards, shard, hidden = w1.shape
    width = n_own.shape[1]
    steps = 2 * per

    @pl.when(step == 0)
    def _():
        gb1[...] = jnp.zeros_like(gb1)

    @pl.when(step < steps)
    def _():
        first = w1[...].reshape(width, hidden)
        second = w2[...].reshape(hidden, width)
        dst = pl.ds(pl.multiple_of(step * chunk, chunk), chunk)
        mine = step < per
        n2[dst, :] = jnp.where(mine, n_own[...], n_other[...])
        gb[dst, :] = jnp.where(mine, g_own[...], g_other[...])
        before = dot(n2[dst, :], first) + b1[...]
        grad_act = dot(gb[dst, :], second, NT)
        cdf = 0.5 + 0.5 * lax.erf(before * math.sqrt(0.5))
        act[dst, :] = (before * cdf).astype(BF)
        slope = cdf + before * (jnp.exp(-0.5 * before * before) * (1.0 / math.sqrt(2.0 * math.pi)))
        grad_before = slope * grad_act
        gbef[dst, :] = grad_before.astype(BF)
        gb1[...] += jnp.sum(gbef[dst, :].astype(F32), 0, keepdims=True)
        value = dot(act[dst, :], second)
        back = dot(gbef[dst, :], first, NT)
        if aliased:
            value = value + out_in[...]
            back = back + gn_in[...]
        out[...] = value
        gn[...] = back

    for j in range(shards):

        @pl.when(step == steps + j)
        def _(j=j):
            rows = slice(j * shard, (j + 1) * shard)
            grads[0, 0:shard, :] = dot(n2[:, rows], gbef[...], TN).astype(BF)
            grads[0, shard : 2 * shard, :] = dot(act[:, rows], gb[...], TN).astype(BF)


def mlp_half(n_own, n_other, g_own, g_other, weights, b1, old=(), chunk=288):
    half, width = n_own.shape
    dp = weights.shape[0]
    shard = width // dp
    hidden = width
    chunk = min(chunk, half)
    per = half // chunk
    steps = 2 * per
    tile = pl.BlockSpec((chunk, width), lambda i: (jnp.minimum(i, steps - 1), 0))
    own = pl.BlockSpec((chunk, width), lambda i: (jnp.minimum(i, per - 1), 0))
    other = pl.BlockSpec((chunk, width), lambda i: (jnp.clip(i - per, 0, per - 1), 0))
    rows = jax.ShapeDtypeStruct((2 * half, width), F32)
    return pl.pallas_call(
        partial(mlp_kernel, bool(old), per),
        grid=(steps + dp,),
        in_specs=[own, other, own, other]
        + [
            pl.BlockSpec((dp, shard, width), lambda i: (0, 0, 0), pipeline_mode=pl.Buffered(1)),
            whole(1, hidden),
            pl.BlockSpec((dp, shard, width), lambda i: (0, 1, 0), pipeline_mode=pl.Buffered(1)),
        ]
        + [tile] * len(old),
        out_specs=[
            tile,
            tile,
            pl.BlockSpec((1, 2 * shard, width), lambda i: (jnp.maximum(i - steps, 0), 0, 0)),
            whole(1, hidden),
        ],
        out_shape=[
            rows,
            rows,
            jax.ShapeDtypeStruct((dp, 2 * shard, width), BF),
            jax.ShapeDtypeStruct((1, hidden), F32),
        ],
        input_output_aliases={7: 0, 8: 1} if old else {},
        scratch_shapes=[pltpu.VMEM((2 * half, width), BF)] * 4,
        compiler_params=params(1, 63),
        cost_estimate=busy(35),
        name="mlp_half",
    )(n_own, n_other, g_own, g_other, weights, b1, weights, *old)


def select_kernel(ng, np_, nc, at, qkv, fc1, fc2, proj, own, *slabs):
    i_p, i_c = at[1], at[2]
    shard = fc1.shape[0]
    width = proj.shape[1]
    hidden = fc1.shape[1]
    chips = ng * np_
    unit = hidden // (chips * nc)
    part = unit // 2
    piece = proj.shape[0] // nc
    shard_lanes = proj.shape[0]
    lanes = own.shape[1] // 3
    pieces = lanes // piece
    per = fc2.shape[0] // (nc * unit)
    for c in range(nc):

        @pl.when(i_c == c)
        def _(c=c):
            for u in range(2):
                for z in range(chips):
                    src = (z * nc + c) * unit + u * part
                    slabs[u][0:shard, z * part : (z + 1) * part] = fc1[:, src : src + part]
                for b in range(per):
                    src = (b * nc + c) * unit + u * part
                    dst = shard + b * part
                    slabs[u][dst : dst + part, :] = fc2[src : src + part, :]
            slabs[0][2 * shard : 2 * shard + piece, :] = proj[c * piece : (c + 1) * piece, :]

        for p in range(np_):

            @pl.when((i_c == c) & (i_p == p))
            def _(c=c, p=p):
                for q in range(pieces):
                    for t in range(3):
                        src = t * width + (p * pieces + q) * shard_lanes + c * piece
                        dst = (3 * q + t) * piece
                        own[:, dst : dst + piece] = qkv[:, src : src + piece]


def select(at, qkv, fc1, fc2, proj, ng, np_, nc, lanes):
    shard, width = proj.shape[0], proj.shape[1]
    return pl.pallas_call(
        partial(select_kernel, ng, np_, nc),
        in_specs=[pl.BlockSpec(memory_space=pltpu.SMEM)] + [pl.BlockSpec(memory_space=pltpu.VMEM)] * 4,
        out_specs=[pl.BlockSpec(memory_space=pltpu.VMEM)] * 3,
        out_shape=[
            jax.ShapeDtypeStruct((shard, 3 * lanes), BF),
            jax.ShapeDtypeStruct((2 * shard + shard // nc, width), BF),
            jax.ShapeDtypeStruct((2 * shard, width), BF),
        ],
        compiler_params=pltpu.CompilerParams(vmem_limit_bytes=40 << 20),
        cost_estimate=FREE,
        name="select",
    )(at, qkv, fc1, fc2, proj)


def start_kernel(sizes, split, patches, own, vec, rows, full, vecs, local, send, recv):
    dp, ng, np_ = sizes
    i_dp, i_g, i_p, i_c = (lax.axis_index(name) for name in ("dp", "g", "p", "c"))
    count = patches.shape[1]
    step = count // split

    barrier = pltpu.get_barrier_semaphore()
    peers = [{"dp": i_dp ^ k} for k in range(1, dp)]
    peers += [{"g": i_g ^ k} for k in range(1, ng)]
    peers += [{"p": i_p ^ k} for k in range(1, np_)]
    peers += [{"c": 1 - i_c}]
    for peer in peers:
        pl.semaphore_signal(barrier, inc=1, device_id=peer, device_id_type=pl.DeviceIdType.MESH)
    pl.semaphore_wait(barrier, len(peers))

    used = []

    def remote(src, dst, peer):
        n = len(used)
        copy = pltpu.make_async_remote_copy(
            src_ref=src,
            dst_ref=dst,
            send_sem=send.at[n],
            recv_sem=recv.at[n],
            device_id=peer,
            device_id_type=pl.DeviceIdType.MESH,
        )
        used.append(copy)
        return copy

    def place(g, p, c, part):
        start = ((g * np_ + p) * 2 + c) * count + part * step
        return rows.at[pl.ds(pl.multiple_of(start, 8), step)]

    mine = [patches.at[i_g, pl.ds(part * step, step)] for part in range(split)]
    home = [pltpu.make_async_copy(mine[part], place(i_g, i_p, i_c, part), local.at[part]) for part in range(split)]
    home.append(pltpu.make_async_copy(own, full.at[i_dp], local.at[split]))
    home.append(pltpu.make_async_copy(vec, vecs.at[i_dp], local.at[split + 1]))

    far = {}
    for part in range(split):
        for bit in range(1, ng):
            src = patches.at[i_g ^ bit, pl.ds(part * step, step)]
            far[bit, part] = remote(src, place(i_g, i_p, i_c, part), {"g": i_g ^ bit})
            far[bit, part].start()
    over_dp = []
    for bit in range(1, dp):
        over_dp.append(remote(vec, vecs.at[i_dp], {"dp": i_dp ^ bit}))
        over_dp.append(remote(own, full.at[i_dp], {"dp": i_dp ^ bit}))
    for copy in over_dp:
        copy.start()
    near = {}
    for bit in range(1, np_):
        for part in range(split):
            near[bit, part] = remote(mine[part], place(i_g, i_p, i_c, part), {"p": i_p ^ bit})
            near[bit, part].start()
    cores = []
    for part in range(split):
        cores.append(remote(mine[part], place(i_g, i_p, i_c, part), {"c": 1 - i_c}))
        cores[-1].start()
    for copy in home:
        copy.start()

    onward = {}
    for part in range(split):
        for bit in range(1, ng):
            far[bit, part].wait_recv()
            came = place(i_g ^ bit, i_p, i_c, part)
            for bit_p in range(1, np_):
                onward[bit, bit_p, part] = remote(came, came, {"p": i_p ^ bit_p})
                onward[bit, bit_p, part].start()
            cores.append(remote(came, came, {"c": 1 - i_c}))
            cores[-1].start()
        for bit in range(1, np_):
            near[bit, part].wait_recv()
            came = place(i_g, i_p ^ bit, i_c, part)
            cores.append(remote(came, came, {"c": 1 - i_c}))
            cores[-1].start()
    for (bit, bit_p, part), copy in onward.items():
        copy.wait_recv()
        came = place(i_g ^ bit, i_p ^ bit_p, i_c, part)
        cores.append(remote(came, came, {"c": 1 - i_c}))
        cores[-1].start()
    for copy in over_dp + cores:
        copy.wait_recv()
    for copy in used:
        copy.wait_send()
    for copy in home:
        copy.wait()


def start_exchange(patches, own, vec, sizes, split=3):
    dp, ng, np_ = sizes
    images, count, width = patches.shape
    chunk_copies = ng * np_ + (ng - 1) + (np_ - 1) + (ng - 1) * (np_ - 1)
    copies = 2 * (dp - 1) + split * chunk_copies
    hbm = pl.BlockSpec(memory_space=pl.ANY)
    return pl.pallas_call(
        partial(start_kernel, sizes, split),
        in_specs=[hbm] * 3,
        out_specs=[hbm] * 3,
        out_shape=[
            jax.ShapeDtypeStruct((ng * np_ * 2 * count, width), BF),
            jax.ShapeDtypeStruct((dp,) + own.shape, BF),
            jax.ShapeDtypeStruct((dp,) + vec.shape, BF),
        ],
        scratch_shapes=[
            pltpu.SemaphoreType.DMA((split + 2,)),
            pltpu.SemaphoreType.DMA((copies,)),
            pltpu.SemaphoreType.DMA((copies,)),
        ],
        compiler_params=pltpu.CompilerParams(collective_id=0, has_side_effects=True),
        cost_estimate=FREE,
        name="start_exchange",
    )(patches, own, vec)


class Links:
    def __init__(self, send, recv):
        self.send, self.recv, self.copies = send, recv, []

    def __call__(self, src, dst, peer):
        n = len(self.copies)
        copy = pltpu.make_async_remote_copy(
            src_ref=src,
            dst_ref=dst,
            send_sem=self.send.at[n],
            recv_sem=self.recv.at[n],
            device_id=peer,
            device_id_type=pl.DeviceIdType.MESH,
        )
        copy.start()
        self.copies.append(copy)
        return copy

    def drain(self):
        for copy in self.copies:
            copy.wait_send()


def meet(peers):
    barrier = pltpu.get_barrier_semaphore()
    for peer in peers:
        pl.semaphore_signal(barrier, inc=1, device_id=peer, device_id_type=pl.DeviceIdType.MESH)
    pl.semaphore_wait(barrier, len(peers))


def finish_kernel(sizes, split, pieces, part_w, *refs):
    dp, ng, np_ = sizes
    chips = ng * np_
    ranks = chips * 2
    raw, normed = refs[:2]
    dx = refs[2 : 2 + pieces]
    tables = refs[2 + pieces : 2 + 2 * pieces]
    refs = refs[2 + 2 * pieces :]
    w, inputs, grad_mid, gain, early, proj_in = refs[:6]
    parts_a, parts_b = refs[6 : 6 + chips], refs[6 + chips : 6 + 2 * chips]
    (home, owned, out_vec, out_tab, out_fc1, out_fc2, out_proj,
     dx_all, norm_all, dx_ring, raw_ring, keep, away, came, pair, far, slab_out, slabs, cells, taken,
     sums, lane_sums, vec, vec_out, vec_dp, vec_z, vec_c, tab, tab_dp, tab_z, tab_c, tab_all,
     give, got, give_p, got_p, proj_out, proj_got, sem, send, recv, cell_send, cell_recv) = refs[6 + 2 * chips :]
    i_dp, i_g, i_p, i_c = places()
    i_z = i_g * np_ + i_p
    i_s = i_z * 2 + i_c
    count, width = keep.shape[1], keep.shape[2]
    step = count // split
    shard = owned.shape[0]
    cell = owned.shape[1] // 3
    lanes = dx_all.shape[2]
    core = {"c": 1 - i_c}
    chip_peer = lambda k: {"g": i_g ^ (k // np_), "p": i_p ^ (k % np_)}
    peers = [{"dp": i_dp ^ k} for k in range(1, dp)]
    for k in range(1, ranks):
        peers.append({"g": i_g ^ (k // (np_ * 2)), "p": i_p ^ ((k // 2) % np_), "c": i_c ^ (k % 2)})
    meet(peers)
    link = Links(send, recv)

    z_of = lambda k: (i_g ^ (k // np_)) * np_ + (i_p ^ (k % np_))
    part_rows = lambda part: pl.ds(part * step, step)
    far_slots, near_slots = list(range(np_, chips)), list(range(np_))
    jobs = [(k, b) for group in (far_slots, near_slots) for b in (1, 0) for k in group]
    loads = {}

    def load(n):
        if n < len(jobs):
            k, b = jobs[n]
            start = (z_of(k) * 2 + (i_c ^ b)) * count
            at = pl.ds(pl.multiple_of(start, 8), count)
            slot = n % 2
            loads[n] = [pltpu.make_async_copy(raw.at[at], raw_ring.at[slot], sem.at[slot * (1 + pieces)])]
            for q in range(pieces):
                loads[n].append(
                    pltpu.make_async_copy(dx[q].at[at], dx_ring.at[slot, q], sem.at[slot * (1 + pieces) + 1 + q])
                )
            for copy in loads[n]:
                copy.start()

    load(0)
    load(1)
    whole_loads = [pltpu.make_async_copy(normed, norm_all, sem.at[2 * (1 + pieces)])]
    for q in range(pieces):
        whole_loads.append(pltpu.make_async_copy(dx[q], dx_all.at[q], sem.at[2 * (1 + pieces) + 1 + q]))
    for copy in whole_loads:
        copy.start()
    sums[...] = jnp.zeros_like(sums)
    lane_sums[...] = jnp.zeros_like(lane_sums)
    from_core = {}

    def rows(n):
        k, b = jobs[n]
        slot = n % 2
        for copy in loads[n]:
            copy.wait()
        normal = normal_rows(raw_ring[slot].astype(F32))
        total = None
        for q in range(pieces):
            value = dx_ring[slot, q]
            term = dot(value, w[:, q * lanes : (q + 1) * lanes], NT)
            total = term if total is None else total + term
            lane_sums[q : q + 1, :] += jnp.sum(value.astype(F32), 0, keepdims=True)
        sums[0:1, :] += jnp.sum(total * normal, 0, keepdims=True)
        sums[1:2, :] += jnp.sum(total, 0, keepdims=True)
        if b:
            away[k] = total.astype(BF)
            from_core[k] = link(away.at[k], came.at[k], core)
        else:
            keep[k] = total.astype(BF)
        load(n + 2)

    from_pair = {}

    def over_cores(slots):
        for k in slots:
            from_core[k].wait_recv()
            for part in range(split):
                at = part_rows(part)
                keep[k, at, :] = (keep[k, at, :].astype(F32) + came[k, at, :].astype(F32)).astype(BF)
                if k % np_:
                    dst = pair.at[k // np_, k % np_, at]
                    from_pair[k // np_, k % np_, part] = link(keep.at[k, at], dst, {"p": i_p ^ (k % np_)})

    def over_pair(bit_g, part):
        at = part_rows(part)
        value = keep[bit_g * np_, at, :].astype(F32)
        for bit_p in range(1, np_):
            from_pair[bit_g, bit_p, part].wait_recv()
            value = value + pair[bit_g, bit_p, at, :].astype(F32)
        return value

    half = len(far_slots) * 2
    for n in range(half):
        rows(n)

    part_lanes = parts_a[0].shape[1]
    for z in range(chips):
        proj_out[z] = proj_in[:, z * part_lanes : (z + 1) * part_lanes]
    from_chip = [link(proj_out.at[z_of(k)], proj_got.at[k], chip_peer(k)) for k in range(1, chips)]
    over_cores(far_slots)

    for copy in whole_loads:
        copy.wait()
    for j in range(dp):
        for q in range(pieces):
            slab_out[j, q] = dot(norm_all[:, j * shard : (j + 1) * shard], dx_all[q], TN).astype(BF)
    from_dp = [link(slab_out.at[i_dp ^ bit], slabs.at[bit], {"dp": i_dp ^ bit}) for bit in range(1, dp)]

    from_far = {}
    for part in range(split):
        at = part_rows(part)
        for bit_g in range(1, ng):
            pair[bit_g, 0, at, :] = over_pair(bit_g, part).astype(BF)
            from_far[bit_g, part] = link(pair.at[bit_g, 0, at], far.at[bit_g, at], {"g": i_g ^ bit_g})
    for n in range(half, len(jobs)):
        rows(n)

    vec[...] = jnp.zeros_like(vec)
    vec[0:2, :] = sums[0:2, :]
    vec[4:12, :] = early[...]
    for p in range(np_):
        for c in range(2):

            @pl.when((i_p == p) & (i_c == c))
            def _(p=p, c=c):
                for q in range(pieces):
                    at = (p * pieces + q) * shard + c * part_w
                    vec[2:3, at : at + part_w] = lane_sums[q : q + 1, 0:part_w]
                    vec[3:4, at : at + part_w] = lane_sums[q : q + 1, 2 * part_w : 3 * part_w]

    table = tables[0][...]
    for ref in tables[1:]:
        table = table + ref[...]
    tab[...] = table
    tab_rows = tab.shape[0] // dp
    tab_at = lambda j: pl.ds(pl.multiple_of(j * tab_rows, 8), tab_rows)
    for j in range(dp):
        vec_out[j] = vec[:, j * shard : (j + 1) * shard]
    vec_dp[i_dp] = vec_out[i_dp]
    tab_dp[i_dp] = tab[tab_at(i_dp), :]
    small = []
    for bit in range(1, dp):
        small.append(link(vec_out.at[i_dp ^ bit], vec_dp.at[i_dp], {"dp": i_dp ^ bit}))
        small.append(link(tab.at[tab_at(i_dp ^ bit)], tab_dp.at[i_dp], {"dp": i_dp ^ bit}))

    def sum_of(ref, n):
        value = ref[0]
        for i in range(1, n):
            value = value + ref[i]
        return value

    over_cores(near_slots)
    for copy in small:
        copy.wait_recv()
    vec_z[i_z] = sum_of(vec_dp, dp)
    tab_z[i_z] = sum_of(tab_dp, dp)
    small = []
    for k in range(1, chips):
        small.append(link(vec_z.at[i_z], vec_z.at[i_z], chip_peer(k)))
        small.append(link(tab_z.at[i_z], tab_z.at[i_z], chip_peer(k)))

    hidden_rows = give.shape[1]
    per_rows = part_lanes
    swaps = []

    def halves(value, there):
        cols = value.shape[1] // 2
        mine = jnp.where(i_c == 0, value[:, :cols], value[:, cols:])
        there[...] = jnp.where(i_c == 0, value[:, cols:], value[:, :cols]).astype(BF)
        return mine

    def place_fc2(u, c, value):
        for b in range(hidden_rows // per_rows):
            start = ((b * 2 + c) * 2 + u) * per_rows
            out_fc2[pl.ds(pl.multiple_of(start, 8), per_rows), :] = value[b * per_rows : (b + 1) * per_rows, :]

    def place_proj(c, value):
        out_proj[pl.ds(pl.multiple_of(c * value.shape[0], 8), value.shape[0]), :] = value

    for u, parts in ((0, parts_a), (1, parts_b)):
        value = parts[0][...].astype(F32)
        for ref in parts[1:]:
            value = value + ref[...].astype(F32)
        out_fc1[:, u * per_rows : (u + 1) * per_rows] = value[0:shard]
        place_fc2(u, i_c, halves(value[shard:], give.at[u]))
        swaps.append(link(give.at[u], got.at[u], core))
    value = proj_out[i_z].astype(F32)
    for k in range(1, chips):
        from_chip[k - 1].wait_recv()
        value = value + proj_got[k].astype(F32)
    place_proj(i_c, halves(value, give_p))
    swaps.append(link(give_p, got_p, core))

    for copy in from_dp:
        copy.wait_recv()
    sent_cells = []
    for q in range(pieces):
        value = slab_out[i_dp, q].astype(F32)
        for bit in range(1, dp):
            value = value + slabs[bit, q].astype(F32)
        value = value.astype(BF)
        for t in range(3):
            for u in range(part_w // cell):
                n = len(sent_cells)
                lane = t * part_w + u * cell
                cells[n] = value[:, lane : lane + cell]
                unit = (t * width + (i_p * pieces + q) * shard + i_c * part_w) // cell + u
                owner = unit // 3
                slot = unit % 3
                dst = taken.at[i_g, slot]
                o_c = owner % 2
                o_p = (owner // 2) % np_
                o_g = owner // (2 * np_)

                @pl.when(owner == i_s)
                def _(n=n, dst=dst, slot=slot):
                    pltpu.make_async_copy(cells.at[n], dst, cell_recv.at[i_g * 3 + slot]).start()

                @pl.when(owner != i_s)
                def _(n=n, dst=dst, slot=slot, o_g=o_g, o_p=o_p, o_c=o_c):
                    pltpu.make_async_remote_copy(
                        src_ref=cells.at[n],
                        dst_ref=dst,
                        send_sem=cell_send.at[n],
                        recv_sem=cell_recv.at[i_g * 3 + slot],
                        device_id={"g": o_g, "p": o_p, "c": o_c},
                        device_id_type=pl.DeviceIdType.MESH,
                    ).start()

                sent_cells.append(owner)

    def arrived(image, at, value):
        grad, _ = norm_back(inputs[image, at, :].astype(F32), gain[...], value)
        home[image, at, :] = (grad_mid[image, at, :] + grad).astype(BF)

    for part in range(split):
        arrived(i_g, part_rows(part), over_pair(0, part))
    for copy in small:
        copy.wait_recv()
    vec_c[i_c] = sum_of(vec_z, chips)
    tab_c[i_c] = sum_of(tab_z, chips)
    small = [link(vec_c.at[i_c], vec_c.at[i_c], core), link(tab_c.at[i_c], tab_c.at[i_c], core)]
    for copy in swaps:
        copy.wait_recv()
    for u in range(2):
        place_fc2(u, 1 - i_c, got[u].astype(F32))
    place_proj(1 - i_c, got_p[...].astype(F32))
    for copy in small:
        copy.wait_recv()
    out_vec[...] = sum_of(vec_c, 2)
    tab_all[i_dp] = sum_of(tab_c, 2)
    small = [link(tab_all.at[i_dp], tab_all.at[i_dp], {"dp": i_dp ^ bit}) for bit in range(1, dp)]
    for part in range(split):
        at = part_rows(part)
        for bit_g in range(1, ng):
            from_far[bit_g, part].wait_recv()
            arrived(i_g ^ bit_g, at, far[bit_g, at, :].astype(F32))
    for slot in range(3):
        value = None
        for g in range(ng):
            pltpu.make_async_copy(cells.at[0], taken.at[g, slot], cell_recv.at[g * 3 + slot]).wait()
            term = taken[g, slot].astype(F32)
            value = term if value is None else value + term
        owned[:, slot * cell : (slot + 1) * cell] = value
    for copy in small:
        copy.wait_recv()
    for j in range(dp):
        out_tab[j * tab_rows : (j + 1) * tab_rows, :] = tab_all[j]
    for n, owner in enumerate(sent_cells):

        @pl.when(owner != i_s)
        def _(n=n):
            pltpu.make_async_copy(cells.at[n], cells.at[n], cell_send.at[n]).wait()

    link.drain()


def finish(raw, normed, dx, tables, w, inputs, grad_mid, gain, early, proj_in, parts, sizes, part_w, split=3):
    count = inputs.shape[1]
    dp, ng, np_ = sizes
    chips = ng * np_
    pieces = len(dx)
    seq_len, width = raw.shape
    lanes = dx[0].shape[1]
    shard = width // dp
    cell = width // (chips * 2)
    total_cells = pieces * 3 * (part_w // cell)
    parts_a, parts_b = parts
    part_lanes = parts_a[0].shape[1]
    hidden_rows = parts_a[0].shape[0] - shard
    piece_rows = proj_in.shape[0]
    copies = chips + split * (ng * (np_ - 1) + ng - 1) + (chips - 1) + (dp - 1) * 4 + 2 * (chips - 1) + 5
    hbm = pl.BlockSpec(memory_space=pl.ANY)
    vmem = pl.BlockSpec(memory_space=pltpu.VMEM)
    table = tables[0].shape
    block = (table[0] // dp, table[1])
    return pl.pallas_call(
        partial(finish_kernel, sizes, split, pieces, part_w),
        in_specs=[hbm] * (2 + pieces) + [vmem] * (pieces + 6 + 2 * chips),
        out_specs=[vmem] * 7,
        out_shape=[
            jax.ShapeDtypeStruct((ng, count, width), BF),
            jax.ShapeDtypeStruct((shard, 3 * cell), F32),
            jax.ShapeDtypeStruct((16, shard), F32),
            jax.ShapeDtypeStruct(table, F32),
            jax.ShapeDtypeStruct((shard, 2 * part_lanes), F32),
            jax.ShapeDtypeStruct((4 * hidden_rows, part_lanes // 2), F32),
            jax.ShapeDtypeStruct((2 * piece_rows, part_lanes // 2), F32),
        ],
        scratch_shapes=[
            pltpu.VMEM((pieces, seq_len, lanes), BF),
            pltpu.VMEM((seq_len, width), BF),
            pltpu.VMEM((2, pieces, count, lanes), BF),
            pltpu.VMEM((2, count, width), BF),
            pltpu.VMEM((chips, count, width), BF),
            pltpu.VMEM((chips, count, width), BF),
            pltpu.VMEM((chips, count, width), BF),
            pltpu.VMEM((ng, np_, count, width), BF),
            pltpu.VMEM((ng, count, width), BF),
            pltpu.VMEM((dp, pieces, shard, lanes), BF),
            pltpu.VMEM((dp, pieces, shard, lanes), BF),
            pltpu.VMEM((total_cells, shard, cell), BF),
            pltpu.VMEM((ng, 3, shard, cell), BF),
            pltpu.VMEM((8, width), F32),
            pltpu.VMEM((8, lanes), F32),
            pltpu.VMEM((16, width), F32),
            pltpu.VMEM((dp, 16, shard), F32),
            pltpu.VMEM((dp, 16, shard), F32),
            pltpu.VMEM((chips, 16, shard), F32),
            pltpu.VMEM((2, 16, shard), F32),
            pltpu.VMEM(table, F32),
            pltpu.VMEM((dp,) + block, F32),
            pltpu.VMEM((chips,) + block, F32),
            pltpu.VMEM((2,) + block, F32),
            pltpu.VMEM((dp,) + block, F32),
            pltpu.VMEM((2, hidden_rows, part_lanes // 2), BF),
            pltpu.VMEM((2, hidden_rows, part_lanes // 2), BF),
            pltpu.VMEM((piece_rows, part_lanes // 2), BF),
            pltpu.VMEM((piece_rows, part_lanes // 2), BF),
            pltpu.VMEM((chips, piece_rows, part_lanes), BF),
            pltpu.VMEM((chips, piece_rows, part_lanes), BF),
            pltpu.SemaphoreType.DMA((2 * (1 + pieces) + 1 + pieces,)),
            pltpu.SemaphoreType.DMA((copies,)),
            pltpu.SemaphoreType.DMA((copies,)),
            pltpu.SemaphoreType.DMA((total_cells,)),
            pltpu.SemaphoreType.DMA((3 * ng,)),
        ],
        compiler_params=pltpu.CompilerParams(collective_id=1, has_side_effects=True, vmem_limit_bytes=63 << 20),
        cost_estimate=FREE,
        name="finish",
    )(raw, normed, *dx, *tables, w, inputs, grad_mid, gain, early, proj_in, *parts_a, *parts_b)


def places():
    return tuple(lax.axis_index(name) for name in ("dp", "g", "p", "c"))


def middle_kernel(sizes, near, *refs):
    dp, ng, np_ = sizes
    far = refs[:np_]
    (w, patches, bias, gain, shift, mid, two_own, two_other, mixed,
     pieces, mine, away, came, sem, send, recv) = refs[np_:]
    i_dp, i_g, i_p, i_c = places()
    rows = patches.shape[1]
    core = {"c": 1 - i_c}
    meet([core] + [{"p": i_p ^ k} for k in range(1, np_)])
    link = Links(send, recv)
    here = pltpu.make_async_copy(near.at[i_p], pieces.at[0], sem.at[0])
    here.start()
    arrive = [link(near.at[i_p ^ k], pieces.at[k], {"p": i_p ^ k}) for k in range(1, np_)]

    def split(piece, p, image):
        for swap in range(2):

            @pl.when(i_c == swap)
            def _(swap=swap):
                for b in range(2):
                    mixed[p, b, image] = piece[(swap ^ b) * rows : ((swap ^ b) + 1) * rows, :]

    def product(b, image):
        total = None
        for p in range(np_):
            term = dot(mixed[p, b, image], w[p])
            total = term if total is None else total + term
        return total

    other = []
    for bit in (1, 0):
        image = i_g ^ bit
        if bit:
            for k in range(np_):
                split(far[k], i_p ^ k, image)
        else:
            here.wait()
            for copy in arrive:
                copy.wait_recv()
            for k in range(np_):
                split(pieces.at[k], i_p ^ k, image)
        away[image] = product(1, image)
        other.append(link(away.at[image], came.at[image], core))
        mine[image] = product(0, image)
    back = []
    for bit in (1, 0):
        image = i_g ^ bit
        other[1 - bit].wait_recv()
        value = patches[image].astype(F32) + mine[image] + came[image] + bias[...]
        mid[image] = value
        two_own[image] = (normal_rows(value) * gain[...] + shift[...]).astype(BF)
        back.append(link(two_own.at[image], two_other.at[image], core))
    for copy in back:
        copy.wait_recv()
    link.drain()


def middle_rows(near, far, w, patches, bias, gain, shift, sizes):
    dp, ng, np_ = sizes
    images, rows, width = patches.shape
    lanes = near.shape[2]
    vmem = pl.BlockSpec(memory_space=pltpu.VMEM)
    copies = np_ - 1 + 2 * images
    own = jax.ShapeDtypeStruct((images, rows, width), BF)
    return pl.pallas_call(
        partial(middle_kernel, sizes),
        in_specs=[pl.BlockSpec(memory_space=pl.ANY)] + [vmem] * (len(far) + 5),
        out_specs=[vmem] * 4,
        out_shape=[
            jax.ShapeDtypeStruct((images, rows, width), F32),
            own,
            own,
            jax.ShapeDtypeStruct((np_, 2, images, rows, lanes), BF),
        ],
        scratch_shapes=[
            pltpu.VMEM((np_, 2 * rows, lanes), BF),
            pltpu.VMEM((images, rows, width), F32),
            pltpu.VMEM((images, rows, width), F32),
            pltpu.VMEM((images, rows, width), F32),
            pltpu.SemaphoreType.DMA((1,)),
            pltpu.SemaphoreType.DMA((copies,)),
            pltpu.SemaphoreType.DMA((copies,)),
        ],
        compiler_params=pltpu.CompilerParams(collective_id=2, has_side_effects=True, vmem_limit_bytes=48 << 20),
        cost_estimate=FREE,
        name="middle_rows",
    )(near, *far, w, patches, bias, gain, shift)


def norm_back(values, gain, upstream):
    center = values - jnp.mean(values, -1, keepdims=True)
    spread = jnp.mean(center * center, -1, keepdims=True)
    inverse = lax.rsqrt(spread + EPSILON)
    normal = center * inverse
    scaled = upstream * gain
    inner = jnp.mean(scaled * normal, -1, keepdims=True)
    return inverse * (scaled - jnp.mean(scaled, -1, keepdims=True) - normal * inner), normal


def turn_kernel(sizes, mid, gn, out, branch, gain, shift, w, mixed, output, grad_mid, heads, grad_proj, sums,
                back_own, back_other, gn_own, gn_came, out_own, out_came, stage, sem, send, recv):
    dp, ng, np_ = sizes
    i_dp, i_g, i_p, i_c = places()
    images, rows, width = mid.shape
    i_z = i_g * np_ + i_p
    core = {"c": 1 - i_c}
    peers = [core]
    for k in range(1, ng * np_):
        peers.append({"g": i_g ^ (k // np_), "p": i_p ^ (k % np_)})
    meet(peers)
    link = Links(send, recv)
    turns = [i_g ^ 1, i_g]

    def half(ref, b, image):
        start = (b * images + image) * rows
        return ref.at[pl.ds(pl.multiple_of(start, 8), rows)]

    loads = []
    crossed = []
    for n, image in enumerate(turns):
        crossed.append(link(half(gn, 1, image), gn_came.at[image], core))
        loads.append(pltpu.make_async_copy(half(gn, 0, image), gn_own.at[image], sem.at[n]))
        loads[-1].start()
    locals_ = []
    sums[...] = jnp.zeros_like(sums)

    def give(n, b):
        image = turns[n]
        source = (back_own if b == 0 else back_other)[image]
        for k in range(np_):
            slot = (n * np_ + k) * 2 + b
            stage[slot] = dot(source, w[i_p ^ k], NT).astype(BF)
            start = (i_z * 2 + (i_c ^ b)) * rows
            dst = heads.at[pl.ds(pl.multiple_of(start, 8), rows)]
            if n == 1 and k == 0:
                locals_.append(pltpu.make_async_copy(stage.at[slot], dst, sem.at[2 * images + b]))
                locals_[-1].start()
            else:
                arrivals.append(link(stage.at[slot], dst, {"g": image, "p": i_p ^ k}))

    arrivals = []
    others = []
    for n, image in enumerate(turns):
        loads[n].wait()
        crossed[n].wait_recv()
        grad_two = gn_own[image] + gn_came[image]
        grad_out = branch[image].astype(F32)
        grad_norm, normal = norm_back(mid[image], gain[...], grad_two)
        grad = grad_out + grad_norm
        grad_mid[image] = grad
        back_own[image] = grad.astype(BF)
        others.append(link(back_own.at[image], back_other.at[image], core))
        sums[0:1, :] += jnp.sum(grad_two * normal, 0, keepdims=True)
        sums[1:2, :] += jnp.sum(grad_two, 0, keepdims=True)
        sums[2:3, :] += jnp.sum(back_own[image].astype(F32), 0, keepdims=True)
        sums[3:4, :] += jnp.sum(grad_out, 0, keepdims=True)
        give(n, 0)
    outs = []
    for n, image in enumerate(turns):
        others[n].wait_recv()
        give(n, 1)
        outs.append(link(half(out, 1, image), out_came.at[image], core))
        loads.append(pltpu.make_async_copy(half(out, 0, image), out_own.at[image], sem.at[images + n]))
        loads[-1].start()
    for p in range(np_):
        total = None
        for b, source in ((0, back_own), (1, back_other)):
            for image in range(images):
                term = dot(mixed[p, b, image], source[image], TN)
                total = term if total is None else total + term
        grad_proj[p] = total.astype(BF)
    for n, image in enumerate(turns):
        loads[images + n].wait()
        outs[n].wait_recv()
        value = mid[image] + out_own[image] + out_came[image] + shift[...]
        output[image] = value.astype(BF)
    for copy in locals_:
        copy.wait()
    for copy in arrivals:
        copy.wait_recv()
    link.drain()


def turn(mid, gn, out, branch, gain, shift, w, mixed, sizes):
    dp, ng, np_ = sizes
    images, rows, width = mid.shape
    lanes = w.shape[1]
    chips = ng * np_
    vmem = pl.BlockSpec(memory_space=pltpu.VMEM)
    hbm = pl.BlockSpec(memory_space=pl.ANY)
    copies = 3 * images + 2 * (chips - 1)
    own = (images, rows, width)
    return pl.pallas_call(
        partial(turn_kernel, sizes),
        in_specs=[vmem, hbm, hbm] + [vmem] * 5,
        out_specs=[vmem, vmem, hbm, vmem, vmem],
        out_shape=[
            jax.ShapeDtypeStruct(own, BF),
            jax.ShapeDtypeStruct(own, F32),
            jax.ShapeDtypeStruct((chips * 2 * rows, lanes), BF),
            jax.ShapeDtypeStruct((np_, lanes, width), BF),
            jax.ShapeDtypeStruct((8, width), F32),
        ],
        scratch_shapes=[
            pltpu.VMEM(own, BF),
            pltpu.VMEM(own, BF),
            pltpu.VMEM(own, F32),
            pltpu.VMEM(own, F32),
            pltpu.VMEM(own, F32),
            pltpu.VMEM(own, F32),
            pltpu.VMEM((chips * 2, rows, lanes), BF),
            pltpu.SemaphoreType.DMA((2 * images + 2,)),
            pltpu.SemaphoreType.DMA((copies,)),
            pltpu.SemaphoreType.DMA((copies,)),
        ],
        compiler_params=pltpu.CompilerParams(collective_id=3, has_side_effects=True, vmem_limit_bytes=56 << 20),
        cost_estimate=FREE,
        name="turn",
    )(mid, gn, out, branch, gain, shift, w, mixed)


def flip(value, axis, size, bit):
    return lax.ppermute(value, axis, [(i, i ^ bit) for i in range(size)])


def pick(value, index, axis=0):
    return lax.dynamic_index_in_dim(value, index, axis, keepdims=False)


def gather_pieces(value, axis, size, me):
    full = jnp.zeros((size,) + value.shape, value.dtype)
    full = lax.dynamic_update_index_in_dim(full, value, me, 0)
    for bit in range(1, size):
        full = lax.dynamic_update_index_in_dim(full, flip(value, axis, size, bit), me ^ bit, 0)
    return full


def scatter_sum(value, axis, size, me):
    total = pick(value, me).astype(F32)
    for bit in range(1, size):
        total = total + flip(pick(value, me ^ bit), axis, size, bit).astype(F32)
    return total


def tie(*values):
    return lax.optimization_barrier(values)


def after(value, *others):
    return tie(value, *others)[0]


def on_device(
    patches,
    ln1_gain,
    ln1_bias,
    qkv_weight,
    q_bias,
    v_bias,
    proj_weight,
    proj_bias,
    ln2_gain,
    ln2_bias,
    fc1_weight,
    fc1_bias,
    fc2_weight,
    fc2_bias,
    rel_pos_h,
    rel_pos_w,
    cotangent,
):
    images, row_count, width = patches.shape
    dp, ng, np_, nc = (lax.axis_size(name) for name in ("dp", "g", "p", "c"))
    i_dp, i_g, i_p, i_c = (lax.axis_index(name) for name in ("dp", "g", "p", "c"))
    chips = ng * np_
    i_z = i_g * np_ + i_p
    ranks = chips * nc
    seq_len = ranks * row_count
    own_rows = images * row_count
    heads = H * images // ranks
    shard_heads = H // dp
    core_heads = shard_heads // nc
    piece = core_heads * HD
    pieces = heads // core_heads
    lanes = heads * HD
    hidden = fc1_weight.shape[1]
    unit = hidden // ranks
    shard = width // dp
    per = hidden // dp // (nc * unit)
    side = (rel_pos_h.shape[0] + 1) // 2

    core_bias = pick(fc1_bias.reshape(per, nc, 2, unit // 2), i_c, 1).transpose(1, 0, 2)
    packed = jnp.concatenate(
        [
            jnp.stack([ln1_gain, ln1_bias, q_bias, v_bias, proj_bias, ln2_gain, ln2_bias, fc2_bias]),
            core_bias.reshape(-1, shard),
        ]
    )
    spot = jnp.stack([i_g, i_p, i_c])
    qkv_own, slab_a, slab_b = select(spot, qkv_weight, fc1_weight, fc2_weight, proj_weight, ng, np_, nc, lanes)
    weights_a = lax.all_gather(slab_a, "dp", axis=0)
    weights_b = lax.all_gather(slab_b, "dp", axis=0)
    proj_half = weights_a[:, 2 * shard :]
    raw, qkv_full, vectors = start_exchange(patches, qkv_own, packed, (dp, ng, np_))
    qkv_full = qkv_full.reshape(width, 3 * lanes)
    vectors = vectors.astype(F32)
    whole_vec = vectors.transpose(1, 0, 2).reshape(-1, width)
    gain_one, shift_one, q_shift, v_shift, proj_shift, gain_two, shift_two, fc2_shift = whole_vec[:8]
    fc1_shift = vectors[:, 8:].reshape(dp, 2, -1).transpose(1, 0, 2).reshape(2, 1, -1)

    starts = [
        part * width + (i_p * pieces + q) * shard_heads * HD + i_c * piece
        for q in range(pieces)
        for part in range(3)
    ]
    zero = jnp.zeros((piece,), F32)
    biases = []
    for q in range(pieces):
        at = starts[3 * q]
        biases += [lax.dynamic_slice_in_dim(q_shift, at, piece, 0), zero]
        biases += [lax.dynamic_slice_in_dim(v_shift, at, piece, 0)]
    qkv_shift = jnp.concatenate(biases)[None]

    branch_own = cotangent.reshape(own_rows, width)
    branch_other = flip(branch_own, "c", nc, 1)

    tables = flip_tables(rel_pos_h, rel_pos_w)
    normed, query, key_rows, value_rows = qkv_rows(
        raw, gain_one[None], shift_one[None], qkv_full, qkv_shift, tables, pieces, core_heads, side
    )
    far_att, att_f, query_a = attend(i_g ^ 1, query, key_rows, value_rows, side, ng)
    far_att = far_att.reshape(np_, nc * row_count, lanes)
    arrived = {}
    for bit_p in range(np_):
        arrived[1, bit_p] = flip(pick(far_att, i_p ^ bit_p), ("g", "p"), chips, np_ + bit_p)
    near_att, att_f, query_a = attend(i_g, query, key_rows, value_rows, side, ng, (att_f, query_a))
    near_att, *pinned = tie(near_att, *[arrived[1, k] for k in range(np_)])
    for k in range(np_):
        arrived[1, k] = pinned[k]
    near_att = near_att.reshape(np_, nc * row_count, lanes)
    proj_rows = proj_half.reshape(np_, lanes, width)
    sizes = (dp, ng, np_)
    middle, two_own, two_other, mixed = middle_rows(
        near_att,
        [arrived[1, k] for k in range(np_)],
        proj_rows,
        patches,
        proj_shift[None],
        gain_two[None],
        shift_two[None],
        sizes,
    )
    two_own, two_other = two_own.reshape(own_rows, width), two_other.reshape(own_rows, width)

    def over_dp(value):
        return lax.psum_scatter(value.reshape(-1, value.shape[-1]), "dp", scatter_dimension=0, tiled=True)

    out_a, back_a, grads_a, bias_a = mlp_half(
        two_own, two_other, branch_own, branch_other, weights_a, fc1_shift[0]
    )
    sum_a = over_dp(grads_a)
    out_b, back_b, grads_b, bias_b = mlp_half(
        two_own, two_other, branch_own, branch_other, weights_b, fc1_shift[1], (out_a, back_a)
    )
    output, grad_middle, grad_heads, grad_proj, early = turn(
        middle, back_b, out_b, cotangent, gain_two[None], fc2_shift[None], proj_rows, mixed, sizes
    )
    sum_b = over_dp(grads_b)
    sum_p = over_dp(grad_proj.reshape(dp, piece, width))

    def pieces_over_chips(value):
        split = value.reshape(value.shape[0], chips, width // chips).transpose(1, 0, 2)
        sent = [flip(pick(split, i_z ^ bit), ("g", "p"), chips, bit) for bit in range(1, chips)]
        return [pick(split, i_z)] + sent

    grad_heads, sum_a = tie(grad_heads, sum_a)
    sum_a = pieces_over_chips(sum_a)
    dx = []
    grad_tables = []
    for q in range(pieces):
        rows, table = attend_back(
            q * core_heads, core_heads, query_a, key_rows, value_rows, att_f, grad_heads, tables, side
        )
        if q == 0:
            rows, *sum_a = tie(rows, *sum_a)
            sum_b = pieces_over_chips(after(sum_b, rows))
            key_rows = after(key_rows, rows)
        elif q == 1:
            rows, *sum_b = tie(rows, *sum_b)
        dx.append(rows)
        grad_tables.append(table)
    dx[-1], sum_p = tie(dx[-1], sum_p)

    bias_half = jnp.stack([bias_a.reshape(dp, per, unit // 2), bias_b.reshape(dp, per, unit // 2)], 2)
    bias_half = bias_half.reshape(dp * per, 1, unit)
    bias_full = jnp.concatenate([bias_half] * nc, 1)
    core = lax.broadcasted_iota(jnp.int32, bias_full.shape, 1)
    bias_full = jnp.where(core == i_c, bias_full, 0.0).reshape(dp, -1, shard)
    early = jnp.concatenate([early[:4], bias_full.transpose(1, 0, 2).reshape(-1, width)])
    grad_patches, out_qkv, vec, rel, out_fc1, out_fc2, out_proj = finish(
        raw,
        normed,
        dx,
        grad_tables,
        qkv_full,
        patches,
        grad_middle,
        gain_one[None],
        early,
        sum_p,
        (sum_a, sum_b),
        sizes,
        piece,
    )
    entries = rel_pos_h.shape[0]
    rel = [rel[:entries, :HD][::-1], rel[128 : 128 + entries, :HD][::-1]]
    fc1_vec = vec[8:12].reshape(-1)

    return (
        output,
        grad_patches,
        vec[0],
        vec[1],
        out_qkv,
        vec[2],
        vec[3],
        out_proj,
        vec[6],
        vec[4],
        vec[5],
        out_fc1,
        fc1_vec,
        out_fc2,
        vec[7],
        rel[0],
        rel[1],
    )


def solution(mesh):
    dp, ranks = mesh.shape["dp"], mesh.shape["seq"]

    def call(*args):
        images = args[0].shape[0] // dp
        shape = (dp, images, ranks // images // 2, 2)
        fine = jax.sharding.Mesh(mesh.devices.reshape(shape), ("dp", "g", "p", "c"))
        seq = ("g", "p", "c")
        tokens, rows, both = P("dp", seq, None), P("dp", None), P("dp", seq)
        vec = P("dp")
        return jax.shard_map(
            on_device,
            mesh=fine,
            in_specs=(
                tokens, vec, vec, rows, vec, vec, rows, vec, vec, vec, rows, vec, rows, vec, P(), P(), tokens
            ),
            out_specs=(
                tokens, tokens, vec, vec, both, vec, vec, both, vec, vec, vec, both, vec, both, vec, P(), P()
            ),
            check_vma=False,
        )(*args)

    return call
```

```python
import math
from functools import partial

import jax
import jax.numpy as jnp
from jax import lax
from jax.experimental import pallas as pl
from jax.experimental.pallas import tpu as pltpu
from jax.sharding import PartitionSpec as P

H = 16
HD = 80
EPSILON = 1e-06
NT = (((1,), (1,)), ((), ()))
TN = (((0,), (0,)), ((), ()))
BF = jnp.bfloat16
F32 = jnp.float32
LOG2E = 1.4426950408889634
FACTOR = LOG2E / math.sqrt(HD)
FREE = pl.CostEstimate(flops=1, bytes_accessed=1, transcendentals=0)


def busy(gflops):
    return pl.CostEstimate(flops=gflops * 10**9, bytes_accessed=1, transcendentals=0)


def dot(a, b, dims=(((1,), (0,)), ((), ()))):
    return lax.dot_general(a, b, dims, preferred_element_type=F32)


def params(axes, mib=60):
    return pltpu.CompilerParams(
        dimension_semantics=("arbitrary",) * axes, vmem_limit_bytes=mib << 20
    )


def whole(*shape):
    return pl.BlockSpec(shape, lambda *at: (0,) * len(shape), pipeline_mode=pl.Buffered(1))


def flip_tables(rel_h, rel_w):
    entries = rel_h.shape[0]
    pad = ((0, 128 - entries), (0, 0))
    return jnp.concatenate([jnp.pad(rel_h[::-1], pad), jnp.pad(rel_w[::-1], pad)], 0)


def normal_rows(values):
    center = values - jnp.mean(values, -1, keepdims=True)
    spread = jnp.mean(center * center, -1, keepdims=True)
    return center * lax.rsqrt(spread + EPSILON)


def qkv_kernel(pieces, group_heads, side, sub, raw, gain, shift, w, bias, tables, normed, qa, kp, vp):
    count = raw.shape[0] // sub
    width = group_heads * HD
    lane = lax.broadcasted_iota(jnp.int32, (sub, 128), 1)
    group_lane = lax.broadcasted_iota(jnp.int32, (side, 128), 1)
    group_row = lax.broadcasted_iota(jnp.int32, (side, 128), 0)
    col_hot = (group_lane == group_row) | ((group_lane >= side) & (group_lane < side + 3))
    col_hot = jnp.where(col_hot, 1.0, 0.0).astype(BF)
    col_hot = jnp.concatenate([col_hot] * (sub // side), 0)

    def product(n):
        part = slice(n * sub, (n + 1) * sub)
        rows_n = (normal_rows(raw[part, :].astype(F32)) * gain[...] + shift[...]).astype(BF)
        normed[part, :] = rows_n
        return (dot(rows_n, w[...]) + bias[...]).astype(BF)

    ahead = product(0)
    for m in range(count):
        joined = ahead
        if m + 1 < count:
            ahead = product(m + 1)
        part = slice(m * sub, (m + 1) * sub)
        first_row = (pl.program_id(0) * count + m) * (sub // side)
        hot = []
        for i in range(sub // side):
            hot.append(jnp.where(group_lane == first_row + (HD + i), 1.0, 0.0).astype(BF))
        row_hot = jnp.concatenate(hot, 0)
        for n in range(pieces * group_heads):
            q_at = (n // group_heads) * 3 * width + (n % group_heads) * HD
            q = joined[:, q_at : q_at + HD]
            g = dot(q, tables[...], NT) * math.sqrt(HD)
            gh = []
            gw = []
            for i in range(sub // side):
                rows = g[i * side : (i + 1) * side]
                gh.append(pltpu.roll(rows[:, :128], first_row + (33 + i), axis=1))
                gw.append(pltpu.roll(rows[:, 128:], 81, axis=1, stride=1, stride_axis=0))
            qa[n, part, 0:128] = jnp.concatenate(gh, 0).astype(BF)
            qa[n, part, 0:HD] = q
            qa[n, part, 128:256] = jnp.where(lane < side, jnp.concatenate(gw, 0), 0.0).astype(BF)
            kp[n, part, 0:128] = row_hot
            kp[n, part, 128:256] = col_hot
            kp[n, part, 0:HD] = joined[:, q_at + width : q_at + width + HD]
            vp[n, part, :] = jnp.ones((sub, 128), BF)
            vp[n, part, 0:HD] = joined[:, q_at + 2 * width : q_at + 2 * width + HD]


def qkv_rows(raw, gain, shift, w, bias, tables, pieces, group_heads, side, rows=384, sub=192):
    seq_len, width = raw.shape
    lanes = w.shape[1]
    heads = pieces * group_heads
    return pl.pallas_call(
        partial(qkv_kernel, pieces, group_heads, side, sub),
        grid=(seq_len // rows,),
        in_specs=[
            pl.BlockSpec((rows, width), lambda i: (i, 0)),
            whole(1, width),
            whole(1, width),
            whole(width, lanes),
            whole(1, lanes),
            whole(256, HD),
        ],
        out_specs=[
            pl.BlockSpec((rows, width), lambda i: (i, 0)),
            pl.BlockSpec((heads, rows, 256), lambda i: (0, i, 0)),
            pl.BlockSpec((heads, rows, 256), lambda i: (0, i, 0)),
            pl.BlockSpec((heads, rows, 128), lambda i: (0, i, 0)),
        ],
        out_shape=[
            jax.ShapeDtypeStruct((seq_len, width), BF),
            jax.ShapeDtypeStruct((heads, seq_len, 256), BF),
            jax.ShapeDtypeStruct((heads, seq_len, 256), BF),
            jax.ShapeDtypeStruct((heads, seq_len, 128), BF),
        ],
        compiler_params=params(1),
        cost_estimate=FREE,
        name="qkv_rows",
    )(raw, gain, shift, w, bias, tables)


def attend_kernel(heads, side, aliased, sub, at, qa, kp, vp, *refs):
    o, of, qo = refs[2:] if aliased else refs
    rows = qa.shape[1]
    h = pl.program_id(0)
    base = pl.multiple_of(pl.program_id(1) * rows, rows)
    lane = lax.broadcasted_iota(jnp.int32, (sub, 128), 1)
    count = rows // sub
    scores = [dot(qa[0, 0:sub, :], kp[0], NT)]
    outs = []
    for n in range(count):
        part = slice(n * sub, (n + 1) * sub)
        if n + 1 < count:
            scores.append(dot(qa[0, (n + 1) * sub : (n + 2) * sub, :], kp[0], NT))
        s = scores[n]
        m = jnp.max(s, -1, keepdims=True)
        p = jnp.exp2(s * FACTOR - m * FACTOR).astype(BF)
        out = dot(p, vp[0])
        total = out[:, HD : HD + 1]
        out = out / total
        norm = m + jnp.log2(total) / FACTOR
        hi = norm.astype(BF).astype(F32)
        mid = (norm - hi).astype(BF).astype(F32)
        low = norm - hi - mid
        old = qa[0, part, 128:256].astype(F32)
        old = jnp.where(lane == side, -hi, old)
        old = jnp.where(lane == side + 1, -mid, old)
        old = jnp.where(lane == side + 2, -low, old)
        qo[0, part, 0:128] = qa[0, part, 0:128]
        qo[0, part, 128:256] = old.astype(BF)
        outs.append(out)
    out = jnp.concatenate(outs, 0)
    part = pl.ds(base, rows)
    for n in range(heads):

        @pl.when(h == n)
        def _(n=n):
            o[part, n * HD : (n + 1) * HD] = out[:, 0:HD].astype(BF)
            of[part, n * HD : (n + 1) * HD] = out[:, 0:HD]


def attend(group, qa, kp, vp, side, groups, old=(), tq=1152, sub=576):
    heads, seq_len, _ = qa.shape
    rows = seq_len // groups
    steps = rows // tq
    lanes = heads * HD
    query = pl.BlockSpec((1, tq, 256), lambda h, i, at: (h, at[0] * steps + i, 0))
    return pl.pallas_call(
        partial(attend_kernel, heads, side, bool(old), sub),
        grid_spec=pltpu.PrefetchScalarGridSpec(
            num_scalar_prefetch=1,
            grid=(heads, steps),
            in_specs=[
                query,
                pl.BlockSpec((1, seq_len, 256), lambda h, i, at: (h, 0, 0)),
                pl.BlockSpec((1, seq_len, 128), lambda h, i, at: (h, 0, 0)),
            ]
            + [pl.BlockSpec(memory_space=pl.ANY)] * len(old),
            out_specs=[
                pl.BlockSpec((rows, lanes), lambda h, i, at: (0, 0)),
                pl.BlockSpec((rows, lanes), lambda h, i, at: (at[0], 0)),
                query,
            ],
        ),
        out_shape=[
            jax.ShapeDtypeStruct((rows, lanes), BF),
            jax.ShapeDtypeStruct((seq_len, lanes), F32),
            jax.ShapeDtypeStruct((heads, seq_len, 256), BF),
        ],
        input_output_aliases={4: 1, 5: 2} if old else {},
        compiler_params=params(2),
        cost_estimate=busy(20),
        name="attend",
    )(jnp.stack([group]), qa, kp, vp, *old)


def attend_back_kernel(heads, first, side, uc, qa_ref, kp, vp, of, go, tables, hot, dx, gt, kt, dop, dk, dv, dq):
    seq_len = kp.shape[1]
    tb = qa_ref.shape[1]
    h = pl.program_id(0)
    step = pl.program_id(1)
    last = pl.num_programs(1) - 1
    scale = HD ** (-0.5)
    rows = seq_len // 9

    @pl.when((h == 0) & (step == 0))
    def _():
        gt[...] = jnp.zeros_like(gt)

        blocks, high, wide = go.shape
        total_lanes = of.shape[1]
        fold = wide // total_lanes
        if fold == 1:
            high = rows

        def prep(i, c):
            lane = lax.broadcasted_iota(jnp.int32, (high, 128), 1)
            for s in range(fold):
                part = pl.ds(pl.multiple_of((i * fold + s) * high, high), high)
                for n in range(heads):
                    at = (first + n) * HD
                    if fold == 1:
                        rows_go = flat_go[part, at : at + HD]
                    else:
                        rows_go = go[i, :, s * total_lanes + at : s * total_lanes + at + HD]
                    inner = jnp.sum(rows_go.astype(F32) * of[part, at : at + HD], -1, keepdims=True)
                    hi = inner.astype(BF).astype(F32)
                    tail = jnp.where(lane == HD, -hi, jnp.where(lane == HD + 1, hi - inner, 0.0))
                    dop[n, part, :] = tail.astype(BF)
                    dop[n, part, 0:HD] = rows_go
            return c

        flat_go = go.at[0]
        lax.fori_loop(0, seq_len // (fold * high), prep, 0)

    @pl.when(step == 0)
    def _():
        def prep(i, c):
            part = pl.ds(pl.multiple_of(i * rows, rows), rows)
            kt[0:128, part] = kp[0, part, 0:128].T
            kt[128 : 128 + side, part] = hot[:, part]
            dk[part, :] = jnp.zeros((rows, 128), F32)
            dv[part, :] = jnp.zeros((rows, 128), F32)
            return c

        lax.fori_loop(0, 9, prep, 0)

    base = pl.ds(pl.multiple_of(step * tb, tb), tb)
    qa = qa_ref[0]
    do = dop[h, base, :]

    def scores(j):
        part = slice(j * uc, (j + 1) * uc)
        return dot(kp[0, part, :], qa, NT), dot(vp[0, part, :], do, NT)

    acc = None
    count = seq_len // uc
    ahead = scores(0)
    for j in range(count):
        s, dp = ahead
        if j + 1 < count:
            ahead = scores(j + 1)
        part = slice(j * uc, (j + 1) * uc)
        p = jnp.exp2(s * FACTOR)
        ds = (p * dp).astype(BF)
        dv[part, :] += dot(p.astype(BF), do)
        dk[part, :] += dot(ds, qa[:, 0:128])
        term = dot(kt[:, part], ds)
        acc = term if acc is None else acc + term
    acc = jnp.concatenate([acc, jnp.zeros((256 - HD - 2 * side, tb), F32)], 0).T
    lane = lax.broadcasted_iota(jnp.int32, (tb, 128), 1)
    groups = tb // side
    rel_h = jnp.where(lane < HD, 0.0, acc[:, :128])
    rel_w = jnp.where(lane < side, acc[:, 128:], 0.0)
    back_h = []
    back_w = []
    for i in range(groups):
        part = slice(i * side, (i + 1) * side)
        back_h.append(pltpu.roll(rel_h[part], 256 - 33 - step * groups - i, axis=1))
        back_w.append(pltpu.roll(rel_w[part], 0, axis=1, stride=1, stride_axis=0))
    both = jnp.concatenate([jnp.concatenate(back_h, 0), jnp.concatenate(back_w, 0)], 1).astype(BF)
    dq[base, :] = acc[:, :HD] * scale + dot(both, tables[...])
    gt[...] += dot(both, qa[:, 0:128], TN)

    width = heads * HD
    for n in range(heads):

        @pl.when((h == n) & (step == last))
        def _(n=n):
            def post(i, c):
                part = pl.ds(pl.multiple_of(i * rows, rows), rows)
                at = n * HD
                dx[part, at : at + HD] = dq[part, :].astype(BF)
                dx[part, width + at : width + at + HD] = (dk[part, 0:HD] * scale).astype(BF)
                dx[part, 2 * width + at : 2 * width + at + HD] = dv[part, 0:HD].astype(BF)
                return c

            lax.fori_loop(0, 9, post, 0)


def attend_back(first, count, qa, kp, vp, of, go, tables, hot, side, tb=768, uc=256):
    heads, seq_len, _ = qa.shape
    lanes = heads * HD
    if go.shape[2] == lanes:
        go = go.reshape(1, seq_len, lanes)
    return pl.pallas_call(
        partial(attend_back_kernel, count, first, side, uc),
        grid=(count, seq_len // tb),
        in_specs=[
            pl.BlockSpec((1, tb, 256), lambda h, i: (first + h, i, 0)),
            pl.BlockSpec((1, seq_len, 256), lambda h, i: (first + h, 0, 0)),
            pl.BlockSpec((1, seq_len, 128), lambda h, i: (first + h, 0, 0)),
            whole(seq_len, lanes),
            whole(*go.shape),
            whole(256, HD),
            whole(side, seq_len),
        ],
        out_specs=[whole(seq_len, 3 * count * HD), whole(256, 128)],
        out_shape=[
            jax.ShapeDtypeStruct((seq_len, 3 * count * HD), BF),
            jax.ShapeDtypeStruct((256, 128), F32),
        ],
        scratch_shapes=[
            pltpu.VMEM((HD + 2 * side, seq_len), BF),
            pltpu.VMEM((count, seq_len, 128), BF),
            pltpu.VMEM((seq_len, 128), F32),
            pltpu.VMEM((seq_len, 128), F32),
            pltpu.VMEM((seq_len, HD), F32),
        ],
        compiler_params=params(2),
        cost_estimate=busy(50),
        name="attend_back",
    )(qa, kp, vp, of, go, tables, hot)


def mlp_kernel(aliased, per, n_own, n_other, g_own, g_other, w1, b1, w2, *refs):
    if aliased:
        out_in, gn_in, out, gn, grads, gb1, n2, gb, act, gbef = refs
    else:
        out, gn, grads, gb1, n2, gb, act, gbef = refs
    step = pl.program_id(0)
    chunk = out.shape[0]
    shards, shard, hidden = w1.shape
    width = n_own.shape[1]
    steps = 2 * per

    @pl.when(step == 0)
    def _():
        gb1[...] = jnp.zeros_like(gb1)

    @pl.when(step < steps)
    def _():
        first = w1[...].reshape(width, hidden)
        second = w2[...].reshape(hidden, width)
        dst = pl.ds(pl.multiple_of(step * chunk, chunk), chunk)
        mine = step < per
        n2[dst, :] = jnp.where(mine, n_own[...], n_other[...])
        gb[dst, :] = jnp.where(mine, g_own[...], g_other[...])
        before = dot(n2[dst, :], first) + b1[...]
        grad_act = dot(gb[dst, :], second, NT)
        cdf = 0.5 + 0.5 * lax.erf(before * math.sqrt(0.5))
        act[dst, :] = (before * cdf).astype(BF)
        slope = cdf + before * (jnp.exp(-0.5 * before * before) * (1.0 / math.sqrt(2.0 * math.pi)))
        grad_before = slope * grad_act
        gbef[dst, :] = grad_before.astype(BF)
        gb1[...] += jnp.sum(gbef[dst, :].astype(F32), 0, keepdims=True)
        value = dot(act[dst, :], second)
        back = dot(gbef[dst, :], first, NT)
        if aliased:
            value = value + out_in[...]
            back = back + gn_in[...]
        out[...] = value
        gn[...] = back

    for j in range(shards):

        @pl.when(step == steps + j)
        def _(j=j):
            rows = slice(j * shard, (j + 1) * shard)
            grads[0, 0:shard, :] = dot(n2[:, rows], gbef[...], TN).astype(BF)
            grads[0, shard : 2 * shard, :] = dot(act[:, rows], gb[...], TN).astype(BF)


def mlp_half(n_own, n_other, g_own, g_other, weights, b1, old=(), chunk=288):
    half, width = n_own.shape
    dp = weights.shape[0]
    shard = width // dp
    hidden = width
    chunk = min(chunk, half)
    per = half // chunk
    steps = 2 * per
    tile = pl.BlockSpec((chunk, width), lambda i: (jnp.minimum(i, steps - 1), 0))
    own = pl.BlockSpec((chunk, width), lambda i: (jnp.minimum(i, per - 1), 0))
    other = pl.BlockSpec((chunk, width), lambda i: (jnp.clip(i - per, 0, per - 1), 0))
    rows = jax.ShapeDtypeStruct((2 * half, width), F32)
    return pl.pallas_call(
        partial(mlp_kernel, bool(old), per),
        grid=(steps + dp,),
        in_specs=[own, other, own, other]
        + [
            pl.BlockSpec((dp, shard, width), lambda i: (0, 0, 0), pipeline_mode=pl.Buffered(1)),
            whole(1, hidden),
            pl.BlockSpec((dp, shard, width), lambda i: (0, 1, 0), pipeline_mode=pl.Buffered(1)),
        ]
        + [tile] * len(old),
        out_specs=[
            tile,
            tile,
            pl.BlockSpec((1, 2 * shard, width), lambda i: (jnp.maximum(i - steps, 0), 0, 0)),
            whole(1, hidden),
        ],
        out_shape=[
            rows,
            rows,
            jax.ShapeDtypeStruct((dp, 2 * shard, width), BF),
            jax.ShapeDtypeStruct((1, hidden), F32),
        ],
        input_output_aliases={7: 0, 8: 1} if old else {},
        scratch_shapes=[pltpu.VMEM((2 * half, width), BF)] * 4,
        compiler_params=params(1, 63),
        cost_estimate=busy(35),
        name="mlp_half",
    )(n_own, n_other, g_own, g_other, weights, b1, weights, *old)


def select_kernel(ng, np_, nc, at, qkv, fc1, fc2, proj, own, *slabs):
    i_p, i_c = at[1], at[2]
    shard = fc1.shape[0]
    width = proj.shape[1]
    hidden = fc1.shape[1]
    chips = ng * np_
    unit = hidden // (chips * nc)
    part = unit // 2
    piece = proj.shape[0] // nc
    shard_lanes = proj.shape[0]
    lanes = own.shape[1] // 3
    pieces = lanes // piece
    per = fc2.shape[0] // (nc * unit)
    for c in range(nc):

        @pl.when(i_c == c)
        def _(c=c):
            for u in range(2):
                for z in range(chips):
                    src = (z * nc + c) * unit + u * part
                    slabs[u][0:shard, z * part : (z + 1) * part] = fc1[:, src : src + part]
                for b in range(per):
                    src = (b * nc + c) * unit + u * part
                    dst = shard + b * part
                    slabs[u][dst : dst + part, :] = fc2[src : src + part, :]
            slabs[0][2 * shard : 2 * shard + piece, :] = proj[c * piece : (c + 1) * piece, :]

        for p in range(np_):

            @pl.when((i_c == c) & (i_p == p))
            def _(c=c, p=p):
                for q in range(pieces):
                    for t in range(3):
                        src = t * width + (p * pieces + q) * shard_lanes + c * piece
                        dst = (3 * q + t) * piece
                        own[:, dst : dst + piece] = qkv[:, src : src + piece]


def select(at, qkv, fc1, fc2, proj, ng, np_, nc, lanes):
    shard, width = proj.shape[0], proj.shape[1]
    return pl.pallas_call(
        partial(select_kernel, ng, np_, nc),
        in_specs=[pl.BlockSpec(memory_space=pltpu.SMEM)] + [pl.BlockSpec(memory_space=pltpu.VMEM)] * 4,
        out_specs=[pl.BlockSpec(memory_space=pltpu.VMEM)] * 3,
        out_shape=[
            jax.ShapeDtypeStruct((shard, 3 * lanes), BF),
            jax.ShapeDtypeStruct((2 * shard + shard // nc, width), BF),
            jax.ShapeDtypeStruct((2 * shard, width), BF),
        ],
        compiler_params=pltpu.CompilerParams(vmem_limit_bytes=40 << 20),
        cost_estimate=FREE,
        name="select",
    )(at, qkv, fc1, fc2, proj)


def start_kernel(sizes, split, patches, own, vec, rows, full, vecs, local, send, recv):
    dp, ng, np_ = sizes
    i_dp, i_g, i_p, i_c = (lax.axis_index(name) for name in ("dp", "g", "p", "c"))
    count = patches.shape[1]
    step = count // split

    barrier = pltpu.get_barrier_semaphore()
    peers = [{"dp": i_dp ^ k} for k in range(1, dp)]
    peers += [{"g": i_g ^ k} for k in range(1, ng)]
    peers += [{"p": i_p ^ k} for k in range(1, np_)]
    peers += [{"c": 1 - i_c}]
    for peer in peers:
        pl.semaphore_signal(barrier, inc=1, device_id=peer, device_id_type=pl.DeviceIdType.MESH)
    pl.semaphore_wait(barrier, len(peers))

    used = []

    def remote(src, dst, peer):
        n = len(used)
        copy = pltpu.make_async_remote_copy(
            src_ref=src,
            dst_ref=dst,
            send_sem=send.at[n],
            recv_sem=recv.at[n],
            device_id=peer,
            device_id_type=pl.DeviceIdType.MESH,
        )
        used.append(copy)
        return copy

    def place(g, p, c, part):
        start = ((g * np_ + p) * 2 + c) * count + part * step
        return rows.at[pl.ds(pl.multiple_of(start, 8), step)]

    mine = [patches.at[i_g, pl.ds(part * step, step)] for part in range(split)]
    home = [pltpu.make_async_copy(mine[part], place(i_g, i_p, i_c, part), local.at[part]) for part in range(split)]
    home.append(pltpu.make_async_copy(own, full.at[i_dp], local.at[split]))
    home.append(pltpu.make_async_copy(vec, vecs.at[i_dp], local.at[split + 1]))

    far = {}
    for part in range(split):
        for bit in range(1, ng):
            src = patches.at[i_g ^ bit, pl.ds(part * step, step)]
            far[bit, part] = remote(src, place(i_g, i_p, i_c, part), {"g": i_g ^ bit})
            far[bit, part].start()
    over_dp = []
    for bit in range(1, dp):
        over_dp.append(remote(vec, vecs.at[i_dp], {"dp": i_dp ^ bit}))
        over_dp.append(remote(own, full.at[i_dp], {"dp": i_dp ^ bit}))
    for copy in over_dp:
        copy.start()
    near = {}
    for bit in range(1, np_):
        for part in range(split):
            near[bit, part] = remote(mine[part], place(i_g, i_p, i_c, part), {"p": i_p ^ bit})
            near[bit, part].start()
    cores = []
    for part in range(split):
        cores.append(remote(mine[part], place(i_g, i_p, i_c, part), {"c": 1 - i_c}))
        cores[-1].start()
    for copy in home:
        copy.start()

    onward = {}
    for part in range(split):
        for bit in range(1, ng):
            far[bit, part].wait_recv()
            came = place(i_g ^ bit, i_p, i_c, part)
            for bit_p in range(1, np_):
                onward[bit, bit_p, part] = remote(came, came, {"p": i_p ^ bit_p})
                onward[bit, bit_p, part].start()
            cores.append(remote(came, came, {"c": 1 - i_c}))
            cores[-1].start()
        for bit in range(1, np_):
            near[bit, part].wait_recv()
            came = place(i_g, i_p ^ bit, i_c, part)
            cores.append(remote(came, came, {"c": 1 - i_c}))
            cores[-1].start()
    for (bit, bit_p, part), copy in onward.items():
        copy.wait_recv()
        came = place(i_g ^ bit, i_p ^ bit_p, i_c, part)
        cores.append(remote(came, came, {"c": 1 - i_c}))
        cores[-1].start()
    for copy in over_dp + cores:
        copy.wait_recv()
    for copy in used:
        copy.wait_send()
    for copy in home:
        copy.wait()


def start_exchange(patches, own, vec, sizes):
    dp, ng, np_ = sizes
    images, count, width = patches.shape
    split = 6 if count % 48 == 0 else 3
    chunk_copies = ng * np_ + (ng - 1) + (np_ - 1) + (ng - 1) * (np_ - 1)
    copies = 2 * (dp - 1) + split * chunk_copies
    hbm = pl.BlockSpec(memory_space=pl.ANY)
    return pl.pallas_call(
        partial(start_kernel, sizes, split),
        in_specs=[hbm] * 3,
        out_specs=[hbm] * 3,
        out_shape=[
            jax.ShapeDtypeStruct((ng * np_ * 2 * count, width), BF),
            jax.ShapeDtypeStruct((dp,) + own.shape, BF),
            jax.ShapeDtypeStruct((dp,) + vec.shape, BF),
        ],
        scratch_shapes=[
            pltpu.SemaphoreType.DMA((split + 2,)),
            pltpu.SemaphoreType.DMA((copies,)),
            pltpu.SemaphoreType.DMA((copies,)),
        ],
        compiler_params=pltpu.CompilerParams(collective_id=0, has_side_effects=True),
        cost_estimate=FREE,
        name="start_exchange",
    )(patches, own, vec)


class Links:
    def __init__(self, send, recv):
        self.send, self.recv, self.copies = send, recv, []

    def __call__(self, src, dst, peer):
        n = len(self.copies)
        copy = pltpu.make_async_remote_copy(
            src_ref=src,
            dst_ref=dst,
            send_sem=self.send.at[n],
            recv_sem=self.recv.at[n],
            device_id=peer,
            device_id_type=pl.DeviceIdType.MESH,
        )
        copy.start()
        self.copies.append(copy)
        return copy

    def drain(self):
        for copy in self.copies:
            copy.wait_send()


def meet(peers):
    barrier = pltpu.get_barrier_semaphore()
    for peer in peers:
        pl.semaphore_signal(barrier, inc=1, device_id=peer, device_id_type=pl.DeviceIdType.MESH)
    pl.semaphore_wait(barrier, len(peers))


def finish_kernel(sizes, split, pieces, part_w, *refs):
    dp, ng, np_ = sizes
    chips = ng * np_
    ranks = chips * 2
    raw, normed = refs[:2]
    dx = refs[2 : 2 + pieces]
    tables = refs[2 + pieces : 2 + 2 * pieces]
    refs = refs[2 + 2 * pieces :]
    w, inputs, grad_mid, gain, early, proj_in = refs[:6]
    parts_a, parts_b = refs[6 : 6 + chips], refs[6 + chips : 6 + 2 * chips]
    (home, owned, out_vec, out_tab, out_fc1, out_fc2, out_proj,
     dx_all, norm_all, dx_ring, raw_ring, keep, away, came, pair, far, slab_out, slabs, cells, taken,
     sums, lane_sums, vec, vec_out, vec_dp, vec_z, vec_c, tab, tab_dp, tab_z, tab_c, tab_all,
     give, got, give_p, got_p, proj_out, proj_got, sem, send, recv, cell_send, cell_recv) = refs[6 + 2 * chips :]
    i_dp, i_g, i_p, i_c = places()
    i_z = i_g * np_ + i_p
    i_s = i_z * 2 + i_c
    count, width = keep.shape[1], keep.shape[2]
    step = count // split
    shard = owned.shape[0]
    cell = owned.shape[1] // 3
    lanes = dx_all.shape[2]
    core = {"c": 1 - i_c}
    chip_peer = lambda k: {"g": i_g ^ (k // np_), "p": i_p ^ (k % np_)}
    peers = [{"dp": i_dp ^ k} for k in range(1, dp)]
    for k in range(1, ranks):
        peers.append({"g": i_g ^ (k // (np_ * 2)), "p": i_p ^ ((k // 2) % np_), "c": i_c ^ (k % 2)})
    meet(peers)
    link = Links(send, recv)

    z_of = lambda k: (i_g ^ (k // np_)) * np_ + (i_p ^ (k % np_))
    part_rows = lambda part: pl.ds(part * step, step)
    far_slots, near_slots = list(range(np_, chips)), list(range(np_))
    jobs = [(k, b) for group in (far_slots, near_slots) for b in (1, 0) for k in group]
    loads = {}

    def load(n):
        if n < len(jobs):
            k, b = jobs[n]
            start = (z_of(k) * 2 + (i_c ^ b)) * count
            at = pl.ds(pl.multiple_of(start, 8), count)
            slot = n % 2
            loads[n] = [pltpu.make_async_copy(raw.at[at], raw_ring.at[slot], sem.at[slot * (1 + pieces)])]
            for q in range(pieces):
                loads[n].append(
                    pltpu.make_async_copy(dx[q].at[at], dx_ring.at[slot, q], sem.at[slot * (1 + pieces) + 1 + q])
                )
            for copy in loads[n]:
                copy.start()

    load(0)
    load(1)
    whole_loads = [pltpu.make_async_copy(normed, norm_all, sem.at[2 * (1 + pieces)])]
    for q in range(pieces):
        whole_loads.append(pltpu.make_async_copy(dx[q], dx_all.at[q], sem.at[2 * (1 + pieces) + 1 + q]))
    for copy in whole_loads:
        copy.start()
    sums[...] = jnp.zeros_like(sums)
    lane_sums[...] = jnp.zeros_like(lane_sums)
    from_core = {}

    def rows(n):
        k, b = jobs[n]
        slot = n % 2
        for copy in loads[n]:
            copy.wait()
        normal = normal_rows(raw_ring[slot].astype(F32))
        total = None
        for q in range(pieces):
            value = dx_ring[slot, q]
            term = dot(value, w[:, q * lanes : (q + 1) * lanes], NT)
            total = term if total is None else total + term
            lane_sums[q : q + 1, :] += jnp.sum(value.astype(F32), 0, keepdims=True)
        sums[0:1, :] += jnp.sum(total * normal, 0, keepdims=True)
        sums[1:2, :] += jnp.sum(total, 0, keepdims=True)
        if b:
            away[k] = total.astype(BF)
            from_core[k] = link(away.at[k], came.at[k], core)
        else:
            keep[k] = total.astype(BF)
        load(n + 2)

    from_pair = {}

    def over_cores(slots):
        for k in slots:
            from_core[k].wait_recv()
            for part in range(split):
                at = part_rows(part)
                keep[k, at, :] = (keep[k, at, :].astype(F32) + came[k, at, :].astype(F32)).astype(BF)
                if k % np_:
                    dst = pair.at[k // np_, k % np_, at]
                    from_pair[k // np_, k % np_, part] = link(keep.at[k, at], dst, {"p": i_p ^ (k % np_)})

    def over_pair(bit_g, part):
        at = part_rows(part)
        value = keep[bit_g * np_, at, :].astype(F32)
        for bit_p in range(1, np_):
            from_pair[bit_g, bit_p, part].wait_recv()
            value = value + pair[bit_g, bit_p, at, :].astype(F32)
        return value

    half = len(far_slots) * 2
    for n in range(half):
        rows(n)

    part_lanes = parts_a[0].shape[1]
    for z in range(chips):
        proj_out[z] = proj_in[:, z * part_lanes : (z + 1) * part_lanes]
    from_chip = [link(proj_out.at[z_of(k)], proj_got.at[k], chip_peer(k)) for k in range(1, chips)]
    over_cores(far_slots)

    for copy in whole_loads:
        copy.wait()
    for j in range(dp):
        for q in range(pieces):
            slab_out[j, q] = dot(norm_all[:, j * shard : (j + 1) * shard], dx_all[q], TN).astype(BF)
    from_dp = [link(slab_out.at[i_dp ^ bit], slabs.at[bit], {"dp": i_dp ^ bit}) for bit in range(1, dp)]

    from_far = {}
    for part in range(split):
        at = part_rows(part)
        for bit_g in range(1, ng):
            pair[bit_g, 0, at, :] = over_pair(bit_g, part).astype(BF)
            from_far[bit_g, part] = link(pair.at[bit_g, 0, at], far.at[bit_g, at], {"g": i_g ^ bit_g})
    for n in range(half, len(jobs)):
        rows(n)

    vec[...] = jnp.zeros_like(vec)
    vec[0:2, :] = sums[0:2, :]
    vec[4:12, :] = early[...]
    for p in range(np_):
        for c in range(2):

            @pl.when((i_p == p) & (i_c == c))
            def _(p=p, c=c):
                for q in range(pieces):
                    at = (p * pieces + q) * shard + c * part_w
                    vec[2:3, at : at + part_w] = lane_sums[q : q + 1, 0:part_w]
                    vec[3:4, at : at + part_w] = lane_sums[q : q + 1, 2 * part_w : 3 * part_w]

    table = tables[0][...]
    for ref in tables[1:]:
        table = table + ref[...]
    tab[...] = table
    tab_rows = tab.shape[0] // dp
    tab_at = lambda j: pl.ds(pl.multiple_of(j * tab_rows, 8), tab_rows)
    for j in range(dp):
        vec_out[j] = vec[:, j * shard : (j + 1) * shard]
    vec_dp[i_dp] = vec_out[i_dp]
    tab_dp[i_dp] = tab[tab_at(i_dp), :]
    small = []
    for bit in range(1, dp):
        small.append(link(vec_out.at[i_dp ^ bit], vec_dp.at[i_dp], {"dp": i_dp ^ bit}))
        small.append(link(tab.at[tab_at(i_dp ^ bit)], tab_dp.at[i_dp], {"dp": i_dp ^ bit}))

    def sum_of(ref, n):
        value = ref[0]
        for i in range(1, n):
            value = value + ref[i]
        return value

    over_cores(near_slots)
    for copy in small:
        copy.wait_recv()
    vec_z[i_z] = sum_of(vec_dp, dp)
    tab_z[i_z] = sum_of(tab_dp, dp)
    small = []
    for k in range(1, chips):
        small.append(link(vec_z.at[i_z], vec_z.at[i_z], chip_peer(k)))
        small.append(link(tab_z.at[i_z], tab_z.at[i_z], chip_peer(k)))

    hidden_rows = give.shape[1]
    per_rows = part_lanes
    swaps = []

    def halves(value, there):
        cols = value.shape[1] // 2
        mine = jnp.where(i_c == 0, value[:, :cols], value[:, cols:])
        there[...] = jnp.where(i_c == 0, value[:, cols:], value[:, :cols]).astype(BF)
        return mine

    def place_fc2(u, c, value):
        for b in range(hidden_rows // per_rows):
            start = ((b * 2 + c) * 2 + u) * per_rows
            out_fc2[pl.ds(pl.multiple_of(start, 8), per_rows), :] = value[b * per_rows : (b + 1) * per_rows, :]

    def place_proj(c, value):
        out_proj[pl.ds(pl.multiple_of(c * value.shape[0], 8), value.shape[0]), :] = value

    for u, parts in ((0, parts_a), (1, parts_b)):
        value = parts[0][...].astype(F32)
        for ref in parts[1:]:
            value = value + ref[...].astype(F32)
        out_fc1[:, u * per_rows : (u + 1) * per_rows] = value[0:shard]
        place_fc2(u, i_c, halves(value[shard:], give.at[u]))
        swaps.append(link(give.at[u], got.at[u], core))
    value = proj_out[i_z].astype(F32)
    for k in range(1, chips):
        from_chip[k - 1].wait_recv()
        value = value + proj_got[k].astype(F32)
    place_proj(i_c, halves(value, give_p))
    swaps.append(link(give_p, got_p, core))

    for copy in from_dp:
        copy.wait_recv()
    sent_cells = []
    for q in range(pieces):
        value = slab_out[i_dp, q].astype(F32)
        for bit in range(1, dp):
            value = value + slabs[bit, q].astype(F32)
        value = value.astype(BF)
        for t in range(3):
            for u in range(part_w // cell):
                n = len(sent_cells)
                lane = t * part_w + u * cell
                quarter = shard // 4
                for i in range(4):
                    cells[n, :, i * cell : (i + 1) * cell] = value[i * quarter : (i + 1) * quarter, lane : lane + cell]
                unit = (t * width + (i_p * pieces + q) * shard + i_c * part_w) // cell + u
                owner = unit // 3
                slot = unit % 3
                dst = taken.at[i_g, slot]
                o_c = owner % 2
                o_p = (owner // 2) % np_
                o_g = owner // (2 * np_)

                @pl.when(owner == i_s)
                def _(n=n, dst=dst, slot=slot):
                    pltpu.make_async_copy(cells.at[n], dst, cell_recv.at[i_g * 3 + slot]).start()

                @pl.when(owner != i_s)
                def _(n=n, dst=dst, slot=slot, o_g=o_g, o_p=o_p, o_c=o_c):
                    pltpu.make_async_remote_copy(
                        src_ref=cells.at[n],
                        dst_ref=dst,
                        send_sem=cell_send.at[n],
                        recv_sem=cell_recv.at[i_g * 3 + slot],
                        device_id={"g": o_g, "p": o_p, "c": o_c},
                        device_id_type=pl.DeviceIdType.MESH,
                    ).start()

                sent_cells.append(owner)

    def arrived(image, at, value):
        grad, _ = norm_back(inputs[image, at, :].astype(F32), gain[...], value)
        home[image, at, :] = (grad_mid[image, at, :] + grad).astype(BF)

    for part in range(split):
        arrived(i_g, part_rows(part), over_pair(0, part))
    for copy in small:
        copy.wait_recv()
    vec_c[i_c] = sum_of(vec_z, chips)
    tab_c[i_c] = sum_of(tab_z, chips)
    small = [link(vec_c.at[i_c], vec_c.at[i_c], core), link(tab_c.at[i_c], tab_c.at[i_c], core)]
    for copy in swaps:
        copy.wait_recv()
    for u in range(2):
        place_fc2(u, 1 - i_c, got[u].astype(F32))
    place_proj(1 - i_c, got_p[...].astype(F32))
    for copy in small:
        copy.wait_recv()
    out_vec[...] = sum_of(vec_c, 2)
    tab_all[i_dp] = sum_of(tab_c, 2)
    small = [link(tab_all.at[i_dp], tab_all.at[i_dp], {"dp": i_dp ^ bit}) for bit in range(1, dp)]
    for part in range(split):
        at = part_rows(part)
        for bit_g in range(1, ng):
            from_far[bit_g, part].wait_recv()
            arrived(i_g ^ bit_g, at, far[bit_g, at, :].astype(F32))
    for slot in range(3):
        value = None
        for g in range(ng):
            pltpu.make_async_copy(cells.at[0], taken.at[g, slot], cell_recv.at[g * 3 + slot]).wait()
            term = taken[g, slot].astype(F32)
            value = term if value is None else value + term
        quarter = shard // 4
        for i in range(4):
            rows_at = slice(i * quarter, (i + 1) * quarter)
            owned[rows_at, slot * cell : (slot + 1) * cell] = value[:, i * cell : (i + 1) * cell]
    for copy in small:
        copy.wait_recv()
    for j in range(dp):
        out_tab[j * tab_rows : (j + 1) * tab_rows, :] = tab_all[j]
    for n, owner in enumerate(sent_cells):

        @pl.when(owner != i_s)
        def _(n=n):
            pltpu.make_async_copy(cells.at[n], cells.at[n], cell_send.at[n]).wait()

    link.drain()


def finish(raw, normed, dx, tables, w, inputs, grad_mid, gain, early, proj_in, parts, sizes, part_w, split=3):
    count = inputs.shape[1]
    dp, ng, np_ = sizes
    chips = ng * np_
    pieces = len(dx)
    seq_len, width = raw.shape
    lanes = dx[0].shape[1]
    shard = width // dp
    cell = width // (chips * 2)
    total_cells = pieces * 3 * (part_w // cell)
    parts_a, parts_b = parts
    part_lanes = parts_a[0].shape[1]
    hidden_rows = parts_a[0].shape[0] - shard
    piece_rows = proj_in.shape[0]
    copies = chips + split * (ng * (np_ - 1) + ng - 1) + (chips - 1) + (dp - 1) * 4 + 2 * (chips - 1) + 5
    hbm = pl.BlockSpec(memory_space=pl.ANY)
    vmem = pl.BlockSpec(memory_space=pltpu.VMEM)
    table = tables[0].shape
    block = (table[0] // dp, table[1])
    return pl.pallas_call(
        partial(finish_kernel, sizes, split, pieces, part_w),
        in_specs=[hbm] * (2 + pieces) + [vmem] * (pieces + 6 + 2 * chips),
        out_specs=[vmem] * 7,
        out_shape=[
            jax.ShapeDtypeStruct((ng, count, width), BF),
            jax.ShapeDtypeStruct((shard, 3 * cell), F32),
            jax.ShapeDtypeStruct((16, shard), F32),
            jax.ShapeDtypeStruct(table, F32),
            jax.ShapeDtypeStruct((shard, 2 * part_lanes), F32),
            jax.ShapeDtypeStruct((4 * hidden_rows, part_lanes // 2), F32),
            jax.ShapeDtypeStruct((2 * piece_rows, part_lanes // 2), F32),
        ],
        scratch_shapes=[
            pltpu.VMEM((pieces, seq_len, lanes), BF),
            pltpu.VMEM((seq_len, width), BF),
            pltpu.VMEM((2, pieces, count, lanes), BF),
            pltpu.VMEM((2, count, width), BF),
            pltpu.VMEM((chips, count, width), BF),
            pltpu.VMEM((chips, count, width), BF),
            pltpu.VMEM((chips, count, width), BF),
            pltpu.VMEM((ng, np_, count, width), BF),
            pltpu.VMEM((ng, count, width), BF),
            pltpu.VMEM((dp, pieces, shard, lanes), BF),
            pltpu.VMEM((dp, pieces, shard, lanes), BF),
            pltpu.VMEM((total_cells, shard // 4, 4 * cell), BF),
            pltpu.VMEM((ng, 3, shard // 4, 4 * cell), BF),
            pltpu.VMEM((8, width), F32),
            pltpu.VMEM((8, lanes), F32),
            pltpu.VMEM((16, width), F32),
            pltpu.VMEM((dp, 16, shard), F32),
            pltpu.VMEM((dp, 16, shard), F32),
            pltpu.VMEM((chips, 16, shard), F32),
            pltpu.VMEM((2, 16, shard), F32),
            pltpu.VMEM(table, F32),
            pltpu.VMEM((dp,) + block, F32),
            pltpu.VMEM((chips,) + block, F32),
            pltpu.VMEM((2,) + block, F32),
            pltpu.VMEM((dp,) + block, F32),
            pltpu.VMEM((2, hidden_rows, part_lanes // 2), BF),
            pltpu.VMEM((2, hidden_rows, part_lanes // 2), BF),
            pltpu.VMEM((piece_rows, part_lanes // 2), BF),
            pltpu.VMEM((piece_rows, part_lanes // 2), BF),
            pltpu.VMEM((chips, piece_rows, part_lanes), BF),
            pltpu.VMEM((chips, piece_rows, part_lanes), BF),
            pltpu.SemaphoreType.DMA((2 * (1 + pieces) + 1 + pieces,)),
            pltpu.SemaphoreType.DMA((copies,)),
            pltpu.SemaphoreType.DMA((copies,)),
            pltpu.SemaphoreType.DMA((total_cells,)),
            pltpu.SemaphoreType.DMA((3 * ng,)),
        ],
        compiler_params=pltpu.CompilerParams(collective_id=1, has_side_effects=True, vmem_limit_bytes=63 << 20),
        cost_estimate=FREE,
        name="finish",
    )(raw, normed, *dx, *tables, w, inputs, grad_mid, gain, early, proj_in, *parts_a, *parts_b)


def split_kernel(chips, at, value, *outs):
    for z in range(chips):

        @pl.when(at[0] == z)
        def _(z=z):
            for n in range(chips):
                lanes = outs[n].shape[1]
                outs[n][...] = value[:, (z ^ n) * lanes : ((z ^ n) + 1) * lanes]


def split_columns(value, index, chips):
    rows, width = value.shape
    vmem = pl.BlockSpec(memory_space=pltpu.VMEM)
    return pl.pallas_call(
        partial(split_kernel, chips),
        in_specs=[pl.BlockSpec(memory_space=pltpu.SMEM), vmem],
        out_specs=[vmem] * chips,
        out_shape=[jax.ShapeDtypeStruct((rows, width // chips), value.dtype)] * chips,
        cost_estimate=FREE,
        name="split_columns",
    )(jnp.stack([index]), value)


def places():
    return tuple(lax.axis_index(name) for name in ("dp", "g", "p", "c"))


def proj_copy(w, held, sem):
    piece = held.shape[1]
    copy = pltpu.make_async_copy(w.at[:, pl.ds(4 * piece, piece)], held, sem)
    copy.start()
    return copy


def rows_of(w, p, np_):
    dp, piece, width = w.shape
    if dp >= np_:
        each = dp // np_
        return w[pl.ds(p * each, each)].reshape(each * piece, width)
    raise NotImplementedError


def middle_kernel(sizes, near, *refs):
    dp, ng, np_ = sizes
    far = refs[:np_]
    (w_all, patches, bias, gain, shift, mid, two_own, two_other, mixed,
     w, pieces, mine, away, came, sem, send, recv) = refs[np_:]
    i_dp, i_g, i_p, i_c = places()
    proj = proj_copy(w_all, w, sem.at[1])
    rows = patches.shape[1]
    core = {"c": 1 - i_c}
    meet([core] + [{"p": i_p ^ k} for k in range(1, np_)])
    link = Links(send, recv)
    here = pltpu.make_async_copy(near.at[i_p], pieces.at[0], sem.at[0])
    here.start()
    arrive = [link(near.at[i_p ^ k], pieces.at[k], {"p": i_p ^ k}) for k in range(1, np_)]

    def split(piece, p, image):
        for swap in range(2):

            @pl.when(i_c == swap)
            def _(swap=swap):
                for b in range(2):
                    mixed[p, b, image] = piece[(swap ^ b) * rows : ((swap ^ b) + 1) * rows, :]

    def product(b, image):
        total = None
        for p in range(np_):
            term = dot(mixed[p, b, image], rows_of(w, p, np_))
            total = term if total is None else total + term
        return total

    other = []
    proj.wait()
    for bit in (1, 0):
        image = i_g ^ bit
        if bit:
            for k in range(np_):
                split(far[k], i_p ^ k, image)
        else:
            here.wait()
            for copy in arrive:
                copy.wait_recv()
            for k in range(np_):
                split(pieces.at[k], i_p ^ k, image)
        away[image] = product(1, image)
        other.append(link(away.at[image], came.at[image], core))
        mine[image] = product(0, image)
    back = []
    for bit in (1, 0):
        image = i_g ^ bit
        other[1 - bit].wait_recv()
        value = patches[image].astype(F32) + mine[image] + came[image] + bias[...]
        mid[image] = value
        two_own[image] = (normal_rows(value) * gain[...] + shift[...]).astype(BF)
        back.append(link(two_own.at[image], two_other.at[image], core))
    for copy in back:
        copy.wait_recv()
    link.drain()


def middle_rows(near, far, w, patches, bias, gain, shift, sizes):
    dp, ng, np_ = sizes
    images, rows, width = patches.shape
    lanes = near.shape[2]
    vmem = pl.BlockSpec(memory_space=pltpu.VMEM)
    copies = np_ - 1 + 2 * images
    own = jax.ShapeDtypeStruct((images, rows, width), BF)
    return pl.pallas_call(
        partial(middle_kernel, sizes),
        in_specs=[pl.BlockSpec(memory_space=pl.ANY)] + [vmem] * len(far) + [pl.BlockSpec(memory_space=pl.ANY)] + [vmem] * 4,
        out_specs=[vmem] * 4,
        out_shape=[
            jax.ShapeDtypeStruct((images, rows, width), F32),
            own,
            own,
            jax.ShapeDtypeStruct((np_, 2, images, rows, lanes), BF),
        ],
        scratch_shapes=[
            pltpu.VMEM((dp, w.shape[1] // 5, width), BF),
            pltpu.VMEM((np_, 2 * rows, lanes), BF),
            pltpu.VMEM((images, rows, width), F32),
            pltpu.VMEM((images, rows, width), F32),
            pltpu.VMEM((images, rows, width), F32),
            pltpu.SemaphoreType.DMA((2,)),
            pltpu.SemaphoreType.DMA((copies,)),
            pltpu.SemaphoreType.DMA((copies,)),
        ],
        compiler_params=pltpu.CompilerParams(collective_id=2, has_side_effects=True, vmem_limit_bytes=48 << 20),
        cost_estimate=FREE,
        name="middle_rows",
    )(near, *far, w, patches, bias, gain, shift)


def norm_back(values, gain, upstream):
    center = values - jnp.mean(values, -1, keepdims=True)
    spread = jnp.mean(center * center, -1, keepdims=True)
    inverse = lax.rsqrt(spread + EPSILON)
    normal = center * inverse
    scaled = upstream * gain
    inner = jnp.mean(scaled * normal, -1, keepdims=True)
    return inverse * (scaled - jnp.mean(scaled, -1, keepdims=True) - normal * inner), normal


def turn_kernel(sizes, mid, gn, out, branch, gain, shift, w_all, mixed, output, grad_mid, heads, grad_proj, sums,
                w, back_own, back_other, gn_own, gn_came, out_own, out_came, stage, sem, send, recv):
    dp, ng, np_ = sizes
    i_dp, i_g, i_p, i_c = places()
    images, rows, width = mid.shape
    fold = rows // stage.shape[1]
    i_z = i_g * np_ + i_p
    core = {"c": 1 - i_c}
    peers = [core]
    for k in range(1, ng * np_):
        peers.append({"g": i_g ^ (k // np_), "p": i_p ^ (k % np_)})
    meet(peers)
    link = Links(send, recv)
    turns = [i_g ^ 1, i_g]
    proj = proj_copy(w_all, w, sem.at[2 * images + 2])

    def half(ref, b, image):
        start = (b * images + image) * rows
        return ref.at[pl.ds(pl.multiple_of(start, 8), rows)]

    loads = []
    crossed = []
    for n, image in enumerate(turns):
        crossed.append(link(half(gn, 1, image), gn_came.at[image], core))
        loads.append(pltpu.make_async_copy(half(gn, 0, image), gn_own.at[image], sem.at[n]))
        loads[-1].start()
    locals_ = []
    sums[...] = jnp.zeros_like(sums)

    def give(n, b):
        image = turns[n]
        source = (back_own if b == 0 else back_other)[image]
        for k in range(np_):
            slot = (n * np_ + k) * 2 + b
            value = dot(source, rows_of(w, i_p ^ k, np_), NT).astype(BF)
            lanes = value.shape[1]
            for s in range(fold):
                stage[slot, :, s * lanes : (s + 1) * lanes] = value[s * rows // fold : (s + 1) * rows // fold]
            dst = heads.at[i_z * 2 + (i_c ^ b)]
            if n == 1 and k == 0:
                locals_.append(pltpu.make_async_copy(stage.at[slot], dst, sem.at[2 * images + b]))
                locals_[-1].start()
            else:
                arrivals.append(link(stage.at[slot], dst, {"g": image, "p": i_p ^ k}))

    arrivals = []
    others = []
    for n, image in enumerate(turns):
        loads[n].wait()
        crossed[n].wait_recv()
        grad_two = gn_own[image] + gn_came[image]
        grad_out = branch[image].astype(F32)
        grad_norm, normal = norm_back(mid[image], gain[...], grad_two)
        grad = grad_out + grad_norm
        grad_mid[image] = grad
        back_own[image] = grad.astype(BF)
        others.append(link(back_own.at[image], back_other.at[image], core))
        sums[0:1, :] += jnp.sum(grad_two * normal, 0, keepdims=True)
        sums[1:2, :] += jnp.sum(grad_two, 0, keepdims=True)
        sums[2:3, :] += jnp.sum(back_own[image].astype(F32), 0, keepdims=True)
        sums[3:4, :] += jnp.sum(grad_out, 0, keepdims=True)
        if n == 0:
            proj.wait()
        give(n, 0)
    outs = []
    for n, image in enumerate(turns):
        others[n].wait_recv()
        give(n, 1)
        outs.append(link(half(out, 1, image), out_came.at[image], core))
        loads.append(pltpu.make_async_copy(half(out, 0, image), out_own.at[image], sem.at[images + n]))
        loads[-1].start()
    for p in range(np_):
        total = None
        for b, source in ((0, back_own), (1, back_other)):
            for image in range(images):
                term = dot(mixed[p, b, image], source[image], TN)
                total = term if total is None else total + term
        grad_proj[p] = total.astype(BF)
    for n, image in enumerate(turns):
        loads[images + n].wait()
        outs[n].wait_recv()
        value = mid[image] + out_own[image] + out_came[image] + shift[...]
        output[image] = value.astype(BF)
    for copy in locals_:
        copy.wait()
    for copy in arrivals:
        copy.wait_recv()
    link.drain()


def turn(mid, gn, out, branch, gain, shift, w, mixed, sizes):
    dp, ng, np_ = sizes
    images, rows, width = mid.shape
    lanes = mixed.shape[4]
    fold = 2 if rows % 32 == 0 else 1
    chips = ng * np_
    vmem = pl.BlockSpec(memory_space=pltpu.VMEM)
    hbm = pl.BlockSpec(memory_space=pl.ANY)
    copies = 3 * images + 2 * (chips - 1)
    own = (images, rows, width)
    return pl.pallas_call(
        partial(turn_kernel, sizes),
        in_specs=[vmem, hbm, hbm, vmem, vmem, vmem, hbm, vmem],
        out_specs=[vmem, vmem, hbm, vmem, vmem],
        out_shape=[
            jax.ShapeDtypeStruct(own, BF),
            jax.ShapeDtypeStruct(own, F32),
            jax.ShapeDtypeStruct((chips * 2, rows // fold, lanes * fold), BF),
            jax.ShapeDtypeStruct((np_, lanes, width), BF),
            jax.ShapeDtypeStruct((8, width), F32),
        ],
        scratch_shapes=[
            pltpu.VMEM((dp, w.shape[1] // 5, width), BF),
            pltpu.VMEM(own, BF),
            pltpu.VMEM(own, BF),
            pltpu.VMEM(own, F32),
            pltpu.VMEM(own, F32),
            pltpu.VMEM(own, F32),
            pltpu.VMEM(own, F32),
            pltpu.VMEM((chips * 2, rows // fold, lanes * fold), BF),
            pltpu.SemaphoreType.DMA((2 * images + 3,)),
            pltpu.SemaphoreType.DMA((copies,)),
            pltpu.SemaphoreType.DMA((copies,)),
        ],
        compiler_params=pltpu.CompilerParams(collective_id=3, has_side_effects=True, vmem_limit_bytes=56 << 20),
        cost_estimate=FREE,
        name="turn",
    )(mid, gn, out, branch, gain, shift, w, mixed)


def flip(value, axis, size, bit):
    return lax.ppermute(value, axis, [(i, i ^ bit) for i in range(size)])


def pick(value, index, axis=0):
    return lax.dynamic_index_in_dim(value, index, axis, keepdims=False)


def gather_pieces(value, axis, size, me):
    full = jnp.zeros((size,) + value.shape, value.dtype)
    full = lax.dynamic_update_index_in_dim(full, value, me, 0)
    for bit in range(1, size):
        full = lax.dynamic_update_index_in_dim(full, flip(value, axis, size, bit), me ^ bit, 0)
    return full


def scatter_sum(value, axis, size, me):
    total = pick(value, me).astype(F32)
    for bit in range(1, size):
        total = total + flip(pick(value, me ^ bit), axis, size, bit).astype(F32)
    return total


def tie(*values):
    return lax.optimization_barrier(values)


def after(value, *others):
    return tie(value, *others)[0]


def on_device(
    patches,
    ln1_gain,
    ln1_bias,
    qkv_weight,
    q_bias,
    v_bias,
    proj_weight,
    proj_bias,
    ln2_gain,
    ln2_bias,
    fc1_weight,
    fc1_bias,
    fc2_weight,
    fc2_bias,
    rel_pos_h,
    rel_pos_w,
    cotangent,
):
    images, row_count, width = patches.shape
    dp, ng, np_, nc = (lax.axis_size(name) for name in ("dp", "g", "p", "c"))
    i_dp, i_g, i_p, i_c = (lax.axis_index(name) for name in ("dp", "g", "p", "c"))
    chips = ng * np_
    i_z = i_g * np_ + i_p
    ranks = chips * nc
    seq_len = ranks * row_count
    own_rows = images * row_count
    heads = H * images // ranks
    shard_heads = H // dp
    core_heads = shard_heads // nc
    piece = core_heads * HD
    pieces = heads // core_heads
    lanes = heads * HD
    hidden = fc1_weight.shape[1]
    unit = hidden // ranks
    shard = width // dp
    per = hidden // dp // (nc * unit)
    side = (rel_pos_h.shape[0] + 1) // 2

    core_bias = pick(fc1_bias.reshape(per, nc, 2, unit // 2), i_c, 1).transpose(1, 0, 2)
    packed = jnp.concatenate(
        [
            jnp.stack([ln1_gain, ln1_bias, q_bias, v_bias, proj_bias, ln2_gain, ln2_bias, fc2_bias]),
            core_bias.reshape(-1, shard),
        ]
    )
    spot = jnp.stack([i_g, i_p, i_c])
    qkv_own, slab_a, slab_b = select(spot, qkv_weight, fc1_weight, fc2_weight, proj_weight, ng, np_, nc, lanes)
    weights_a = lax.all_gather(slab_a, "dp", axis=0)
    weights_b = lax.all_gather(slab_b, "dp", axis=0)
    raw, qkv_full, vectors = start_exchange(patches, qkv_own, packed, (dp, ng, np_))
    qkv_full = qkv_full.reshape(width, 3 * lanes)
    vectors = vectors.astype(F32)
    whole_vec = vectors.transpose(1, 0, 2).reshape(-1, width)
    gain_one, shift_one, q_shift, v_shift, proj_shift, gain_two, shift_two, fc2_shift = whole_vec[:8]
    fc1_shift = vectors[:, 8:].reshape(dp, 2, -1).transpose(1, 0, 2).reshape(2, 1, -1)

    starts = [
        part * width + (i_p * pieces + q) * shard_heads * HD + i_c * piece
        for q in range(pieces)
        for part in range(3)
    ]
    zero = jnp.zeros((piece,), F32)
    biases = []
    for q in range(pieces):
        at = starts[3 * q]
        biases += [lax.dynamic_slice_in_dim(q_shift, at, piece, 0), zero]
        biases += [lax.dynamic_slice_in_dim(v_shift, at, piece, 0)]
    qkv_shift = jnp.concatenate(biases)[None]

    branch_own = cotangent.reshape(own_rows, width)
    branch_other = flip(branch_own, "c", nc, 1)

    tables = flip_tables(rel_pos_h, rel_pos_w)
    back_tables = flip_tables(rel_pos_h, rel_pos_w[::-1])
    token = lax.broadcasted_iota(jnp.int32, (side, seq_len), 1)
    column = lax.broadcasted_iota(jnp.int32, (side, seq_len), 0)
    col_hot = (token % side == side - 1 - column).astype(BF)
    normed, query, key_rows, value_rows = qkv_rows(
        raw, gain_one[None], shift_one[None], qkv_full, qkv_shift, tables, pieces, core_heads, side
    )
    far_att, att_f, query_a = attend(i_g ^ 1, query, key_rows, value_rows, side, ng)
    far_att = far_att.reshape(np_, nc * row_count, lanes)
    arrived = {}
    for bit_p in range(np_):
        arrived[1, bit_p] = flip(pick(far_att, i_p ^ bit_p), ("g", "p"), chips, np_ + bit_p)
    near_att, att_f, query_a = attend(i_g, query, key_rows, value_rows, side, ng, (att_f, query_a))
    near_att, *pinned = tie(near_att, *[arrived[1, k] for k in range(np_)])
    for k in range(np_):
        arrived[1, k] = pinned[k]
    near_att = near_att.reshape(np_, nc * row_count, lanes)
    sizes = (dp, ng, np_)
    middle, two_own, two_other, mixed = middle_rows(
        near_att,
        [arrived[1, k] for k in range(np_)],
        weights_a,
        patches,
        proj_shift[None],
        gain_two[None],
        shift_two[None],
        sizes,
    )
    two_own, two_other = two_own.reshape(own_rows, width), two_other.reshape(own_rows, width)

    def over_dp(value):
        return lax.psum_scatter(value.reshape(-1, value.shape[-1]), "dp", scatter_dimension=0, tiled=True)

    out_a, back_a, grads_a, bias_a = mlp_half(
        two_own, two_other, branch_own, branch_other, weights_a, fc1_shift[0]
    )
    sum_a = over_dp(grads_a)
    out_b, back_b, grads_b, bias_b = mlp_half(
        two_own, two_other, branch_own, branch_other, weights_b, fc1_shift[1], (out_a, back_a)
    )
    output, grad_middle, grad_heads, grad_proj, early = turn(
        middle, back_b, out_b, cotangent, gain_two[None], fc2_shift[None], weights_a, mixed, sizes
    )
    sum_b = over_dp(grads_b)
    sum_p = over_dp(grad_proj.reshape(dp, piece, width))

    def pieces_over_chips(value):
        blocks = split_columns(value, i_z, chips)
        return [blocks[0]] + [flip(blocks[bit], ("g", "p"), chips, bit) for bit in range(1, chips)]

    grad_heads, sum_a = tie(grad_heads, sum_a)
    sum_a = pieces_over_chips(sum_a)
    dx = []
    grad_tables = []
    for q in range(pieces):
        rows, table = attend_back(
            q * core_heads, core_heads, query_a, key_rows, value_rows, att_f, grad_heads, back_tables, col_hot, side
        )
        if q == 0:
            rows, *sum_a = tie(rows, *sum_a)
            sum_b = pieces_over_chips(after(sum_b, rows))
            key_rows = after(key_rows, rows)
        elif q == 1:
            rows, *sum_b = tie(rows, *sum_b)
        dx.append(rows)
        grad_tables.append(table)
    dx[-1], sum_p = tie(dx[-1], sum_p)

    bias_half = jnp.stack([bias_a.reshape(dp, per, unit // 2), bias_b.reshape(dp, per, unit // 2)], 2)
    bias_half = bias_half.reshape(dp * per, 1, unit)
    bias_full = jnp.concatenate([bias_half] * nc, 1)
    core = lax.broadcasted_iota(jnp.int32, bias_full.shape, 1)
    bias_full = jnp.where(core == i_c, bias_full, 0.0).reshape(dp, -1, shard)
    early = jnp.concatenate([early[:4], bias_full.transpose(1, 0, 2).reshape(-1, width)])
    grad_patches, out_qkv, vec, rel, out_fc1, out_fc2, out_proj = finish(
        raw,
        normed,
        dx,
        grad_tables,
        qkv_full,
        patches,
        grad_middle,
        gain_one[None],
        early,
        sum_p,
        (sum_a, sum_b),
        sizes,
        piece,
    )
    entries = rel_pos_h.shape[0]
    rel = [rel[:entries, :HD][::-1], rel[128 : 128 + entries, :HD]]
    fc1_vec = vec[8:12].reshape(-1)

    return (
        output,
        grad_patches,
        vec[0],
        vec[1],
        out_qkv,
        vec[2],
        vec[3],
        out_proj,
        vec[6],
        vec[4],
        vec[5],
        out_fc1,
        fc1_vec,
        out_fc2,
        vec[7],
        rel[0],
        rel[1],
    )


def solution(mesh):
    dp, ranks = mesh.shape["dp"], mesh.shape["seq"]

    def call(*args):
        images = args[0].shape[0] // dp
        shape = (dp, images, ranks // images // 2, 2)
        fine = jax.sharding.Mesh(mesh.devices.reshape(shape), ("dp", "g", "p", "c"))
        seq = ("g", "p", "c")
        tokens, rows, both = P("dp", seq, None), P("dp", None), P("dp", seq)
        vec = P("dp")
        return jax.shard_map(
            on_device,
            mesh=fine,
            in_specs=(
                tokens, vec, vec, rows, vec, vec, rows, vec, vec, vec, rows, vec, rows, vec, P(), P(), tokens
            ),
            out_specs=(
                tokens, tokens, vec, vec, both, vec, vec, both, vec, vec, vec, both, vec, both, vec, P(), P()
            ),
            check_vma=False,
        )(*args)

    return call
```

```python
import math
from functools import partial

import jax
import jax.numpy as jnp
from jax import lax
from jax.experimental import pallas as pl
from jax.experimental.pallas import tpu as pltpu
from jax.sharding import PartitionSpec as P

H = 16
HD = 80
EPSILON = 1e-06
NT = (((1,), (1,)), ((), ()))
TN = (((0,), (0,)), ((), ()))
BF = jnp.bfloat16
F32 = jnp.float32
LOG2E = 1.4426950408889634
FACTOR = LOG2E / math.sqrt(HD)
FREE = pl.CostEstimate(flops=1, bytes_accessed=1, transcendentals=0)


def busy(gflops):
    return pl.CostEstimate(flops=gflops * 10**9, bytes_accessed=1, transcendentals=0)


def dot(a, b, dims=(((1,), (0,)), ((), ()))):
    return lax.dot_general(a, b, dims, preferred_element_type=F32)


def params(axes, mib=60):
    return pltpu.CompilerParams(
        dimension_semantics=("arbitrary",) * axes, vmem_limit_bytes=mib << 20
    )


def whole(*shape):
    return pl.BlockSpec(shape, lambda *at: (0,) * len(shape), pipeline_mode=pl.Buffered(1))


def flip_tables(rel_h, rel_w):
    entries = rel_h.shape[0]
    pad = ((0, 128 - entries), (0, 0))
    return jnp.concatenate([jnp.pad(rel_h[::-1], pad), jnp.pad(rel_w[::-1], pad)], 0)


def normal_rows(values):
    center = values - jnp.mean(values, -1, keepdims=True)
    spread = jnp.mean(center * center, -1, keepdims=True)
    return center * lax.rsqrt(spread + EPSILON)


def qkv_kernel(pieces, group_heads, side, sub, raw, gain, shift, w, bias, tables, normed, qa, kp, vp):
    count = raw.shape[0] // sub
    width = group_heads * HD
    lane = lax.broadcasted_iota(jnp.int32, (sub, 128), 1)
    group_lane = lax.broadcasted_iota(jnp.int32, (side, 128), 1)
    group_row = lax.broadcasted_iota(jnp.int32, (side, 128), 0)
    col_hot = (group_lane == group_row) | ((group_lane >= side) & (group_lane < side + 3))
    col_hot = jnp.where(col_hot, 1.0, 0.0).astype(BF)
    col_hot = jnp.concatenate([col_hot] * (sub // side), 0)

    def product(n):
        part = slice(n * sub, (n + 1) * sub)
        rows_n = (normal_rows(raw[part, :].astype(F32)) * gain[...] + shift[...]).astype(BF)
        normed[part, :] = rows_n
        return (dot(rows_n, w[...]) + bias[...]).astype(BF)

    ahead = product(0)
    for m in range(count):
        joined = ahead
        if m + 1 < count:
            ahead = product(m + 1)
        part = slice(m * sub, (m + 1) * sub)
        first_row = (pl.program_id(0) * count + m) * (sub // side)
        hot = []
        for i in range(sub // side):
            hot.append(jnp.where(group_lane == first_row + (HD + i), 1.0, 0.0).astype(BF))
        row_hot = jnp.concatenate(hot, 0)
        for n in range(pieces * group_heads):
            q_at = (n // group_heads) * 3 * width + (n % group_heads) * HD
            q = joined[:, q_at : q_at + HD]
            g = dot(q, tables[...], NT) * math.sqrt(HD)
            gh = []
            gw = []
            for i in range(sub // side):
                rows = g[i * side : (i + 1) * side]
                gh.append(pltpu.roll(rows[:, :128], first_row + (33 + i), axis=1))
                gw.append(pltpu.roll(rows[:, 128:], 81, axis=1, stride=1, stride_axis=0))
            qa[n, part, 0:128] = jnp.concatenate(gh, 0).astype(BF)
            qa[n, part, 0:HD] = q
            qa[n, part, 128:256] = jnp.where(lane < side, jnp.concatenate(gw, 0), 0.0).astype(BF)
            kp[n, part, 0:128] = row_hot
            kp[n, part, 128:256] = col_hot
            kp[n, part, 0:HD] = joined[:, q_at + width : q_at + width + HD]
            vp[n, part, :] = jnp.ones((sub, 128), BF)
            vp[n, part, 0:HD] = joined[:, q_at + 2 * width : q_at + 2 * width + HD]


def qkv_rows(raw, gain, shift, w, bias, tables, pieces, group_heads, side, rows=384, sub=192):
    seq_len, width = raw.shape
    lanes = w.shape[1]
    heads = pieces * group_heads
    return pl.pallas_call(
        partial(qkv_kernel, pieces, group_heads, side, sub),
        grid=(seq_len // rows,),
        in_specs=[
            pl.BlockSpec((rows, width), lambda i: (i, 0)),
            whole(1, width),
            whole(1, width),
            whole(width, lanes),
            whole(1, lanes),
            whole(256, HD),
        ],
        out_specs=[
            pl.BlockSpec((rows, width), lambda i: (i, 0)),
            pl.BlockSpec((heads, rows, 256), lambda i: (0, i, 0)),
            pl.BlockSpec((heads, rows, 256), lambda i: (0, i, 0)),
            pl.BlockSpec((heads, rows, 128), lambda i: (0, i, 0)),
        ],
        out_shape=[
            jax.ShapeDtypeStruct((seq_len, width), BF),
            jax.ShapeDtypeStruct((heads, seq_len, 256), BF),
            jax.ShapeDtypeStruct((heads, seq_len, 256), BF),
            jax.ShapeDtypeStruct((heads, seq_len, 128), BF),
        ],
        compiler_params=params(1),
        cost_estimate=FREE,
        name="qkv_rows",
    )(raw, gain, shift, w, bias, tables)


def attend_kernel(heads, side, aliased, sub, at, qa, kp, vp, *refs):
    o, of, qo = refs[2:] if aliased else refs
    rows = qa.shape[1]
    h = pl.program_id(0)
    base = pl.multiple_of(pl.program_id(1) * rows, rows)
    lane = lax.broadcasted_iota(jnp.int32, (sub, 128), 1)
    count = rows // sub
    scores = [dot(qa[0, 0:sub, :], kp[0], NT)]
    outs = []
    for n in range(count):
        part = slice(n * sub, (n + 1) * sub)
        if n + 1 < count:
            scores.append(dot(qa[0, (n + 1) * sub : (n + 2) * sub, :], kp[0], NT))
        s = scores[n]
        m = jnp.max(s, -1, keepdims=True)
        p = jnp.exp2(s * FACTOR - m * FACTOR).astype(BF)
        out = dot(p, vp[0])
        total = out[:, HD : HD + 1]
        out = out / total
        norm = m + jnp.log2(total) / FACTOR
        hi = norm.astype(BF).astype(F32)
        mid = (norm - hi).astype(BF).astype(F32)
        low = norm - hi - mid
        old = qa[0, part, 128:256].astype(F32)
        old = jnp.where(lane == side, -hi, old)
        old = jnp.where(lane == side + 1, -mid, old)
        old = jnp.where(lane == side + 2, -low, old)
        qo[0, part, 0:128] = qa[0, part, 0:128]
        qo[0, part, 128:256] = old.astype(BF)
        outs.append(out)
    out = jnp.concatenate(outs, 0)
    part = pl.ds(base, rows)
    for n in range(heads):

        @pl.when(h == n)
        def _(n=n):
            o[part, n * HD : (n + 1) * HD] = out[:, 0:HD].astype(BF)
            of[part, n * HD : (n + 1) * HD] = out[:, 0:HD]


def attend(group, qa, kp, vp, side, groups, old=(), tq=1152, sub=576):
    heads, seq_len, _ = qa.shape
    rows = seq_len // groups
    steps = rows // tq
    lanes = heads * HD
    query = pl.BlockSpec((1, tq, 256), lambda h, i, at: (h, at[0] * steps + i, 0))
    return pl.pallas_call(
        partial(attend_kernel, heads, side, bool(old), sub),
        grid_spec=pltpu.PrefetchScalarGridSpec(
            num_scalar_prefetch=1,
            grid=(heads, steps),
            in_specs=[
                query,
                pl.BlockSpec((1, seq_len, 256), lambda h, i, at: (h, 0, 0)),
                pl.BlockSpec((1, seq_len, 128), lambda h, i, at: (h, 0, 0)),
            ]
            + [pl.BlockSpec(memory_space=pl.ANY)] * len(old),
            out_specs=[
                pl.BlockSpec((rows, lanes), lambda h, i, at: (0, 0)),
                pl.BlockSpec((rows, lanes), lambda h, i, at: (at[0], 0)),
                query,
            ],
        ),
        out_shape=[
            jax.ShapeDtypeStruct((rows, lanes), BF),
            jax.ShapeDtypeStruct((seq_len, lanes), F32),
            jax.ShapeDtypeStruct((heads, seq_len, 256), BF),
        ],
        input_output_aliases={4: 1, 5: 2} if old else {},
        compiler_params=params(2),
        cost_estimate=busy(20),
        name="attend",
    )(jnp.stack([group]), qa, kp, vp, *old)


def attend_back_kernel(heads, first, side, uc, qa_ref, kp, vp, of, go, tables, hot, dx, gt, kt, dop, dk, dv, dq):
    seq_len = kp.shape[1]
    tb = qa_ref.shape[1]
    h = pl.program_id(0)
    step = pl.program_id(1)
    last = pl.num_programs(1) - 1
    scale = HD ** (-0.5)
    rows = seq_len // 9

    @pl.when((h == 0) & (step == 0))
    def _():
        gt[...] = jnp.zeros_like(gt)

        blocks, high, wide = go.shape
        total_lanes = of.shape[1]
        fold = wide // total_lanes
        if fold == 1:
            high = rows

        def prep(i, c):
            lane = lax.broadcasted_iota(jnp.int32, (high, 128), 1)
            for s in range(fold):
                part = pl.ds(pl.multiple_of((i * fold + s) * high, high), high)
                for n in range(heads):
                    at = (first + n) * HD
                    if fold == 1:
                        rows_go = flat_go[part, at : at + HD]
                    else:
                        rows_go = go[i, :, s * total_lanes + at : s * total_lanes + at + HD]
                    inner = jnp.sum(rows_go.astype(F32) * of[part, at : at + HD], -1, keepdims=True)
                    hi = inner.astype(BF).astype(F32)
                    tail = jnp.where(lane == HD, -hi, jnp.where(lane == HD + 1, hi - inner, 0.0))
                    dop[n, part, :] = tail.astype(BF)
                    dop[n, part, 0:HD] = rows_go
            return c

        flat_go = go.at[0]
        lax.fori_loop(0, seq_len // (fold * high), prep, 0, unroll=2)

    @pl.when(step == 0)
    def _():
        def prep(i, c):
            part = pl.ds(pl.multiple_of(i * rows, rows), rows)
            kt[0:128, part] = kp[0, part, 0:128].T
            kt[128 : 128 + side, part] = hot[:, part]
            dk[part, :] = jnp.zeros((rows, 128), F32)
            dv[part, :] = jnp.zeros((rows, 128), F32)
            return c

        lax.fori_loop(0, 9, prep, 0)

    base = pl.ds(pl.multiple_of(step * tb, tb), tb)
    qa = qa_ref[0]
    do = dop[h, base, :]

    def scores(j):
        part = slice(j * uc, (j + 1) * uc)
        return dot(kp[0, part, :], qa, NT), dot(vp[0, part, :], do, NT)

    acc = None
    count = seq_len // uc
    ahead = scores(0)
    for j in range(count):
        s, dp = ahead
        if j + 1 < count:
            ahead = scores(j + 1)
        part = slice(j * uc, (j + 1) * uc)
        p = jnp.exp2(s * FACTOR)
        ds = (p * dp).astype(BF)
        dv[part, :] += dot(p.astype(BF), do)
        dk[part, :] += dot(ds, qa[:, 0:128])
        term = dot(kt[:, part], ds)
        acc = term if acc is None else acc + term
    acc = jnp.concatenate([acc, jnp.zeros((256 - HD - 2 * side, tb), F32)], 0).T
    lane = lax.broadcasted_iota(jnp.int32, (tb, 128), 1)
    groups = tb // side
    rel_h = jnp.where(lane < HD, 0.0, acc[:, :128])
    rel_w = jnp.where(lane < side, acc[:, 128:], 0.0)
    back_h = []
    back_w = []
    for i in range(groups):
        part = slice(i * side, (i + 1) * side)
        back_h.append(pltpu.roll(rel_h[part], 256 - 33 - step * groups - i, axis=1))
        back_w.append(pltpu.roll(rel_w[part], 0, axis=1, stride=1, stride_axis=0))
    both = jnp.concatenate([jnp.concatenate(back_h, 0), jnp.concatenate(back_w, 0)], 1).astype(BF)
    dq[base, :] = acc[:, :HD] * scale + dot(both, tables[...])
    gt[...] += dot(both, qa[:, 0:128], TN)

    width = heads * HD
    for n in range(heads):

        @pl.when((h == n) & (step == last))
        def _(n=n):
            def post(i, c):
                part = pl.ds(pl.multiple_of(i * rows, rows), rows)
                at = n * HD
                dx[part, at : at + HD] = dq[part, :].astype(BF)
                dx[part, width + at : width + at + HD] = (dk[part, 0:HD] * scale).astype(BF)
                dx[part, 2 * width + at : 2 * width + at + HD] = dv[part, 0:HD].astype(BF)
                return c

            lax.fori_loop(0, 9, post, 0)


def attend_back(first, count, qa, kp, vp, of, go, tables, hot, side, tb=768, uc=256):
    heads, seq_len, _ = qa.shape
    lanes = heads * HD
    if go.shape[2] == lanes:
        go = go.reshape(1, seq_len, lanes)
    return pl.pallas_call(
        partial(attend_back_kernel, count, first, side, uc),
        grid=(count, seq_len // tb),
        in_specs=[
            pl.BlockSpec((1, tb, 256), lambda h, i: (first + h, i, 0)),
            pl.BlockSpec((1, seq_len, 256), lambda h, i: (first + h, 0, 0)),
            pl.BlockSpec((1, seq_len, 128), lambda h, i: (first + h, 0, 0)),
            whole(seq_len, lanes),
            whole(*go.shape),
            whole(256, HD),
            whole(side, seq_len),
        ],
        out_specs=[whole(seq_len, 3 * count * HD), whole(256, 128)],
        out_shape=[
            jax.ShapeDtypeStruct((seq_len, 3 * count * HD), BF),
            jax.ShapeDtypeStruct((256, 128), F32),
        ],
        scratch_shapes=[
            pltpu.VMEM((HD + 2 * side, seq_len), BF),
            pltpu.VMEM((count, seq_len, 128), BF),
            pltpu.VMEM((seq_len, 128), F32),
            pltpu.VMEM((seq_len, 128), F32),
            pltpu.VMEM((seq_len, HD), F32),
        ],
        compiler_params=params(2),
        cost_estimate=busy(50),
        name="attend_back",
    )(qa, kp, vp, of, go, tables, hot)


def mlp_kernel(aliased, per, n_own, n_other, g_own, g_other, w1, b1, w2, *refs):
    if aliased:
        out_in, gn_in, out, gn, grads, gb1, n2, gb, act, gbef = refs
    else:
        out, gn, grads, gb1, n2, gb, act, gbef = refs
    step = pl.program_id(0)
    chunk = out.shape[0]
    shards, shard, hidden = w1.shape
    width = n_own.shape[1]
    steps = 2 * per

    @pl.when(step == 0)
    def _():
        gb1[...] = jnp.zeros_like(gb1)

    @pl.when(step < steps)
    def _():
        first = w1[...].reshape(width, hidden)
        second = w2[...].reshape(hidden, width)
        dst = pl.ds(pl.multiple_of(step * chunk, chunk), chunk)
        mine = step < per
        n2[dst, :] = jnp.where(mine, n_own[...], n_other[...])
        gb[dst, :] = jnp.where(mine, g_own[...], g_other[...])
        before = dot(n2[dst, :], first) + b1[...]
        grad_act = dot(gb[dst, :], second, NT)
        cdf = 0.5 + 0.5 * lax.erf(before * math.sqrt(0.5))
        act[dst, :] = (before * cdf).astype(BF)
        slope = cdf + before * (jnp.exp(-0.5 * before * before) * (1.0 / math.sqrt(2.0 * math.pi)))
        grad_before = slope * grad_act
        gbef[dst, :] = grad_before.astype(BF)
        gb1[...] += jnp.sum(gbef[dst, :].astype(F32), 0, keepdims=True)
        value = dot(act[dst, :], second)
        back = dot(gbef[dst, :], first, NT)
        if aliased:
            value = value + out_in[...]
            back = back + gn_in[...]
        out[...] = value
        gn[...] = back

    for j in range(shards):

        @pl.when(step == steps + j)
        def _(j=j):
            rows = slice(j * shard, (j + 1) * shard)
            grads[0, 0:shard, :] = dot(n2[:, rows], gbef[...], TN).astype(BF)
            grads[0, shard : 2 * shard, :] = dot(act[:, rows], gb[...], TN).astype(BF)


def mlp_half(n_own, n_other, g_own, g_other, weights, b1, old=(), chunk=288):
    half, width = n_own.shape
    dp = weights.shape[0]
    shard = width // dp
    hidden = width
    chunk = min(chunk, half)
    per = half // chunk
    steps = 2 * per
    tile = pl.BlockSpec((chunk, width), lambda i: (jnp.minimum(i, steps - 1), 0))
    own = pl.BlockSpec((chunk, width), lambda i: (jnp.minimum(i, per - 1), 0))
    other = pl.BlockSpec((chunk, width), lambda i: (jnp.clip(i - per, 0, per - 1), 0))
    rows = jax.ShapeDtypeStruct((2 * half, width), F32)
    return pl.pallas_call(
        partial(mlp_kernel, bool(old), per),
        grid=(steps + dp,),
        in_specs=[own, other, own, other]
        + [
            pl.BlockSpec((dp, shard, width), lambda i: (0, 0, 0), pipeline_mode=pl.Buffered(1)),
            whole(1, hidden),
            pl.BlockSpec((dp, shard, width), lambda i: (0, 1, 0), pipeline_mode=pl.Buffered(1)),
        ]
        + [tile] * len(old),
        out_specs=[
            tile,
            tile,
            pl.BlockSpec((1, 2 * shard, width), lambda i: (jnp.maximum(i - steps, 0), 0, 0)),
            whole(1, hidden),
        ],
        out_shape=[
            rows,
            rows,
            jax.ShapeDtypeStruct((dp, 2 * shard, width), BF),
            jax.ShapeDtypeStruct((1, hidden), F32),
        ],
        input_output_aliases={7: 0, 8: 1} if old else {},
        scratch_shapes=[pltpu.VMEM((2 * half, width), BF)] * 4,
        compiler_params=params(1, 63),
        cost_estimate=busy(35),
        name="mlp_half",
    )(n_own, n_other, g_own, g_other, weights, b1, weights, *old)


def select_kernel(ng, np_, nc, at, qkv_in, fc1_in, fc2_in, proj_in, own, *refs):
    slabs = refs[:2]
    qkv, fc1, fc2, proj, sem = refs[2:]
    loads = []
    for n, (src, dst) in enumerate(((qkv_in, qkv), (proj_in, proj), (fc1_in, fc1), (fc2_in, fc2))):
        loads.append(pltpu.make_async_copy(src, dst, sem.at[n]))
        loads[-1].start()
    i_p, i_c = at[1], at[2]
    shard = fc1.shape[0]
    width = proj.shape[1]
    hidden = fc1.shape[1]
    chips = ng * np_
    unit = hidden // (chips * nc)
    part = unit // 2
    piece = proj.shape[0] // nc
    shard_lanes = proj.shape[0]
    lanes = own.shape[1] // 3
    pieces = lanes // piece
    per = fc2.shape[0] // (nc * unit)
    loads[0].wait()
    for c in range(nc):
        for p in range(np_):

            @pl.when((i_c == c) & (i_p == p))
            def _(c=c, p=p):
                for q in range(pieces):
                    for t in range(3):
                        src = t * width + (p * pieces + q) * shard_lanes + c * piece
                        dst = (3 * q + t) * piece
                        own[:, dst : dst + piece] = qkv[:, src : src + piece]

    for copy in loads[1:]:
        copy.wait()
    for c in range(nc):

        @pl.when(i_c == c)
        def _(c=c):
            for u in range(2):
                for z in range(chips):
                    src = (z * nc + c) * unit + u * part
                    slabs[u][0:shard, z * part : (z + 1) * part] = fc1[:, src : src + part]
                for b in range(per):
                    src = (b * nc + c) * unit + u * part
                    dst = shard + b * part
                    slabs[u][dst : dst + part, :] = fc2[src : src + part, :]
            slabs[0][2 * shard : 2 * shard + piece, :] = proj[c * piece : (c + 1) * piece, :]


def select(at, qkv, fc1, fc2, proj, ng, np_, nc, lanes):
    shard, width = proj.shape[0], proj.shape[1]
    return pl.pallas_call(
        partial(select_kernel, ng, np_, nc),
        in_specs=[pl.BlockSpec(memory_space=pltpu.SMEM)] + [pl.BlockSpec(memory_space=pltpu.HBM)] * 4,
        out_specs=[pl.BlockSpec(memory_space=pltpu.VMEM)] * 3,
        scratch_shapes=[pltpu.VMEM(value.shape, BF) for value in (qkv, fc1, fc2, proj)]
        + [pltpu.SemaphoreType.DMA((4,))],
        out_shape=[
            jax.ShapeDtypeStruct((shard, 3 * lanes), BF),
            jax.ShapeDtypeStruct((2 * shard + shard // nc, width), BF),
            jax.ShapeDtypeStruct((2 * shard, width), BF),
        ],
        compiler_params=pltpu.CompilerParams(vmem_limit_bytes=63 << 20),
        cost_estimate=FREE,
        name="select",
    )(at, qkv, fc1, fc2, proj)


def start_kernel(sizes, split, patches, own, vec, rows, full, vecs, local, send, recv):
    dp, ng, np_ = sizes
    i_dp, i_g, i_p, i_c = (lax.axis_index(name) for name in ("dp", "g", "p", "c"))
    count = patches.shape[1]
    step = count // split

    barrier = pltpu.get_barrier_semaphore()
    peers = [{"dp": i_dp ^ k} for k in range(1, dp)]
    peers += [{"g": i_g ^ k} for k in range(1, ng)]
    peers += [{"p": i_p ^ k} for k in range(1, np_)]
    peers += [{"c": 1 - i_c}]
    for peer in peers:
        pl.semaphore_signal(barrier, inc=1, device_id=peer, device_id_type=pl.DeviceIdType.MESH)
    pl.semaphore_wait(barrier, len(peers))

    used = []

    def remote(src, dst, peer):
        n = len(used)
        copy = pltpu.make_async_remote_copy(
            src_ref=src,
            dst_ref=dst,
            send_sem=send.at[n],
            recv_sem=recv.at[n],
            device_id=peer,
            device_id_type=pl.DeviceIdType.MESH,
        )
        used.append(copy)
        return copy

    def place(g, p, c, part):
        start = ((g * np_ + p) * 2 + c) * count + part * step
        return rows.at[pl.ds(pl.multiple_of(start, 8), step)]

    mine = [patches.at[i_g, pl.ds(part * step, step)] for part in range(split)]
    home = [pltpu.make_async_copy(mine[part], place(i_g, i_p, i_c, part), local.at[part]) for part in range(split)]
    home.append(pltpu.make_async_copy(own, full.at[i_dp], local.at[split]))
    home.append(pltpu.make_async_copy(vec, vecs.at[i_dp], local.at[split + 1]))

    far = {}
    for part in range(split):
        for bit in range(1, ng):
            src = patches.at[i_g ^ bit, pl.ds(part * step, step)]
            far[bit, part] = remote(src, place(i_g, i_p, i_c, part), {"g": i_g ^ bit})
            far[bit, part].start()
    over_dp = []
    for bit in range(1, dp):
        over_dp.append(remote(vec, vecs.at[i_dp], {"dp": i_dp ^ bit}))
        over_dp.append(remote(own, full.at[i_dp], {"dp": i_dp ^ bit}))
    for copy in over_dp:
        copy.start()
    near = {}
    for bit in range(1, np_):
        for part in range(split):
            near[bit, part] = remote(mine[part], place(i_g, i_p, i_c, part), {"p": i_p ^ bit})
            near[bit, part].start()
    cores = []
    for part in range(split):
        cores.append(remote(mine[part], place(i_g, i_p, i_c, part), {"c": 1 - i_c}))
        cores[-1].start()
    for copy in home:
        copy.start()

    onward = {}
    for part in range(split):
        for bit in range(1, ng):
            far[bit, part].wait_recv()
            came = place(i_g ^ bit, i_p, i_c, part)
            for bit_p in range(1, np_):
                onward[bit, bit_p, part] = remote(came, came, {"p": i_p ^ bit_p})
                onward[bit, bit_p, part].start()
            cores.append(remote(came, came, {"c": 1 - i_c}))
            cores[-1].start()
        for bit in range(1, np_):
            near[bit, part].wait_recv()
            came = place(i_g, i_p ^ bit, i_c, part)
            cores.append(remote(came, came, {"c": 1 - i_c}))
            cores[-1].start()
    for (bit, bit_p, part), copy in onward.items():
        copy.wait_recv()
        came = place(i_g ^ bit, i_p ^ bit_p, i_c, part)
        cores.append(remote(came, came, {"c": 1 - i_c}))
        cores[-1].start()
    for copy in over_dp + cores:
        copy.wait_recv()
    for copy in used:
        copy.wait_send()
    for copy in home:
        copy.wait()


def start_exchange(patches, own, vec, sizes):
    dp, ng, np_ = sizes
    images, count, width = patches.shape
    split = 6 if count % 48 == 0 else 3
    chunk_copies = ng * np_ + (ng - 1) + (np_ - 1) + (ng - 1) * (np_ - 1)
    copies = 2 * (dp - 1) + split * chunk_copies
    hbm = pl.BlockSpec(memory_space=pl.ANY)
    return pl.pallas_call(
        partial(start_kernel, sizes, split),
        in_specs=[hbm] * 3,
        out_specs=[hbm] * 3,
        out_shape=[
            jax.ShapeDtypeStruct((ng * np_ * 2 * count, width), BF),
            jax.ShapeDtypeStruct((dp,) + own.shape, BF),
            jax.ShapeDtypeStruct((dp,) + vec.shape, BF),
        ],
        scratch_shapes=[
            pltpu.SemaphoreType.DMA((split + 2,)),
            pltpu.SemaphoreType.DMA((copies,)),
            pltpu.SemaphoreType.DMA((copies,)),
        ],
        compiler_params=pltpu.CompilerParams(collective_id=0, has_side_effects=True),
        cost_estimate=FREE,
        name="start_exchange",
    )(patches, own, vec)


class Links:
    def __init__(self, send, recv):
        self.send, self.recv, self.copies = send, recv, []

    def __call__(self, src, dst, peer):
        n = len(self.copies)
        copy = pltpu.make_async_remote_copy(
            src_ref=src,
            dst_ref=dst,
            send_sem=self.send.at[n],
            recv_sem=self.recv.at[n],
            device_id=peer,
            device_id_type=pl.DeviceIdType.MESH,
        )
        copy.start()
        self.copies.append(copy)
        return copy

    def drain(self):
        for copy in self.copies:
            copy.wait_send()


def meet(peers):
    barrier = pltpu.get_barrier_semaphore()
    for peer in peers:
        pl.semaphore_signal(barrier, inc=1, device_id=peer, device_id_type=pl.DeviceIdType.MESH)
    pl.semaphore_wait(barrier, len(peers))


def finish_kernel(sizes, split, pieces, part_w, *refs):
    dp, ng, np_ = sizes
    chips = ng * np_
    ranks = chips * 2
    raw, normed = refs[:2]
    dx = refs[2 : 2 + pieces]
    tables = refs[2 + pieces : 2 + 2 * pieces]
    refs = refs[2 + 2 * pieces :]
    w_in, inputs_in, grad_mid_in, gain, early, proj_in = refs[:6]
    parts_in = refs[6 : 6 + 2 * chips]
    (home, owned, out_vec, out_tab, out_fc1, out_fc2, out_proj,
     dx_all, norm_all, dx_ring, raw_ring, keep, away, came, pair, far, slab_out, slabs, cells, taken,
     sums, lane_sums, vec, vec_out, vec_dp, vec_z, vec_c, tab, tab_dp, tab_z, tab_c, tab_all,
     give, got, give_p, got_p, proj_out, proj_got, w, inputs, grad_mid, parts, late, sem, send, recv, cell_send, cell_recv,
     ) = refs[6 + 2 * chips :]
    w_load = pltpu.make_async_copy(w_in, w, late.at[0])
    w_load.start()
    late_loads = [pltpu.make_async_copy(inputs_in, inputs, late.at[1])]
    late_loads.append(pltpu.make_async_copy(grad_mid_in, grad_mid, late.at[2]))
    for n, ref in enumerate(parts_in):
        late_loads.append(pltpu.make_async_copy(ref, parts.at[n], late.at[3 + n]))
    i_dp, i_g, i_p, i_c = places()
    i_z = i_g * np_ + i_p
    i_s = i_z * 2 + i_c
    count, width = keep.shape[1], keep.shape[2]
    step = count // split
    shard = owned.shape[0]
    cell = owned.shape[1] // 3
    lanes = dx_all.shape[2]
    core = {"c": 1 - i_c}
    chip_peer = lambda k: {"g": i_g ^ (k // np_), "p": i_p ^ (k % np_)}
    peers = [{"dp": i_dp ^ k} for k in range(1, dp)]
    for k in range(1, ranks):
        peers.append({"g": i_g ^ (k // (np_ * 2)), "p": i_p ^ ((k // 2) % np_), "c": i_c ^ (k % 2)})
    meet(peers)
    link = Links(send, recv)

    z_of = lambda k: (i_g ^ (k // np_)) * np_ + (i_p ^ (k % np_))
    part_rows = lambda part: pl.ds(part * step, step)
    far_slots, near_slots = list(range(np_, chips)), list(range(np_))
    jobs = [(k, b) for group in (far_slots, near_slots) for b in (1, 0) for k in group]
    loads = {}

    def load(n):
        if n < len(jobs):
            k, b = jobs[n]
            start = (z_of(k) * 2 + (i_c ^ b)) * count
            at = pl.ds(pl.multiple_of(start, 8), count)
            slot = n % 2
            loads[n] = [pltpu.make_async_copy(raw.at[at], raw_ring.at[slot], sem.at[slot * (1 + pieces)])]
            for q in range(pieces):
                loads[n].append(
                    pltpu.make_async_copy(dx[q].at[at], dx_ring.at[slot, q], sem.at[slot * (1 + pieces) + 1 + q])
                )
            for copy in loads[n]:
                copy.start()

    load(0)
    load(1)
    whole_loads = [pltpu.make_async_copy(normed, norm_all, sem.at[2 * (1 + pieces)])]
    for q in range(pieces):
        whole_loads.append(pltpu.make_async_copy(dx[q], dx_all.at[q], sem.at[2 * (1 + pieces) + 1 + q]))
    for copy in whole_loads:
        copy.start()
    for copy in late_loads:
        copy.start()
    sums[...] = jnp.zeros_like(sums)
    lane_sums[...] = jnp.zeros_like(lane_sums)
    from_core = {}

    def rows(n):
        k, b = jobs[n]
        slot = n % 2
        for copy in loads[n]:
            copy.wait()
        normal = normal_rows(raw_ring[slot].astype(F32))
        total = None
        for q in range(pieces):
            value = dx_ring[slot, q]
            term = dot(value, w[:, q * lanes : (q + 1) * lanes], NT)
            total = term if total is None else total + term
            lane_sums[q : q + 1, :] += jnp.sum(value.astype(F32), 0, keepdims=True)
        sums[0:1, :] += jnp.sum(total * normal, 0, keepdims=True)
        sums[1:2, :] += jnp.sum(total, 0, keepdims=True)
        if b:
            away[k] = total.astype(BF)
            from_core[k] = link(away.at[k], came.at[k], core)
        else:
            keep[k] = total.astype(BF)
        load(n + 2)

    from_pair = {}

    def over_cores(slots):
        for k in slots:
            from_core[k].wait_recv()
            for part in range(split):
                at = part_rows(part)
                keep[k, at, :] = (keep[k, at, :].astype(F32) + came[k, at, :].astype(F32)).astype(BF)
                if k % np_:
                    dst = pair.at[k // np_, k % np_, at]
                    from_pair[k // np_, k % np_, part] = link(keep.at[k, at], dst, {"p": i_p ^ (k % np_)})

    def over_pair(bit_g, part):
        at = part_rows(part)
        value = keep[bit_g * np_, at, :].astype(F32)
        for bit_p in range(1, np_):
            from_pair[bit_g, bit_p, part].wait_recv()
            value = value + pair[bit_g, bit_p, at, :].astype(F32)
        return value

    half = len(far_slots) * 2
    w_load.wait()
    for n in range(half):
        rows(n)

    part_lanes = parts.shape[2]
    for z in range(chips):
        proj_out[z] = proj_in[:, z * part_lanes : (z + 1) * part_lanes]
    from_chip = [link(proj_out.at[z_of(k)], proj_got.at[k], chip_peer(k)) for k in range(1, chips)]
    over_cores(far_slots)

    for copy in whole_loads:
        copy.wait()
    for j in range(dp):
        for q in range(pieces):
            slab_out[j, q] = dot(norm_all[:, j * shard : (j + 1) * shard], dx_all[q], TN).astype(BF)
    from_dp = [link(slab_out.at[i_dp ^ bit], slabs.at[bit], {"dp": i_dp ^ bit}) for bit in range(1, dp)]

    from_far = {}
    for part in range(split):
        at = part_rows(part)
        for bit_g in range(1, ng):
            pair[bit_g, 0, at, :] = over_pair(bit_g, part).astype(BF)
            from_far[bit_g, part] = link(pair.at[bit_g, 0, at], far.at[bit_g, at], {"g": i_g ^ bit_g})
    for n in range(half, len(jobs)):
        rows(n)

    vec[...] = jnp.zeros_like(vec)
    vec[0:2, :] = sums[0:2, :]
    vec[4:12, :] = early[...]
    for p in range(np_):
        for c in range(2):

            @pl.when((i_p == p) & (i_c == c))
            def _(p=p, c=c):
                for q in range(pieces):
                    at = (p * pieces + q) * shard + c * part_w
                    vec[2:3, at : at + part_w] = lane_sums[q : q + 1, 0:part_w]
                    vec[3:4, at : at + part_w] = lane_sums[q : q + 1, 2 * part_w : 3 * part_w]

    table = tables[0][...]
    for ref in tables[1:]:
        table = table + ref[...]
    tab[...] = table
    tab_rows = tab.shape[0] // dp
    tab_at = lambda j: pl.ds(pl.multiple_of(j * tab_rows, 8), tab_rows)
    for j in range(dp):
        vec_out[j] = vec[:, j * shard : (j + 1) * shard]
    vec_dp[i_dp] = vec_out[i_dp]
    tab_dp[i_dp] = tab[tab_at(i_dp), :]
    small = []
    for bit in range(1, dp):
        small.append(link(vec_out.at[i_dp ^ bit], vec_dp.at[i_dp], {"dp": i_dp ^ bit}))
        small.append(link(tab.at[tab_at(i_dp ^ bit)], tab_dp.at[i_dp], {"dp": i_dp ^ bit}))

    def sum_of(ref, n):
        value = ref[0]
        for i in range(1, n):
            value = value + ref[i]
        return value

    over_cores(near_slots)
    for copy in small:
        copy.wait_recv()
    vec_z[i_z] = sum_of(vec_dp, dp)
    tab_z[i_z] = sum_of(tab_dp, dp)
    small = []
    for k in range(1, chips):
        small.append(link(vec_z.at[i_z], vec_z.at[i_z], chip_peer(k)))
        small.append(link(tab_z.at[i_z], tab_z.at[i_z], chip_peer(k)))

    hidden_rows = give.shape[1]
    per_rows = part_lanes
    swaps = []

    def halves(value, there):
        cols = value.shape[1] // 2
        mine = jnp.where(i_c == 0, value[:, :cols], value[:, cols:])
        there[...] = jnp.where(i_c == 0, value[:, cols:], value[:, :cols]).astype(BF)
        return mine

    def place_fc2(u, flip_core, value):
        value = value.T
        for c in range(2):

            @pl.when((i_c ^ flip_core) == c)
            def _(c=c):
                for b in range(hidden_rows // per_rows):
                    start = ((b * 2 + c) * 2 + u) * per_rows
                    out_fc2[:, start : start + per_rows] = value[:, b * per_rows : (b + 1) * per_rows]

    def place_proj(flip_core, value):
        value = value.T
        n = value.shape[1]
        for c in range(2):

            @pl.when((i_c ^ flip_core) == c)
            def _(c=c):
                out_proj[:, c * n : (c + 1) * n] = value

    for copy in late_loads:
        copy.wait()
    for u in range(2):
        value = parts[u * chips].astype(F32)
        for n in range(1, chips):
            value = value + parts[u * chips + n].astype(F32)
        out_fc1[:, u * per_rows : (u + 1) * per_rows] = value[0:shard]
        place_fc2(u, 0, halves(value[shard:], give.at[u]))
        swaps.append(link(give.at[u], got.at[u], core))
    value = proj_out[i_z].astype(F32)
    for k in range(1, chips):
        from_chip[k - 1].wait_recv()
        value = value + proj_got[k].astype(F32)
    place_proj(0, halves(value, give_p))
    swaps.append(link(give_p, got_p, core))

    for copy in from_dp:
        copy.wait_recv()
    sent_cells = []
    for q in range(pieces):
        value = slab_out[i_dp, q].astype(F32)
        for bit in range(1, dp):
            value = value + slabs[bit, q].astype(F32)
        value = value.astype(BF)
        for t in range(3):
            for u in range(part_w // cell):
                n = len(sent_cells)
                lane = t * part_w + u * cell
                quarter = shard // 4
                for i in range(4):
                    cells[n, :, i * cell : (i + 1) * cell] = value[i * quarter : (i + 1) * quarter, lane : lane + cell]
                unit = (t * width + (i_p * pieces + q) * shard + i_c * part_w) // cell + u
                owner = unit // 3
                slot = unit % 3
                dst = taken.at[i_g, slot]
                o_c = owner % 2
                o_p = (owner // 2) % np_
                o_g = owner // (2 * np_)

                @pl.when(owner == i_s)
                def _(n=n, dst=dst, slot=slot):
                    pltpu.make_async_copy(cells.at[n], dst, cell_recv.at[i_g * 3 + slot]).start()

                @pl.when(owner != i_s)
                def _(n=n, dst=dst, slot=slot, o_g=o_g, o_p=o_p, o_c=o_c):
                    pltpu.make_async_remote_copy(
                        src_ref=cells.at[n],
                        dst_ref=dst,
                        send_sem=cell_send.at[n],
                        recv_sem=cell_recv.at[i_g * 3 + slot],
                        device_id={"g": o_g, "p": o_p, "c": o_c},
                        device_id_type=pl.DeviceIdType.MESH,
                    ).start()

                sent_cells.append(owner)

    def arrived(image, at, value):
        grad, _ = norm_back(inputs[image, at, :].astype(F32), gain[...], value)
        home[image, at, :] = (grad_mid[image, at, :] + grad).astype(BF)

    for part in range(split):
        arrived(i_g, part_rows(part), over_pair(0, part))
    for copy in small:
        copy.wait_recv()
    vec_c[i_c] = sum_of(vec_z, chips)
    tab_c[i_c] = sum_of(tab_z, chips)
    small = [link(vec_c.at[i_c], vec_c.at[i_c], core), link(tab_c.at[i_c], tab_c.at[i_c], core)]
    for copy in swaps:
        copy.wait_recv()
    for u in range(2):
        place_fc2(u, 1, got[u].astype(F32))
    place_proj(1, got_p[...].astype(F32))
    for copy in small:
        copy.wait_recv()
    out_vec[...] = sum_of(vec_c, 2)
    tab_all[i_dp] = sum_of(tab_c, 2)
    small = [link(tab_all.at[i_dp], tab_all.at[i_dp], {"dp": i_dp ^ bit}) for bit in range(1, dp)]
    for part in range(split):
        at = part_rows(part)
        for bit_g in range(1, ng):
            from_far[bit_g, part].wait_recv()
            arrived(i_g ^ bit_g, at, far[bit_g, at, :].astype(F32))
    for slot in range(3):
        value = None
        for g in range(ng):
            pltpu.make_async_copy(cells.at[0], taken.at[g, slot], cell_recv.at[g * 3 + slot]).wait()
            term = taken[g, slot].astype(F32)
            value = term if value is None else value + term
        quarter = shard // 4
        for i in range(4):
            rows_at = slice(i * quarter, (i + 1) * quarter)
            owned[rows_at, slot * cell : (slot + 1) * cell] = value[:, i * cell : (i + 1) * cell]
    for copy in small:
        copy.wait_recv()
    for j in range(dp):
        out_tab[j * tab_rows : (j + 1) * tab_rows, :] = tab_all[j]
    for n, owner in enumerate(sent_cells):

        @pl.when(owner != i_s)
        def _(n=n):
            pltpu.make_async_copy(cells.at[n], cells.at[n], cell_send.at[n]).wait()

    link.drain()


def finish(raw, normed, dx, tables, w, inputs, grad_mid, gain, early, proj_in, parts, sizes, part_w, split=3):
    count = inputs.shape[1]
    dp, ng, np_ = sizes
    chips = ng * np_
    pieces = len(dx)
    seq_len, width = raw.shape
    lanes = dx[0].shape[1]
    shard = width // dp
    cell = width // (chips * 2)
    total_cells = pieces * 3 * (part_w // cell)
    parts_a, parts_b = parts
    part_lanes = parts_a[0].shape[1]
    hidden_rows = parts_a[0].shape[0] - shard
    piece_rows = proj_in.shape[0]
    copies = chips + split * (ng * (np_ - 1) + ng - 1) + (chips - 1) + (dp - 1) * 4 + 2 * (chips - 1) + 5
    hbm = pl.BlockSpec(memory_space=pltpu.HBM)
    vmem = pl.BlockSpec(memory_space=pltpu.VMEM)
    table = tables[0].shape
    block = (table[0] // dp, table[1])
    return pl.pallas_call(
        partial(finish_kernel, sizes, split, pieces, part_w),
        in_specs=[hbm] * (2 + pieces) + [vmem] * pieces + [hbm] * 3 + [vmem] * 3 + [hbm] * (2 * chips),
        out_specs=[vmem] * 7,
        out_shape=[
            jax.ShapeDtypeStruct((ng, count, width), BF),
            jax.ShapeDtypeStruct((shard, 3 * cell), F32),
            jax.ShapeDtypeStruct((16, shard), F32),
            jax.ShapeDtypeStruct(table, F32),
            jax.ShapeDtypeStruct((shard, 2 * part_lanes), F32),
            jax.ShapeDtypeStruct((part_lanes // 2, 4 * hidden_rows), F32),
            jax.ShapeDtypeStruct((part_lanes // 2, 2 * piece_rows), F32),
        ],
        scratch_shapes=[
            pltpu.VMEM((pieces, seq_len, lanes), BF),
            pltpu.VMEM((seq_len, width), BF),
            pltpu.VMEM((2, pieces, count, lanes), BF),
            pltpu.VMEM((2, count, width), BF),
            pltpu.VMEM((chips, count, width), BF),
            pltpu.VMEM((chips, count, width), BF),
            pltpu.VMEM((chips, count, width), BF),
            pltpu.VMEM((ng, np_, count, width), BF),
            pltpu.VMEM((ng, count, width), BF),
            pltpu.VMEM((dp, pieces, shard, lanes), BF),
            pltpu.VMEM((dp, pieces, shard, lanes), BF),
            pltpu.VMEM((total_cells, shard // 4, 4 * cell), BF),
            pltpu.VMEM((ng, 3, shard // 4, 4 * cell), BF),
            pltpu.VMEM((8, width), F32),
            pltpu.VMEM((8, lanes), F32),
            pltpu.VMEM((16, width), F32),
            pltpu.VMEM((dp, 16, shard), F32),
            pltpu.VMEM((dp, 16, shard), F32),
            pltpu.VMEM((chips, 16, shard), F32),
            pltpu.VMEM((2, 16, shard), F32),
            pltpu.VMEM(table, F32),
            pltpu.VMEM((dp,) + block, F32),
            pltpu.VMEM((chips,) + block, F32),
            pltpu.VMEM((2,) + block, F32),
            pltpu.VMEM((dp,) + block, F32),
            pltpu.VMEM((2, hidden_rows, part_lanes // 2), BF),
            pltpu.VMEM((2, hidden_rows, part_lanes // 2), BF),
            pltpu.VMEM((piece_rows, part_lanes // 2), BF),
            pltpu.VMEM((piece_rows, part_lanes // 2), BF),
            pltpu.VMEM((chips, piece_rows, part_lanes), BF),
            pltpu.VMEM((chips, piece_rows, part_lanes), BF),
            pltpu.VMEM(w.shape, BF),
            pltpu.VMEM((ng, count, width), BF),
            pltpu.VMEM((ng, count, width), F32),
            pltpu.VMEM((2 * chips,) + parts_a[0].shape, BF),
            pltpu.SemaphoreType.DMA((3 + 2 * chips,)),
            pltpu.SemaphoreType.DMA((2 * (1 + pieces) + 1 + pieces,)),
            pltpu.SemaphoreType.DMA((copies,)),
            pltpu.SemaphoreType.DMA((copies,)),
            pltpu.SemaphoreType.DMA((total_cells,)),
            pltpu.SemaphoreType.DMA((3 * ng,)),
        ],
        compiler_params=pltpu.CompilerParams(collective_id=1, has_side_effects=True, vmem_limit_bytes=63 << 20),
        cost_estimate=FREE,
        name="finish",
    )(raw, normed, *dx, *tables, w, inputs, grad_mid, gain, early, proj_in, *parts_a, *parts_b)


def split_kernel(chips, at, value, *outs):
    for z in range(chips):

        @pl.when(at[0] == z)
        def _(z=z):
            for n in range(chips):
                lanes = outs[n].shape[1]
                outs[n][...] = value[:, (z ^ n) * lanes : ((z ^ n) + 1) * lanes]


def split_columns(value, index, chips):
    rows, width = value.shape
    vmem = pl.BlockSpec(memory_space=pltpu.VMEM)
    return pl.pallas_call(
        partial(split_kernel, chips),
        in_specs=[pl.BlockSpec(memory_space=pltpu.SMEM), vmem],
        out_specs=[vmem] * chips,
        out_shape=[jax.ShapeDtypeStruct((rows, width // chips), value.dtype)] * chips,
        cost_estimate=FREE,
        name="split_columns",
    )(jnp.stack([index]), value)


def places():
    return tuple(lax.axis_index(name) for name in ("dp", "g", "p", "c"))


def proj_copy(w, held, sem):
    piece = held.shape[1]
    copy = pltpu.make_async_copy(w.at[:, pl.ds(4 * piece, piece)], held, sem)
    copy.start()
    return copy


def rows_of(w, p, np_):
    dp, piece, width = w.shape
    if dp >= np_:
        each = dp // np_
        return w[pl.ds(p * each, each)].reshape(each * piece, width)
    raise NotImplementedError


def middle_kernel(sizes, near, *refs):
    dp, ng, np_ = sizes
    far = refs[:np_]
    (w_all, patches, bias, gain, shift, mid, two_own, two_other, mixed,
     w, pieces, mine, away, came, sem, send, recv) = refs[np_:]
    i_dp, i_g, i_p, i_c = places()
    proj = proj_copy(w_all, w, sem.at[1])
    rows = patches.shape[1]
    core = {"c": 1 - i_c}
    meet([core] + [{"p": i_p ^ k} for k in range(1, np_)])
    link = Links(send, recv)
    here = pltpu.make_async_copy(near.at[i_p], pieces.at[0], sem.at[0])
    here.start()
    arrive = [link(near.at[i_p ^ k], pieces.at[k], {"p": i_p ^ k}) for k in range(1, np_)]

    def split(piece, p, image):
        for swap in range(2):

            @pl.when(i_c == swap)
            def _(swap=swap):
                for b in range(2):
                    mixed[p, b, image] = piece[(swap ^ b) * rows : ((swap ^ b) + 1) * rows, :]

    def product(b, image):
        total = None
        for p in range(np_):
            term = dot(mixed[p, b, image], rows_of(w, p, np_))
            total = term if total is None else total + term
        return total

    other = []
    proj.wait()
    for bit in (1, 0):
        image = i_g ^ bit
        if bit:
            for k in range(np_):
                split(far[k], i_p ^ k, image)
        else:
            here.wait()
            for copy in arrive:
                copy.wait_recv()
            for k in range(np_):
                split(pieces.at[k], i_p ^ k, image)
        away[image] = product(1, image)
        other.append(link(away.at[image], came.at[image], core))
        mine[image] = product(0, image)
    back = []
    for bit in (1, 0):
        image = i_g ^ bit
        other[1 - bit].wait_recv()
        value = patches[image].astype(F32) + mine[image] + came[image] + bias[...]
        mid[image] = value
        two_own[image] = (normal_rows(value) * gain[...] + shift[...]).astype(BF)
        back.append(link(two_own.at[image], two_other.at[image], core))
    for copy in back:
        copy.wait_recv()
    link.drain()


def middle_rows(near, far, w, patches, bias, gain, shift, sizes):
    dp, ng, np_ = sizes
    images, rows, width = patches.shape
    lanes = near.shape[2]
    vmem = pl.BlockSpec(memory_space=pltpu.VMEM)
    copies = np_ - 1 + 2 * images
    own = jax.ShapeDtypeStruct((images, rows, width), BF)
    return pl.pallas_call(
        partial(middle_kernel, sizes),
        in_specs=[pl.BlockSpec(memory_space=pl.ANY)] + [vmem] * len(far) + [pl.BlockSpec(memory_space=pl.ANY)] + [vmem] * 4,
        out_specs=[vmem] * 4,
        out_shape=[
            jax.ShapeDtypeStruct((images, rows, width), F32),
            own,
            own,
            jax.ShapeDtypeStruct((np_, 2, images, rows, lanes), BF),
        ],
        scratch_shapes=[
            pltpu.VMEM((dp, w.shape[1] // 5, width), BF),
            pltpu.VMEM((np_, 2 * rows, lanes), BF),
            pltpu.VMEM((images, rows, width), F32),
            pltpu.VMEM((images, rows, width), F32),
            pltpu.VMEM((images, rows, width), F32),
            pltpu.SemaphoreType.DMA((2,)),
            pltpu.SemaphoreType.DMA((copies,)),
            pltpu.SemaphoreType.DMA((copies,)),
        ],
        compiler_params=pltpu.CompilerParams(collective_id=2, has_side_effects=True, vmem_limit_bytes=48 << 20),
        cost_estimate=FREE,
        name="middle_rows",
    )(near, *far, w, patches, bias, gain, shift)


def norm_back(values, gain, upstream):
    center = values - jnp.mean(values, -1, keepdims=True)
    spread = jnp.mean(center * center, -1, keepdims=True)
    inverse = lax.rsqrt(spread + EPSILON)
    normal = center * inverse
    scaled = upstream * gain
    inner = jnp.mean(scaled * normal, -1, keepdims=True)
    return inverse * (scaled - jnp.mean(scaled, -1, keepdims=True) - normal * inner), normal


def turn_kernel(sizes, mid, gn, out, branch, gain, shift, w_all, mixed, output, grad_mid, heads, grad_proj, sums,
                w, back_own, back_other, gn_own, gn_came, out_own, out_came, stage, sem, send, recv):
    dp, ng, np_ = sizes
    i_dp, i_g, i_p, i_c = places()
    images, rows, width = mid.shape
    fold = rows // stage.shape[1]
    i_z = i_g * np_ + i_p
    core = {"c": 1 - i_c}
    peers = [core]
    for k in range(1, ng * np_):
        peers.append({"g": i_g ^ (k // np_), "p": i_p ^ (k % np_)})
    meet(peers)
    link = Links(send, recv)
    turns = [i_g ^ 1, i_g]
    proj = proj_copy(w_all, w, sem.at[2 * images + 2])

    def half(ref, b, image):
        start = (b * images + image) * rows
        return ref.at[pl.ds(pl.multiple_of(start, 8), rows)]

    loads = []
    crossed = []
    for n, image in enumerate(turns):
        crossed.append(link(half(gn, 1, image), gn_came.at[image], core))
        loads.append(pltpu.make_async_copy(half(gn, 0, image), gn_own.at[image], sem.at[n]))
        loads[-1].start()
    locals_ = []
    sums[...] = jnp.zeros_like(sums)

    def give(n, b):
        image = turns[n]
        source = (back_own if b == 0 else back_other)[image]
        for k in range(np_):
            slot = (n * np_ + k) * 2 + b
            value = dot(source, rows_of(w, i_p ^ k, np_), NT).astype(BF)
            lanes = value.shape[1]
            for s in range(fold):
                stage[slot, :, s * lanes : (s + 1) * lanes] = value[s * rows // fold : (s + 1) * rows // fold]
            dst = heads.at[i_z * 2 + (i_c ^ b)]
            if n == 1 and k == 0:
                locals_.append(pltpu.make_async_copy(stage.at[slot], dst, sem.at[2 * images + b]))
                locals_[-1].start()
            else:
                arrivals.append(link(stage.at[slot], dst, {"g": image, "p": i_p ^ k}))

    arrivals = []
    others = []
    for n, image in enumerate(turns):
        loads[n].wait()
        crossed[n].wait_recv()
        grad_two = gn_own[image] + gn_came[image]
        grad_out = branch[image].astype(F32)
        grad_norm, normal = norm_back(mid[image], gain[...], grad_two)
        grad = grad_out + grad_norm
        grad_mid[image] = grad
        back_own[image] = grad.astype(BF)
        others.append(link(back_own.at[image], back_other.at[image], core))
        sums[0:1, :] += jnp.sum(grad_two * normal, 0, keepdims=True)
        sums[1:2, :] += jnp.sum(grad_two, 0, keepdims=True)
        sums[2:3, :] += jnp.sum(back_own[image].astype(F32), 0, keepdims=True)
        sums[3:4, :] += jnp.sum(grad_out, 0, keepdims=True)
        if n == 0:
            proj.wait()
        give(n, 0)
    outs = []
    for n, image in enumerate(turns):
        others[n].wait_recv()
        give(n, 1)
        outs.append(link(half(out, 1, image), out_came.at[image], core))
        loads.append(pltpu.make_async_copy(half(out, 0, image), out_own.at[image], sem.at[images + n]))
        loads[-1].start()
    for p in range(np_):
        total = None
        for b, source in ((0, back_own), (1, back_other)):
            for image in range(images):
                term = dot(mixed[p, b, image], source[image], TN)
                total = term if total is None else total + term
        grad_proj[p] = total.astype(BF)
    for n, image in enumerate(turns):
        loads[images + n].wait()
        outs[n].wait_recv()
        value = mid[image] + out_own[image] + out_came[image] + shift[...]
        output[image] = value.astype(BF)
    for copy in locals_:
        copy.wait()
    for copy in arrivals:
        copy.wait_recv()
    link.drain()


def turn(mid, gn, out, branch, gain, shift, w, mixed, sizes):
    dp, ng, np_ = sizes
    images, rows, width = mid.shape
    lanes = mixed.shape[4]
    fold = 2 if rows % 32 == 0 else 1
    chips = ng * np_
    vmem = pl.BlockSpec(memory_space=pltpu.VMEM)
    hbm = pl.BlockSpec(memory_space=pl.ANY)
    copies = 3 * images + 2 * (chips - 1)
    own = (images, rows, width)
    return pl.pallas_call(
        partial(turn_kernel, sizes),
        in_specs=[vmem, hbm, hbm, vmem, vmem, vmem, hbm, vmem],
        out_specs=[vmem, vmem, hbm, vmem, vmem],
        out_shape=[
            jax.ShapeDtypeStruct(own, BF),
            jax.ShapeDtypeStruct(own, F32),
            jax.ShapeDtypeStruct((chips * 2, rows // fold, lanes * fold), BF),
            jax.ShapeDtypeStruct((np_, lanes, width), BF),
            jax.ShapeDtypeStruct((8, width), F32),
        ],
        scratch_shapes=[
            pltpu.VMEM((dp, w.shape[1] // 5, width), BF),
            pltpu.VMEM(own, BF),
            pltpu.VMEM(own, BF),
            pltpu.VMEM(own, F32),
            pltpu.VMEM(own, F32),
            pltpu.VMEM(own, F32),
            pltpu.VMEM(own, F32),
            pltpu.VMEM((chips * 2, rows // fold, lanes * fold), BF),
            pltpu.SemaphoreType.DMA((2 * images + 3,)),
            pltpu.SemaphoreType.DMA((copies,)),
            pltpu.SemaphoreType.DMA((copies,)),
        ],
        compiler_params=pltpu.CompilerParams(collective_id=3, has_side_effects=True, vmem_limit_bytes=56 << 20),
        cost_estimate=FREE,
        name="turn",
    )(mid, gn, out, branch, gain, shift, w, mixed)


def flip(value, axis, size, bit):
    return lax.ppermute(value, axis, [(i, i ^ bit) for i in range(size)])


def pick(value, index, axis=0):
    return lax.dynamic_index_in_dim(value, index, axis, keepdims=False)


def gather_pieces(value, axis, size, me):
    full = jnp.zeros((size,) + value.shape, value.dtype)
    full = lax.dynamic_update_index_in_dim(full, value, me, 0)
    for bit in range(1, size):
        full = lax.dynamic_update_index_in_dim(full, flip(value, axis, size, bit), me ^ bit, 0)
    return full


def scatter_sum(value, axis, size, me):
    total = pick(value, me).astype(F32)
    for bit in range(1, size):
        total = total + flip(pick(value, me ^ bit), axis, size, bit).astype(F32)
    return total


def tie(*values):
    return lax.optimization_barrier(values)


def after(value, *others):
    return tie(value, *others)[0]


def on_device(
    patches,
    ln1_gain,
    ln1_bias,
    qkv_weight,
    q_bias,
    v_bias,
    proj_weight,
    proj_bias,
    ln2_gain,
    ln2_bias,
    fc1_weight,
    fc1_bias,
    fc2_weight,
    fc2_bias,
    rel_pos_h,
    rel_pos_w,
    cotangent,
):
    images, row_count, width = patches.shape
    dp, ng, np_, nc = (lax.axis_size(name) for name in ("dp", "g", "p", "c"))
    i_dp, i_g, i_p, i_c = (lax.axis_index(name) for name in ("dp", "g", "p", "c"))
    chips = ng * np_
    i_z = i_g * np_ + i_p
    ranks = chips * nc
    seq_len = ranks * row_count
    own_rows = images * row_count
    heads = H * images // ranks
    shard_heads = H // dp
    core_heads = shard_heads // nc
    piece = core_heads * HD
    pieces = heads // core_heads
    lanes = heads * HD
    hidden = fc1_weight.shape[1]
    unit = hidden // ranks
    shard = width // dp
    per = hidden // dp // (nc * unit)
    side = (rel_pos_h.shape[0] + 1) // 2

    core_bias = pick(fc1_bias.reshape(per, nc, 2, unit // 2), i_c, 1).transpose(1, 0, 2)
    packed = jnp.concatenate(
        [
            jnp.stack([ln1_gain, ln1_bias, q_bias, v_bias, proj_bias, ln2_gain, ln2_bias, fc2_bias]),
            core_bias.reshape(-1, shard),
        ]
    )
    spot = jnp.stack([i_g, i_p, i_c])
    qkv_own, slab_a, slab_b = select(spot, qkv_weight, fc1_weight, fc2_weight, proj_weight, ng, np_, nc, lanes)
    weights_a = lax.all_gather(slab_a, "dp", axis=0)
    weights_b = lax.all_gather(slab_b, "dp", axis=0)
    raw, qkv_full, vectors = start_exchange(patches, qkv_own, packed, (dp, ng, np_))
    qkv_full = qkv_full.reshape(width, 3 * lanes)
    vectors = vectors.astype(F32)
    whole_vec = vectors.transpose(1, 0, 2).reshape(-1, width)
    gain_one, shift_one, q_shift, v_shift, proj_shift, gain_two, shift_two, fc2_shift = whole_vec[:8]
    fc1_shift = vectors[:, 8:].reshape(dp, 2, -1).transpose(1, 0, 2).reshape(2, 1, -1)

    starts = [
        part * width + (i_p * pieces + q) * shard_heads * HD + i_c * piece
        for q in range(pieces)
        for part in range(3)
    ]
    zero = jnp.zeros((piece,), F32)
    biases = []
    for q in range(pieces):
        at = starts[3 * q]
        biases += [lax.dynamic_slice_in_dim(q_shift, at, piece, 0), zero]
        biases += [lax.dynamic_slice_in_dim(v_shift, at, piece, 0)]
    qkv_shift = jnp.concatenate(biases)[None]

    branch_own = cotangent.reshape(own_rows, width)
    branch_other = flip(branch_own, "c", nc, 1)

    tables = flip_tables(rel_pos_h, rel_pos_w)
    back_tables = flip_tables(rel_pos_h, rel_pos_w[::-1])
    token = lax.broadcasted_iota(jnp.int32, (side, seq_len), 1)
    column = lax.broadcasted_iota(jnp.int32, (side, seq_len), 0)
    col_hot = (token % side == side - 1 - column).astype(BF)
    normed, query, key_rows, value_rows = qkv_rows(
        raw, gain_one[None], shift_one[None], qkv_full, qkv_shift, tables, pieces, core_heads, side
    )
    far_att, att_f, query_a = attend(i_g ^ 1, query, key_rows, value_rows, side, ng)
    far_att = far_att.reshape(np_, nc * row_count, lanes)
    arrived = {}
    for bit_p in range(np_):
        arrived[1, bit_p] = flip(pick(far_att, i_p ^ bit_p), ("g", "p"), chips, np_ + bit_p)
    near_att, att_f, query_a = attend(i_g, query, key_rows, value_rows, side, ng, (att_f, query_a))
    near_att, *pinned = tie(near_att, *[arrived[1, k] for k in range(np_)])
    for k in range(np_):
        arrived[1, k] = pinned[k]
    near_att = near_att.reshape(np_, nc * row_count, lanes)
    sizes = (dp, ng, np_)
    middle, two_own, two_other, mixed = middle_rows(
        near_att,
        [arrived[1, k] for k in range(np_)],
        weights_a,
        patches,
        proj_shift[None],
        gain_two[None],
        shift_two[None],
        sizes,
    )
    two_own, two_other = two_own.reshape(own_rows, width), two_other.reshape(own_rows, width)

    def over_dp(value):
        return lax.psum_scatter(value.reshape(-1, value.shape[-1]), "dp", scatter_dimension=0, tiled=True)

    out_a, back_a, grads_a, bias_a = mlp_half(
        two_own, two_other, branch_own, branch_other, weights_a, fc1_shift[0]
    )
    sum_a = over_dp(grads_a)
    out_b, back_b, grads_b, bias_b = mlp_half(
        two_own, two_other, branch_own, branch_other, weights_b, fc1_shift[1], (out_a, back_a)
    )
    output, grad_middle, grad_heads, grad_proj, early = turn(
        middle, back_b, out_b, cotangent, gain_two[None], fc2_shift[None], weights_a, mixed, sizes
    )
    sum_b = over_dp(grads_b)
    sum_p = over_dp(grad_proj.reshape(dp, piece, width))

    def pieces_over_chips(value):
        blocks = split_columns(value, i_z, chips)
        return [blocks[0]] + [flip(blocks[bit], ("g", "p"), chips, bit) for bit in range(1, chips)]

    grad_heads, sum_a = tie(grad_heads, sum_a)
    sum_a = pieces_over_chips(sum_a)
    dx = []
    grad_tables = []
    for q in range(pieces):
        rows, table = attend_back(
            q * core_heads, core_heads, query_a, key_rows, value_rows, att_f, grad_heads, back_tables, col_hot, side
        )
        if q == 0:
            rows, *sum_a = tie(rows, *sum_a)
            sum_b = pieces_over_chips(after(sum_b, rows))
            key_rows = after(key_rows, rows)
        elif q == 1:
            rows, *sum_b = tie(rows, *sum_b)
        dx.append(rows)
        grad_tables.append(table)
    dx[-1], sum_p = tie(dx[-1], sum_p)

    bias_half = jnp.stack([bias_a.reshape(dp, per, unit // 2), bias_b.reshape(dp, per, unit // 2)], 2)
    bias_half = bias_half.reshape(dp * per, 1, unit)
    bias_full = jnp.concatenate([bias_half] * nc, 1)
    core = lax.broadcasted_iota(jnp.int32, bias_full.shape, 1)
    bias_full = jnp.where(core == i_c, bias_full, 0.0).reshape(dp, -1, shard)
    early = jnp.concatenate([early[:4], bias_full.transpose(1, 0, 2).reshape(-1, width)])
    grad_patches, out_qkv, vec, rel, out_fc1, out_fc2, out_proj = finish(
        raw,
        normed,
        dx,
        grad_tables,
        qkv_full,
        patches,
        grad_middle,
        gain_one[None],
        early,
        sum_p,
        (sum_a, sum_b),
        sizes,
        piece,
    )
    entries = rel_pos_h.shape[0]
    rel = [rel[:entries, :HD][::-1], rel[128 : 128 + entries, :HD]]
    fc1_vec = vec[8:12].reshape(-1)
    out_fc2, out_proj = out_fc2.T, out_proj.T

    return (
        output,
        grad_patches,
        vec[0],
        vec[1],
        out_qkv,
        vec[2],
        vec[3],
        out_proj,
        vec[6],
        vec[4],
        vec[5],
        out_fc1,
        fc1_vec,
        out_fc2,
        vec[7],
        rel[0],
        rel[1],
    )


def solution(mesh):
    dp, ranks = mesh.shape["dp"], mesh.shape["seq"]

    def call(*args):
        images = args[0].shape[0] // dp
        shape = (dp, images, ranks // images // 2, 2)
        fine = jax.sharding.Mesh(mesh.devices.reshape(shape), ("dp", "g", "p", "c"))
        seq = ("g", "p", "c")
        tokens, rows, both = P("dp", seq, None), P("dp", None), P("dp", seq)
        vec = P("dp")
        return jax.shard_map(
            on_device,
            mesh=fine,
            in_specs=(
                tokens, vec, vec, rows, vec, vec, rows, vec, vec, vec, rows, vec, rows, vec, P(), P(), tokens
            ),
            out_specs=(
                tokens, tokens, vec, vec, both, vec, vec, both, vec, vec, vec, both, vec, both, vec, P(), P()
            ),
            check_vma=False,
        )(*args)

    return call
```

```python
import math
from functools import partial

import jax
import jax.numpy as jnp
from jax import lax
from jax.experimental import pallas as pl
from jax.experimental.pallas import tpu as pltpu
from jax.sharding import PartitionSpec as P

H = 16
HD = 80
EPSILON = 1e-06
NT = (((1,), (1,)), ((), ()))
TN = (((0,), (0,)), ((), ()))
BF = jnp.bfloat16
F32 = jnp.float32
LOG2E = 1.4426950408889634
FACTOR = LOG2E / math.sqrt(HD)
FREE = pl.CostEstimate(flops=1, bytes_accessed=1, transcendentals=0)


def busy(gflops):
    return pl.CostEstimate(flops=gflops * 10**9, bytes_accessed=1, transcendentals=0)


def dot(a, b, dims=(((1,), (0,)), ((), ()))):
    return lax.dot_general(a, b, dims, preferred_element_type=F32)


def params(axes, mib=60):
    return pltpu.CompilerParams(
        dimension_semantics=("arbitrary",) * axes, vmem_limit_bytes=mib << 20
    )


def whole(*shape):
    return pl.BlockSpec(shape, lambda *at: (0,) * len(shape), pipeline_mode=pl.Buffered(1))


def flip_tables(rel_h, rel_w):
    entries = rel_h.shape[0]
    pad = ((0, 128 - entries), (0, 0))
    return jnp.concatenate([jnp.pad(rel_h[::-1], pad), jnp.pad(rel_w[::-1], pad)], 0)


def normal_rows(values):
    center = values - jnp.mean(values, -1, keepdims=True)
    spread = jnp.mean(center * center, -1, keepdims=True)
    return center * lax.rsqrt(spread + EPSILON)


def qkv_kernel(pieces, group_heads, side, sub, raw, gain, shift, w, bias, tables, normed, qa, kp, vp):
    count = raw.shape[0] // sub
    width = group_heads * HD
    lane = lax.broadcasted_iota(jnp.int32, (sub, 128), 1)
    group_lane = lax.broadcasted_iota(jnp.int32, (side, 128), 1)
    group_row = lax.broadcasted_iota(jnp.int32, (side, 128), 0)
    col_hot = (group_lane == group_row) | ((group_lane >= side) & (group_lane < side + 3))
    col_hot = jnp.where(col_hot, 1.0, 0.0).astype(BF)
    col_hot = jnp.concatenate([col_hot] * (sub // side), 0)

    def product(n):
        part = slice(n * sub, (n + 1) * sub)
        rows_n = (normal_rows(raw[part, :].astype(F32)) * gain[...] + shift[...]).astype(BF)
        normed[part, :] = rows_n
        return (dot(rows_n, w[...]) + bias[...]).astype(BF)

    ahead = product(0)
    for m in range(count):
        joined = ahead
        if m + 1 < count:
            ahead = product(m + 1)
        part = slice(m * sub, (m + 1) * sub)
        first_row = (pl.program_id(0) * count + m) * (sub // side)
        hot = []
        for i in range(sub // side):
            hot.append(jnp.where(group_lane == first_row + (HD + i), 1.0, 0.0).astype(BF))
        row_hot = jnp.concatenate(hot, 0)
        for n in range(pieces * group_heads):
            q_at = (n // group_heads) * 3 * width + (n % group_heads) * HD
            q = joined[:, q_at : q_at + HD]
            g = dot(q, tables[...], NT) * math.sqrt(HD)
            gh = []
            gw = []
            for i in range(sub // side):
                rows = g[i * side : (i + 1) * side]
                gh.append(pltpu.roll(rows[:, :128], first_row + (33 + i), axis=1))
                gw.append(pltpu.roll(rows[:, 128:], 81, axis=1, stride=1, stride_axis=0))
            qa[n, part, 0:128] = jnp.concatenate(gh, 0).astype(BF)
            qa[n, part, 0:HD] = q
            qa[n, part, 128:256] = jnp.where(lane < side, jnp.concatenate(gw, 0), 0.0).astype(BF)
            kp[n, part, 0:128] = row_hot
            kp[n, part, 128:256] = col_hot
            kp[n, part, 0:HD] = joined[:, q_at + width : q_at + width + HD]
            vp[n, part, :] = jnp.ones((sub, 128), BF)
            vp[n, part, 0:HD] = joined[:, q_at + 2 * width : q_at + 2 * width + HD]


def qkv_rows(raw, gain, shift, w, bias, tables, pieces, group_heads, side, rows=384, sub=192):
    seq_len, width = raw.shape
    lanes = w.shape[1]
    heads = pieces * group_heads
    return pl.pallas_call(
        partial(qkv_kernel, pieces, group_heads, side, sub),
        grid=(seq_len // rows,),
        in_specs=[
            pl.BlockSpec((rows, width), lambda i: (i, 0)),
            whole(1, width),
            whole(1, width),
            whole(width, lanes),
            whole(1, lanes),
            whole(256, HD),
        ],
        out_specs=[
            pl.BlockSpec((rows, width), lambda i: (i, 0)),
            pl.BlockSpec((heads, rows, 256), lambda i: (0, i, 0)),
            pl.BlockSpec((heads, rows, 256), lambda i: (0, i, 0)),
            pl.BlockSpec((heads, rows, 128), lambda i: (0, i, 0)),
        ],
        out_shape=[
            jax.ShapeDtypeStruct((seq_len, width), BF),
            jax.ShapeDtypeStruct((heads, seq_len, 256), BF),
            jax.ShapeDtypeStruct((heads, seq_len, 256), BF),
            jax.ShapeDtypeStruct((heads, seq_len, 128), BF),
        ],
        compiler_params=params(1),
        cost_estimate=FREE,
        name="qkv_rows",
    )(raw, gain, shift, w, bias, tables)


def attend_kernel(heads, side, aliased, sub, at, qa, kp, vp, *refs):
    o, of, qo = refs[2:] if aliased else refs
    rows = qa.shape[1]
    h = pl.program_id(0)
    base = pl.multiple_of(pl.program_id(1) * rows, rows)
    lane = lax.broadcasted_iota(jnp.int32, (sub, 128), 1)
    count = rows // sub
    scores = [dot(qa[0, 0:sub, :], kp[0], NT)]
    outs = []
    for n in range(count):
        part = slice(n * sub, (n + 1) * sub)
        if n + 1 < count:
            scores.append(dot(qa[0, (n + 1) * sub : (n + 2) * sub, :], kp[0], NT))
        s = scores[n]
        m = jnp.max(s, -1, keepdims=True)
        p = jnp.exp2(s * FACTOR - m * FACTOR).astype(BF)
        out = dot(p, vp[0])
        total = out[:, HD : HD + 1]
        out = out / total
        norm = m + jnp.log2(total) / FACTOR
        hi = norm.astype(BF).astype(F32)
        mid = (norm - hi).astype(BF).astype(F32)
        low = norm - hi - mid
        old = qa[0, part, 128:256].astype(F32)
        old = jnp.where(lane == side, -hi, old)
        old = jnp.where(lane == side + 1, -mid, old)
        old = jnp.where(lane == side + 2, -low, old)
        qo[0, part, 0:128] = qa[0, part, 0:128]
        qo[0, part, 128:256] = old.astype(BF)
        outs.append(out)
    out = jnp.concatenate(outs, 0)
    part = pl.ds(base, rows)
    for n in range(heads):

        @pl.when(h == n)
        def _(n=n):
            o[part, n * HD : (n + 1) * HD] = out[:, 0:HD].astype(BF)
            of[part, n * HD : (n + 1) * HD] = out[:, 0:HD]


def attend(group, qa, kp, vp, side, groups, old=(), tq=1152, sub=576):
    heads, seq_len, _ = qa.shape
    rows = seq_len // groups
    steps = rows // tq
    lanes = heads * HD
    query = pl.BlockSpec((1, tq, 256), lambda h, i, at: (h, at[0] * steps + i, 0))
    return pl.pallas_call(
        partial(attend_kernel, heads, side, bool(old), sub),
        grid_spec=pltpu.PrefetchScalarGridSpec(
            num_scalar_prefetch=1,
            grid=(heads, steps),
            in_specs=[
                query,
                pl.BlockSpec((1, seq_len, 256), lambda h, i, at: (h, 0, 0)),
                pl.BlockSpec((1, seq_len, 128), lambda h, i, at: (h, 0, 0)),
            ]
            + [pl.BlockSpec(memory_space=pl.ANY)] * len(old),
            out_specs=[
                pl.BlockSpec((rows, lanes), lambda h, i, at: (0, 0)),
                pl.BlockSpec((rows, lanes), lambda h, i, at: (at[0], 0)),
                query,
            ],
        ),
        out_shape=[
            jax.ShapeDtypeStruct((rows, lanes), BF),
            jax.ShapeDtypeStruct((seq_len, lanes), F32),
            jax.ShapeDtypeStruct((heads, seq_len, 256), BF),
        ],
        input_output_aliases={4: 1, 5: 2} if old else {},
        compiler_params=params(2),
        cost_estimate=busy(20),
        name="attend",
    )(jnp.stack([group]), qa, kp, vp, *old)


def attend_back_kernel(heads, first, side, uc, qa_ref, kp, vp, of, go, tables, hot, held, dx, gt, passed, kt, dop, dk, dv, dq, sem):
    seq_len = kp.shape[1]
    tb = qa_ref.shape[1]
    h = pl.program_id(0)
    step = pl.program_id(1)
    last = pl.num_programs(1) - 1
    scale = HD ** (-0.5)
    rows = seq_len // 9

    @pl.when((h == 0) & (step == 0))
    def _():
        gt[...] = jnp.zeros_like(gt)
        pltpu.make_async_copy(held, passed, sem.at[0]).start()

        blocks, high, wide = go.shape
        total_lanes = of.shape[1]
        fold = wide // total_lanes
        if fold == 1:
            high = rows

        def prep(i, c):
            lane = lax.broadcasted_iota(jnp.int32, (high, 128), 1)
            for s in range(fold):
                part = pl.ds(pl.multiple_of((i * fold + s) * high, high), high)
                for n in range(heads):
                    at = (first + n) * HD
                    if fold == 1:
                        rows_go = flat_go[part, at : at + HD]
                    else:
                        rows_go = go[i, :, s * total_lanes + at : s * total_lanes + at + HD]
                    inner = jnp.sum(rows_go.astype(F32) * of[part, at : at + HD], -1, keepdims=True)
                    hi = inner.astype(BF).astype(F32)
                    tail = jnp.where(lane == HD, -hi, jnp.where(lane == HD + 1, hi - inner, 0.0))
                    dop[n, part, :] = tail.astype(BF)
                    dop[n, part, 0:HD] = rows_go
            return c

        flat_go = go.at[0]
        lax.fori_loop(0, seq_len // (fold * high), prep, 0, unroll=2)

    @pl.when(step == 0)
    def _():
        def prep(i, c):
            part = pl.ds(pl.multiple_of(i * rows, rows), rows)
            kt[0:128, part] = kp[0, part, 0:128].T
            kt[128 : 128 + side, part] = hot[:, part]
            dk[part, :] = jnp.zeros((rows, 128), F32)
            dv[part, :] = jnp.zeros((rows, 128), F32)
            return c

        lax.fori_loop(0, 9, prep, 0)

    base = pl.ds(pl.multiple_of(step * tb, tb), tb)
    qa = qa_ref[0]
    do = dop[h, base, :]

    def scores(j):
        part = slice(j * uc, (j + 1) * uc)
        return dot(kp[0, part, :], qa, NT), dot(vp[0, part, :], do, NT)

    acc = None
    count = seq_len // uc
    ahead = scores(0)
    for j in range(count):
        s, dp = ahead
        if j + 1 < count:
            ahead = scores(j + 1)
        part = slice(j * uc, (j + 1) * uc)
        p = jnp.exp2(s * FACTOR)
        ds = (p * dp).astype(BF)
        dv[part, :] += dot(p.astype(BF), do)
        dk[part, :] += dot(ds, qa[:, 0:128])
        term = dot(kt[:, part], ds)
        acc = term if acc is None else acc + term
    acc = jnp.concatenate([acc, jnp.zeros((256 - HD - 2 * side, tb), F32)], 0).T
    lane = lax.broadcasted_iota(jnp.int32, (tb, 128), 1)
    groups = tb // side
    rel_h = jnp.where(lane < HD, 0.0, acc[:, :128])
    rel_w = jnp.where(lane < side, acc[:, 128:], 0.0)
    back_h = []
    back_w = []
    for i in range(groups):
        part = slice(i * side, (i + 1) * side)
        back_h.append(pltpu.roll(rel_h[part], 256 - 33 - step * groups - i, axis=1))
        back_w.append(pltpu.roll(rel_w[part], 0, axis=1, stride=1, stride_axis=0))
    both = jnp.concatenate([jnp.concatenate(back_h, 0), jnp.concatenate(back_w, 0)], 1).astype(BF)
    dq[base, :] = acc[:, :HD] * scale + dot(both, tables[...])
    gt[...] += dot(both, qa[:, 0:128], TN)

    @pl.when((h == heads - 1) & (step == last))
    def _():
        pltpu.make_async_copy(held, passed, sem.at[0]).wait()

    width = heads * HD
    for n in range(heads):

        @pl.when((h == n) & (step == last))
        def _(n=n):
            def post(i, c):
                part = pl.ds(pl.multiple_of(i * rows, rows), rows)
                at = n * HD
                dx[part, at : at + HD] = dq[part, :].astype(BF)
                dx[part, width + at : width + at + HD] = (dk[part, 0:HD] * scale).astype(BF)
                dx[part, 2 * width + at : 2 * width + at + HD] = dv[part, 0:HD].astype(BF)
                return c

            lax.fori_loop(0, 9, post, 0)


def attend_back(first, count, qa, kp, vp, of, go, tables, hot, held, side, tb=768, uc=256):
    heads, seq_len, _ = qa.shape
    lanes = heads * HD
    if go.shape[2] == lanes:
        go = go.reshape(1, seq_len, lanes)
    return pl.pallas_call(
        partial(attend_back_kernel, count, first, side, uc),
        grid=(count, seq_len // tb),
        in_specs=[
            pl.BlockSpec((1, tb, 256), lambda h, i: (first + h, i, 0)),
            pl.BlockSpec((1, seq_len, 256), lambda h, i: (first + h, 0, 0)),
            pl.BlockSpec((1, seq_len, 128), lambda h, i: (first + h, 0, 0)),
            whole(seq_len, lanes),
            whole(*go.shape),
            whole(256, HD),
            whole(side, seq_len),
            pl.BlockSpec(memory_space=pltpu.HBM),
        ],
        out_specs=[whole(seq_len, 3 * count * HD), whole(256, 128), pl.BlockSpec(memory_space=pltpu.HBM)],
        out_shape=[
            jax.ShapeDtypeStruct((seq_len, 3 * count * HD), BF),
            jax.ShapeDtypeStruct((256, 128), F32),
            jax.ShapeDtypeStruct(held.shape, held.dtype),
        ],
        scratch_shapes=[
            pltpu.VMEM((HD + 2 * side, seq_len), BF),
            pltpu.VMEM((count, seq_len, 128), BF),
            pltpu.VMEM((seq_len, 128), F32),
            pltpu.VMEM((seq_len, 128), F32),
            pltpu.VMEM((seq_len, HD), F32),
            pltpu.SemaphoreType.DMA((1,)),
        ],
        compiler_params=params(2),
        cost_estimate=busy(50),
        name="attend_back",
    )(qa, kp, vp, of, go, tables, hot, held)


def mlp_kernel(aliased, per, n_own, n_other, g_own, g_other, w1, b1, w2, *refs):
    if aliased:
        out_in, gn_in, out, gn, grads, gb1, n2, gb, act, gbef = refs
    else:
        out, gn, grads, gb1, n2, gb, act, gbef = refs
    step = pl.program_id(0)
    chunk = out.shape[0]
    shards, shard, hidden = w1.shape
    width = n_own.shape[1]
    steps = 2 * per

    @pl.when(step == 0)
    def _():
        gb1[...] = jnp.zeros_like(gb1)

    @pl.when(step < steps)
    def _():
        first = w1[...].reshape(width, hidden)
        second = w2[...].reshape(hidden, width)
        dst = pl.ds(pl.multiple_of(step * chunk, chunk), chunk)
        mine = step < per
        n2[dst, :] = jnp.where(mine, n_own[...], n_other[...])
        gb[dst, :] = jnp.where(mine, g_own[...], g_other[...])
        before = dot(n2[dst, :], first) + b1[...]
        grad_act = dot(gb[dst, :], second, NT)
        cdf = 0.5 + 0.5 * lax.erf(before * math.sqrt(0.5))
        act[dst, :] = (before * cdf).astype(BF)
        slope = cdf + before * (jnp.exp(-0.5 * before * before) * (1.0 / math.sqrt(2.0 * math.pi)))
        grad_before = slope * grad_act
        gbef[dst, :] = grad_before.astype(BF)
        gb1[...] += jnp.sum(gbef[dst, :].astype(F32), 0, keepdims=True)
        value = dot(act[dst, :], second)
        back = dot(gbef[dst, :], first, NT)
        if aliased:
            value = value + out_in[...]
            back = back + gn_in[...]
        out[...] = value
        gn[...] = back

    for j in range(shards):

        @pl.when(step == steps + j)
        def _(j=j):
            rows = slice(j * shard, (j + 1) * shard)
            grads[0, 0:shard, :] = dot(n2[:, rows], gbef[...], TN).astype(BF)
            grads[0, shard : 2 * shard, :] = dot(act[:, rows], gb[...], TN).astype(BF)


def mlp_half(n_own, n_other, g_own, g_other, weights, b1, old=(), chunk=288):
    half, width = n_own.shape
    dp = weights.shape[0]
    shard = width // dp
    hidden = width
    chunk = min(chunk, half)
    per = half // chunk
    steps = 2 * per
    tile = pl.BlockSpec((chunk, width), lambda i: (jnp.minimum(i, steps - 1), 0))
    own = pl.BlockSpec((chunk, width), lambda i: (jnp.minimum(i, per - 1), 0))
    other = pl.BlockSpec((chunk, width), lambda i: (jnp.clip(i - per, 0, per - 1), 0))
    rows = jax.ShapeDtypeStruct((2 * half, width), F32)
    return pl.pallas_call(
        partial(mlp_kernel, bool(old), per),
        grid=(steps + dp,),
        in_specs=[own, other, own, other]
        + [
            pl.BlockSpec((dp, shard, width), lambda i: (0, 0, 0), pipeline_mode=pl.Buffered(1)),
            whole(1, hidden),
            pl.BlockSpec((dp, shard, width), lambda i: (0, 1, 0), pipeline_mode=pl.Buffered(1)),
        ]
        + [tile] * len(old),
        out_specs=[
            tile,
            tile,
            pl.BlockSpec((1, 2 * shard, width), lambda i: (jnp.maximum(i - steps, 0), 0, 0)),
            whole(1, hidden),
        ],
        out_shape=[
            rows,
            rows,
            jax.ShapeDtypeStruct((dp, 2 * shard, width), BF),
            jax.ShapeDtypeStruct((1, hidden), F32),
        ],
        input_output_aliases={7: 0, 8: 1} if old else {},
        scratch_shapes=[pltpu.VMEM((2 * half, width), BF)] * 4,
        compiler_params=params(1, 63),
        cost_estimate=busy(35),
        name="mlp_half",
    )(n_own, n_other, g_own, g_other, weights, b1, weights, *old)


def select_kernel(ng, np_, nc, at, qkv_in, fc1_in, fc2_in, proj_in, own, *refs):
    slabs = refs[:2]
    qkv, fc1, fc2, proj, sem = refs[2:]
    loads = []
    for n, (src, dst) in enumerate(((qkv_in, qkv), (proj_in, proj), (fc1_in, fc1), (fc2_in, fc2))):
        loads.append(pltpu.make_async_copy(src, dst, sem.at[n]))
        loads[-1].start()
    i_p, i_c = at[1], at[2]
    shard = fc1.shape[0]
    width = proj.shape[1]
    hidden = fc1.shape[1]
    chips = ng * np_
    unit = hidden // (chips * nc)
    part = unit // 2
    piece = proj.shape[0] // nc
    shard_lanes = proj.shape[0]
    lanes = own.shape[1] // 3
    pieces = lanes // piece
    per = fc2.shape[0] // (nc * unit)
    loads[0].wait()
    for c in range(nc):
        for p in range(np_):

            @pl.when((i_c == c) & (i_p == p))
            def _(c=c, p=p):
                for q in range(pieces):
                    for t in range(3):
                        src = t * width + (p * pieces + q) * shard_lanes + c * piece
                        dst = (3 * q + t) * piece
                        own[:, dst : dst + piece] = qkv[:, src : src + piece]

    for copy in loads[1:]:
        copy.wait()
    for c in range(nc):

        @pl.when(i_c == c)
        def _(c=c):
            for u in range(2):
                for z in range(chips):
                    src = (z * nc + c) * unit + u * part
                    slabs[u][0:shard, z * part : (z + 1) * part] = fc1[:, src : src + part]
                for b in range(per):
                    src = (b * nc + c) * unit + u * part
                    dst = shard + b * part
                    slabs[u][dst : dst + part, :] = fc2[src : src + part, :]
            slabs[0][2 * shard : 2 * shard + piece, :] = proj[c * piece : (c + 1) * piece, :]


def select(at, qkv, fc1, fc2, proj, ng, np_, nc, lanes):
    shard, width = proj.shape[0], proj.shape[1]
    return pl.pallas_call(
        partial(select_kernel, ng, np_, nc),
        in_specs=[pl.BlockSpec(memory_space=pltpu.SMEM)] + [pl.BlockSpec(memory_space=pltpu.HBM)] * 4,
        out_specs=[pl.BlockSpec(memory_space=pltpu.VMEM)] * 3,
        scratch_shapes=[pltpu.VMEM(value.shape, BF) for value in (qkv, fc1, fc2, proj)]
        + [pltpu.SemaphoreType.DMA((4,))],
        out_shape=[
            jax.ShapeDtypeStruct((shard, 3 * lanes), BF),
            jax.ShapeDtypeStruct((2 * shard + shard // nc, width), BF),
            jax.ShapeDtypeStruct((2 * shard, width), BF),
        ],
        compiler_params=pltpu.CompilerParams(vmem_limit_bytes=63 << 20),
        cost_estimate=FREE,
        name="select",
    )(at, qkv, fc1, fc2, proj)


def start_kernel(sizes, split, patches, own, vec, rows, full, vecs, local, send, recv):
    dp, ng, np_ = sizes
    i_dp, i_g, i_p, i_c = (lax.axis_index(name) for name in ("dp", "g", "p", "c"))
    count = patches.shape[1]
    step = count // split

    barrier = pltpu.get_barrier_semaphore()
    peers = [{"dp": i_dp ^ k} for k in range(1, dp)]
    peers += [{"g": i_g ^ k} for k in range(1, ng)]
    peers += [{"p": i_p ^ k} for k in range(1, np_)]
    peers += [{"c": 1 - i_c}]
    for peer in peers:
        pl.semaphore_signal(barrier, inc=1, device_id=peer, device_id_type=pl.DeviceIdType.MESH)
    pl.semaphore_wait(barrier, len(peers))

    used = []

    def remote(src, dst, peer):
        n = len(used)
        copy = pltpu.make_async_remote_copy(
            src_ref=src,
            dst_ref=dst,
            send_sem=send.at[n],
            recv_sem=recv.at[n],
            device_id=peer,
            device_id_type=pl.DeviceIdType.MESH,
        )
        used.append(copy)
        return copy

    def place(g, p, c, part):
        start = ((g * np_ + p) * 2 + c) * count + part * step
        return rows.at[pl.ds(pl.multiple_of(start, 8), step)]

    mine = [patches.at[i_g, pl.ds(part * step, step)] for part in range(split)]
    home = [pltpu.make_async_copy(mine[part], place(i_g, i_p, i_c, part), local.at[part]) for part in range(split)]
    home.append(pltpu.make_async_copy(own, full.at[i_dp], local.at[split]))
    home.append(pltpu.make_async_copy(vec, vecs.at[i_dp], local.at[split + 1]))

    far = {}
    for part in range(split):
        for bit in range(1, ng):
            src = patches.at[i_g ^ bit, pl.ds(part * step, step)]
            far[bit, part] = remote(src, place(i_g, i_p, i_c, part), {"g": i_g ^ bit})
            far[bit, part].start()
    over_dp = []
    for bit in range(1, dp):
        over_dp.append(remote(vec, vecs.at[i_dp], {"dp": i_dp ^ bit}))
        over_dp.append(remote(own, full.at[i_dp], {"dp": i_dp ^ bit}))
    for copy in over_dp:
        copy.start()
    near = {}
    for bit in range(1, np_):
        for part in range(split):
            near[bit, part] = remote(mine[part], place(i_g, i_p, i_c, part), {"p": i_p ^ bit})
            near[bit, part].start()
    cores = []
    for part in range(split):
        cores.append(remote(mine[part], place(i_g, i_p, i_c, part), {"c": 1 - i_c}))
        cores[-1].start()
    for copy in home:
        copy.start()

    onward = {}
    for part in range(split):
        for bit in range(1, ng):
            far[bit, part].wait_recv()
            came = place(i_g ^ bit, i_p, i_c, part)
            for bit_p in range(1, np_):
                onward[bit, bit_p, part] = remote(came, came, {"p": i_p ^ bit_p})
                onward[bit, bit_p, part].start()
            cores.append(remote(came, came, {"c": 1 - i_c}))
            cores[-1].start()
        for bit in range(1, np_):
            near[bit, part].wait_recv()
            came = place(i_g, i_p ^ bit, i_c, part)
            cores.append(remote(came, came, {"c": 1 - i_c}))
            cores[-1].start()
    for (bit, bit_p, part), copy in onward.items():
        copy.wait_recv()
        came = place(i_g ^ bit, i_p ^ bit_p, i_c, part)
        cores.append(remote(came, came, {"c": 1 - i_c}))
        cores[-1].start()
    for copy in over_dp + cores:
        copy.wait_recv()
    for copy in used:
        copy.wait_send()
    for copy in home:
        copy.wait()


def start_exchange(patches, own, vec, sizes):
    dp, ng, np_ = sizes
    images, count, width = patches.shape
    split = 6 if count % 48 == 0 else 3
    chunk_copies = ng * np_ + (ng - 1) + (np_ - 1) + (ng - 1) * (np_ - 1)
    copies = 2 * (dp - 1) + split * chunk_copies
    hbm = pl.BlockSpec(memory_space=pl.ANY)
    return pl.pallas_call(
        partial(start_kernel, sizes, split),
        in_specs=[hbm] * 3,
        out_specs=[hbm] * 3,
        out_shape=[
            jax.ShapeDtypeStruct((ng * np_ * 2 * count, width), BF),
            jax.ShapeDtypeStruct((dp,) + own.shape, BF),
            jax.ShapeDtypeStruct((dp,) + vec.shape, BF),
        ],
        scratch_shapes=[
            pltpu.SemaphoreType.DMA((split + 2,)),
            pltpu.SemaphoreType.DMA((copies,)),
            pltpu.SemaphoreType.DMA((copies,)),
        ],
        compiler_params=pltpu.CompilerParams(collective_id=0, has_side_effects=True),
        cost_estimate=FREE,
        name="start_exchange",
    )(patches, own, vec)


class Links:
    def __init__(self, send, recv):
        self.send, self.recv, self.copies = send, recv, []

    def __call__(self, src, dst, peer):
        n = len(self.copies)
        copy = pltpu.make_async_remote_copy(
            src_ref=src,
            dst_ref=dst,
            send_sem=self.send.at[n],
            recv_sem=self.recv.at[n],
            device_id=peer,
            device_id_type=pl.DeviceIdType.MESH,
        )
        copy.start()
        self.copies.append(copy)
        return copy

    def drain(self):
        for copy in self.copies:
            copy.wait_send()


def meet(peers):
    barrier = pltpu.get_barrier_semaphore()
    for peer in peers:
        pl.semaphore_signal(barrier, inc=1, device_id=peer, device_id_type=pl.DeviceIdType.MESH)
    pl.semaphore_wait(barrier, len(peers))


def finish_kernel(sizes, split, pieces, part_w, *refs):
    dp, ng, np_ = sizes
    chips = ng * np_
    ranks = chips * 2
    raw, normed = refs[:2]
    dx = refs[2 : 2 + pieces]
    tables = refs[2 + pieces : 2 + 2 * pieces]
    refs = refs[2 + 2 * pieces :]
    w_in, inputs_in, grad_mid_in, gain, early, proj_in = refs[:6]
    parts_in = refs[6 : 6 + 2 * chips]
    (home, owned, out_vec, out_tab, out_fc1, out_fc2, out_proj,
     dx_all, norm_all, dx_ring, raw_ring, keep, away, came, pair, far, slab_out, slabs, cells, taken,
     sums, lane_sums, vec, vec_out, vec_dp, vec_z, vec_c, tab, tab_dp, tab_z, tab_c, tab_all,
     give, got, give_p, got_p, proj_out, proj_got, w, inputs, grad_mid, parts, late, sem, send, recv, cell_send, cell_recv,
     ) = refs[6 + 2 * chips :]
    w_load = pltpu.make_async_copy(w_in, w, late.at[0])
    w_load.start()
    late_loads = [pltpu.make_async_copy(inputs_in, inputs, late.at[1])]
    late_loads.append(pltpu.make_async_copy(grad_mid_in, grad_mid, late.at[2]))
    for n, ref in enumerate(parts_in):
        late_loads.append(pltpu.make_async_copy(ref, parts.at[n], late.at[3 + n]))
    i_dp, i_g, i_p, i_c = places()
    i_z = i_g * np_ + i_p
    i_s = i_z * 2 + i_c
    count, width = keep.shape[1], keep.shape[2]
    step = count // split
    shard = owned.shape[0]
    cell = owned.shape[1] // 3
    lanes = dx_all.shape[2]
    core = {"c": 1 - i_c}
    chip_peer = lambda k: {"g": i_g ^ (k // np_), "p": i_p ^ (k % np_)}
    peers = [{"dp": i_dp ^ k} for k in range(1, dp)]
    for k in range(1, ranks):
        peers.append({"g": i_g ^ (k // (np_ * 2)), "p": i_p ^ ((k // 2) % np_), "c": i_c ^ (k % 2)})
    meet(peers)
    link = Links(send, recv)

    z_of = lambda k: (i_g ^ (k // np_)) * np_ + (i_p ^ (k % np_))
    part_rows = lambda part: pl.ds(part * step, step)
    far_slots, near_slots = list(range(np_, chips)), list(range(np_))
    jobs = [(k, b) for group in (far_slots, near_slots) for b in (1, 0) for k in group]
    loads = {}

    def load(n):
        if n < len(jobs):
            k, b = jobs[n]
            start = (z_of(k) * 2 + (i_c ^ b)) * count
            at = pl.ds(pl.multiple_of(start, 8), count)
            slot = n % 2
            loads[n] = [pltpu.make_async_copy(raw.at[at], raw_ring.at[slot], sem.at[slot * (1 + pieces)])]
            for q in range(pieces):
                loads[n].append(
                    pltpu.make_async_copy(dx[q].at[at], dx_ring.at[slot, q], sem.at[slot * (1 + pieces) + 1 + q])
                )
            for copy in loads[n]:
                copy.start()

    load(0)
    load(1)
    whole_loads = [pltpu.make_async_copy(normed, norm_all, sem.at[2 * (1 + pieces)])]
    for q in range(pieces):
        whole_loads.append(pltpu.make_async_copy(dx[q], dx_all.at[q], sem.at[2 * (1 + pieces) + 1 + q]))
    for copy in whole_loads:
        copy.start()
    for copy in late_loads:
        copy.start()
    sums[...] = jnp.zeros_like(sums)
    lane_sums[...] = jnp.zeros_like(lane_sums)
    from_core = {}

    def rows(n):
        k, b = jobs[n]
        slot = n % 2
        for copy in loads[n]:
            copy.wait()
        normal = normal_rows(raw_ring[slot].astype(F32))
        total = None
        for q in range(pieces):
            value = dx_ring[slot, q]
            term = dot(value, w[:, q * lanes : (q + 1) * lanes], NT)
            total = term if total is None else total + term
            lane_sums[q : q + 1, :] += jnp.sum(value.astype(F32), 0, keepdims=True)
        sums[0:1, :] += jnp.sum(total * normal, 0, keepdims=True)
        sums[1:2, :] += jnp.sum(total, 0, keepdims=True)
        if b:
            away[k] = total.astype(BF)
            from_core[k] = link(away.at[k], came.at[k], core)
        else:
            keep[k] = total.astype(BF)
        load(n + 2)

    from_pair = {}

    def over_cores(slots):
        for k in slots:
            from_core[k].wait_recv()
            for part in range(split):
                at = part_rows(part)
                keep[k, at, :] = (keep[k, at, :].astype(F32) + came[k, at, :].astype(F32)).astype(BF)
                if k % np_:
                    dst = pair.at[k // np_, k % np_, at]
                    from_pair[k // np_, k % np_, part] = link(keep.at[k, at], dst, {"p": i_p ^ (k % np_)})

    def over_pair(bit_g, part):
        at = part_rows(part)
        value = keep[bit_g * np_, at, :].astype(F32)
        for bit_p in range(1, np_):
            from_pair[bit_g, bit_p, part].wait_recv()
            value = value + pair[bit_g, bit_p, at, :].astype(F32)
        return value

    half = len(far_slots) * 2
    w_load.wait()
    for n in range(half):
        rows(n)

    part_lanes = parts.shape[2]
    for z in range(chips):
        proj_out[z] = proj_in[:, z * part_lanes : (z + 1) * part_lanes]
    from_chip = [link(proj_out.at[z_of(k)], proj_got.at[k], chip_peer(k)) for k in range(1, chips)]
    over_cores(far_slots)

    for copy in whole_loads:
        copy.wait()
    for j in range(dp):
        for q in range(pieces):
            slab_out[j, q] = dot(norm_all[:, j * shard : (j + 1) * shard], dx_all[q], TN).astype(BF)
    from_dp = [link(slab_out.at[i_dp ^ bit], slabs.at[bit], {"dp": i_dp ^ bit}) for bit in range(1, dp)]

    from_far = {}
    for part in range(split):
        at = part_rows(part)
        for bit_g in range(1, ng):
            pair[bit_g, 0, at, :] = over_pair(bit_g, part).astype(BF)
            from_far[bit_g, part] = link(pair.at[bit_g, 0, at], far.at[bit_g, at], {"g": i_g ^ bit_g})
    for n in range(half, len(jobs)):
        rows(n)

    vec[...] = jnp.zeros_like(vec)
    vec[0:2, :] = sums[0:2, :]
    vec[4:12, :] = early[...]
    for p in range(np_):
        for c in range(2):

            @pl.when((i_p == p) & (i_c == c))
            def _(p=p, c=c):
                for q in range(pieces):
                    at = (p * pieces + q) * shard + c * part_w
                    vec[2:3, at : at + part_w] = lane_sums[q : q + 1, 0:part_w]
                    vec[3:4, at : at + part_w] = lane_sums[q : q + 1, 2 * part_w : 3 * part_w]

    table = tables[0][...]
    for ref in tables[1:]:
        table = table + ref[...]
    tab[...] = table
    tab_rows = tab.shape[0] // dp
    tab_at = lambda j: pl.ds(pl.multiple_of(j * tab_rows, 8), tab_rows)
    for j in range(dp):
        vec_out[j] = vec[:, j * shard : (j + 1) * shard]
    vec_dp[i_dp] = vec_out[i_dp]
    tab_dp[i_dp] = tab[tab_at(i_dp), :]
    small = []
    for bit in range(1, dp):
        small.append(link(vec_out.at[i_dp ^ bit], vec_dp.at[i_dp], {"dp": i_dp ^ bit}))
        small.append(link(tab.at[tab_at(i_dp ^ bit)], tab_dp.at[i_dp], {"dp": i_dp ^ bit}))

    def sum_of(ref, n):
        value = ref[0]
        for i in range(1, n):
            value = value + ref[i]
        return value

    over_cores(near_slots)
    for copy in small:
        copy.wait_recv()
    vec_z[i_z] = sum_of(vec_dp, dp)
    tab_z[i_z] = sum_of(tab_dp, dp)
    small = []
    for k in range(1, chips):
        small.append(link(vec_z.at[i_z], vec_z.at[i_z], chip_peer(k)))
        small.append(link(tab_z.at[i_z], tab_z.at[i_z], chip_peer(k)))

    hidden_rows = give.shape[1]
    per_rows = part_lanes
    swaps = []

    def halves(value, there):
        cols = value.shape[1] // 2
        mine = jnp.where(i_c == 0, value[:, :cols], value[:, cols:])
        there[...] = jnp.where(i_c == 0, value[:, cols:], value[:, :cols]).astype(BF)
        return mine

    def place_fc2(u, flip_core, value):
        value = value.T
        for c in range(2):

            @pl.when((i_c ^ flip_core) == c)
            def _(c=c):
                for b in range(hidden_rows // per_rows):
                    start = ((b * 2 + c) * 2 + u) * per_rows
                    out_fc2[:, start : start + per_rows] = value[:, b * per_rows : (b + 1) * per_rows]

    def place_proj(flip_core, value):
        value = value.T
        n = value.shape[1]
        for c in range(2):

            @pl.when((i_c ^ flip_core) == c)
            def _(c=c):
                out_proj[:, c * n : (c + 1) * n] = value

    for copy in late_loads:
        copy.wait()
    for u in range(2):
        value = parts[u * chips].astype(F32)
        for n in range(1, chips):
            value = value + parts[u * chips + n].astype(F32)
        out_fc1[:, u * per_rows : (u + 1) * per_rows] = value[0:shard]
        place_fc2(u, 0, halves(value[shard:], give.at[u]))
        swaps.append(link(give.at[u], got.at[u], core))
    value = proj_out[i_z].astype(F32)
    for k in range(1, chips):
        from_chip[k - 1].wait_recv()
        value = value + proj_got[k].astype(F32)
    place_proj(0, halves(value, give_p))
    swaps.append(link(give_p, got_p, core))

    for copy in from_dp:
        copy.wait_recv()
    sent_cells = []
    for q in range(pieces):
        value = slab_out[i_dp, q].astype(F32)
        for bit in range(1, dp):
            value = value + slabs[bit, q].astype(F32)
        value = value.astype(BF)
        for t in range(3):
            for u in range(part_w // cell):
                n = len(sent_cells)
                lane = t * part_w + u * cell
                quarter = shard // 4
                for i in range(4):
                    cells[n, :, i * cell : (i + 1) * cell] = value[i * quarter : (i + 1) * quarter, lane : lane + cell]
                unit = (t * width + (i_p * pieces + q) * shard + i_c * part_w) // cell + u
                owner = unit // 3
                slot = unit % 3
                dst = taken.at[i_g, slot]
                o_c = owner % 2
                o_p = (owner // 2) % np_
                o_g = owner // (2 * np_)

                @pl.when(owner == i_s)
                def _(n=n, dst=dst, slot=slot):
                    pltpu.make_async_copy(cells.at[n], dst, cell_recv.at[i_g * 3 + slot]).start()

                @pl.when(owner != i_s)
                def _(n=n, dst=dst, slot=slot, o_g=o_g, o_p=o_p, o_c=o_c):
                    pltpu.make_async_remote_copy(
                        src_ref=cells.at[n],
                        dst_ref=dst,
                        send_sem=cell_send.at[n],
                        recv_sem=cell_recv.at[i_g * 3 + slot],
                        device_id={"g": o_g, "p": o_p, "c": o_c},
                        device_id_type=pl.DeviceIdType.MESH,
                    ).start()

                sent_cells.append(owner)

    def arrived(image, at, value):
        grad, _ = norm_back(inputs[image, at, :].astype(F32), gain[...], value)
        home[image, at, :] = (grad_mid[image, at, :] + grad).astype(BF)

    for part in range(split):
        arrived(i_g, part_rows(part), over_pair(0, part))
    for copy in small:
        copy.wait_recv()
    vec_c[i_c] = sum_of(vec_z, chips)
    tab_c[i_c] = sum_of(tab_z, chips)
    small = [link(vec_c.at[i_c], vec_c.at[i_c], core), link(tab_c.at[i_c], tab_c.at[i_c], core)]
    for copy in swaps:
        copy.wait_recv()
    for u in range(2):
        place_fc2(u, 1, got[u].astype(F32))
    place_proj(1, got_p[...].astype(F32))
    for copy in small:
        copy.wait_recv()
    out_vec[...] = sum_of(vec_c, 2)
    tab_all[i_dp] = sum_of(tab_c, 2)
    small = [link(tab_all.at[i_dp], tab_all.at[i_dp], {"dp": i_dp ^ bit}) for bit in range(1, dp)]
    for part in range(split):
        at = part_rows(part)
        for bit_g in range(1, ng):
            from_far[bit_g, part].wait_recv()
            arrived(i_g ^ bit_g, at, far[bit_g, at, :].astype(F32))
    for slot in range(3):
        value = None
        for g in range(ng):
            pltpu.make_async_copy(cells.at[0], taken.at[g, slot], cell_recv.at[g * 3 + slot]).wait()
            term = taken[g, slot].astype(F32)
            value = term if value is None else value + term
        quarter = shard // 4
        for i in range(4):
            rows_at = slice(i * quarter, (i + 1) * quarter)
            owned[rows_at, slot * cell : (slot + 1) * cell] = value[:, i * cell : (i + 1) * cell]
    for copy in small:
        copy.wait_recv()
    for j in range(dp):
        out_tab[j * tab_rows : (j + 1) * tab_rows, :] = tab_all[j]
    for n, owner in enumerate(sent_cells):

        @pl.when(owner != i_s)
        def _(n=n):
            pltpu.make_async_copy(cells.at[n], cells.at[n], cell_send.at[n]).wait()

    link.drain()


def finish(raw, normed, dx, tables, w, inputs, grad_mid, gain, early, proj_in, parts, sizes, part_w, split=3):
    count = inputs.shape[1]
    dp, ng, np_ = sizes
    chips = ng * np_
    pieces = len(dx)
    seq_len, width = raw.shape
    lanes = dx[0].shape[1]
    shard = width // dp
    cell = width // (chips * 2)
    total_cells = pieces * 3 * (part_w // cell)
    parts_a, parts_b = parts
    part_lanes = parts_a[0].shape[1]
    hidden_rows = parts_a[0].shape[0] - shard
    piece_rows = proj_in.shape[0]
    copies = chips + split * (ng * (np_ - 1) + ng - 1) + (chips - 1) + (dp - 1) * 4 + 2 * (chips - 1) + 5
    hbm = pl.BlockSpec(memory_space=pltpu.HBM)
    vmem = pl.BlockSpec(memory_space=pltpu.VMEM)
    table = tables[0].shape
    block = (table[0] // dp, table[1])
    return pl.pallas_call(
        partial(finish_kernel, sizes, split, pieces, part_w),
        in_specs=[hbm] * (2 + pieces) + [vmem] * pieces + [hbm] * 3 + [vmem] * 3 + [hbm] * (2 * chips),
        out_specs=[vmem] * 7,
        out_shape=[
            jax.ShapeDtypeStruct((ng, count, width), BF),
            jax.ShapeDtypeStruct((shard, 3 * cell), F32),
            jax.ShapeDtypeStruct((16, shard), F32),
            jax.ShapeDtypeStruct(table, F32),
            jax.ShapeDtypeStruct((shard, 2 * part_lanes), F32),
            jax.ShapeDtypeStruct((part_lanes // 2, 4 * hidden_rows), F32),
            jax.ShapeDtypeStruct((part_lanes // 2, 2 * piece_rows), F32),
        ],
        scratch_shapes=[
            pltpu.VMEM((pieces, seq_len, lanes), BF),
            pltpu.VMEM((seq_len, width), BF),
            pltpu.VMEM((2, pieces, count, lanes), BF),
            pltpu.VMEM((2, count, width), BF),
            pltpu.VMEM((chips, count, width), BF),
            pltpu.VMEM((chips, count, width), BF),
            pltpu.VMEM((chips, count, width), BF),
            pltpu.VMEM((ng, np_, count, width), BF),
            pltpu.VMEM((ng, count, width), BF),
            pltpu.VMEM((dp, pieces, shard, lanes), BF),
            pltpu.VMEM((dp, pieces, shard, lanes), BF),
            pltpu.VMEM((total_cells, shard // 4, 4 * cell), BF),
            pltpu.VMEM((ng, 3, shard // 4, 4 * cell), BF),
            pltpu.VMEM((8, width), F32),
            pltpu.VMEM((8, lanes), F32),
            pltpu.VMEM((16, width), F32),
            pltpu.VMEM((dp, 16, shard), F32),
            pltpu.VMEM((dp, 16, shard), F32),
            pltpu.VMEM((chips, 16, shard), F32),
            pltpu.VMEM((2, 16, shard), F32),
            pltpu.VMEM(table, F32),
            pltpu.VMEM((dp,) + block, F32),
            pltpu.VMEM((chips,) + block, F32),
            pltpu.VMEM((2,) + block, F32),
            pltpu.VMEM((dp,) + block, F32),
            pltpu.VMEM((2, hidden_rows, part_lanes // 2), BF),
            pltpu.VMEM((2, hidden_rows, part_lanes // 2), BF),
            pltpu.VMEM((piece_rows, part_lanes // 2), BF),
            pltpu.VMEM((piece_rows, part_lanes // 2), BF),
            pltpu.VMEM((chips, piece_rows, part_lanes), BF),
            pltpu.VMEM((chips, piece_rows, part_lanes), BF),
            pltpu.VMEM(w.shape, BF),
            pltpu.VMEM((ng, count, width), BF),
            pltpu.VMEM((ng, count, width), F32),
            pltpu.VMEM((2 * chips,) + parts_a[0].shape, BF),
            pltpu.SemaphoreType.DMA((3 + 2 * chips,)),
            pltpu.SemaphoreType.DMA((2 * (1 + pieces) + 1 + pieces,)),
            pltpu.SemaphoreType.DMA((copies,)),
            pltpu.SemaphoreType.DMA((copies,)),
            pltpu.SemaphoreType.DMA((total_cells,)),
            pltpu.SemaphoreType.DMA((3 * ng,)),
        ],
        compiler_params=pltpu.CompilerParams(collective_id=1, has_side_effects=True, vmem_limit_bytes=63 << 20),
        cost_estimate=FREE,
        name="finish",
    )(raw, normed, *dx, *tables, w, inputs, grad_mid, gain, early, proj_in, *parts_a, *parts_b)


def split_kernel(chips, at, value, *outs):
    for z in range(chips):

        @pl.when(at[0] == z)
        def _(z=z):
            for n in range(chips):
                lanes = outs[n].shape[1]
                outs[n][...] = value[:, (z ^ n) * lanes : ((z ^ n) + 1) * lanes]


def split_columns(value, index, chips):
    rows, width = value.shape
    vmem = pl.BlockSpec(memory_space=pltpu.VMEM)
    return pl.pallas_call(
        partial(split_kernel, chips),
        in_specs=[pl.BlockSpec(memory_space=pltpu.SMEM), vmem],
        out_specs=[vmem] * chips,
        out_shape=[jax.ShapeDtypeStruct((rows, width // chips), value.dtype)] * chips,
        cost_estimate=FREE,
        name="split_columns",
    )(jnp.stack([index]), value)


def places():
    return tuple(lax.axis_index(name) for name in ("dp", "g", "p", "c"))


def proj_copy(w, held, sem):
    piece = held.shape[1]
    copy = pltpu.make_async_copy(w.at[:, pl.ds(4 * piece, piece)], held, sem)
    copy.start()
    return copy


def rows_of(w, p, np_):
    dp, piece, width = w.shape
    if dp >= np_:
        each = dp // np_
        return w[pl.ds(p * each, each)].reshape(each * piece, width)
    raise NotImplementedError


def middle_kernel(sizes, near, *refs):
    dp, ng, np_ = sizes
    far = refs[:np_]
    (w_all, patches, bias, gain, shift, mid, two_own, two_other, mixed,
     w, pieces, mine, away, came, sem, send, recv) = refs[np_:]
    i_dp, i_g, i_p, i_c = places()
    proj = proj_copy(w_all, w, sem.at[1])
    rows = patches.shape[1]
    core = {"c": 1 - i_c}
    meet([core] + [{"p": i_p ^ k} for k in range(1, np_)])
    link = Links(send, recv)
    here = pltpu.make_async_copy(near.at[i_p], pieces.at[0], sem.at[0])
    here.start()
    arrive = [link(near.at[i_p ^ k], pieces.at[k], {"p": i_p ^ k}) for k in range(1, np_)]

    def split(piece, p, image):
        for swap in range(2):

            @pl.when(i_c == swap)
            def _(swap=swap):
                for b in range(2):
                    mixed[p, b, image] = piece[(swap ^ b) * rows : ((swap ^ b) + 1) * rows, :]

    def product(b, image):
        total = None
        for p in range(np_):
            term = dot(mixed[p, b, image], rows_of(w, p, np_))
            total = term if total is None else total + term
        return total

    other = []
    proj.wait()
    for bit in (1, 0):
        image = i_g ^ bit
        if bit:
            for k in range(np_):
                split(far[k], i_p ^ k, image)
        else:
            here.wait()
            for copy in arrive:
                copy.wait_recv()
            for k in range(np_):
                split(pieces.at[k], i_p ^ k, image)
        away[image] = product(1, image)
        other.append(link(away.at[image], came.at[image], core))
        mine[image] = product(0, image)
    back = []
    for bit in (1, 0):
        image = i_g ^ bit
        other[1 - bit].wait_recv()
        value = patches[image].astype(F32) + mine[image] + came[image] + bias[...]
        mid[image] = value
        two_own[image] = (normal_rows(value) * gain[...] + shift[...]).astype(BF)
        back.append(link(two_own.at[image], two_other.at[image], core))
    for copy in back:
        copy.wait_recv()
    link.drain()


def middle_rows(near, far, w, patches, bias, gain, shift, sizes):
    dp, ng, np_ = sizes
    images, rows, width = patches.shape
    lanes = near.shape[2]
    vmem = pl.BlockSpec(memory_space=pltpu.VMEM)
    copies = np_ - 1 + 2 * images
    own = jax.ShapeDtypeStruct((images, rows, width), BF)
    return pl.pallas_call(
        partial(middle_kernel, sizes),
        in_specs=[pl.BlockSpec(memory_space=pl.ANY)] + [vmem] * len(far) + [pl.BlockSpec(memory_space=pl.ANY)] + [vmem] * 4,
        out_specs=[vmem] * 4,
        out_shape=[
            jax.ShapeDtypeStruct((images, rows, width), F32),
            own,
            own,
            jax.ShapeDtypeStruct((np_, 2, images, rows, lanes), BF),
        ],
        scratch_shapes=[
            pltpu.VMEM((dp, w.shape[1] // 5, width), BF),
            pltpu.VMEM((np_, 2 * rows, lanes), BF),
            pltpu.VMEM((images, rows, width), F32),
            pltpu.VMEM((images, rows, width), F32),
            pltpu.VMEM((images, rows, width), F32),
            pltpu.SemaphoreType.DMA((2,)),
            pltpu.SemaphoreType.DMA((copies,)),
            pltpu.SemaphoreType.DMA((copies,)),
        ],
        compiler_params=pltpu.CompilerParams(collective_id=2, has_side_effects=True, vmem_limit_bytes=48 << 20),
        cost_estimate=FREE,
        name="middle_rows",
    )(near, *far, w, patches, bias, gain, shift)


def norm_back(values, gain, upstream):
    center = values - jnp.mean(values, -1, keepdims=True)
    spread = jnp.mean(center * center, -1, keepdims=True)
    inverse = lax.rsqrt(spread + EPSILON)
    normal = center * inverse
    scaled = upstream * gain
    inner = jnp.mean(scaled * normal, -1, keepdims=True)
    return inverse * (scaled - jnp.mean(scaled, -1, keepdims=True) - normal * inner), normal


def turn_kernel(sizes, mid, gn, out, branch, gain, shift, w_all, mixed, output, grad_mid, heads, grad_proj, sums,
                w, back_own, back_other, gn_own, gn_came, out_own, out_came, stage, sem, send, recv):
    dp, ng, np_ = sizes
    i_dp, i_g, i_p, i_c = places()
    images, rows, width = mid.shape
    fold = rows // stage.shape[1]
    i_z = i_g * np_ + i_p
    core = {"c": 1 - i_c}
    peers = [core]
    for k in range(1, ng * np_):
        peers.append({"g": i_g ^ (k // np_), "p": i_p ^ (k % np_)})
    meet(peers)
    link = Links(send, recv)
    turns = [i_g ^ 1, i_g]
    proj = proj_copy(w_all, w, sem.at[2 * images + 2])

    def half(ref, b, image):
        start = (b * images + image) * rows
        return ref.at[pl.ds(pl.multiple_of(start, 8), rows)]

    loads = []
    crossed = []
    for n, image in enumerate(turns):
        crossed.append(link(half(gn, 1, image), gn_came.at[image], core))
        loads.append(pltpu.make_async_copy(half(gn, 0, image), gn_own.at[image], sem.at[n]))
        loads[-1].start()
    locals_ = []
    sums[...] = jnp.zeros_like(sums)

    def give(n, b):
        image = turns[n]
        source = (back_own if b == 0 else back_other)[image]
        for k in range(np_):
            slot = (n * np_ + k) * 2 + b
            value = dot(source, rows_of(w, i_p ^ k, np_), NT).astype(BF)
            lanes = value.shape[1]
            for s in range(fold):
                stage[slot, :, s * lanes : (s + 1) * lanes] = value[s * rows // fold : (s + 1) * rows // fold]
            dst = heads.at[i_z * 2 + (i_c ^ b)]
            if n == 1 and k == 0:
                locals_.append(pltpu.make_async_copy(stage.at[slot], dst, sem.at[2 * images + b]))
                locals_[-1].start()
            else:
                arrivals.append(link(stage.at[slot], dst, {"g": image, "p": i_p ^ k}))

    arrivals = []
    others = []
    for n, image in enumerate(turns):
        loads[n].wait()
        crossed[n].wait_recv()
        grad_two = gn_own[image] + gn_came[image]
        grad_out = branch[image].astype(F32)
        grad_norm, normal = norm_back(mid[image], gain[...], grad_two)
        grad = grad_out + grad_norm
        grad_mid[image] = grad
        back_own[image] = grad.astype(BF)
        others.append(link(back_own.at[image], back_other.at[image], core))
        sums[0:1, :] += jnp.sum(grad_two * normal, 0, keepdims=True)
        sums[1:2, :] += jnp.sum(grad_two, 0, keepdims=True)
        sums[2:3, :] += jnp.sum(back_own[image].astype(F32), 0, keepdims=True)
        sums[3:4, :] += jnp.sum(grad_out, 0, keepdims=True)
        if n == 0:
            proj.wait()
        give(n, 0)
    outs = []
    for n, image in enumerate(turns):
        others[n].wait_recv()
        give(n, 1)
        outs.append(link(half(out, 1, image), out_came.at[image], core))
        loads.append(pltpu.make_async_copy(half(out, 0, image), out_own.at[image], sem.at[images + n]))
        loads[-1].start()
    for p in range(np_):
        total = None
        for b, source in ((0, back_own), (1, back_other)):
            for image in range(images):
                term = dot(mixed[p, b, image], source[image], TN)
                total = term if total is None else total + term
        grad_proj[p] = total.astype(BF)
    for n, image in enumerate(turns):
        loads[images + n].wait()
        outs[n].wait_recv()
        value = mid[image] + out_own[image] + out_came[image] + shift[...]
        output[image] = value.astype(BF)
    for copy in locals_:
        copy.wait()
    for copy in arrivals:
        copy.wait_recv()
    link.drain()


def turn(mid, gn, out, branch, gain, shift, w, mixed, sizes):
    dp, ng, np_ = sizes
    images, rows, width = mid.shape
    lanes = mixed.shape[4]
    fold = 2 if rows % 32 == 0 else 1
    chips = ng * np_
    vmem = pl.BlockSpec(memory_space=pltpu.VMEM)
    hbm = pl.BlockSpec(memory_space=pl.ANY)
    copies = 3 * images + 2 * (chips - 1)
    own = (images, rows, width)
    return pl.pallas_call(
        partial(turn_kernel, sizes),
        in_specs=[vmem, hbm, hbm, vmem, vmem, vmem, hbm, vmem],
        out_specs=[vmem, vmem, hbm, vmem, vmem],
        out_shape=[
            jax.ShapeDtypeStruct(own, BF),
            jax.ShapeDtypeStruct(own, F32),
            jax.ShapeDtypeStruct((chips * 2, rows // fold, lanes * fold), BF),
            jax.ShapeDtypeStruct((np_, lanes, width), BF),
            jax.ShapeDtypeStruct((8, width), F32),
        ],
        scratch_shapes=[
            pltpu.VMEM((dp, w.shape[1] // 5, width), BF),
            pltpu.VMEM(own, BF),
            pltpu.VMEM(own, BF),
            pltpu.VMEM(own, F32),
            pltpu.VMEM(own, F32),
            pltpu.VMEM(own, F32),
            pltpu.VMEM(own, F32),
            pltpu.VMEM((chips * 2, rows // fold, lanes * fold), BF),
            pltpu.SemaphoreType.DMA((2 * images + 3,)),
            pltpu.SemaphoreType.DMA((copies,)),
            pltpu.SemaphoreType.DMA((copies,)),
        ],
        compiler_params=pltpu.CompilerParams(collective_id=3, has_side_effects=True, vmem_limit_bytes=56 << 20),
        cost_estimate=FREE,
        name="turn",
    )(mid, gn, out, branch, gain, shift, w, mixed)


def flip(value, axis, size, bit):
    return lax.ppermute(value, axis, [(i, i ^ bit) for i in range(size)])


def pick(value, index, axis=0):
    return lax.dynamic_index_in_dim(value, index, axis, keepdims=False)


def gather_pieces(value, axis, size, me):
    full = jnp.zeros((size,) + value.shape, value.dtype)
    full = lax.dynamic_update_index_in_dim(full, value, me, 0)
    for bit in range(1, size):
        full = lax.dynamic_update_index_in_dim(full, flip(value, axis, size, bit), me ^ bit, 0)
    return full


def scatter_sum(value, axis, size, me):
    total = pick(value, me).astype(F32)
    for bit in range(1, size):
        total = total + flip(pick(value, me ^ bit), axis, size, bit).astype(F32)
    return total


def tie(*values):
    return lax.optimization_barrier(values)


def after(value, *others):
    return tie(value, *others)[0]


def on_device(
    patches,
    ln1_gain,
    ln1_bias,
    qkv_weight,
    q_bias,
    v_bias,
    proj_weight,
    proj_bias,
    ln2_gain,
    ln2_bias,
    fc1_weight,
    fc1_bias,
    fc2_weight,
    fc2_bias,
    rel_pos_h,
    rel_pos_w,
    cotangent,
):
    images, row_count, width = patches.shape
    dp, ng, np_, nc = (lax.axis_size(name) for name in ("dp", "g", "p", "c"))
    i_dp, i_g, i_p, i_c = (lax.axis_index(name) for name in ("dp", "g", "p", "c"))
    chips = ng * np_
    i_z = i_g * np_ + i_p
    ranks = chips * nc
    seq_len = ranks * row_count
    own_rows = images * row_count
    heads = H * images // ranks
    shard_heads = H // dp
    core_heads = shard_heads // nc
    piece = core_heads * HD
    pieces = heads // core_heads
    lanes = heads * HD
    hidden = fc1_weight.shape[1]
    unit = hidden // ranks
    shard = width // dp
    per = hidden // dp // (nc * unit)
    side = (rel_pos_h.shape[0] + 1) // 2

    core_bias = pick(fc1_bias.reshape(per, nc, 2, unit // 2), i_c, 1).transpose(1, 0, 2)
    packed = jnp.concatenate(
        [
            jnp.stack([ln1_gain, ln1_bias, q_bias, v_bias, proj_bias, ln2_gain, ln2_bias, fc2_bias]),
            core_bias.reshape(-1, shard),
        ]
    )
    spot = jnp.stack([i_g, i_p, i_c])
    qkv_own, slab_a, slab_b = select(spot, qkv_weight, fc1_weight, fc2_weight, proj_weight, ng, np_, nc, lanes)
    weights_a = lax.all_gather(slab_a, "dp", axis=0)
    weights_b = lax.all_gather(slab_b, "dp", axis=0)
    raw, qkv_full, vectors = start_exchange(patches, qkv_own, packed, (dp, ng, np_))
    qkv_full = qkv_full.reshape(width, 3 * lanes)
    vectors = vectors.astype(F32)
    whole_vec = vectors.transpose(1, 0, 2).reshape(-1, width)
    gain_one, shift_one, q_shift, v_shift, proj_shift, gain_two, shift_two, fc2_shift = whole_vec[:8]
    fc1_shift = vectors[:, 8:].reshape(dp, 2, -1).transpose(1, 0, 2).reshape(2, 1, -1)

    starts = [
        part * width + (i_p * pieces + q) * shard_heads * HD + i_c * piece
        for q in range(pieces)
        for part in range(3)
    ]
    zero = jnp.zeros((piece,), F32)
    biases = []
    for q in range(pieces):
        at = starts[3 * q]
        biases += [lax.dynamic_slice_in_dim(q_shift, at, piece, 0), zero]
        biases += [lax.dynamic_slice_in_dim(v_shift, at, piece, 0)]
    qkv_shift = jnp.concatenate(biases)[None]

    branch_own = cotangent.reshape(own_rows, width)
    branch_other = flip(branch_own, "c", nc, 1)

    tables = flip_tables(rel_pos_h, rel_pos_w)
    back_tables = flip_tables(rel_pos_h, rel_pos_w[::-1])
    token = lax.broadcasted_iota(jnp.int32, (side, seq_len), 1)
    column = lax.broadcasted_iota(jnp.int32, (side, seq_len), 0)
    col_hot = (token % side == side - 1 - column).astype(BF)
    normed, query, key_rows, value_rows = qkv_rows(
        raw, gain_one[None], shift_one[None], qkv_full, qkv_shift, tables, pieces, core_heads, side
    )
    far_att, att_f, query_a = attend(i_g ^ 1, query, key_rows, value_rows, side, ng)
    far_att = far_att.reshape(np_, nc * row_count, lanes)
    arrived = {}
    for bit_p in range(np_):
        arrived[1, bit_p] = flip(pick(far_att, i_p ^ bit_p), ("g", "p"), chips, np_ + bit_p)
    near_att, att_f, query_a = attend(i_g, query, key_rows, value_rows, side, ng, (att_f, query_a))
    near_att, *pinned = tie(near_att, *[arrived[1, k] for k in range(np_)])
    for k in range(np_):
        arrived[1, k] = pinned[k]
    near_att = near_att.reshape(np_, nc * row_count, lanes)
    sizes = (dp, ng, np_)
    middle, two_own, two_other, mixed = middle_rows(
        near_att,
        [arrived[1, k] for k in range(np_)],
        weights_a,
        patches,
        proj_shift[None],
        gain_two[None],
        shift_two[None],
        sizes,
    )
    two_own, two_other = two_own.reshape(own_rows, width), two_other.reshape(own_rows, width)

    def over_dp(value):
        return lax.psum_scatter(value.reshape(-1, value.shape[-1]), "dp", scatter_dimension=0, tiled=True)

    out_a, back_a, grads_a, bias_a = mlp_half(
        two_own, two_other, branch_own, branch_other, weights_a, fc1_shift[0]
    )
    sum_a = over_dp(grads_a)
    out_b, back_b, grads_b, bias_b = mlp_half(
        two_own, two_other, branch_own, branch_other, weights_b, fc1_shift[1], (out_a, back_a)
    )
    output, grad_middle, grad_heads, grad_proj, early = turn(
        middle, back_b, out_b, cotangent, gain_two[None], fc2_shift[None], weights_a, mixed, sizes
    )
    sum_b = over_dp(grads_b)
    sum_p = over_dp(grad_proj.reshape(dp, piece, width))

    def pieces_over_chips(value):
        blocks = split_columns(value, i_z, chips)
        return [blocks[0]] + [flip(blocks[bit], ("g", "p"), chips, bit) for bit in range(1, chips)]

    grad_heads, sum_a = tie(grad_heads, sum_a)
    sum_a = pieces_over_chips(sum_a)
    dx = []
    grad_tables = []
    for q in range(pieces):
        rows, table, output = attend_back(
            q * core_heads, core_heads, query_a, key_rows, value_rows, att_f, grad_heads, back_tables, col_hot, output, side
        )
        if q == 0:
            rows, *sum_a = tie(rows, *sum_a)
            sum_b = pieces_over_chips(after(sum_b, rows))
            key_rows = after(key_rows, rows)
        elif q == 1:
            rows, *sum_b = tie(rows, *sum_b)
        dx.append(rows)
        grad_tables.append(table)
    dx[-1], sum_p = tie(dx[-1], sum_p)

    bias_half = jnp.stack([bias_a.reshape(dp, per, unit // 2), bias_b.reshape(dp, per, unit // 2)], 2)
    bias_half = bias_half.reshape(dp * per, 1, unit)
    bias_full = jnp.concatenate([bias_half] * nc, 1)
    core = lax.broadcasted_iota(jnp.int32, bias_full.shape, 1)
    bias_full = jnp.where(core == i_c, bias_full, 0.0).reshape(dp, -1, shard)
    early = jnp.concatenate([early[:4], bias_full.transpose(1, 0, 2).reshape(-1, width)])
    grad_patches, out_qkv, vec, rel, out_fc1, out_fc2, out_proj = finish(
        raw,
        normed,
        dx,
        grad_tables,
        qkv_full,
        patches,
        grad_middle,
        gain_one[None],
        early,
        sum_p,
        (sum_a, sum_b),
        sizes,
        piece,
    )
    entries = rel_pos_h.shape[0]
    rel = [rel[:entries, :HD][::-1], rel[128 : 128 + entries, :HD]]
    fc1_vec = vec[8:12].reshape(-1)
    out_fc2, out_proj = out_fc2.T, out_proj.T

    return (
        output,
        grad_patches,
        vec[0],
        vec[1],
        out_qkv,
        vec[2],
        vec[3],
        out_proj,
        vec[6],
        vec[4],
        vec[5],
        out_fc1,
        fc1_vec,
        out_fc2,
        vec[7],
        rel[0],
        rel[1],
    )


def solution(mesh):
    dp, ranks = mesh.shape["dp"], mesh.shape["seq"]

    def call(*args):
        images = args[0].shape[0] // dp
        shape = (dp, images, ranks // images // 2, 2)
        fine = jax.sharding.Mesh(mesh.devices.reshape(shape), ("dp", "g", "p", "c"))
        seq = ("g", "p", "c")
        tokens, rows, both = P("dp", seq, None), P("dp", None), P("dp", seq)
        vec = P("dp")
        return jax.shard_map(
            on_device,
            mesh=fine,
            in_specs=(
                tokens, vec, vec, rows, vec, vec, rows, vec, vec, vec, rows, vec, rows, vec, P(), P(), tokens
            ),
            out_specs=(
                tokens, tokens, vec, vec, both, vec, vec, both, vec, vec, vec, both, vec, both, vec, P(), P()
            ),
            check_vma=False,
        )(*args)

    return call
```
